256 devices in a mesh: grp: 8 (over x, core), slab: 32 (over y, z).
Axes of the slice: x: 4, y: 4, z: 8, core: 2. Of those that a mesh axis runs over, the one named last changes fastest.
Arguments:
- images: bfloat16 [8192, 16384], P(('grp', 'slab')), may hold values from -40 to 40
- image_class: int32 [8192], P(('grp', 'slab')), may hold values from 0 to 31, as said below
- image_ctf: int32 [8192], P(('grp', 'slab')), may hold values from 0 to 63
- class_owner: int32 [32], replicated, may hold values from 0 to 31, as said below
- references: bfloat16 [32, 16384], P('slab'), may hold values from -4 to 4
- ctf_table: bfloat16 [64, 8192], replicated, may hold values from -1.01 to 1.01
- x_base: int32 [32, 64], replicated, may hold values from 0 to 254
- y_base: int32 [32, 64], replicated, may hold values from 0 to 254
- x_frac: float32 [32, 64], replicated, may hold values from 0 to 1
- y_frac: float32 [32, 64], replicated, may hold values from 0 to 1
- z_offset: int32 [32, 128], replicated, may hold values from -1 to 1
- z_frac: float32 [32, 128], replicated, may hold values from 0 to 1
Outputs:
- volume: float32 [3, 256, 256, 256], P(None, 'slab', 'grp')
The draws below stay inside these ranges and needn't reach their ends.
Inputs may be any that keep to these rules, and one draw needn't show every extreme that they name: `image_class`: among the 32 images of one device (aligned blocks of rows) at most 4 name one class, and in every block some class is named by exactly 4. `class_owner`: every index of slab owns exactly one class.
All inputs are finite; a program needn't handle non-finite values.
Results may differ from the reference program's by a relative error of at most 0.014.
Values may be sent and summed in bfloat16 or wider, within the bound.
A program may use at most 128 MiB of HBM per device.

```python
import math
import jax
import jax.numpy as jnp
from jax import lax

ROWS = 128
HALF = 64
SHIFTS = 128
CTF_GROUPS = 64
IMG_DEV = 32
PIX = 8192
VOL = 256
CLASSES = 32
CAP = 4
IMAGES = 8192
BAND = 4
Z_DEV = 8
N_GRP = 8
N_SLAB = 32


def owner_table(key):
    return jax.random.permutation(jax.random.fold_in(key, 101), CLASSES).astype(jnp.int32)


def class_table(key):
    base_key = jax.random.fold_in(key, 202)
    favour_key, noise_key, full_key, order_key = jax.random.split(base_key, 4)
    blocks = IMAGES // IMG_DEV
    slot_count = CLASSES * CAP
    slot_class = jnp.repeat(jnp.arange(CLASSES, dtype=jnp.int32), CAP)
    favour = jax.random.randint(favour_key, (CLASSES,), 0, 3, dtype=jnp.int32)
    noise_rank = jax.random.randint(noise_key, (blocks, slot_count), 0, 48, dtype=jnp.int32)
    filled = jax.random.randint(full_key, (blocks,), 0, CLASSES, dtype=jnp.int32)
    scores = favour[slot_class][None, :] * 32 + noise_rank
    scores = jnp.where(slot_class[None, :] == filled[:, None], 4096, scores)
    scores = scores * slot_count + jnp.arange(slot_count, dtype=jnp.int32)[None, :]
    picked = lax.top_k(scores, IMG_DEV)[1]
    chosen = slot_class[picked]
    shuffle_keys = jax.random.randint(order_key, (blocks, IMG_DEV), 0, 1 << 20, dtype=jnp.int32) * IMG_DEV + jnp.arange(IMG_DEV, dtype=jnp.int32)[None, :]
    shuffle_order = jnp.argsort(shuffle_keys, axis=1, stable=True)
    return jnp.take_along_axis(chosen, shuffle_order, axis=1).reshape(IMAGES).astype(jnp.int32)


def transfer_groups(key):
    return jax.random.randint(jax.random.fold_in(key, 303), (IMAGES,), 0, CTF_GROUPS, dtype=jnp.int32)


def reference_table(key):
    return jnp.clip(jax.random.normal(jax.random.fold_in(key, 404), (CLASSES, 2 * PIX), jnp.float32), -4.0, 4.0)


def ctf_values(key):
    defocus_key, shift_key = jax.random.split(jax.random.fold_in(key, 505))
    freq_rows = (jnp.arange(ROWS) - ROWS // 2).astype(jnp.float32)
    freq_cols = jnp.arange(HALF).astype(jnp.float32)
    radius = ((freq_rows[:, None] * freq_rows[:, None] + freq_cols[None, :] * freq_cols[None, :]) / float(ROWS // 2 * (ROWS // 2))).reshape(PIX)
    defocus = jnp.exp(jax.random.uniform(defocus_key, (CTF_GROUPS, 1), jnp.float32, math.log(8.0), math.log(40.0)))
    offset = jax.random.uniform(shift_key, (CTF_GROUPS, 1), jnp.float32, 0.0, 0.3)
    phase_angle = defocus * radius[None, :] + offset
    return -(0.995 * jnp.sin(phase_angle) + 0.1 * jnp.cos(phase_angle)) * jnp.exp(-0.25 * radius[None, :])


def draw_class_owner(key, part):
    return owner_table(key)


def draw_image_class(key, part):
    return class_table(key)


def draw_image_ctf(key, part):
    return transfer_groups(key)


def draw_references(key, part):
    return reference_table(key).astype(jnp.bfloat16)


def draw_ctf_table(key, part):
    return ctf_values(key).astype(jnp.bfloat16)


def draw_images(key, part):
    frames = jnp.clip(jax.random.normal(jax.random.fold_in(key, 606), (IMAGES, 2 * PIX), jnp.float32), -5.0, 5.0)
    return frames.astype(jnp.bfloat16)


def place_ends(entries, stream_key, smallest, largest):
    longest = entries.shape.index(max(entries.shape))
    spots = []
    for shift in (0, 1):
        where = [jax.random.randint(jax.random.fold_in(stream_key, axis), (), 0, length) for axis, length in enumerate(entries.shape)]
        where[longest] = (where[longest] + shift) % entries.shape[longest]
        spots.append(tuple(where))
    return entries.at[spots[0]].set(smallest).at[spots[1]].set(largest)


def setup_inputs(seed: int = 0) -> dict:
    key_list = jax.random.split(jax.random.key(seed), 13)
    return {
        "images": draw_images(jax.random.fold_in(key_list[12], 71), 0),
        "image_class": draw_image_class(jax.random.fold_in(key_list[12], 71), 0),
        "image_ctf": draw_image_ctf(jax.random.fold_in(key_list[12], 71), 0),
        "class_owner": draw_class_owner(jax.random.fold_in(key_list[12], 71), 0),
        "references": draw_references(jax.random.fold_in(key_list[12], 71), 0),
        "ctf_table": draw_ctf_table(jax.random.fold_in(key_list[12], 71), 0),
        "x_base": place_ends(jax.random.randint(key_list[6], (CLASSES, HALF), 0, VOL - 1), jax.random.fold_in(key_list[6], 1), 0, (VOL - 1) - 1).astype(jnp.int32),
        "y_base": place_ends(jax.random.randint(key_list[7], (CLASSES, HALF), 0, VOL - 1), jax.random.fold_in(key_list[7], 1), 0, (VOL - 1) - 1).astype(jnp.int32),
        "x_frac": jnp.clip(jax.random.uniform(key_list[8], (CLASSES, HALF), jnp.float32, 0.0, 1.0), 0.0, 1.0),
        "y_frac": jnp.clip(jax.random.uniform(key_list[9], (CLASSES, HALF), jnp.float32, 0.0, 1.0), 0.0, 1.0),
        "z_offset": place_ends(jax.random.randint(key_list[10], (CLASSES, ROWS), -1, 2), jax.random.fold_in(key_list[10], 1), -1, 1).astype(jnp.int32),
        "z_frac": jnp.clip(jax.random.uniform(key_list[11], (CLASSES, ROWS), jnp.float32, 0.0, 1.0), 0.0, 1.0),
    }


def phase_table():
    shift_ids = jnp.arange(SHIFTS)
    shift_rows = (shift_ids // 8 - SHIFTS // 16).astype(jnp.float32)
    shift_cols = (shift_ids % 8 - 4).astype(jnp.float32)
    freq_rows = (jnp.arange(ROWS) - ROWS // 2).astype(jnp.float32)
    freq_cols = jnp.arange(HALF).astype(jnp.float32)
    angles = (freq_rows[None, :, None] * shift_rows[:, None, None] + freq_cols[None, None, :] * shift_cols[:, None, None]) * (2.0 * math.pi / ROWS)
    angles = angles.reshape(SHIFTS, ROWS * HALF)
    return jnp.concatenate([jnp.cos(angles), jnp.sin(angles)], axis=1).astype(jnp.bfloat16)

def align_frames(frames, ctf_rows, ref_rows, phase, score_scale):
    pixels = ctf_rows.shape[1]
    frame_re = frames[:, :pixels].astype(jnp.float32)
    frame_im = frames[:, pixels:].astype(jnp.float32)
    ref_re = ref_rows[:, :pixels].astype(jnp.float32)
    ref_im = ref_rows[:, pixels:].astype(jnp.float32)
    weight = ctf_rows.astype(jnp.float32)
    cross_terms = jnp.concatenate([weight * (ref_re * frame_re + ref_im * frame_im), weight * (ref_re * frame_im - ref_im * frame_re)], axis=1).astype(jnp.bfloat16)
    scores = score_scale * jnp.dot(cross_terms, phase.T, preferred_element_type=jnp.float32)
    shift_probs = jax.nn.softmax(scores, axis=1).astype(jnp.bfloat16)
    shift_mix = jnp.dot(shift_probs, phase, preferred_element_type=jnp.float32)
    mix_re = shift_mix[:, :pixels]
    mix_im = shift_mix[:, pixels:]
    return jnp.concatenate([weight * (frame_re * mix_re + frame_im * mix_im), weight * (frame_im * mix_re - frame_re * mix_im), weight * weight], axis=1)

def reference(images, image_class, image_ctf, class_owner, references, ctf_table, x_base, y_base, x_frac, y_frac, z_offset, z_frac):
    phase = phase_table()
    score_scale = 2.0 / math.sqrt(2.0 * PIX)
    data_scale = 1.0 / math.sqrt(IMG_DEV * N_GRP)
    weight_scale = 1.0 / (IMG_DEV * N_GRP)
    channel_scale = jnp.concatenate([jnp.full((2 * PIX,), data_scale, jnp.float32), jnp.full((PIX,), weight_scale, jnp.float32)])
    per_group = N_SLAB * IMG_DEV
    frames = images.reshape(N_GRP, per_group, 2 * PIX)
    classes = image_class.reshape(N_GRP, per_group)
    ctf_indices = image_ctf.reshape(N_GRP, per_group)

    def group_sums(inputs):
        group_frames, group_classes, group_ctf = inputs
        ref_rows = references[class_owner[group_classes]]
        ctf_rows = ctf_table[group_ctf]
        stacked = align_frames(group_frames, ctf_rows, ref_rows, phase, score_scale)
        member = (group_classes[None, :] == jnp.arange(CLASSES, dtype=jnp.int32)[:, None]).astype(jnp.float32)
        totals = jnp.dot(member, stacked, precision=lax.Precision.HIGHEST, preferred_element_type=jnp.float32)
        return (totals * channel_scale[None, :]).astype(jnp.bfloat16)
    class_sums = lax.optimization_barrier(lax.map(group_sums, (frames, classes, ctf_indices)))
    planes = Z_DEV + 2
    row_local = jnp.arange(ROWS, dtype=jnp.int32) % BAND
    target = 2 * row_local[None, :] + z_offset + 1
    plane_ids = jnp.arange(planes, dtype=jnp.int32)
    depth_weight = jnp.where(plane_ids[None, None, :] == target[:, :, None], (1.0 - z_frac)[:, :, None], 0.0)
    depth_weight = depth_weight + jnp.where(plane_ids[None, None, :] == target[:, :, None] + 1, z_frac[:, :, None], 0.0)
    depth_weight = depth_weight.astype(jnp.float32).reshape(CLASSES, N_SLAB, BAND, planes)
    y_low = lax.optimization_barrier((1.0 - y_frac).astype(jnp.bfloat16))
    y_high = lax.optimization_barrier(y_frac.astype(jnp.bfloat16))
    x_low = lax.optimization_barrier((1.0 - x_frac).astype(jnp.bfloat16))
    x_high = lax.optimization_barrier(x_frac.astype(jnp.bfloat16))
    corners = [(y_base, y_low, x_base, x_low), (y_base, y_low, x_base + 1, x_high), (y_base + 1, y_high, x_base, x_low), (y_base + 1, y_high, x_base + 1, x_high)]

    def insert_group(running, group_class_sums):
        shaped = group_class_sums.reshape(CLASSES, 3, N_SLAB, BAND, HALF).astype(jnp.float32)
        sectioned = jnp.einsum('cksra,csrj->cksaj', shaped, depth_weight, precision=lax.Precision.HIGHEST)
        partial_volume = jnp.zeros((VOL, VOL, N_SLAB, 3, planes), jnp.float32)
        for rows_at, row_weight, cols_at, col_weight in corners:
            lifted = (row_weight[:, None, None, :, None].astype(jnp.float32) * sectioned).astype(jnp.bfloat16)
            lifted = lax.optimization_barrier(lifted)
            values = lifted.astype(jnp.float32) * col_weight[:, None, None, :, None].astype(jnp.float32)
            values = values.transpose(0, 3, 2, 1, 4).reshape(CLASSES * HALF, N_SLAB, 3, planes)
            partial_volume = partial_volume.at[rows_at.reshape(-1), cols_at.reshape(-1)].add(values)
        rounded = lax.optimization_barrier(partial_volume.astype(jnp.bfloat16)).astype(jnp.float32)
        slab_volume = rounded[:, :, :, :, 1:planes - 1]
        slab_volume = slab_volume.at[:, :, :-1, :, Z_DEV - 1].add(rounded[:, :, 1:, :, 0])
        slab_volume = slab_volume.at[:, :, 1:, :, 0].add(rounded[:, :, :-1, :, planes - 1])
        return (running + slab_volume, None)
    running, _ = lax.scan(insert_group, jnp.zeros((VOL, VOL, N_SLAB, 3, Z_DEV), jnp.float32), class_sums)
    return running.transpose(3, 2, 4, 0, 1).reshape(3, VOL, VOL, VOL)
```

```python
import math

import jax
import jax.numpy as jnp
from jax import lax
from jax.experimental import pallas as pl
from jax.experimental.pallas import tpu as pltpu
from jax.sharding import PartitionSpec as P

SHIFTS = 128


def padded_2(x, sides, width):
    for axis, dim in sides:
        devices, length = (lax.axis_size(axis), x.shape[dim])
        up = [(i, (i + 1) % devices) for i in range(devices - 1)]
        down = [(j, i) for i, j in up]
        last = lax.slice_in_dim(x, length - width, length, axis=dim)
        first = lax.slice_in_dim(x, 0, width, axis=dim)
        before = lax.ppermute(last, axis, up)
        after = lax.ppermute(first, axis, down)
        x = jnp.concatenate([before, x, after], axis=dim)
    return x


def phase_table(row_count, half_cols):
    shift_ids = jnp.arange(SHIFTS)
    shift_rows = (shift_ids // 8 - SHIFTS // 16).astype(jnp.float32)
    shift_cols = (shift_ids % 8 - 4).astype(jnp.float32)
    freq_rows = (jnp.arange(row_count) - row_count // 2).astype(jnp.float32)
    freq_cols = jnp.arange(half_cols).astype(jnp.float32)
    angles = (
        freq_rows[None, :, None] * shift_rows[:, None, None]
        + freq_cols[None, None, :] * shift_cols[:, None, None]
    ) * (2.0 * math.pi / row_count)
    angles = angles.reshape(SHIFTS, row_count * half_cols)
    return jnp.concatenate([jnp.cos(angles), jnp.sin(angles)], axis=1).astype(jnp.bfloat16)


def align_frames(frames, ctf_rows, ref_rows, phase, score_scale):
    pixels = ctf_rows.shape[1]
    frame_re = frames[:, :pixels].astype(jnp.float32)
    frame_im = frames[:, pixels:].astype(jnp.float32)
    ref_re = ref_rows[:, :pixels].astype(jnp.float32)
    ref_im = ref_rows[:, pixels:].astype(jnp.float32)
    weight = ctf_rows.astype(jnp.float32)
    cross_terms = jnp.concatenate(
        [
            weight * (ref_re * frame_re + ref_im * frame_im),
            weight * (ref_re * frame_im - ref_im * frame_re),
        ],
        axis=1,
    ).astype(jnp.bfloat16)
    scores = score_scale * jnp.einsum(
        "np,sp->ns", cross_terms, phase, preferred_element_type=jnp.float32
    )
    shift_probs = jax.nn.softmax(scores, axis=1).astype(jnp.bfloat16)
    shift_mix = jnp.dot(shift_probs, phase, preferred_element_type=jnp.float32)
    mix_re = shift_mix[:, :pixels]
    mix_im = shift_mix[:, pixels:]
    return jnp.concatenate(
        [
            weight * (frame_re * mix_re + frame_im * mix_im),
            weight * (frame_im * mix_re - frame_re * mix_im),
            weight * weight,
        ],
        axis=1,
    )


def stencil_weights(base_cell, fraction, side_cells):
    cell_ids = jnp.arange(side_cells, dtype=jnp.int32)
    dense_weight = jnp.where(
        cell_ids[None, None, :] == base_cell[:, :, None], (1.0 - fraction)[:, :, None], 0.0
    )
    dense_weight = dense_weight + jnp.where(
        cell_ids[None, None, :] == base_cell[:, :, None] + 1, fraction[:, :, None], 0.0
    )
    return dense_weight.astype(jnp.bfloat16)


def local(
    images,
    image_class,
    image_ctf,
    class_owner,
    references,
    ctf_table,
    x_base,
    y_base,
    x_frac,
    y_frac,
    z_offset,
    z_frac,
):
    slab_count = lax.axis_size("slab")
    group_count = lax.axis_size("grp")
    frame_count = images.shape[0]
    pixels = ctf_table.shape[1]
    groups_ctf = ctf_table.shape[0]
    row_count = z_offset.shape[1]
    half_cols = x_base.shape[1]
    class_count = class_owner.shape[0]
    side_cells = 2 * row_count
    band_rows = row_count // slab_count
    plane_count = 2 * band_rows + 2
    phase = phase_table(row_count, half_cols)
    score_scale = 2.0 / math.sqrt(2.0 * pixels)
    channel_scale = jnp.array(
        [
            1.0 / math.sqrt(frame_count * group_count),
            1.0 / math.sqrt(frame_count * group_count),
            1.0 / (frame_count * group_count),
        ],
        jnp.float32,
    )
    class_ids = jnp.arange(class_count, dtype=jnp.int32)
    owner_of = jnp.sum(
        jnp.where(image_class[:, None] == class_ids[None, :], class_owner[None, :], 0), axis=1
    )
    capacity = max(4, 2 * frame_count // slab_count)
    frame_ids = jnp.arange(frame_count, dtype=jnp.int32)
    earlier = (owner_of[None, :] == owner_of[:, None]) & (frame_ids[None, :] < frame_ids[:, None])
    slot_rank = jnp.sum(earlier.astype(jnp.int32), axis=1)
    slot_index = owner_of * capacity + slot_rank
    placed = slot_index[None, :] == jnp.arange(slab_count * capacity, dtype=jnp.int32)[:, None]
    outgoing = jnp.dot(
        placed.astype(jnp.bfloat16), images, preferred_element_type=jnp.float32
    ).astype(jnp.bfloat16)
    outgoing = outgoing.reshape(slab_count, capacity, 2 * pixels)
    slot_ctf = jnp.sum(jnp.where(placed, image_ctf[None, :], 0), axis=1)
    slot_valid = jnp.sum(placed.astype(jnp.int32), axis=1)
    details = jnp.stack([slot_ctf, slot_valid], axis=1).reshape(slab_count, capacity, 2)
    own_ref = references[0]
    frames = lax.all_to_all(outgoing, "slab", split_axis=0, concat_axis=0, tiled=True)
    slot_info = lax.all_to_all(details, "slab", split_axis=0, concat_axis=0, tiled=True)
    sources = frames.shape[0]
    item_count = frames.shape[1]
    flat_frames = frames.reshape(sources * item_count, 2 * pixels)
    group_ids = slot_info[:, :, 0].reshape(sources * item_count)
    used_rows = slot_info[:, :, 1].reshape(sources * item_count).astype(jnp.float32)
    chosen = (group_ids[:, None] == jnp.arange(groups_ctf, dtype=jnp.int32)[None, :]).astype(
        jnp.bfloat16
    )
    ctf_rows = jnp.dot(chosen, ctf_table, preferred_element_type=jnp.float32).astype(jnp.bfloat16)
    ref_rows = jnp.broadcast_to(own_ref[None, :], flat_frames.shape)
    stacked = align_frames(flat_frames, ctf_rows, ref_rows, phase, score_scale) * used_rows[:, None]
    per_item = jnp.sum(stacked.reshape(sources, item_count, 3 * pixels), axis=0)
    totals = jnp.sum(per_item, axis=0).reshape(3, pixels) * channel_scale[:, None]
    totals = lax.psum(totals, "grp")
    padded_rows = jnp.pad(
        totals.reshape(3, row_count, half_cols), ((0, 0), (band_rows, band_rows), (0, 0))
    ).reshape(3, slab_count + 2, band_rows, half_cols)
    outgoing_bands = jnp.stack(
        [padded_rows[:, k : k + slab_count] for k in range(3)], axis=2
    ).astype(jnp.bfloat16)
    outgoing_bands = outgoing_bands.transpose(1, 0, 2, 3, 4).reshape(
        slab_count, 3, 3 * band_rows, half_cols
    )
    arrived = lax.all_to_all(outgoing_bands, "slab", split_axis=0, concat_axis=0, tiled=True)
    owned_by = (class_owner[:, None] == jnp.arange(slab_count, dtype=jnp.int32)[None, :]).astype(
        jnp.bfloat16
    )
    class_bands = jnp.dot(
        owned_by,
        arrived.reshape(slab_count, 3 * 3 * band_rows * half_cols),
        preferred_element_type=jnp.float32,
    ).reshape(class_count, 3, 3 * band_rows, half_cols)
    slab_index = lax.axis_index("slab")
    group_index = lax.axis_index("grp")
    z_dev = 2 * band_rows
    offset_pad = jnp.pad(z_offset, ((0, 0), (band_rows, band_rows)))
    frac_pad = jnp.pad(z_frac, ((0, 0), (band_rows, band_rows)))
    local_offset = lax.dynamic_slice_in_dim(offset_pad, slab_index * band_rows, 3 * band_rows, 1)
    local_frac = lax.dynamic_slice_in_dim(frac_pad, slab_index * band_rows, 3 * band_rows, 1)
    row_ids = jnp.arange(3 * band_rows, dtype=jnp.int32)
    band_shift = (row_ids // band_rows - 1) * z_dev - 1
    target = 2 * (row_ids % band_rows)[None, :] + local_offset + 1 + band_shift[None, :]
    plane_ids = jnp.arange(z_dev, dtype=jnp.int32)
    depth_weight = jnp.where(
        plane_ids[None, None, :] == target[:, :, None], (1.0 - local_frac)[:, :, None], 0.0
    )
    depth_weight = depth_weight + jnp.where(
        plane_ids[None, None, :] == target[:, :, None] + 1, local_frac[:, :, None], 0.0
    )
    sectioned = jnp.einsum(
        "ckra,crz->kzca",
        class_bands,
        depth_weight,
        precision=lax.Precision.HIGHEST,
    ).reshape(3 * z_dev, class_count * half_cols)
    y_rows = side_cells // group_count
    y_ids = group_index * y_rows + jnp.arange(y_rows, dtype=jnp.int32)
    row_weights = jnp.where(
        y_ids[:, None, None] == y_base[None, :, :], (1.0 - y_frac)[None, :, :], 0.0
    )
    row_weights = row_weights + jnp.where(
        y_ids[:, None, None] == y_base[None, :, :] + 1, y_frac[None, :, :], 0.0
    )
    row_weights = row_weights.astype(jnp.bfloat16).reshape(y_rows, class_count * half_cols)
    col_weights = stencil_weights(x_base, x_frac, side_cells).reshape(
        class_count * half_cols, side_cells
    )
    inserted = insert_planes(row_weights, sectioned, col_weights)
    return inserted.reshape(3, z_dev, y_rows, side_cells)


def insert_kernel(rows_ref, sec_ref, cols_ref, out_ref):
    def body(i, carry):
        lifted = (
            rows_ref[...].astype(jnp.float32) * sec_ref[pl.ds(i, 1), :]
        ).astype(jnp.bfloat16)
        out_ref[i] = jnp.dot(lifted, cols_ref[...], preferred_element_type=jnp.float32)
        return carry

    lax.fori_loop(0, sec_ref.shape[0], body, 0)


def insert_planes(row_weights, sectioned, col_weights):
    planes = sectioned.shape[0]
    y_rows, depth = row_weights.shape
    side = col_weights.shape[1]
    return pl.pallas_call(
        insert_kernel,
        out_shape=jax.ShapeDtypeStruct((planes, y_rows, side), jnp.float32),
        in_specs=[pl.BlockSpec(memory_space=pltpu.VMEM)] * 3,
        out_specs=pl.BlockSpec(memory_space=pltpu.VMEM),
        cost_estimate=pl.CostEstimate(
            flops=2 * planes * y_rows * depth * side,
            transcendentals=0,
            bytes_accessed=2 * y_rows * depth + 4 * planes * depth + 2 * depth * side
            + 4 * planes * y_rows * side,
        ),
    )(row_weights, sectioned, col_weights)


def solution(mesh):
    in_specs = (
        P(("grp", "slab"), None),
        P(("grp", "slab")),
        P(("grp", "slab")),
        P(),
        P("slab", None),
        P(),
        P(),
        P(),
        P(),
        P(),
        P(),
        P(),
    )
    out_specs = P(None, "slab", "grp", None)
    return jax.shard_map(local, mesh=mesh, in_specs=in_specs, out_specs=out_specs, check_vma=False)
```

```python
import math

import jax
import jax.numpy as jnp
from jax import lax
from jax.experimental import pallas as pl
from jax.experimental.pallas import tpu as pltpu
from jax.sharding import PartitionSpec as P

SHIFTS = 128


def phase_table(row_count, half_cols):
    shift_ids = jnp.arange(SHIFTS)
    shift_rows = (shift_ids // 8 - SHIFTS // 16).astype(jnp.float32)
    shift_cols = (shift_ids % 8 - 4).astype(jnp.float32)
    freq_rows = (jnp.arange(row_count) - row_count // 2).astype(jnp.float32)
    freq_cols = jnp.arange(half_cols).astype(jnp.float32)
    step = 2.0 * math.pi / row_count
    row_angle = shift_rows[:, None] * freq_rows[None, :] * step
    col_angle = shift_cols[:, None] * freq_cols[None, :] * step
    cos_r, sin_r = jnp.cos(row_angle)[:, :, None], jnp.sin(row_angle)[:, :, None]
    cos_c, sin_c = jnp.cos(col_angle)[:, None, :], jnp.sin(col_angle)[:, None, :]
    cos_t = (cos_r * cos_c - sin_r * sin_c).reshape(SHIFTS, row_count * half_cols)
    sin_t = (sin_r * cos_c + cos_r * sin_c).reshape(SHIFTS, row_count * half_cols)
    return jnp.concatenate([cos_t, sin_t], axis=1).astype(jnp.bfloat16)


def align_frames(frames, ctf_rows, ref_rows, phase, score_scale):
    pixels = ctf_rows.shape[1]
    frame_re = frames[:, :pixels].astype(jnp.float32)
    frame_im = frames[:, pixels:].astype(jnp.float32)
    ref_re = ref_rows[:, :pixels].astype(jnp.float32)
    ref_im = ref_rows[:, pixels:].astype(jnp.float32)
    weight = ctf_rows.astype(jnp.float32)
    cross_terms = jnp.concatenate(
        [
            weight * (ref_re * frame_re + ref_im * frame_im),
            weight * (ref_re * frame_im - ref_im * frame_re),
        ],
        axis=1,
    ).astype(jnp.bfloat16)
    scores = score_scale * jnp.einsum(
        "np,sp->ns", cross_terms, phase, preferred_element_type=jnp.float32
    )
    shift_probs = jax.nn.softmax(scores, axis=1).astype(jnp.bfloat16)
    shift_mix = jnp.dot(shift_probs, phase, preferred_element_type=jnp.float32)
    mix_re = shift_mix[:, :pixels]
    mix_im = shift_mix[:, pixels:]
    return jnp.concatenate(
        [
            weight * (frame_re * mix_re + frame_im * mix_im),
            weight * (frame_im * mix_re - frame_re * mix_im),
            weight * weight,
        ],
        axis=1,
    )


def stencil_weights(base_cell, fraction, side_cells):
    cell_ids = jnp.arange(side_cells, dtype=jnp.int32)
    dense_weight = jnp.where(
        cell_ids[None, None, :] == base_cell[:, :, None], (1.0 - fraction)[:, :, None], 0.0
    )
    dense_weight = dense_weight + jnp.where(
        cell_ids[None, None, :] == base_cell[:, :, None] + 1, fraction[:, :, None], 0.0
    )
    return dense_weight.astype(jnp.bfloat16)


def local(
    images,
    image_class,
    image_ctf,
    class_owner,
    references,
    ctf_table,
    x_base,
    y_base,
    x_frac,
    y_frac,
    z_offset,
    z_frac,
):
    slab_count = lax.axis_size("slab")
    group_count = lax.axis_size("grp")
    frame_count = images.shape[0]
    pixels = ctf_table.shape[1]
    groups_ctf = ctf_table.shape[0]
    row_count = z_offset.shape[1]
    half_cols = x_base.shape[1]
    class_count = class_owner.shape[0]
    side_cells = 2 * row_count
    band_rows = row_count // slab_count
    band_pixels = band_rows * half_cols
    z_dev = 2 * band_rows
    phase = phase_table(row_count, half_cols)
    score_scale = 2.0 / math.sqrt(2.0 * pixels)
    channel_scale = jnp.array(
        [
            1.0 / math.sqrt(frame_count * group_count),
            1.0 / math.sqrt(frame_count * group_count),
            1.0 / (frame_count * group_count),
        ],
        jnp.float32,
    )
    all_refs = lax.all_gather(references, "slab", axis=0, tiled=True)
    class_ids = jnp.arange(class_count, dtype=jnp.int32)
    owner_of = jnp.sum(
        jnp.where(image_class[:, None] == class_ids[None, :], class_owner[None, :], 0), axis=1
    )
    pick_ref = (owner_of[:, None] == jnp.arange(slab_count, dtype=jnp.int32)[None, :]).astype(
        jnp.bfloat16
    )
    ref_rows = jnp.dot(pick_ref, all_refs, preferred_element_type=jnp.float32).astype(
        jnp.bfloat16
    )
    pick_ctf = (image_ctf[:, None] == jnp.arange(groups_ctf, dtype=jnp.int32)[None, :]).astype(
        jnp.bfloat16
    )
    ctf_rows = jnp.dot(pick_ctf, ctf_table, preferred_element_type=jnp.float32).astype(
        jnp.bfloat16
    )
    stacked = align_frames(images, ctf_rows, ref_rows, phase, score_scale)
    member = (class_ids[:, None] == image_class[None, :]).astype(jnp.float32)
    partial = jnp.dot(
        member, stacked, precision=lax.Precision.HIGHEST, preferred_element_type=jnp.float32
    ).reshape(class_count, 3, pixels) * channel_scale[None, :, None]
    pieces = slab_count * group_count
    partial = partial.reshape(class_count, 3, pieces, pixels // pieces)
    piece = lax.psum_scatter(partial, ("slab", "grp"), scatter_dimension=2, tiled=True)
    band = lax.all_gather(piece, "grp", axis=2, tiled=True).reshape(
        class_count, 3, band_rows, half_cols
    )
    up = [(i, i + 1) for i in range(slab_count - 1)]
    down = [(i + 1, i) for i in range(slab_count - 1)]
    from_below = lax.ppermute(band[:, :, band_rows - 1 :], "slab", up)
    from_above = lax.ppermute(band[:, :, :1], "slab", down)
    class_bands = jnp.concatenate([from_below, band, from_above], axis=2)
    slab_index = lax.axis_index("slab")
    group_index = lax.axis_index("grp")
    offset_pad = jnp.pad(z_offset, ((0, 0), (1, 1)))
    frac_pad = jnp.pad(z_frac, ((0, 0), (1, 1)))
    rows_held = band_rows + 2
    local_offset = lax.dynamic_slice_in_dim(offset_pad, slab_index * band_rows, rows_held, 1)
    local_frac = lax.dynamic_slice_in_dim(frac_pad, slab_index * band_rows, rows_held, 1)
    row_ids = jnp.arange(rows_held, dtype=jnp.int32) + (band_rows - 1)
    band_shift = (row_ids // band_rows - 1) * z_dev - 1
    target = 2 * (row_ids % band_rows)[None, :] + local_offset + 1 + band_shift[None, :]
    plane_ids = jnp.arange(z_dev, dtype=jnp.int32)
    depth_weight = jnp.where(
        plane_ids[None, None, :] == target[:, :, None], (1.0 - local_frac)[:, :, None], 0.0
    )
    depth_weight = depth_weight + jnp.where(
        plane_ids[None, None, :] == target[:, :, None] + 1, local_frac[:, :, None], 0.0
    )
    sectioned = jnp.einsum(
        "ckra,crz->kzca",
        class_bands,
        depth_weight,
        precision=lax.Precision.HIGHEST,
    ).reshape(3 * z_dev, class_count * half_cols)
    y_rows = side_cells // group_count
    y_ids = group_index * y_rows + jnp.arange(y_rows, dtype=jnp.int32)
    row_weights = jnp.where(
        y_ids[:, None, None] == y_base[None, :, :], (1.0 - y_frac)[None, :, :], 0.0
    )
    row_weights = row_weights + jnp.where(
        y_ids[:, None, None] == y_base[None, :, :] + 1, y_frac[None, :, :], 0.0
    )
    row_weights = row_weights.astype(jnp.bfloat16).reshape(y_rows, class_count * half_cols)
    col_weights = stencil_weights(x_base, x_frac, side_cells).reshape(
        class_count * half_cols, side_cells
    )
    inserted = insert_planes(row_weights, sectioned, col_weights)
    return inserted.reshape(3, z_dev, y_rows, side_cells)


def insert_kernel(rows_ref, sec_ref, cols_ref, out_ref, lifted_ref):
    y_rows = rows_ref.shape[0]

    def body(i, carry):
        start = pl.multiple_of(i * y_rows, y_rows)
        lifted_ref[pl.ds(start, y_rows), :] = (
            rows_ref[...].astype(jnp.float32) * sec_ref[pl.ds(i, 1), :]
        ).astype(jnp.bfloat16)
        return carry

    lax.fori_loop(0, sec_ref.shape[0], body, 0)
    out_ref[...] = jnp.dot(lifted_ref[...], cols_ref[...], preferred_element_type=jnp.float32)


def insert_planes(row_weights, sectioned, col_weights):
    planes = sectioned.shape[0]
    y_rows, depth = row_weights.shape
    side = col_weights.shape[1]
    return pl.pallas_call(
        insert_kernel,
        out_shape=jax.ShapeDtypeStruct((planes * y_rows, side), jnp.float32),
        in_specs=[pl.BlockSpec(memory_space=pltpu.VMEM)] * 3,
        out_specs=pl.BlockSpec(memory_space=pltpu.VMEM),
        scratch_shapes=[pltpu.VMEM((planes * y_rows, depth), jnp.bfloat16)],
        cost_estimate=pl.CostEstimate(
            flops=2 * planes * y_rows * depth * side,
            transcendentals=0,
            bytes_accessed=2 * y_rows * depth + 4 * planes * depth + 2 * depth * side
            + 4 * planes * y_rows * side,
        ),
    )(row_weights, sectioned, col_weights)


def solution(mesh):
    in_specs = (
        P(("grp", "slab"), None),
        P(("grp", "slab")),
        P(("grp", "slab")),
        P(),
        P("slab", None),
        P(),
        P(),
        P(),
        P(),
        P(),
        P(),
        P(),
    )
    out_specs = P(None, "slab", "grp", None)
    return jax.shard_map(local, mesh=mesh, in_specs=in_specs, out_specs=out_specs, check_vma=False)
```

```python
import functools
import math

import jax
import jax.numpy as jnp
from jax import lax
from jax.experimental import pallas as pl
from jax.experimental.pallas import tpu as pltpu
from jax.sharding import PartitionSpec as P

SHIFTS = 128


def phase_table(row_count, half_cols):
    shift_ids = jnp.arange(SHIFTS)
    shift_rows = (shift_ids // 8 - SHIFTS // 16).astype(jnp.float32)
    shift_cols = (shift_ids % 8 - 4).astype(jnp.float32)
    lanes = 128
    per_lane_row = lanes // half_cols
    blocks = row_count * half_cols // lanes
    block_rows = (jnp.arange(blocks) * per_lane_row - row_count // 2).astype(jnp.float32)
    lane_ids = jnp.arange(lanes)
    lane_rows = (lane_ids // half_cols).astype(jnp.float32)
    lane_cols = (lane_ids % half_cols).astype(jnp.float32)
    step = 2.0 * math.pi / row_count
    block_angle = shift_rows[:, None] * block_rows[None, :] * step
    lane_angle = (
        shift_rows[:, None] * lane_rows[None, :] + shift_cols[:, None] * lane_cols[None, :]
    ) * step
    cos_b, sin_b = jnp.cos(block_angle)[:, :, None], jnp.sin(block_angle)[:, :, None]
    cos_l, sin_l = jnp.cos(lane_angle)[:, None, :], jnp.sin(lane_angle)[:, None, :]
    cos_t = (cos_b * cos_l - sin_b * sin_l).reshape(SHIFTS, row_count * half_cols)
    sin_t = (sin_b * cos_l + cos_b * sin_l).reshape(SHIFTS, row_count * half_cols)
    return jnp.concatenate([cos_t, sin_t], axis=1).astype(jnp.bfloat16)


def exchange_kernel(count, axis, other, same, x_ref, out_ref, local_sem, send_sems, recv_sems):
    me = lax.axis_index(axis)
    fixed = lax.axis_index(other)

    def device(peer):
        return (fixed, peer) if axis == "slab" else (peer, fixed)

    def block(peer):
        return x_ref.at[0] if same else x_ref.at[peer]

    barrier = pltpu.get_barrier_semaphore()
    for k in range(1, count):
        pl.semaphore_signal(
            barrier,
            1,
            device_id=device(lax.rem(me + k, count)),
            device_id_type=pl.DeviceIdType.MESH,
        )
    pl.semaphore_wait(barrier, count - 1)
    own = pltpu.make_async_copy(block(me), out_ref.at[me], local_sem)
    own.start()
    copies = []
    for k in range(1, count):
        peer = lax.rem(me + k, count)
        copy = pltpu.make_async_remote_copy(
            src_ref=block(peer),
            dst_ref=out_ref.at[me],
            send_sem=send_sems.at[k],
            recv_sem=recv_sems.at[k],
            device_id=device(peer),
            device_id_type=pl.DeviceIdType.MESH,
        )
        copy.start()
        copies.append(copy)
    own.wait()
    for copy in copies:
        copy.wait_send()
        copy.wait_recv()


def exchange(x, axis, other, same, collective_id):
    count = lax.axis_size(axis)
    shape = (count,) + x.shape[1:]
    return pl.pallas_call(
        functools.partial(exchange_kernel, count, axis, other, same),
        out_shape=jax.ShapeDtypeStruct(shape, x.dtype),
        in_specs=[pl.BlockSpec(memory_space=pltpu.VMEM)],
        out_specs=pl.BlockSpec(memory_space=pltpu.VMEM),
        scratch_shapes=[
            pltpu.SemaphoreType.DMA(()),
            pltpu.SemaphoreType.DMA((count,)),
            pltpu.SemaphoreType.DMA((count,)),
        ],
        compiler_params=pltpu.CompilerParams(collective_id=collective_id, has_side_effects=True),
    )(x)


def align_frames(frames, ctf_rows, ref_rows, phase, score_scale):
    pixels = ctf_rows.shape[1]
    frame_re = frames[:, :pixels].astype(jnp.float32)
    frame_im = frames[:, pixels:].astype(jnp.float32)
    ref_re = ref_rows[:, :pixels].astype(jnp.float32)
    ref_im = ref_rows[:, pixels:].astype(jnp.float32)
    weight = ctf_rows.astype(jnp.float32)
    cross_terms = jnp.concatenate(
        [
            weight * (ref_re * frame_re + ref_im * frame_im),
            weight * (ref_re * frame_im - ref_im * frame_re),
        ],
        axis=1,
    ).astype(jnp.bfloat16)
    scores = score_scale * jnp.einsum(
        "np,sp->ns", cross_terms, phase, preferred_element_type=jnp.float32
    )
    shift_probs = jax.nn.softmax(scores, axis=1).astype(jnp.bfloat16)
    shift_mix = jnp.dot(shift_probs, phase, preferred_element_type=jnp.float32)
    mix_re = shift_mix[:, :pixels]
    mix_im = shift_mix[:, pixels:]
    return jnp.concatenate(
        [
            weight * (frame_re * mix_re + frame_im * mix_im),
            weight * (frame_im * mix_re - frame_re * mix_im),
            weight * weight,
        ],
        axis=1,
    )


def stencil_weights(base_cell, fraction, side_cells):
    cell_ids = jnp.arange(side_cells, dtype=jnp.int32)
    dense_weight = jnp.where(
        cell_ids[None, None, :] == base_cell[:, :, None], (1.0 - fraction)[:, :, None], 0.0
    )
    dense_weight = dense_weight + jnp.where(
        cell_ids[None, None, :] == base_cell[:, :, None] + 1, fraction[:, :, None], 0.0
    )
    return dense_weight.astype(jnp.bfloat16)


def local(
    images,
    image_class,
    image_ctf,
    class_owner,
    references,
    ctf_table,
    x_base,
    y_base,
    x_frac,
    y_frac,
    z_offset,
    z_frac,
):
    slab_count = lax.axis_size("slab")
    group_count = lax.axis_size("grp")
    frame_count = images.shape[0]
    pixels = ctf_table.shape[1]
    groups_ctf = ctf_table.shape[0]
    row_count = z_offset.shape[1]
    half_cols = x_base.shape[1]
    class_count = class_owner.shape[0]
    side_cells = 2 * row_count
    band_rows = row_count // slab_count
    band_pixels = band_rows * half_cols
    z_dev = 2 * band_rows
    phase = phase_table(row_count, half_cols)
    score_scale = 2.0 / math.sqrt(2.0 * pixels)
    channel_scale = jnp.array(
        [
            1.0 / math.sqrt(frame_count * group_count),
            1.0 / math.sqrt(frame_count * group_count),
            1.0 / (frame_count * group_count),
        ],
        jnp.float32,
    )
    lanes = 128
    all_refs = exchange(
        references.reshape(1, -1, lanes), "slab", "grp", True, 0
    ).reshape(slab_count, 2 * pixels)
    class_ids = jnp.arange(class_count, dtype=jnp.int32)
    owner_of = jnp.sum(
        jnp.where(image_class[:, None] == class_ids[None, :], class_owner[None, :], 0), axis=1
    )
    pick_ref = (owner_of[:, None] == jnp.arange(slab_count, dtype=jnp.int32)[None, :]).astype(
        jnp.bfloat16
    )
    ref_rows = jnp.dot(pick_ref, all_refs, preferred_element_type=jnp.float32).astype(
        jnp.bfloat16
    )
    pick_ctf = (image_ctf[:, None] == jnp.arange(groups_ctf, dtype=jnp.int32)[None, :]).astype(
        jnp.bfloat16
    )
    ctf_rows = jnp.dot(pick_ctf, ctf_table, preferred_element_type=jnp.float32).astype(
        jnp.bfloat16
    )
    stacked = align_frames(images, ctf_rows, ref_rows, phase, score_scale)
    member = (class_ids[:, None] == image_class[None, :]).astype(jnp.float32)
    partial = jnp.dot(
        member, stacked, precision=lax.Precision.HIGHEST, preferred_element_type=jnp.float32
    ).reshape(class_count, 3, pixels) * channel_scale[None, :, None]
    by_band = partial.reshape(class_count, 3, slab_count, band_pixels).transpose(2, 0, 1, 3)
    by_band = by_band.astype(jnp.bfloat16).reshape(slab_count, -1, lanes)
    arrived = exchange(by_band, "slab", "grp", False, 1)
    group_band = jnp.sum(arrived.astype(jnp.float32), axis=0).astype(jnp.bfloat16)
    grouped = exchange(group_band[None], "grp", "slab", True, 2)
    band = jnp.sum(grouped.astype(jnp.float32), axis=0).reshape(
        class_count, 3, band_rows, half_cols
    )
    up = [(i, i + 1) for i in range(slab_count - 1)]
    down = [(i + 1, i) for i in range(slab_count - 1)]
    from_below = lax.ppermute(band[:, :, band_rows - 1 :], "slab", up)
    from_above = lax.ppermute(band[:, :, :1], "slab", down)
    class_bands = jnp.concatenate([from_below, band, from_above], axis=2)
    slab_index = lax.axis_index("slab")
    group_index = lax.axis_index("grp")
    offset_pad = jnp.pad(z_offset, ((0, 0), (1, 1)))
    frac_pad = jnp.pad(z_frac, ((0, 0), (1, 1)))
    rows_held = band_rows + 2
    local_offset = lax.dynamic_slice_in_dim(offset_pad, slab_index * band_rows, rows_held, 1)
    local_frac = lax.dynamic_slice_in_dim(frac_pad, slab_index * band_rows, rows_held, 1)
    row_ids = jnp.arange(rows_held, dtype=jnp.int32) + (band_rows - 1)
    band_shift = (row_ids // band_rows - 1) * z_dev - 1
    target = 2 * (row_ids % band_rows)[None, :] + local_offset + 1 + band_shift[None, :]
    plane_ids = jnp.arange(z_dev, dtype=jnp.int32)
    depth_weight = jnp.where(
        plane_ids[None, None, :] == target[:, :, None], (1.0 - local_frac)[:, :, None], 0.0
    )
    depth_weight = depth_weight + jnp.where(
        plane_ids[None, None, :] == target[:, :, None] + 1, local_frac[:, :, None], 0.0
    )
    sectioned = jnp.einsum(
        "ckra,crz->kzca",
        class_bands,
        depth_weight,
        precision=lax.Precision.HIGHEST,
    ).reshape(3 * z_dev, class_count * half_cols)
    y_rows = side_cells // group_count
    y_ids = group_index * y_rows + jnp.arange(y_rows, dtype=jnp.int32)
    row_weights = jnp.where(
        y_ids[:, None, None] == y_base[None, :, :], (1.0 - y_frac)[None, :, :], 0.0
    )
    row_weights = row_weights + jnp.where(
        y_ids[:, None, None] == y_base[None, :, :] + 1, y_frac[None, :, :], 0.0
    )
    row_weights = row_weights.astype(jnp.bfloat16).reshape(y_rows, class_count * half_cols)
    col_weights = stencil_weights(x_base, x_frac, side_cells).reshape(
        class_count * half_cols, side_cells
    )
    inserted = insert_planes(row_weights, sectioned, col_weights)
    return inserted.reshape(3, z_dev, y_rows, side_cells)


def insert_kernel(rows_ref, sec_ref, cols_ref, out_ref, lifted_ref):
    y_rows = rows_ref.shape[0]

    def body(i, carry):
        start = pl.multiple_of(i * y_rows, y_rows)
        lifted_ref[pl.ds(start, y_rows), :] = (
            rows_ref[...].astype(jnp.float32) * sec_ref[pl.ds(i, 1), :]
        ).astype(jnp.bfloat16)
        return carry

    lax.fori_loop(0, sec_ref.shape[0], body, 0)
    out_ref[...] = jnp.dot(lifted_ref[...], cols_ref[...], preferred_element_type=jnp.float32)


def insert_planes(row_weights, sectioned, col_weights):
    planes = sectioned.shape[0]
    y_rows, depth = row_weights.shape
    side = col_weights.shape[1]
    return pl.pallas_call(
        insert_kernel,
        out_shape=jax.ShapeDtypeStruct((planes * y_rows, side), jnp.float32),
        in_specs=[pl.BlockSpec(memory_space=pltpu.VMEM)] * 3,
        out_specs=pl.BlockSpec(memory_space=pltpu.VMEM),
        scratch_shapes=[pltpu.VMEM((planes * y_rows, depth), jnp.bfloat16)],
        cost_estimate=pl.CostEstimate(
            flops=2 * planes * y_rows * depth * side,
            transcendentals=0,
            bytes_accessed=2 * y_rows * depth + 4 * planes * depth + 2 * depth * side
            + 4 * planes * y_rows * side,
        ),
    )(row_weights, sectioned, col_weights)


def solution(mesh):
    in_specs = (
        P(("grp", "slab"), None),
        P(("grp", "slab")),
        P(("grp", "slab")),
        P(),
        P("slab", None),
        P(),
        P(),
        P(),
        P(),
        P(),
        P(),
        P(),
    )
    out_specs = P(None, "slab", "grp", None)
    return jax.shard_map(local, mesh=mesh, in_specs=in_specs, out_specs=out_specs, check_vma=False)
```

```python
import functools
import math

import jax
import jax.numpy as jnp
from jax import lax
from jax.experimental import pallas as pl
from jax.experimental.pallas import tpu as pltpu
from jax.sharding import PartitionSpec as P

SHIFTS = 128


def phase_table(row_count, half_cols):
    shift_ids = jnp.arange(SHIFTS)
    shift_rows = (shift_ids // 8 - SHIFTS // 16).astype(jnp.float32)
    shift_cols = (shift_ids % 8 - 4).astype(jnp.float32)
    lanes = 128
    per_lane_row = lanes // half_cols
    blocks = row_count * half_cols // lanes
    block_rows = (jnp.arange(blocks) * per_lane_row - row_count // 2).astype(jnp.float32)
    lane_ids = jnp.arange(lanes)
    lane_rows = (lane_ids // half_cols).astype(jnp.float32)
    lane_cols = (lane_ids % half_cols).astype(jnp.float32)
    step = 2.0 * math.pi / row_count
    block_angle = shift_rows[:, None] * block_rows[None, :] * step
    lane_angle = (
        shift_rows[:, None] * lane_rows[None, :] + shift_cols[:, None] * lane_cols[None, :]
    ) * step
    cos_b, sin_b = jnp.cos(block_angle)[:, :, None], jnp.sin(block_angle)[:, :, None]
    cos_l, sin_l = jnp.cos(lane_angle)[:, None, :], jnp.sin(lane_angle)[:, None, :]
    cos_t = (cos_b * cos_l - sin_b * sin_l).reshape(SHIFTS, row_count * half_cols)
    sin_t = (sin_b * cos_l + cos_b * sin_l).reshape(SHIFTS, row_count * half_cols)
    return jnp.concatenate([cos_t, sin_t], axis=1).astype(jnp.bfloat16)


def exchange_kernel(count, place, same, x_ref, out_ref, local_sem, send_sems, recv_sems):
    me, device = place()
    barrier = pltpu.get_barrier_semaphore()
    for k in range(1, count):
        pl.semaphore_signal(
            barrier,
            1,
            device_id=device(lax.rem(me + k, count)),
            device_id_type=pl.DeviceIdType.MESH,
        )
    pl.semaphore_wait(barrier, count - 1)

    def block(peer):
        return x_ref.at[0] if same else x_ref.at[peer]

    own = pltpu.make_async_copy(block(me), out_ref.at[me], local_sem)
    own.start()
    copies = []
    for k in range(1, count):
        peer = lax.rem(me + k, count)
        copy = pltpu.make_async_remote_copy(
            src_ref=block(peer),
            dst_ref=out_ref.at[me],
            send_sem=send_sems.at[k],
            recv_sem=recv_sems.at[k],
            device_id=device(peer),
            device_id_type=pl.DeviceIdType.MESH,
        )
        copy.start()
        copies.append(copy)
    own.wait()
    for copy in copies:
        copy.wait_send()
        copy.wait_recv()


def slab_place():
    group = lax.axis_index("grp")
    return lax.axis_index("slab"), lambda peer: (group, peer)


def core_place():
    group, slab = lax.axis_index("grp"), lax.axis_index("slab")
    return lax.rem(group, 2), lambda peer: (group - lax.rem(group, 2) + peer, slab)


def chip_place():
    group, slab = lax.axis_index("grp"), lax.axis_index("slab")
    return group // 2, lambda peer: (2 * peer + lax.rem(group, 2), slab)


def exchange(x, count, place, same, collective_id):
    shape = (count,) + x.shape[1:]
    return pl.pallas_call(
        functools.partial(exchange_kernel, count, place, same),
        out_shape=jax.ShapeDtypeStruct(shape, x.dtype),
        in_specs=[pl.BlockSpec(memory_space=pltpu.VMEM)],
        out_specs=pl.BlockSpec(memory_space=pltpu.VMEM),
        scratch_shapes=[
            pltpu.SemaphoreType.DMA(()),
            pltpu.SemaphoreType.DMA((count,)),
            pltpu.SemaphoreType.DMA((count,)),
        ],
        compiler_params=pltpu.CompilerParams(collective_id=collective_id, has_side_effects=True),
    )(x)


def align_frames(frames, ctf_rows, ref_rows, phase, score_scale):
    pixels = ctf_rows.shape[1]
    frame_re = frames[:, :pixels].astype(jnp.float32)
    frame_im = frames[:, pixels:].astype(jnp.float32)
    ref_re = ref_rows[:, :pixels].astype(jnp.float32)
    ref_im = ref_rows[:, pixels:].astype(jnp.float32)
    weight = ctf_rows.astype(jnp.float32)
    cross_terms = jnp.concatenate(
        [
            weight * (ref_re * frame_re + ref_im * frame_im),
            weight * (ref_re * frame_im - ref_im * frame_re),
        ],
        axis=1,
    ).astype(jnp.bfloat16)
    scores = score_scale * jnp.einsum(
        "np,sp->ns", cross_terms, phase, preferred_element_type=jnp.float32
    )
    shift_probs = jax.nn.softmax(scores, axis=1).astype(jnp.bfloat16)
    shift_mix = jnp.dot(shift_probs, phase, preferred_element_type=jnp.float32)
    mix_re = shift_mix[:, :pixels]
    mix_im = shift_mix[:, pixels:]
    return jnp.concatenate(
        [
            weight * (frame_re * mix_re + frame_im * mix_im),
            weight * (frame_im * mix_re - frame_re * mix_im),
            weight * weight,
        ],
        axis=1,
    )


def stencil_weights(base_cell, fraction, side_cells):
    cell_ids = jnp.arange(side_cells, dtype=jnp.int32)
    dense_weight = jnp.where(
        cell_ids[None, None, :] == base_cell[:, :, None], (1.0 - fraction)[:, :, None], 0.0
    )
    dense_weight = dense_weight + jnp.where(
        cell_ids[None, None, :] == base_cell[:, :, None] + 1, fraction[:, :, None], 0.0
    )
    return dense_weight.astype(jnp.bfloat16)


def local(
    images,
    image_class,
    image_ctf,
    class_owner,
    references,
    ctf_table,
    x_base,
    y_base,
    x_frac,
    y_frac,
    z_offset,
    z_frac,
):
    slab_count = lax.axis_size("slab")
    group_count = lax.axis_size("grp")
    frame_count = images.shape[0]
    pixels = ctf_table.shape[1]
    groups_ctf = ctf_table.shape[0]
    row_count = z_offset.shape[1]
    half_cols = x_base.shape[1]
    class_count = class_owner.shape[0]
    side_cells = 2 * row_count
    band_rows = row_count // slab_count
    band_pixels = band_rows * half_cols
    z_dev = 2 * band_rows
    phase = phase_table(row_count, half_cols)
    score_scale = 2.0 / math.sqrt(2.0 * pixels)
    channel_scale = jnp.array(
        [
            1.0 / math.sqrt(frame_count * group_count),
            1.0 / math.sqrt(frame_count * group_count),
            1.0 / (frame_count * group_count),
        ],
        jnp.float32,
    )
    lanes = 128
    core = lax.rem(lax.axis_index("grp"), 2)
    ref_halves = references.reshape(2, -1, lanes)
    my_half = lax.dynamic_slice_in_dim(ref_halves, core, 1, 0)
    half_refs = exchange(my_half, slab_count, slab_place, True, 0)
    both_halves = exchange(half_refs.reshape(1, -1, lanes), 2, core_place, True, 1)
    all_refs = both_halves.reshape(2, slab_count, pixels).transpose(1, 0, 2).reshape(
        slab_count, 2 * pixels
    )
    class_ids = jnp.arange(class_count, dtype=jnp.int32)
    owner_of = jnp.sum(
        jnp.where(image_class[:, None] == class_ids[None, :], class_owner[None, :], 0), axis=1
    )
    pick_ref = (owner_of[:, None] == jnp.arange(slab_count, dtype=jnp.int32)[None, :]).astype(
        jnp.bfloat16
    )
    ref_rows = jnp.dot(pick_ref, all_refs, preferred_element_type=jnp.float32).astype(
        jnp.bfloat16
    )
    pick_ctf = (image_ctf[:, None] == jnp.arange(groups_ctf, dtype=jnp.int32)[None, :]).astype(
        jnp.bfloat16
    )
    ctf_rows = jnp.dot(pick_ctf, ctf_table, preferred_element_type=jnp.float32).astype(
        jnp.bfloat16
    )
    stacked = align_frames(images, ctf_rows, ref_rows, phase, score_scale)
    member = (class_ids[:, None] == image_class[None, :]).astype(jnp.float32)
    partial = jnp.dot(
        member, stacked, precision=lax.Precision.HIGHEST, preferred_element_type=jnp.float32
    ).reshape(class_count, 3, pixels) * channel_scale[None, :, None]
    by_half = partial.reshape(class_count, 3, slab_count, 2, band_pixels // 2).transpose(
        3, 2, 0, 1, 4
    ).reshape(2, -1, lanes)
    paired = exchange(by_half, 2, core_place, False, 2)
    pair_sum = (paired[0] + paired[1]).astype(jnp.bfloat16).reshape(slab_count, -1, lanes)
    arrived = exchange(pair_sum, slab_count, slab_place, False, 3)
    chip_band = jnp.sum(arrived.astype(jnp.float32), axis=0).astype(jnp.bfloat16)
    chips = exchange(chip_band[None], group_count // 2, chip_place, True, 4)
    half_band = jnp.sum(chips.astype(jnp.float32), axis=0)
    full = exchange(half_band[None], 2, core_place, True, 5)
    band = full.reshape(2, class_count, 3, band_pixels // 2).transpose(1, 2, 0, 3).reshape(
        class_count, 3, band_rows, half_cols
    )
    up = [(i, i + 1) for i in range(slab_count - 1)]
    down = [(i + 1, i) for i in range(slab_count - 1)]
    from_below = lax.ppermute(band[:, :, band_rows - 1 :], "slab", up)
    from_above = lax.ppermute(band[:, :, :1], "slab", down)
    class_bands = jnp.concatenate([from_below, band, from_above], axis=2)
    slab_index = lax.axis_index("slab")
    group_index = lax.axis_index("grp")
    offset_pad = jnp.pad(z_offset, ((0, 0), (1, 1)))
    frac_pad = jnp.pad(z_frac, ((0, 0), (1, 1)))
    rows_held = band_rows + 2
    local_offset = lax.dynamic_slice_in_dim(offset_pad, slab_index * band_rows, rows_held, 1)
    local_frac = lax.dynamic_slice_in_dim(frac_pad, slab_index * band_rows, rows_held, 1)
    row_ids = jnp.arange(rows_held, dtype=jnp.int32) + (band_rows - 1)
    band_shift = (row_ids // band_rows - 1) * z_dev - 1
    target = 2 * (row_ids % band_rows)[None, :] + local_offset + 1 + band_shift[None, :]
    plane_ids = jnp.arange(z_dev, dtype=jnp.int32)
    depth_weight = jnp.where(
        plane_ids[None, None, :] == target[:, :, None], (1.0 - local_frac)[:, :, None], 0.0
    )
    depth_weight = depth_weight + jnp.where(
        plane_ids[None, None, :] == target[:, :, None] + 1, local_frac[:, :, None], 0.0
    )
    sectioned = jnp.einsum(
        "ckra,crz->kzca",
        class_bands,
        depth_weight,
        precision=lax.Precision.HIGHEST,
    ).reshape(3 * z_dev, class_count * half_cols)
    y_rows = side_cells // group_count
    y_ids = group_index * y_rows + jnp.arange(y_rows, dtype=jnp.int32)
    row_weights = jnp.where(
        y_ids[:, None, None] == y_base[None, :, :], (1.0 - y_frac)[None, :, :], 0.0
    )
    row_weights = row_weights + jnp.where(
        y_ids[:, None, None] == y_base[None, :, :] + 1, y_frac[None, :, :], 0.0
    )
    row_weights = row_weights.astype(jnp.bfloat16).reshape(y_rows, class_count * half_cols)
    col_weights = stencil_weights(x_base, x_frac, side_cells).reshape(
        class_count * half_cols, side_cells
    )
    inserted = insert_planes(row_weights, sectioned, col_weights)
    return inserted.reshape(3, z_dev, y_rows, side_cells)


def insert_kernel(rows_ref, sec_ref, cols_ref, out_ref, lifted_ref):
    y_rows = rows_ref.shape[0]

    def body(i, carry):
        start = pl.multiple_of(i * y_rows, y_rows)
        lifted_ref[pl.ds(start, y_rows), :] = (
            rows_ref[...].astype(jnp.float32) * sec_ref[pl.ds(i, 1), :]
        ).astype(jnp.bfloat16)
        return carry

    lax.fori_loop(0, sec_ref.shape[0], body, 0)
    out_ref[...] = jnp.dot(lifted_ref[...], cols_ref[...], preferred_element_type=jnp.float32)


def insert_planes(row_weights, sectioned, col_weights):
    planes = sectioned.shape[0]
    y_rows, depth = row_weights.shape
    side = col_weights.shape[1]
    return pl.pallas_call(
        insert_kernel,
        out_shape=jax.ShapeDtypeStruct((planes * y_rows, side), jnp.float32),
        in_specs=[pl.BlockSpec(memory_space=pltpu.VMEM)] * 3,
        out_specs=pl.BlockSpec(memory_space=pltpu.VMEM),
        scratch_shapes=[pltpu.VMEM((planes * y_rows, depth), jnp.bfloat16)],
        cost_estimate=pl.CostEstimate(
            flops=2 * planes * y_rows * depth * side,
            transcendentals=0,
            bytes_accessed=2 * y_rows * depth + 4 * planes * depth + 2 * depth * side
            + 4 * planes * y_rows * side,
        ),
    )(row_weights, sectioned, col_weights)


def solution(mesh):
    in_specs = (
        P(("grp", "slab"), None),
        P(("grp", "slab")),
        P(("grp", "slab")),
        P(),
        P("slab", None),
        P(),
        P(),
        P(),
        P(),
        P(),
        P(),
        P(),
    )
    out_specs = P(None, "slab", "grp", None)
    return jax.shard_map(local, mesh=mesh, in_specs=in_specs, out_specs=out_specs, check_vma=False)
```

```python
import functools
import math

import jax
import jax.numpy as jnp
from jax import lax
from jax.experimental import pallas as pl
from jax.experimental.pallas import tpu as pltpu
from jax.sharding import PartitionSpec as P

SHIFTS = 128


def phase_table(row_count, half_cols):
    shift_ids = jnp.arange(SHIFTS)
    shift_rows = (shift_ids // 8 - SHIFTS // 16).astype(jnp.float32)
    shift_cols = (shift_ids % 8 - 4).astype(jnp.float32)
    lanes = 128
    per_lane_row = lanes // half_cols
    blocks = row_count * half_cols // lanes
    block_rows = (jnp.arange(blocks) * per_lane_row - row_count // 2).astype(jnp.float32)
    lane_ids = jnp.arange(lanes)
    lane_rows = (lane_ids // half_cols).astype(jnp.float32)
    lane_cols = (lane_ids % half_cols).astype(jnp.float32)
    step = 2.0 * math.pi / row_count
    block_angle = shift_rows[:, None] * block_rows[None, :] * step
    lane_angle = (
        shift_rows[:, None] * lane_rows[None, :] + shift_cols[:, None] * lane_cols[None, :]
    ) * step
    cos_b, sin_b = jnp.cos(block_angle)[:, :, None], jnp.sin(block_angle)[:, :, None]
    cos_l, sin_l = jnp.cos(lane_angle)[:, None, :], jnp.sin(lane_angle)[:, None, :]
    cos_t = (cos_b * cos_l - sin_b * sin_l).reshape(SHIFTS, row_count * half_cols)
    sin_t = (sin_b * cos_l + cos_b * sin_l).reshape(SHIFTS, row_count * half_cols)
    return jnp.concatenate([cos_t, sin_t], axis=1).astype(jnp.bfloat16)


def exchange_kernel(count, place, pick, x_ref, out_ref, local_sem, send_sems, recv_sems):
    me, device = place()
    barrier = pltpu.get_barrier_semaphore()
    for k in range(1, count):
        pl.semaphore_signal(
            barrier,
            1,
            device_id=device(lax.rem(me + k, count)),
            device_id_type=pl.DeviceIdType.MESH,
        )
    pl.semaphore_wait(barrier, count - 1)

    def block(peer):
        return pick(x_ref, peer)

    own = pltpu.make_async_copy(block(me), out_ref.at[me], local_sem)
    own.start()
    copies = []
    for k in range(1, count):
        peer = lax.rem(me + k, count)
        copy = pltpu.make_async_remote_copy(
            src_ref=block(peer),
            dst_ref=out_ref.at[me],
            send_sem=send_sems.at[k],
            recv_sem=recv_sems.at[k],
            device_id=device(peer),
            device_id_type=pl.DeviceIdType.MESH,
        )
        copy.start()
        copies.append(copy)
    own.wait()
    for copy in copies:
        copy.wait_send()
        copy.wait_recv()


def slab_place():
    group = lax.axis_index("grp")
    return lax.axis_index("slab"), lambda peer: (group, peer)


def core_place():
    group, slab = lax.axis_index("grp"), lax.axis_index("slab")
    return lax.rem(group, 2), lambda peer: (group - lax.rem(group, 2) + peer, slab)


def chip_place():
    group, slab = lax.axis_index("grp"), lax.axis_index("slab")
    return group // 2, lambda peer: (2 * peer + lax.rem(group, 2), slab)


def whole(x_ref, peer):
    return x_ref.at[0]


def row_block(x_ref, peer):
    return x_ref.at[peer]


def lane_block(x_ref, peer):
    width = x_ref.shape[1] // lax.axis_size("slab")
    return x_ref.at[:, pl.ds(pl.multiple_of(peer * width, width), width)]


def exchange(x, count, place, pick, collective_id, block_shape):
    shape = (count,) + block_shape
    return pl.pallas_call(
        functools.partial(exchange_kernel, count, place, pick),
        out_shape=jax.ShapeDtypeStruct(shape, x.dtype),
        in_specs=[pl.BlockSpec(memory_space=pltpu.VMEM)],
        out_specs=pl.BlockSpec(memory_space=pltpu.VMEM),
        scratch_shapes=[
            pltpu.SemaphoreType.DMA(()),
            pltpu.SemaphoreType.DMA((count,)),
            pltpu.SemaphoreType.DMA((count,)),
        ],
        compiler_params=pltpu.CompilerParams(collective_id=collective_id, has_side_effects=True),
    )(x)


def align_frames(frames, ctf_rows, ref_re, ref_im, phase, score_scale):
    pixels = ctf_rows.shape[1]
    frame_re = frames[:, :pixels].astype(jnp.float32)
    frame_im = frames[:, pixels:].astype(jnp.float32)
    ref_re = ref_re.astype(jnp.float32)
    ref_im = ref_im.astype(jnp.float32)
    weight = ctf_rows.astype(jnp.float32)
    cross_terms = jnp.concatenate(
        [
            weight * (ref_re * frame_re + ref_im * frame_im),
            weight * (ref_re * frame_im - ref_im * frame_re),
        ],
        axis=1,
    ).astype(jnp.bfloat16)
    scores = score_scale * jnp.einsum(
        "np,sp->ns", cross_terms, phase, preferred_element_type=jnp.float32
    )
    shift_probs = jax.nn.softmax(scores, axis=1).astype(jnp.bfloat16)
    shift_mix = jnp.dot(shift_probs, phase, preferred_element_type=jnp.float32)
    mix_re = shift_mix[:, :pixels]
    mix_im = shift_mix[:, pixels:]
    return jnp.concatenate(
        [
            weight * (frame_re * mix_re + frame_im * mix_im),
            weight * (frame_im * mix_re - frame_re * mix_im),
            weight * weight,
        ],
        axis=1,
    )


def stencil_weights(base_cell, fraction, side_cells):
    cell_ids = jnp.arange(side_cells, dtype=jnp.int32)
    dense_weight = jnp.where(
        cell_ids[None, None, :] == base_cell[:, :, None], (1.0 - fraction)[:, :, None], 0.0
    )
    dense_weight = dense_weight + jnp.where(
        cell_ids[None, None, :] == base_cell[:, :, None] + 1, fraction[:, :, None], 0.0
    )
    return dense_weight.astype(jnp.bfloat16)


def local(
    images,
    image_class,
    image_ctf,
    class_owner,
    references,
    ctf_table,
    x_base,
    y_base,
    x_frac,
    y_frac,
    z_offset,
    z_frac,
):
    slab_count = lax.axis_size("slab")
    group_count = lax.axis_size("grp")
    frame_count = images.shape[0]
    pixels = ctf_table.shape[1]
    groups_ctf = ctf_table.shape[0]
    row_count = z_offset.shape[1]
    half_cols = x_base.shape[1]
    class_count = class_owner.shape[0]
    side_cells = 2 * row_count
    band_rows = row_count // slab_count
    band_pixels = band_rows * half_cols
    z_dev = 2 * band_rows
    phase = phase_table(row_count, half_cols)
    score_scale = 2.0 / math.sqrt(2.0 * pixels)
    channel_scale = jnp.array(
        [
            1.0 / math.sqrt(frame_count * group_count),
            1.0 / math.sqrt(frame_count * group_count),
            1.0 / (frame_count * group_count),
        ],
        jnp.float32,
    )
    lanes = 128
    core = lax.rem(lax.axis_index("grp"), 2)
    ref_halves = references.reshape(2, -1, lanes)
    my_half = lax.dynamic_slice_in_dim(ref_halves, core, 1, 0)
    half_refs = exchange(my_half, slab_count, slab_place, whole, 0, my_half.shape[1:])
    both_halves = exchange(
        half_refs.reshape(1, -1, lanes), 2, core_place, whole, 1, (slab_count * pixels // lanes, lanes)
    ).reshape(2, slab_count, pixels)
    class_ids = jnp.arange(class_count, dtype=jnp.int32)
    owner_of = jnp.sum(
        jnp.where(image_class[:, None] == class_ids[None, :], class_owner[None, :], 0), axis=1
    )
    pick_ref = (owner_of[:, None] == jnp.arange(slab_count, dtype=jnp.int32)[None, :]).astype(
        jnp.bfloat16
    )
    ref_re = jnp.dot(pick_ref, both_halves[0], preferred_element_type=jnp.float32).astype(
        jnp.bfloat16
    )
    ref_im = jnp.dot(pick_ref, both_halves[1], preferred_element_type=jnp.float32).astype(
        jnp.bfloat16
    )
    pick_ctf = (image_ctf[:, None] == jnp.arange(groups_ctf, dtype=jnp.int32)[None, :]).astype(
        jnp.bfloat16
    )
    ctf_rows = jnp.dot(pick_ctf, ctf_table, preferred_element_type=jnp.float32).astype(
        jnp.bfloat16
    )
    stacked = align_frames(images, ctf_rows, ref_re, ref_im, phase, score_scale)
    member = (class_ids[:, None] == image_class[None, :]).astype(jnp.float32)
    partial = jnp.dot(
        member, stacked, precision=lax.Precision.HIGHEST, preferred_element_type=jnp.float32
    ).reshape(class_count, 3, pixels) * channel_scale[None, :, None]
    half_rows = class_count // 2 * 3
    by_half = partial.reshape(2, half_rows, pixels)
    paired = exchange(by_half, 2, core_place, row_block, 2, (half_rows, pixels))
    pair_sum = (paired[0] + paired[1]).astype(jnp.bfloat16)
    arrived = exchange(pair_sum, slab_count, slab_place, lane_block, 3, (half_rows, band_pixels))
    chip_band = jnp.sum(arrived.astype(jnp.float32), axis=0).astype(jnp.bfloat16)
    chips = exchange(chip_band[None], group_count // 2, chip_place, whole, 4, chip_band.shape)
    half_band = jnp.sum(chips.astype(jnp.float32), axis=0)
    full = exchange(half_band[None], 2, core_place, whole, 5, half_band.shape)
    band = full.reshape(class_count, 3, band_rows, half_cols)
    up = [(i, i + 1) for i in range(slab_count - 1)]
    down = [(i + 1, i) for i in range(slab_count - 1)]
    from_below = lax.ppermute(band[:, :, band_rows - 1 :], "slab", up)
    from_above = lax.ppermute(band[:, :, :1], "slab", down)
    class_bands = jnp.concatenate([from_below, band, from_above], axis=2)
    slab_index = lax.axis_index("slab")
    group_index = lax.axis_index("grp")
    offset_pad = jnp.pad(z_offset, ((0, 0), (1, 1)))
    frac_pad = jnp.pad(z_frac, ((0, 0), (1, 1)))
    rows_held = band_rows + 2
    local_offset = lax.dynamic_slice_in_dim(offset_pad, slab_index * band_rows, rows_held, 1)
    local_frac = lax.dynamic_slice_in_dim(frac_pad, slab_index * band_rows, rows_held, 1)
    row_ids = jnp.arange(rows_held, dtype=jnp.int32) + (band_rows - 1)
    band_shift = (row_ids // band_rows - 1) * z_dev - 1
    target = 2 * (row_ids % band_rows)[None, :] + local_offset + 1 + band_shift[None, :]
    plane_ids = jnp.arange(z_dev, dtype=jnp.int32)
    depth_weight = jnp.where(
        plane_ids[None, None, :] == target[:, :, None], (1.0 - local_frac)[:, :, None], 0.0
    )
    depth_weight = depth_weight + jnp.where(
        plane_ids[None, None, :] == target[:, :, None] + 1, local_frac[:, :, None], 0.0
    )
    sectioned = jnp.einsum(
        "ckra,crz->kzca",
        class_bands,
        depth_weight,
        precision=lax.Precision.HIGHEST,
    ).reshape(3 * z_dev, class_count * half_cols)
    y_rows = side_cells // group_count
    y_ids = group_index * y_rows + jnp.arange(y_rows, dtype=jnp.int32)
    row_weights = jnp.where(
        y_ids[:, None, None] == y_base[None, :, :], (1.0 - y_frac)[None, :, :], 0.0
    )
    row_weights = row_weights + jnp.where(
        y_ids[:, None, None] == y_base[None, :, :] + 1, y_frac[None, :, :], 0.0
    )
    row_weights = row_weights.astype(jnp.bfloat16).reshape(y_rows, class_count * half_cols)
    col_weights = stencil_weights(x_base, x_frac, side_cells).reshape(
        class_count * half_cols, side_cells
    )
    inserted = insert_planes(row_weights, sectioned, col_weights)
    return inserted.reshape(3, z_dev, y_rows, side_cells)


def insert_kernel(rows_ref, sec_ref, cols_ref, out_ref, lifted_ref):
    y_rows = rows_ref.shape[0]

    def body(i, carry):
        start = pl.multiple_of(i * y_rows, y_rows)
        lifted_ref[pl.ds(start, y_rows), :] = (
            rows_ref[...].astype(jnp.float32) * sec_ref[pl.ds(i, 1), :]
        ).astype(jnp.bfloat16)
        return carry

    lax.fori_loop(0, sec_ref.shape[0], body, 0)
    out_ref[...] = jnp.dot(lifted_ref[...], cols_ref[...], preferred_element_type=jnp.float32)


def insert_planes(row_weights, sectioned, col_weights):
    planes = sectioned.shape[0]
    y_rows, depth = row_weights.shape
    side = col_weights.shape[1]
    return pl.pallas_call(
        insert_kernel,
        out_shape=jax.ShapeDtypeStruct((planes * y_rows, side), jnp.float32),
        in_specs=[pl.BlockSpec(memory_space=pltpu.VMEM)] * 3,
        out_specs=pl.BlockSpec(memory_space=pltpu.VMEM),
        scratch_shapes=[pltpu.VMEM((planes * y_rows, depth), jnp.bfloat16)],
        cost_estimate=pl.CostEstimate(
            flops=2 * planes * y_rows * depth * side,
            transcendentals=0,
            bytes_accessed=2 * y_rows * depth + 4 * planes * depth + 2 * depth * side
            + 4 * planes * y_rows * side,
        ),
    )(row_weights, sectioned, col_weights)


def solution(mesh):
    in_specs = (
        P(("grp", "slab"), None),
        P(("grp", "slab")),
        P(("grp", "slab")),
        P(),
        P("slab", None),
        P(),
        P(),
        P(),
        P(),
        P(),
        P(),
        P(),
    )
    out_specs = P(None, "slab", "grp", None)
    return jax.shard_map(local, mesh=mesh, in_specs=in_specs, out_specs=out_specs, check_vma=False)
```

```python
import functools
import math

import jax
import jax.numpy as jnp
from jax import lax
from jax.experimental import pallas as pl
from jax.experimental.pallas import tpu as pltpu
from jax.sharding import PartitionSpec as P

SHIFTS = 128


def phase_table(row_count, half_cols):
    shift_ids = jnp.arange(SHIFTS)
    shift_rows = (shift_ids // 8 - SHIFTS // 16).astype(jnp.float32)
    shift_cols = (shift_ids % 8 - 4).astype(jnp.float32)
    lanes = 128
    per_lane_row = lanes // half_cols
    blocks = row_count * half_cols // lanes
    block_rows = (jnp.arange(blocks) * per_lane_row - row_count // 2).astype(jnp.float32)
    lane_ids = jnp.arange(lanes)
    lane_rows = (lane_ids // half_cols).astype(jnp.float32)
    lane_cols = (lane_ids % half_cols).astype(jnp.float32)
    step = 2.0 * math.pi / row_count
    block_angle = shift_rows[:, None] * block_rows[None, :] * step
    lane_angle = (
        shift_rows[:, None] * lane_rows[None, :] + shift_cols[:, None] * lane_cols[None, :]
    ) * step
    cos_b, sin_b = jnp.cos(block_angle)[:, :, None], jnp.sin(block_angle)[:, :, None]
    cos_l, sin_l = jnp.cos(lane_angle)[:, None, :], jnp.sin(lane_angle)[:, None, :]
    cos_t = (cos_b * cos_l - sin_b * sin_l).reshape(SHIFTS, row_count * half_cols)
    sin_t = (sin_b * cos_l + cos_b * sin_l).reshape(SHIFTS, row_count * half_cols)
    return jnp.concatenate([cos_t, sin_t], axis=1).astype(jnp.bfloat16)


def exchange_kernel(count, place, picks, *refs):
    parts = len(picks)
    x_refs, out_refs = refs[:parts], refs[parts : 2 * parts]
    local_sems, send_sems, recv_sems = refs[2 * parts :]
    me, device = place()
    barrier = pltpu.get_barrier_semaphore()
    for k in range(1, count):
        pl.semaphore_signal(
            barrier,
            1,
            device_id=device(lax.rem(me + k, count)),
            device_id_type=pl.DeviceIdType.MESH,
        )
    pl.semaphore_wait(barrier, count - 1)
    owns, copies = [], []
    for part, (pick, x_ref, out_ref) in enumerate(zip(picks, x_refs, out_refs)):
        own = pltpu.make_async_copy(pick(x_ref, me), out_ref.at[me], local_sems.at[part])
        own.start()
        owns.append(own)
        for k in range(1, count):
            peer = lax.rem(me + k, count)
            copy = pltpu.make_async_remote_copy(
                src_ref=pick(x_ref, peer),
                dst_ref=out_ref.at[me],
                send_sem=send_sems.at[part, k],
                recv_sem=recv_sems.at[part, k],
                device_id=device(peer),
                device_id_type=pl.DeviceIdType.MESH,
            )
            copy.start()
            copies.append(copy)
    for own in owns:
        own.wait()
    for copy in copies:
        copy.wait_send()
        copy.wait_recv()


def slab_place():
    group = lax.axis_index("grp")
    return lax.axis_index("slab"), lambda peer: (group, peer)


def core_place():
    group, slab = lax.axis_index("grp"), lax.axis_index("slab")
    return lax.rem(group, 2), lambda peer: (group - lax.rem(group, 2) + peer, slab)


def group_place():
    slab = lax.axis_index("slab")
    return lax.axis_index("grp"), lambda peer: (peer, slab)


def whole(x_ref, peer):
    return x_ref.at[0]


def row_block(x_ref, peer):
    return x_ref.at[peer]


def lane_block(x_ref, peer):
    width = x_ref.shape[1] // lax.axis_size("slab")
    return x_ref.at[:, pl.ds(pl.multiple_of(peer * width, width), width)]


def exchange_many(xs, count, place, picks, collective_id, block_shapes):
    parts = len(xs)
    return pl.pallas_call(
        functools.partial(exchange_kernel, count, place, tuple(picks)),
        out_shape=[
            jax.ShapeDtypeStruct((count,) + shape, x.dtype) for x, shape in zip(xs, block_shapes)
        ],
        in_specs=[pl.BlockSpec(memory_space=pltpu.VMEM)] * parts,
        out_specs=[pl.BlockSpec(memory_space=pltpu.VMEM)] * parts,
        scratch_shapes=[
            pltpu.SemaphoreType.DMA((parts,)),
            pltpu.SemaphoreType.DMA((parts, count)),
            pltpu.SemaphoreType.DMA((parts, count)),
        ],
        compiler_params=pltpu.CompilerParams(collective_id=collective_id, has_side_effects=True),
    )(*xs)


def exchange(x, count, place, pick, collective_id, block_shape):
    return exchange_many([x], count, place, [pick], collective_id, [block_shape])[0]


def align_frames(frames, ctf_rows, ref_re, ref_im, phase, score_scale):
    pixels = ctf_rows.shape[1]
    frame_re = frames[:, :pixels].astype(jnp.float32)
    frame_im = frames[:, pixels:].astype(jnp.float32)
    ref_re = ref_re.astype(jnp.float32)
    ref_im = ref_im.astype(jnp.float32)
    weight = ctf_rows.astype(jnp.float32)
    cross_terms = jnp.concatenate(
        [
            weight * (ref_re * frame_re + ref_im * frame_im),
            weight * (ref_re * frame_im - ref_im * frame_re),
        ],
        axis=1,
    ).astype(jnp.bfloat16)
    scores = score_scale * jnp.einsum(
        "np,sp->ns", cross_terms, phase, preferred_element_type=jnp.float32
    )
    shift_probs = jax.nn.softmax(scores, axis=1).astype(jnp.bfloat16)
    shift_mix = jnp.dot(shift_probs, phase, preferred_element_type=jnp.float32)
    mix_re = shift_mix[:, :pixels]
    mix_im = shift_mix[:, pixels:]
    return jnp.concatenate(
        [
            weight * (frame_re * mix_re + frame_im * mix_im),
            weight * (frame_im * mix_re - frame_re * mix_im),
        ],
        axis=1,
    )


def stencil_weights(base_cell, fraction, side_cells):
    cell_ids = jnp.arange(side_cells, dtype=jnp.int32)
    dense_weight = jnp.where(
        cell_ids[None, None, :] == base_cell[:, :, None], (1.0 - fraction)[:, :, None], 0.0
    )
    dense_weight = dense_weight + jnp.where(
        cell_ids[None, None, :] == base_cell[:, :, None] + 1, fraction[:, :, None], 0.0
    )
    return dense_weight.astype(jnp.bfloat16)


def local(
    images,
    image_class,
    image_ctf,
    class_owner,
    references,
    ctf_table,
    x_base,
    y_base,
    x_frac,
    y_frac,
    z_offset,
    z_frac,
):
    slab_count = lax.axis_size("slab")
    group_count = lax.axis_size("grp")
    frame_count = images.shape[0]
    pixels = ctf_table.shape[1]
    groups_ctf = ctf_table.shape[0]
    row_count = z_offset.shape[1]
    half_cols = x_base.shape[1]
    class_count = class_owner.shape[0]
    side_cells = 2 * row_count
    band_rows = row_count // slab_count
    band_pixels = band_rows * half_cols
    z_dev = 2 * band_rows
    phase = phase_table(row_count, half_cols)
    score_scale = 2.0 / math.sqrt(2.0 * pixels)
    channel_scale = jnp.array(
        [
            1.0 / math.sqrt(frame_count * group_count),
            1.0 / math.sqrt(frame_count * group_count),
            1.0 / (frame_count * group_count),
        ],
        jnp.float32,
    )
    lanes = 128
    core = lax.rem(lax.axis_index("grp"), 2)
    ref_halves = references.reshape(2, -1, lanes)
    my_half = lax.dynamic_slice_in_dim(ref_halves, core, 1, 0)
    half_refs = exchange(my_half, slab_count, slab_place, whole, 0, my_half.shape[1:])
    both_halves = exchange(
        half_refs.reshape(1, -1, lanes), 2, core_place, whole, 1, (slab_count * pixels // lanes, lanes)
    ).reshape(2, slab_count, pixels)
    class_ids = jnp.arange(class_count, dtype=jnp.int32)
    owner_of = jnp.sum(
        jnp.where(image_class[:, None] == class_ids[None, :], class_owner[None, :], 0), axis=1
    )
    pick_ref = (owner_of[:, None] == jnp.arange(slab_count, dtype=jnp.int32)[None, :]).astype(
        jnp.bfloat16
    )
    ref_re = jnp.dot(pick_ref, both_halves[0], preferred_element_type=jnp.float32).astype(
        jnp.bfloat16
    )
    ref_im = jnp.dot(pick_ref, both_halves[1], preferred_element_type=jnp.float32).astype(
        jnp.bfloat16
    )
    pick_ctf = (image_ctf[:, None] == jnp.arange(groups_ctf, dtype=jnp.int32)[None, :]).astype(
        jnp.bfloat16
    )
    ctf_rows = jnp.dot(pick_ctf, ctf_table, preferred_element_type=jnp.float32).astype(
        jnp.bfloat16
    )
    stacked = align_frames(images, ctf_rows, ref_re, ref_im, phase, score_scale)
    member = (class_ids[:, None] == image_class[None, :]).astype(jnp.float32)
    partial = jnp.dot(
        member, stacked, precision=lax.Precision.HIGHEST, preferred_element_type=jnp.float32
    ) * channel_scale[0]
    half_rows = class_count // 2 * 2
    by_half = partial.reshape(2, half_rows, pixels)
    class_hits = (class_ids[:, None] == image_class[None, :]).astype(jnp.bfloat16)
    ctf_hits = (image_ctf[:, None] == jnp.arange(groups_ctf, dtype=jnp.int32)[None, :]).astype(
        jnp.bfloat16
    )
    counts = jnp.dot(class_hits, ctf_hits, preferred_element_type=jnp.float32)
    paired, paired_counts = exchange_many(
        [by_half, counts[None]],
        2,
        core_place,
        [row_block, whole],
        2,
        [(half_rows, pixels), counts.shape],
    )
    pair_sum = (paired[0] + paired[1]).astype(jnp.bfloat16)
    arrived, arrived_counts = exchange_many(
        [pair_sum, jnp.sum(paired_counts, axis=0)[None]],
        slab_count,
        slab_place,
        [lane_block, whole],
        3,
        [(half_rows, band_pixels), counts.shape],
    )
    chip_band = jnp.sum(arrived.astype(jnp.float32), axis=0).astype(jnp.bfloat16)
    groups, group_counts = exchange_many(
        [chip_band[None], jnp.sum(arrived_counts, axis=0)[None]],
        group_count,
        group_place,
        [whole, whole],
        4,
        [chip_band.shape, counts.shape],
    )
    band = jnp.sum(
        groups.astype(jnp.float32).reshape(group_count // 2, 2, half_rows, band_pixels), axis=0
    ).reshape(class_count, 2, band_rows, half_cols)
    total_counts = jnp.sum(
        group_counts.reshape(group_count // 2, 2, class_count, groups_ctf)[:, 0], axis=0
    )
    up = [(i, i + 1) for i in range(slab_count - 1)]
    down = [(i + 1, i) for i in range(slab_count - 1)]
    from_below = lax.ppermute(band[:, :, band_rows - 1 :], "slab", up)
    from_above = lax.ppermute(band[:, :, :1], "slab", down)
    data_bands = jnp.concatenate([from_below, band, from_above], axis=2)
    slab_index = lax.axis_index("slab")
    ctf_sq = jnp.pad(
        jnp.square(ctf_table.astype(jnp.float32)), ((0, 0), (half_cols, half_cols))
    )
    window = lax.dynamic_slice_in_dim(
        ctf_sq, slab_index * band_pixels, band_pixels + 2 * half_cols, 1
    )
    weight_rows = jnp.dot(
        total_counts, window, precision=lax.Precision.HIGHEST, preferred_element_type=jnp.float32
    ) * channel_scale[2]
    class_bands = jnp.concatenate(
        [data_bands, weight_rows.reshape(class_count, 1, band_rows + 2, half_cols)], axis=1
    )
    group_index = lax.axis_index("grp")
    offset_pad = jnp.pad(z_offset, ((0, 0), (1, 1)))
    frac_pad = jnp.pad(z_frac, ((0, 0), (1, 1)))
    rows_held = band_rows + 2
    local_offset = lax.dynamic_slice_in_dim(offset_pad, slab_index * band_rows, rows_held, 1)
    local_frac = lax.dynamic_slice_in_dim(frac_pad, slab_index * band_rows, rows_held, 1)
    row_ids = jnp.arange(rows_held, dtype=jnp.int32) + (band_rows - 1)
    band_shift = (row_ids // band_rows - 1) * z_dev - 1
    target = 2 * (row_ids % band_rows)[None, :] + local_offset + 1 + band_shift[None, :]
    plane_ids = jnp.arange(z_dev, dtype=jnp.int32)
    depth_weight = jnp.where(
        plane_ids[None, None, :] == target[:, :, None], (1.0 - local_frac)[:, :, None], 0.0
    )
    depth_weight = depth_weight + jnp.where(
        plane_ids[None, None, :] == target[:, :, None] + 1, local_frac[:, :, None], 0.0
    )
    sectioned = jnp.einsum(
        "ckra,crz->kzca",
        class_bands,
        depth_weight,
        precision=lax.Precision.HIGHEST,
    ).reshape(3 * z_dev, class_count * half_cols)
    y_rows = side_cells // group_count
    y_ids = group_index * y_rows + jnp.arange(y_rows, dtype=jnp.int32)
    row_weights = jnp.where(
        y_ids[:, None, None] == y_base[None, :, :], (1.0 - y_frac)[None, :, :], 0.0
    )
    row_weights = row_weights + jnp.where(
        y_ids[:, None, None] == y_base[None, :, :] + 1, y_frac[None, :, :], 0.0
    )
    row_weights = row_weights.astype(jnp.bfloat16).reshape(y_rows, class_count * half_cols)
    col_weights = stencil_weights(x_base, x_frac, side_cells).reshape(
        class_count * half_cols, side_cells
    )
    inserted = insert_planes(row_weights, sectioned, col_weights)
    return inserted.reshape(3, z_dev, y_rows, side_cells)


def insert_kernel(rows_ref, sec_ref, cols_ref, out_ref, lifted_ref):
    y_rows = rows_ref.shape[0]

    def body(i, carry):
        start = pl.multiple_of(i * y_rows, y_rows)
        lifted_ref[pl.ds(start, y_rows), :] = (
            rows_ref[...].astype(jnp.float32) * sec_ref[pl.ds(i, 1), :]
        ).astype(jnp.bfloat16)
        return carry

    lax.fori_loop(0, sec_ref.shape[0], body, 0)
    out_ref[...] = jnp.dot(lifted_ref[...], cols_ref[...], preferred_element_type=jnp.float32)


def insert_planes(row_weights, sectioned, col_weights):
    planes = sectioned.shape[0]
    y_rows, depth = row_weights.shape
    side = col_weights.shape[1]
    return pl.pallas_call(
        insert_kernel,
        out_shape=jax.ShapeDtypeStruct((planes * y_rows, side), jnp.float32),
        in_specs=[pl.BlockSpec(memory_space=pltpu.VMEM)] * 3,
        out_specs=pl.BlockSpec(memory_space=pltpu.VMEM),
        scratch_shapes=[pltpu.VMEM((planes * y_rows, depth), jnp.bfloat16)],
        cost_estimate=pl.CostEstimate(
            flops=2 * planes * y_rows * depth * side,
            transcendentals=0,
            bytes_accessed=2 * y_rows * depth + 4 * planes * depth + 2 * depth * side
            + 4 * planes * y_rows * side,
        ),
    )(row_weights, sectioned, col_weights)


def solution(mesh):
    in_specs = (
        P(("grp", "slab"), None),
        P(("grp", "slab")),
        P(("grp", "slab")),
        P(),
        P("slab", None),
        P(),
        P(),
        P(),
        P(),
        P(),
        P(),
        P(),
    )
    out_specs = P(None, "slab", "grp", None)
    return jax.shard_map(local, mesh=mesh, in_specs=in_specs, out_specs=out_specs, check_vma=False)
```

```python
import functools
import math

import jax
import jax.numpy as jnp
from jax import lax
from jax.experimental import pallas as pl
from jax.experimental.pallas import tpu as pltpu
from jax.sharding import PartitionSpec as P

SHIFTS = 128
Z_CHIPS = 8


def phase_table(row_count, half_cols):
    shift_ids = jnp.arange(SHIFTS)
    shift_rows = (shift_ids // 8 - SHIFTS // 16).astype(jnp.float32)
    shift_cols = (shift_ids % 8 - 4).astype(jnp.float32)
    lanes = 128
    per_lane_row = lanes // half_cols
    blocks = row_count * half_cols // lanes
    block_rows = (jnp.arange(blocks) * per_lane_row - row_count // 2).astype(jnp.float32)
    lane_ids = jnp.arange(lanes)
    lane_rows = (lane_ids // half_cols).astype(jnp.float32)
    lane_cols = (lane_ids % half_cols).astype(jnp.float32)
    step = 2.0 * math.pi / row_count
    block_angle = shift_rows[:, None] * block_rows[None, :] * step
    lane_angle = (
        shift_rows[:, None] * lane_rows[None, :] + shift_cols[:, None] * lane_cols[None, :]
    ) * step
    cos_b, sin_b = jnp.cos(block_angle)[:, :, None], jnp.sin(block_angle)[:, :, None]
    cos_l, sin_l = jnp.cos(lane_angle)[:, None, :], jnp.sin(lane_angle)[:, None, :]
    cos_t = (cos_b * cos_l - sin_b * sin_l).reshape(SHIFTS, row_count * half_cols)
    sin_t = (sin_b * cos_l + cos_b * sin_l).reshape(SHIFTS, row_count * half_cols)
    return jnp.concatenate([cos_t, sin_t], axis=1).astype(jnp.bfloat16)


def exchange_kernel(count, place, picks, *refs):
    parts = len(picks)
    x_refs, out_refs = refs[:parts], refs[parts : 2 * parts]
    local_sems, send_sems, recv_sems = refs[2 * parts :]
    me, device = place()
    barrier = pltpu.get_barrier_semaphore()
    for k in range(1, count):
        pl.semaphore_signal(
            barrier,
            1,
            device_id=device(lax.rem(me + k, count)),
            device_id_type=pl.DeviceIdType.MESH,
        )
    pl.semaphore_wait(barrier, count - 1)
    owns, copies = [], []
    for part, (pick, x_ref, out_ref) in enumerate(zip(picks, x_refs, out_refs)):
        own = pltpu.make_async_copy(pick(x_ref, me), out_ref.at[me], local_sems.at[part])
        own.start()
        owns.append(own)
        for k in range(1, count):
            peer = lax.rem(me + k, count)
            copy = pltpu.make_async_remote_copy(
                src_ref=pick(x_ref, peer),
                dst_ref=out_ref.at[me],
                send_sem=send_sems.at[part, k],
                recv_sem=recv_sems.at[part, k],
                device_id=device(peer),
                device_id_type=pl.DeviceIdType.MESH,
            )
            copy.start()
            copies.append(copy)
    for own in owns:
        own.wait()
    for copy in copies:
        copy.wait_send()
        copy.wait_recv()


def slab_place():
    group = lax.axis_index("grp")
    return lax.axis_index("slab"), lambda peer: (group, peer)


def core_place():
    group, slab = lax.axis_index("grp"), lax.axis_index("slab")
    return lax.rem(group, 2), lambda peer: (group - lax.rem(group, 2) + peer, slab)


def z_place():
    group, slab = lax.axis_index("grp"), lax.axis_index("slab")
    z = lax.rem(slab, Z_CHIPS)
    return z, lambda peer: (group, slab - z + peer)


def y_place():
    group, slab = lax.axis_index("grp"), lax.axis_index("slab")
    z = lax.rem(slab, Z_CHIPS)
    return slab // Z_CHIPS, lambda peer: (group, peer * Z_CHIPS + z)


def group_place():
    slab = lax.axis_index("slab")
    return lax.axis_index("grp"), lambda peer: (peer, slab)


def whole(x_ref, peer):
    return x_ref.at[0]


def row_block(x_ref, peer):
    return x_ref.at[peer]


def lane_blocks(count):
    def pick(x_ref, peer):
        width = x_ref.shape[1] // count
        return x_ref.at[:, pl.ds(pl.multiple_of(peer * width, width), width)]

    return pick


def exchange_many(xs, count, place, picks, collective_id, block_shapes):
    parts = len(xs)
    return pl.pallas_call(
        functools.partial(exchange_kernel, count, place, tuple(picks)),
        out_shape=[
            jax.ShapeDtypeStruct((count,) + shape, x.dtype) for x, shape in zip(xs, block_shapes)
        ],
        in_specs=[pl.BlockSpec(memory_space=pltpu.VMEM)] * parts,
        out_specs=[pl.BlockSpec(memory_space=pltpu.VMEM)] * parts,
        scratch_shapes=[
            pltpu.SemaphoreType.DMA((parts,)),
            pltpu.SemaphoreType.DMA((parts, count)),
            pltpu.SemaphoreType.DMA((parts, count)),
        ],
        compiler_params=pltpu.CompilerParams(collective_id=collective_id, has_side_effects=True),
    )(*xs)


def exchange(x, count, place, pick, collective_id, block_shape):
    return exchange_many([x], count, place, [pick], collective_id, [block_shape])[0]


def align_frames(frames, ctf_rows, ref_re, ref_im, phase, score_scale):
    pixels = ctf_rows.shape[1]
    frame_re = frames[:, :pixels].astype(jnp.float32)
    frame_im = frames[:, pixels:].astype(jnp.float32)
    ref_re = ref_re.astype(jnp.float32)
    ref_im = ref_im.astype(jnp.float32)
    weight = ctf_rows.astype(jnp.float32)
    cross_terms = jnp.concatenate(
        [
            weight * (ref_re * frame_re + ref_im * frame_im),
            weight * (ref_re * frame_im - ref_im * frame_re),
        ],
        axis=1,
    ).astype(jnp.bfloat16)
    scores = score_scale * jnp.einsum(
        "np,sp->ns", cross_terms, phase, preferred_element_type=jnp.float32
    )
    shift_probs = jax.nn.softmax(scores, axis=1).astype(jnp.bfloat16)
    shift_mix = jnp.dot(shift_probs, phase, preferred_element_type=jnp.float32)
    mix_re = shift_mix[:, :pixels]
    mix_im = shift_mix[:, pixels:]
    return jnp.concatenate(
        [
            weight * (frame_re * mix_re + frame_im * mix_im),
            weight * (frame_im * mix_re - frame_re * mix_im),
        ],
        axis=1,
    )


def stencil_weights(base_cell, fraction, side_cells):
    cell_ids = jnp.arange(side_cells, dtype=jnp.int32)
    dense_weight = jnp.where(
        cell_ids[None, None, :] == base_cell[:, :, None], (1.0 - fraction)[:, :, None], 0.0
    )
    dense_weight = dense_weight + jnp.where(
        cell_ids[None, None, :] == base_cell[:, :, None] + 1, fraction[:, :, None], 0.0
    )
    return dense_weight.astype(jnp.bfloat16)


def local(
    images,
    image_class,
    image_ctf,
    class_owner,
    references,
    ctf_table,
    x_base,
    y_base,
    x_frac,
    y_frac,
    z_offset,
    z_frac,
):
    slab_count = lax.axis_size("slab")
    group_count = lax.axis_size("grp")
    frame_count = images.shape[0]
    pixels = ctf_table.shape[1]
    groups_ctf = ctf_table.shape[0]
    row_count = z_offset.shape[1]
    half_cols = x_base.shape[1]
    class_count = class_owner.shape[0]
    side_cells = 2 * row_count
    band_rows = row_count // slab_count
    band_pixels = band_rows * half_cols
    z_dev = 2 * band_rows
    phase = phase_table(row_count, half_cols)
    score_scale = 2.0 / math.sqrt(2.0 * pixels)
    channel_scale = jnp.array(
        [
            1.0 / math.sqrt(frame_count * group_count),
            1.0 / math.sqrt(frame_count * group_count),
            1.0 / (frame_count * group_count),
        ],
        jnp.float32,
    )
    lanes = 128
    core = lax.rem(lax.axis_index("grp"), 2)
    ref_halves = references.reshape(2, -1, lanes)
    my_half = lax.dynamic_slice_in_dim(ref_halves, core, 1, 0)
    y_chips = slab_count // Z_CHIPS
    row_refs = exchange(my_half, Z_CHIPS, z_place, whole, 0, my_half.shape[1:])
    half_refs = exchange(
        row_refs.reshape(1, -1, lanes), y_chips, y_place, whole, 6, (Z_CHIPS * pixels // lanes, lanes)
    )
    both_halves = exchange(
        half_refs.reshape(1, -1, lanes), 2, core_place, whole, 1, (slab_count * pixels // lanes, lanes)
    ).reshape(2, slab_count, pixels)
    class_ids = jnp.arange(class_count, dtype=jnp.int32)
    owner_of = jnp.sum(
        jnp.where(image_class[:, None] == class_ids[None, :], class_owner[None, :], 0), axis=1
    )
    pick_ref = (owner_of[:, None] == jnp.arange(slab_count, dtype=jnp.int32)[None, :]).astype(
        jnp.bfloat16
    )
    ref_re = jnp.dot(pick_ref, both_halves[0], preferred_element_type=jnp.float32).astype(
        jnp.bfloat16
    )
    ref_im = jnp.dot(pick_ref, both_halves[1], preferred_element_type=jnp.float32).astype(
        jnp.bfloat16
    )
    pick_ctf = (image_ctf[:, None] == jnp.arange(groups_ctf, dtype=jnp.int32)[None, :]).astype(
        jnp.bfloat16
    )
    ctf_rows = jnp.dot(pick_ctf, ctf_table, preferred_element_type=jnp.float32).astype(
        jnp.bfloat16
    )
    stacked = align_frames(images, ctf_rows, ref_re, ref_im, phase, score_scale)
    member = (class_ids[:, None] == image_class[None, :]).astype(jnp.float32)
    partial = jnp.dot(
        member, stacked, precision=lax.Precision.HIGHEST, preferred_element_type=jnp.float32
    ) * channel_scale[0]
    half_rows = class_count // 2 * 2
    class_hits = (class_ids[:, None] == image_class[None, :]).astype(jnp.bfloat16)
    ctf_hits = (image_ctf[:, None] == jnp.arange(groups_ctf, dtype=jnp.int32)[None, :]).astype(
        jnp.bfloat16
    )
    counts = jnp.dot(class_hits, ctf_hits, preferred_element_type=jnp.float32)
    count_rows = class_count * groups_ctf // band_pixels
    tiled_counts = jnp.tile(counts.reshape(count_rows, band_pixels), (1, slab_count))
    rows = half_rows + count_rows
    by_half = jnp.concatenate(
        [partial.reshape(2, half_rows, pixels), jnp.broadcast_to(tiled_counts, (2, count_rows, pixels))],
        axis=1,
    )
    paired = exchange(by_half, 2, core_place, row_block, 2, (rows, pixels))
    pair_sum = (paired[0] + paired[1]).astype(jnp.bfloat16)
    y_chips = slab_count // Z_CHIPS
    by_y = exchange(pair_sum, y_chips, y_place, lane_blocks(y_chips), 3, (rows, pixels // y_chips))
    y_sum = jnp.sum(by_y.astype(jnp.float32), axis=0).astype(jnp.bfloat16)
    arrived = exchange(y_sum, Z_CHIPS, z_place, lane_blocks(Z_CHIPS), 7, (rows, band_pixels))
    chip_band = jnp.sum(arrived.astype(jnp.float32), axis=0).astype(jnp.bfloat16)
    groups = exchange(chip_band[None], group_count, group_place, whole, 4, chip_band.shape)
    groups = groups.astype(jnp.float32).reshape(group_count // 2, 2, rows, band_pixels)
    band = jnp.sum(groups[:, :, :half_rows], axis=0).reshape(class_count, 2, band_rows, half_cols)
    total_counts = jnp.sum(groups[:, 0, half_rows:], axis=0).reshape(class_count, groups_ctf)
    up = [(i, i + 1) for i in range(slab_count - 1)]
    down = [(i + 1, i) for i in range(slab_count - 1)]
    from_below = lax.ppermute(band[:, :, band_rows - 1 :], "slab", up)
    from_above = lax.ppermute(band[:, :, :1], "slab", down)
    data_bands = jnp.concatenate([from_below, band, from_above], axis=2)
    slab_index = lax.axis_index("slab")
    ctf_sq = jnp.pad(
        jnp.square(ctf_table.astype(jnp.float32)), ((0, 0), (half_cols, half_cols))
    )
    window = lax.dynamic_slice_in_dim(
        ctf_sq, slab_index * band_pixels, band_pixels + 2 * half_cols, 1
    )
    weight_rows = jnp.dot(
        total_counts, window, precision=lax.Precision.HIGHEST, preferred_element_type=jnp.float32
    ) * channel_scale[2]
    class_bands = jnp.concatenate(
        [data_bands, weight_rows.reshape(class_count, 1, band_rows + 2, half_cols)], axis=1
    )
    group_index = lax.axis_index("grp")
    offset_pad = jnp.pad(z_offset, ((0, 0), (1, 1)))
    frac_pad = jnp.pad(z_frac, ((0, 0), (1, 1)))
    rows_held = band_rows + 2
    local_offset = lax.dynamic_slice_in_dim(offset_pad, slab_index * band_rows, rows_held, 1)
    local_frac = lax.dynamic_slice_in_dim(frac_pad, slab_index * band_rows, rows_held, 1)
    row_ids = jnp.arange(rows_held, dtype=jnp.int32) + (band_rows - 1)
    band_shift = (row_ids // band_rows - 1) * z_dev - 1
    target = 2 * (row_ids % band_rows)[None, :] + local_offset + 1 + band_shift[None, :]
    plane_ids = jnp.arange(z_dev, dtype=jnp.int32)
    depth_weight = jnp.where(
        plane_ids[None, None, :] == target[:, :, None], (1.0 - local_frac)[:, :, None], 0.0
    )
    depth_weight = depth_weight + jnp.where(
        plane_ids[None, None, :] == target[:, :, None] + 1, local_frac[:, :, None], 0.0
    )
    sectioned = jnp.einsum(
        "ckra,crz->kzca",
        class_bands,
        depth_weight,
        precision=lax.Precision.HIGHEST,
    ).reshape(3 * z_dev, class_count * half_cols)
    y_rows = side_cells // group_count
    y_ids = group_index * y_rows + jnp.arange(y_rows, dtype=jnp.int32)
    row_weights = jnp.where(
        y_ids[:, None, None] == y_base[None, :, :], (1.0 - y_frac)[None, :, :], 0.0
    )
    row_weights = row_weights + jnp.where(
        y_ids[:, None, None] == y_base[None, :, :] + 1, y_frac[None, :, :], 0.0
    )
    row_weights = row_weights.astype(jnp.bfloat16).reshape(y_rows, class_count * half_cols)
    col_weights = stencil_weights(x_base, x_frac, side_cells).reshape(
        class_count * half_cols, side_cells
    )
    inserted = insert_planes(row_weights, sectioned, col_weights)
    return inserted.reshape(3, z_dev, y_rows, side_cells)


def insert_kernel(rows_ref, sec_ref, cols_ref, out_ref, lifted_ref):
    y_rows = rows_ref.shape[0]

    def body(i, carry):
        start = pl.multiple_of(i * y_rows, y_rows)
        lifted_ref[pl.ds(start, y_rows), :] = (
            rows_ref[...].astype(jnp.float32) * sec_ref[pl.ds(i, 1), :]
        ).astype(jnp.bfloat16)
        return carry

    lax.fori_loop(0, sec_ref.shape[0], body, 0)
    out_ref[...] = jnp.dot(lifted_ref[...], cols_ref[...], preferred_element_type=jnp.float32)


def insert_planes(row_weights, sectioned, col_weights):
    planes = sectioned.shape[0]
    y_rows, depth = row_weights.shape
    side = col_weights.shape[1]
    return pl.pallas_call(
        insert_kernel,
        out_shape=jax.ShapeDtypeStruct((planes * y_rows, side), jnp.float32),
        in_specs=[pl.BlockSpec(memory_space=pltpu.VMEM)] * 3,
        out_specs=pl.BlockSpec(memory_space=pltpu.VMEM),
        scratch_shapes=[pltpu.VMEM((planes * y_rows, depth), jnp.bfloat16)],
        cost_estimate=pl.CostEstimate(
            flops=2 * planes * y_rows * depth * side,
            transcendentals=0,
            bytes_accessed=2 * y_rows * depth + 4 * planes * depth + 2 * depth * side
            + 4 * planes * y_rows * side,
        ),
    )(row_weights, sectioned, col_weights)


def solution(mesh):
    in_specs = (
        P(("grp", "slab"), None),
        P(("grp", "slab")),
        P(("grp", "slab")),
        P(),
        P("slab", None),
        P(),
        P(),
        P(),
        P(),
        P(),
        P(),
        P(),
    )
    out_specs = P(None, "slab", "grp", None)
    return jax.shard_map(local, mesh=mesh, in_specs=in_specs, out_specs=out_specs, check_vma=False)
```

```python
import functools
import math

import jax
import jax.numpy as jnp
from jax import lax
from jax.experimental import pallas as pl
from jax.experimental.pallas import tpu as pltpu
from jax.sharding import PartitionSpec as P

SHIFTS = 128
Z_CHIPS = 8


def phase_table(row_count, half_cols):
    shift_ids = jnp.arange(SHIFTS)
    shift_rows = (shift_ids // 8 - SHIFTS // 16).astype(jnp.float32)
    shift_cols = (shift_ids % 8 - 4).astype(jnp.float32)
    lanes = 128
    per_lane_row = lanes // half_cols
    blocks = row_count * half_cols // lanes
    block_rows = (jnp.arange(blocks) * per_lane_row - row_count // 2).astype(jnp.float32)
    lane_ids = jnp.arange(lanes)
    lane_rows = (lane_ids // half_cols).astype(jnp.float32)
    lane_cols = (lane_ids % half_cols).astype(jnp.float32)
    step = 2.0 * math.pi / row_count
    block_angle = shift_rows[:, None] * block_rows[None, :] * step
    lane_angle = (
        shift_rows[:, None] * lane_rows[None, :] + shift_cols[:, None] * lane_cols[None, :]
    ) * step
    cos_b, sin_b = jnp.cos(block_angle)[:, :, None], jnp.sin(block_angle)[:, :, None]
    cos_l, sin_l = jnp.cos(lane_angle)[:, None, :], jnp.sin(lane_angle)[:, None, :]
    cos_t = (cos_b * cos_l - sin_b * sin_l).reshape(SHIFTS, row_count * half_cols)
    sin_t = (sin_b * cos_l + cos_b * sin_l).reshape(SHIFTS, row_count * half_cols)
    return jnp.concatenate([cos_t, sin_t], axis=1).astype(jnp.bfloat16)


def exchange_kernel(count, place, picks, *refs):
    parts = len(picks)
    x_refs, out_refs = refs[:parts], refs[parts : 2 * parts]
    local_sems, send_sems, recv_sems = refs[2 * parts :]
    me, device = place()
    barrier = pltpu.get_barrier_semaphore()
    for k in range(1, count):
        pl.semaphore_signal(
            barrier,
            1,
            device_id=device(lax.rem(me + k, count)),
            device_id_type=pl.DeviceIdType.MESH,
        )
    pl.semaphore_wait(barrier, count - 1)
    owns, copies = [], []
    for part, (pick, x_ref, out_ref) in enumerate(zip(picks, x_refs, out_refs)):
        own = pltpu.make_async_copy(pick(x_ref, me), out_ref.at[me], local_sems.at[part])
        own.start()
        owns.append(own)
        for k in range(1, count):
            peer = lax.rem(me + k, count)
            copy = pltpu.make_async_remote_copy(
                src_ref=pick(x_ref, peer),
                dst_ref=out_ref.at[me],
                send_sem=send_sems.at[part, k],
                recv_sem=recv_sems.at[part, k],
                device_id=device(peer),
                device_id_type=pl.DeviceIdType.MESH,
            )
            copy.start()
            copies.append(copy)
    for own in owns:
        own.wait()
    for copy in copies:
        copy.wait_send()
        copy.wait_recv()


def slab_place():
    group = lax.axis_index("grp")
    return lax.axis_index("slab"), lambda peer: (group, peer)


def core_place():
    group, slab = lax.axis_index("grp"), lax.axis_index("slab")
    return lax.rem(group, 2), lambda peer: (group - lax.rem(group, 2) + peer, slab)


def z_place():
    group, slab = lax.axis_index("grp"), lax.axis_index("slab")
    z = lax.rem(slab, Z_CHIPS)
    return z, lambda peer: (group, slab - z + peer)


def y_place():
    group, slab = lax.axis_index("grp"), lax.axis_index("slab")
    z = lax.rem(slab, Z_CHIPS)
    return slab // Z_CHIPS, lambda peer: (group, peer * Z_CHIPS + z)


def group_place():
    slab = lax.axis_index("slab")
    return lax.axis_index("grp"), lambda peer: (peer, slab)


def whole(x_ref, peer):
    return x_ref.at[0]


def entire(x_ref, peer):
    return x_ref


def row_block(x_ref, peer):
    return x_ref.at[peer]


def lane_blocks(count):
    def pick(x_ref, peer):
        width = x_ref.shape[1] // count
        return x_ref.at[:, pl.ds(pl.multiple_of(peer * width, width), width)]

    return pick


def exchange_many(xs, count, place, picks, collective_id, block_shapes):
    parts = len(xs)
    return pl.pallas_call(
        functools.partial(exchange_kernel, count, place, tuple(picks)),
        out_shape=[
            jax.ShapeDtypeStruct((count,) + shape, x.dtype) for x, shape in zip(xs, block_shapes)
        ],
        in_specs=[pl.BlockSpec(memory_space=pltpu.VMEM)] * parts,
        out_specs=[pl.BlockSpec(memory_space=pltpu.VMEM)] * parts,
        scratch_shapes=[
            pltpu.SemaphoreType.DMA((parts,)),
            pltpu.SemaphoreType.DMA((parts, count)),
            pltpu.SemaphoreType.DMA((parts, count)),
        ],
        compiler_params=pltpu.CompilerParams(collective_id=collective_id, has_side_effects=True),
    )(*xs)


def exchange(x, count, place, pick, collective_id, block_shape):
    return exchange_many([x], count, place, [pick], collective_id, [block_shape])[0]


def signal_all(devices):
    barrier = pltpu.get_barrier_semaphore()
    for device in devices:
        pl.semaphore_signal(barrier, 1, device_id=device, device_id_type=pl.DeviceIdType.MESH)
    pl.semaphore_wait(barrier, len(devices))


def run_phase(count, place, pick, x_ref, out_ref, local_sem, send_sems, recv_sems):
    me, device = place()
    own = pltpu.make_async_copy(pick(x_ref, me), out_ref.at[me], local_sem)
    own.start()
    copies = []
    for k in range(1, count):
        peer = lax.rem(me + k, count)
        copy = pltpu.make_async_remote_copy(
            src_ref=pick(x_ref, peer),
            dst_ref=out_ref.at[me],
            send_sem=send_sems.at[k],
            recv_sem=recv_sems.at[k],
            device_id=device(peer),
            device_id_type=pl.DeviceIdType.MESH,
        )
        copy.start()
        copies.append(copy)
    own.wait()
    for copy in copies:
        copy.wait_send()
        copy.wait_recv()


def peers(count, place):
    me, device = place()
    return [device(lax.rem(me + k, count)) for k in range(1, count)]


def reduce_chain_kernel(y_chips, groups, x_ref, out_ref, core_buf, y_src, y_buf, z_src, z_buf, d_src,
                        local_sems, send_sems, recv_sems):
    signal_all(
        peers(2, core_place)
        + peers(y_chips, y_place)
        + peers(Z_CHIPS, z_place)
        + peers(groups, group_place)
    )
    run_phase(2, core_place, row_block, x_ref, core_buf, local_sems.at[0], send_sems.at[0], recv_sems.at[0])
    y_src[...] = (core_buf[0] + core_buf[1]).astype(y_src.dtype)
    run_phase(
        y_chips, y_place, lane_blocks(y_chips), y_src, y_buf,
        local_sems.at[1], send_sems.at[1], recv_sems.at[1],
    )
    z_src[...] = jnp.sum(y_buf[...].astype(jnp.float32), axis=0).astype(z_src.dtype)
    run_phase(
        Z_CHIPS, z_place, lane_blocks(Z_CHIPS), z_src, z_buf,
        local_sems.at[2], send_sems.at[2], recv_sems.at[2],
    )
    d_src[0] = jnp.sum(z_buf[...].astype(jnp.float32), axis=0).astype(d_src.dtype)
    run_phase(groups, group_place, whole, d_src, out_ref, local_sems.at[3], send_sems.at[3], recv_sems.at[3])


def reduce_chain(x, y_chips, groups, collective_id):
    _, rows, width = x.shape
    band = width // (y_chips * Z_CHIPS)
    wide = 8
    return pl.pallas_call(
        functools.partial(reduce_chain_kernel, y_chips, groups),
        out_shape=jax.ShapeDtypeStruct((groups, rows, band), jnp.bfloat16),
        in_specs=[pl.BlockSpec(memory_space=pltpu.VMEM)],
        out_specs=pl.BlockSpec(memory_space=pltpu.VMEM),
        scratch_shapes=[
            pltpu.VMEM((2, rows, width), x.dtype),
            pltpu.VMEM((rows, width), jnp.bfloat16),
            pltpu.VMEM((y_chips, rows, width // y_chips), jnp.bfloat16),
            pltpu.VMEM((rows, width // y_chips), jnp.bfloat16),
            pltpu.VMEM((Z_CHIPS, rows, band), jnp.bfloat16),
            pltpu.VMEM((1, rows, band), jnp.bfloat16),
            pltpu.SemaphoreType.DMA((4,)),
            pltpu.SemaphoreType.DMA((4, wide)),
            pltpu.SemaphoreType.DMA((4, wide)),
        ],
        compiler_params=pltpu.CompilerParams(collective_id=collective_id, has_side_effects=True),
    )(x)


def gather_chain_kernel(y_chips, x_ref, out_ref, z_buf, y_buf, local_sems, send_sems, recv_sems):
    signal_all(peers(Z_CHIPS, z_place) + peers(y_chips, y_place) + peers(2, core_place))
    run_phase(Z_CHIPS, z_place, whole, x_ref, z_buf, local_sems.at[0], send_sems.at[0], recv_sems.at[0])
    run_phase(y_chips, y_place, entire, z_buf, y_buf, local_sems.at[1], send_sems.at[1], recv_sems.at[1])
    run_phase(2, core_place, entire, y_buf, out_ref, local_sems.at[2], send_sems.at[2], recv_sems.at[2])


def gather_chain(x, y_chips, collective_id):
    _, rows, lanes = x.shape
    return pl.pallas_call(
        functools.partial(gather_chain_kernel, y_chips),
        out_shape=jax.ShapeDtypeStruct((2, y_chips, Z_CHIPS, rows, lanes), x.dtype),
        in_specs=[pl.BlockSpec(memory_space=pltpu.VMEM)],
        out_specs=pl.BlockSpec(memory_space=pltpu.VMEM),
        scratch_shapes=[
            pltpu.VMEM((Z_CHIPS, rows, lanes), x.dtype),
            pltpu.VMEM((y_chips, Z_CHIPS, rows, lanes), x.dtype),
            pltpu.SemaphoreType.DMA((3,)),
            pltpu.SemaphoreType.DMA((3, Z_CHIPS)),
            pltpu.SemaphoreType.DMA((3, Z_CHIPS)),
        ],
        compiler_params=pltpu.CompilerParams(collective_id=collective_id, has_side_effects=True),
    )(x)


def align_frames(frames, ctf_rows, ref_re, ref_im, phase, score_scale):
    pixels = ctf_rows.shape[1]
    frame_re = frames[:, :pixels].astype(jnp.float32)
    frame_im = frames[:, pixels:].astype(jnp.float32)
    ref_re = ref_re.astype(jnp.float32)
    ref_im = ref_im.astype(jnp.float32)
    weight = ctf_rows.astype(jnp.float32)
    cross_terms = jnp.concatenate(
        [
            weight * (ref_re * frame_re + ref_im * frame_im),
            weight * (ref_re * frame_im - ref_im * frame_re),
        ],
        axis=1,
    ).astype(jnp.bfloat16)
    scores = score_scale * jnp.einsum(
        "np,sp->ns", cross_terms, phase, preferred_element_type=jnp.float32
    )
    shift_probs = jax.nn.softmax(scores, axis=1).astype(jnp.bfloat16)
    shift_mix = jnp.dot(shift_probs, phase, preferred_element_type=jnp.float32)
    mix_re = shift_mix[:, :pixels]
    mix_im = shift_mix[:, pixels:]
    return jnp.concatenate(
        [
            weight * (frame_re * mix_re + frame_im * mix_im),
            weight * (frame_im * mix_re - frame_re * mix_im),
        ],
        axis=1,
    )


def stencil_weights(base_cell, fraction, side_cells):
    cell_ids = jnp.arange(side_cells, dtype=jnp.int32)
    dense_weight = jnp.where(
        cell_ids[None, None, :] == base_cell[:, :, None], (1.0 - fraction)[:, :, None], 0.0
    )
    dense_weight = dense_weight + jnp.where(
        cell_ids[None, None, :] == base_cell[:, :, None] + 1, fraction[:, :, None], 0.0
    )
    return dense_weight.astype(jnp.bfloat16)


def local(
    images,
    image_class,
    image_ctf,
    class_owner,
    references,
    ctf_table,
    x_base,
    y_base,
    x_frac,
    y_frac,
    z_offset,
    z_frac,
):
    slab_count = lax.axis_size("slab")
    group_count = lax.axis_size("grp")
    frame_count = images.shape[0]
    pixels = ctf_table.shape[1]
    groups_ctf = ctf_table.shape[0]
    row_count = z_offset.shape[1]
    half_cols = x_base.shape[1]
    class_count = class_owner.shape[0]
    side_cells = 2 * row_count
    band_rows = row_count // slab_count
    band_pixels = band_rows * half_cols
    z_dev = 2 * band_rows
    phase = phase_table(row_count, half_cols)
    score_scale = 2.0 / math.sqrt(2.0 * pixels)
    channel_scale = jnp.array(
        [
            1.0 / math.sqrt(frame_count * group_count),
            1.0 / math.sqrt(frame_count * group_count),
            1.0 / (frame_count * group_count),
        ],
        jnp.float32,
    )
    lanes = 128
    core = lax.rem(lax.axis_index("grp"), 2)
    ref_halves = references.reshape(2, -1, lanes)
    my_half = lax.dynamic_slice_in_dim(ref_halves, core, 1, 0)
    y_chips = slab_count // Z_CHIPS
    both_halves = gather_chain(my_half, y_chips, 0).reshape(2, slab_count, pixels)
    class_ids = jnp.arange(class_count, dtype=jnp.int32)
    owner_of = jnp.sum(
        jnp.where(image_class[:, None] == class_ids[None, :], class_owner[None, :], 0), axis=1
    )
    pick_ref = (owner_of[:, None] == jnp.arange(slab_count, dtype=jnp.int32)[None, :]).astype(
        jnp.bfloat16
    )
    ref_re = jnp.dot(pick_ref, both_halves[0], preferred_element_type=jnp.float32).astype(
        jnp.bfloat16
    )
    ref_im = jnp.dot(pick_ref, both_halves[1], preferred_element_type=jnp.float32).astype(
        jnp.bfloat16
    )
    pick_ctf = (image_ctf[:, None] == jnp.arange(groups_ctf, dtype=jnp.int32)[None, :]).astype(
        jnp.bfloat16
    )
    ctf_rows = jnp.dot(pick_ctf, ctf_table, preferred_element_type=jnp.float32).astype(
        jnp.bfloat16
    )
    stacked = align_frames(images, ctf_rows, ref_re, ref_im, phase, score_scale)
    member = (class_ids[:, None] == image_class[None, :]).astype(jnp.float32)
    partial = jnp.dot(
        member, stacked, precision=lax.Precision.HIGHEST, preferred_element_type=jnp.float32
    ) * channel_scale[0]
    half_rows = class_count // 2 * 2
    class_hits = (class_ids[:, None] == image_class[None, :]).astype(jnp.bfloat16)
    ctf_hits = (image_ctf[:, None] == jnp.arange(groups_ctf, dtype=jnp.int32)[None, :]).astype(
        jnp.bfloat16
    )
    counts = jnp.dot(class_hits, ctf_hits, preferred_element_type=jnp.float32)
    count_rows = class_count * groups_ctf // band_pixels
    tiled_counts = jnp.tile(counts.reshape(count_rows, band_pixels), (1, slab_count))
    rows = half_rows + count_rows
    by_half = jnp.concatenate(
        [partial.reshape(2, half_rows, pixels), jnp.broadcast_to(tiled_counts, (2, count_rows, pixels))],
        axis=1,
    )
    groups = reduce_chain(by_half, slab_count // Z_CHIPS, group_count, 1)
    groups = groups.astype(jnp.float32).reshape(group_count // 2, 2, rows, band_pixels)
    band = jnp.sum(groups[:, :, :half_rows], axis=0).reshape(class_count, 2, band_rows, half_cols)
    total_counts = jnp.sum(groups[:, 0, half_rows:], axis=0).reshape(class_count, groups_ctf)
    up = [(i, i + 1) for i in range(slab_count - 1)]
    down = [(i + 1, i) for i in range(slab_count - 1)]
    from_below = lax.ppermute(band[:, :, band_rows - 1 :], "slab", up)
    from_above = lax.ppermute(band[:, :, :1], "slab", down)
    data_bands = jnp.concatenate([from_below, band, from_above], axis=2)
    slab_index = lax.axis_index("slab")
    ctf_sq = jnp.pad(
        jnp.square(ctf_table.astype(jnp.float32)), ((0, 0), (half_cols, half_cols))
    )
    window = lax.dynamic_slice_in_dim(
        ctf_sq, slab_index * band_pixels, band_pixels + 2 * half_cols, 1
    )
    weight_rows = jnp.dot(
        total_counts, window, precision=lax.Precision.HIGHEST, preferred_element_type=jnp.float32
    ) * channel_scale[2]
    class_bands = jnp.concatenate(
        [data_bands, weight_rows.reshape(class_count, 1, band_rows + 2, half_cols)], axis=1
    )
    group_index = lax.axis_index("grp")
    offset_pad = jnp.pad(z_offset, ((0, 0), (1, 1)))
    frac_pad = jnp.pad(z_frac, ((0, 0), (1, 1)))
    rows_held = band_rows + 2
    local_offset = lax.dynamic_slice_in_dim(offset_pad, slab_index * band_rows, rows_held, 1)
    local_frac = lax.dynamic_slice_in_dim(frac_pad, slab_index * band_rows, rows_held, 1)
    row_ids = jnp.arange(rows_held, dtype=jnp.int32) + (band_rows - 1)
    band_shift = (row_ids // band_rows - 1) * z_dev - 1
    target = 2 * (row_ids % band_rows)[None, :] + local_offset + 1 + band_shift[None, :]
    plane_ids = jnp.arange(z_dev, dtype=jnp.int32)
    depth_weight = jnp.where(
        plane_ids[None, None, :] == target[:, :, None], (1.0 - local_frac)[:, :, None], 0.0
    )
    depth_weight = depth_weight + jnp.where(
        plane_ids[None, None, :] == target[:, :, None] + 1, local_frac[:, :, None], 0.0
    )
    sectioned = jnp.einsum(
        "ckra,crz->kzca",
        class_bands,
        depth_weight,
        precision=lax.Precision.HIGHEST,
    ).reshape(3 * z_dev, class_count * half_cols)
    y_rows = side_cells // group_count
    y_ids = group_index * y_rows + jnp.arange(y_rows, dtype=jnp.int32)
    row_weights = jnp.where(
        y_ids[:, None, None] == y_base[None, :, :], (1.0 - y_frac)[None, :, :], 0.0
    )
    row_weights = row_weights + jnp.where(
        y_ids[:, None, None] == y_base[None, :, :] + 1, y_frac[None, :, :], 0.0
    )
    row_weights = row_weights.astype(jnp.bfloat16).reshape(y_rows, class_count * half_cols)
    col_weights = stencil_weights(x_base, x_frac, side_cells).reshape(
        class_count * half_cols, side_cells
    )
    inserted = insert_planes(row_weights, sectioned, col_weights)
    return inserted.reshape(3, z_dev, y_rows, side_cells)


def insert_kernel(rows_ref, sec_ref, cols_ref, out_ref, lifted_ref):
    y_rows = rows_ref.shape[0]

    def body(i, carry):
        start = pl.multiple_of(i * y_rows, y_rows)
        lifted_ref[pl.ds(start, y_rows), :] = (
            rows_ref[...].astype(jnp.float32) * sec_ref[pl.ds(i, 1), :]
        ).astype(jnp.bfloat16)
        return carry

    lax.fori_loop(0, sec_ref.shape[0], body, 0)
    out_ref[...] = jnp.dot(lifted_ref[...], cols_ref[...], preferred_element_type=jnp.float32)


def insert_planes(row_weights, sectioned, col_weights):
    planes = sectioned.shape[0]
    y_rows, depth = row_weights.shape
    side = col_weights.shape[1]
    return pl.pallas_call(
        insert_kernel,
        out_shape=jax.ShapeDtypeStruct((planes * y_rows, side), jnp.float32),
        in_specs=[pl.BlockSpec(memory_space=pltpu.VMEM)] * 3,
        out_specs=pl.BlockSpec(memory_space=pltpu.VMEM),
        scratch_shapes=[pltpu.VMEM((planes * y_rows, depth), jnp.bfloat16)],
        cost_estimate=pl.CostEstimate(
            flops=2 * planes * y_rows * depth * side,
            transcendentals=0,
            bytes_accessed=2 * y_rows * depth + 4 * planes * depth + 2 * depth * side
            + 4 * planes * y_rows * side,
        ),
    )(row_weights, sectioned, col_weights)


def solution(mesh):
    in_specs = (
        P(("grp", "slab"), None),
        P(("grp", "slab")),
        P(("grp", "slab")),
        P(),
        P("slab", None),
        P(),
        P(),
        P(),
        P(),
        P(),
        P(),
        P(),
    )
    out_specs = P(None, "slab", "grp", None)
    return jax.shard_map(local, mesh=mesh, in_specs=in_specs, out_specs=out_specs, check_vma=False)
```

```python
import functools
import math

import jax
import jax.numpy as jnp
from jax import lax
from jax.experimental import pallas as pl
from jax.experimental.pallas import tpu as pltpu
from jax.sharding import PartitionSpec as P

SHIFTS = 128
Z_CHIPS = 8


def phase_factors(row_count, half_cols):
    shift_ids = jnp.arange(SHIFTS)
    shift_rows = (shift_ids // 8 - SHIFTS // 16).astype(jnp.float32)
    shift_cols = (shift_ids % 8 - 4).astype(jnp.float32)
    lanes = 128
    per_lane_row = lanes // half_cols
    blocks = row_count * half_cols // lanes
    block_rows = (jnp.arange(blocks) * per_lane_row - row_count // 2).astype(jnp.float32)
    lane_ids = jnp.arange(lanes)
    lane_rows = (lane_ids // half_cols).astype(jnp.float32)
    lane_cols = (lane_ids % half_cols).astype(jnp.float32)
    step = 2.0 * math.pi / row_count
    block_angle = shift_rows[:, None] * block_rows[None, :] * step
    lane_angle = (
        shift_rows[:, None] * lane_rows[None, :] + shift_cols[:, None] * lane_cols[None, :]
    ) * step
    return (jnp.cos(block_angle), jnp.sin(block_angle), jnp.cos(lane_angle), jnp.sin(lane_angle))


def exchange_kernel(count, place, picks, *refs):
    parts = len(picks)
    x_refs, out_refs = refs[:parts], refs[parts : 2 * parts]
    local_sems, send_sems, recv_sems = refs[2 * parts :]
    me, device = place()
    barrier = pltpu.get_barrier_semaphore()
    for k in range(1, count):
        pl.semaphore_signal(
            barrier,
            1,
            device_id=device(lax.rem(me + k, count)),
            device_id_type=pl.DeviceIdType.MESH,
        )
    pl.semaphore_wait(barrier, count - 1)
    owns, copies = [], []
    for part, (pick, x_ref, out_ref) in enumerate(zip(picks, x_refs, out_refs)):
        own = pltpu.make_async_copy(pick(x_ref, me), out_ref.at[me], local_sems.at[part])
        own.start()
        owns.append(own)
        for k in range(1, count):
            peer = lax.rem(me + k, count)
            copy = pltpu.make_async_remote_copy(
                src_ref=pick(x_ref, peer),
                dst_ref=out_ref.at[me],
                send_sem=send_sems.at[part, k],
                recv_sem=recv_sems.at[part, k],
                device_id=device(peer),
                device_id_type=pl.DeviceIdType.MESH,
            )
            copy.start()
            copies.append(copy)
    for own in owns:
        own.wait()
    for copy in copies:
        copy.wait_send()
        copy.wait_recv()


def slab_place():
    group = lax.axis_index("grp")
    return lax.axis_index("slab"), lambda peer: (group, peer)


def core_place():
    group, slab = lax.axis_index("grp"), lax.axis_index("slab")
    return lax.rem(group, 2), lambda peer: (group - lax.rem(group, 2) + peer, slab)


def z_place():
    group, slab = lax.axis_index("grp"), lax.axis_index("slab")
    z = lax.rem(slab, Z_CHIPS)
    return z, lambda peer: (group, slab - z + peer)


def y_place():
    group, slab = lax.axis_index("grp"), lax.axis_index("slab")
    z = lax.rem(slab, Z_CHIPS)
    return slab // Z_CHIPS, lambda peer: (group, peer * Z_CHIPS + z)


def group_place():
    slab = lax.axis_index("slab")
    return lax.axis_index("grp"), lambda peer: (peer, slab)


def whole(x_ref, peer):
    return x_ref.at[0]


def entire(x_ref, peer):
    return x_ref


def row_block(x_ref, peer):
    return x_ref.at[peer]


def lane_blocks(count):
    def pick(x_ref, peer):
        width = x_ref.shape[1] // count
        return x_ref.at[:, pl.ds(pl.multiple_of(peer * width, width), width)]

    return pick


def exchange_many(xs, count, place, picks, collective_id, block_shapes):
    parts = len(xs)
    return pl.pallas_call(
        functools.partial(exchange_kernel, count, place, tuple(picks)),
        out_shape=[
            jax.ShapeDtypeStruct((count,) + shape, x.dtype) for x, shape in zip(xs, block_shapes)
        ],
        in_specs=[pl.BlockSpec(memory_space=pltpu.VMEM)] * parts,
        out_specs=[pl.BlockSpec(memory_space=pltpu.VMEM)] * parts,
        scratch_shapes=[
            pltpu.SemaphoreType.DMA((parts,)),
            pltpu.SemaphoreType.DMA((parts, count)),
            pltpu.SemaphoreType.DMA((parts, count)),
        ],
        compiler_params=pltpu.CompilerParams(collective_id=collective_id, has_side_effects=True),
    )(*xs)


def exchange(x, count, place, pick, collective_id, block_shape):
    return exchange_many([x], count, place, [pick], collective_id, [block_shape])[0]


def signal_all(devices):
    barrier = pltpu.get_barrier_semaphore()
    for device in devices:
        pl.semaphore_signal(barrier, 1, device_id=device, device_id_type=pl.DeviceIdType.MESH)
    return lambda: pl.semaphore_wait(barrier, len(devices))


def run_phase(count, place, pick, x_ref, out_ref, local_sem, send_sems, recv_sems):
    me, device = place()
    own = pltpu.make_async_copy(pick(x_ref, me), out_ref.at[me], local_sem)
    own.start()
    copies = []
    for k in range(1, count):
        peer = lax.rem(me + k, count)
        copy = pltpu.make_async_remote_copy(
            src_ref=pick(x_ref, peer),
            dst_ref=out_ref.at[me],
            send_sem=send_sems.at[k],
            recv_sem=recv_sems.at[k],
            device_id=device(peer),
            device_id_type=pl.DeviceIdType.MESH,
        )
        copy.start()
        copies.append(copy)
    own.wait()
    for copy in copies:
        copy.wait_send()
        copy.wait_recv()


def peers(count, place):
    me, device = place()
    return [device(lax.rem(me + k, count)) for k in range(1, count)]


def stencil_kernel(ybase_ref, yfrac_ref, xbase_ref, xfrac_ref, rows_ref, cols_ref):
    y_rows = rows_ref.shape[0]
    y_ids = lax.axis_index("grp") * y_rows + lax.broadcasted_iota(jnp.int32, rows_ref.shape, 0)
    y_base, y_frac = ybase_ref[...], yfrac_ref[...]
    rows = jnp.where(y_ids == y_base, 1.0 - y_frac, 0.0) + jnp.where(y_ids == y_base + 1, y_frac, 0.0)
    rows_ref[...] = rows.astype(rows_ref.dtype)
    x_ids = lax.broadcasted_iota(jnp.int32, cols_ref.shape, 1)
    x_base, x_frac = xbase_ref[...], xfrac_ref[...]
    cols = jnp.where(x_ids == x_base, 1.0 - x_frac, 0.0) + jnp.where(x_ids == x_base + 1, x_frac, 0.0)
    cols_ref[...] = cols.astype(cols_ref.dtype)


def reduce_chain_kernel(y_chips, groups, x_ref, ybase_ref, yfrac_ref, xbase_ref, xfrac_ref,
                        out_ref, rows_ref, cols_ref, core_buf, y_src, y_buf, z_src, z_buf, d_src,
                        local_sems, send_sems, recv_sems):
    arrive = signal_all(
        peers(2, core_place)
        + peers(y_chips, y_place)
        + peers(Z_CHIPS, z_place)
        + peers(groups, group_place)
    )
    stencil_kernel(ybase_ref, yfrac_ref, xbase_ref, xfrac_ref, rows_ref, cols_ref)
    arrive()
    run_phase(2, core_place, row_block, x_ref, core_buf, local_sems.at[0], send_sems.at[0], recv_sems.at[0])
    y_src[...] = (core_buf[0] + core_buf[1]).astype(y_src.dtype)
    run_phase(
        y_chips, y_place, lane_blocks(y_chips), y_src, y_buf,
        local_sems.at[1], send_sems.at[1], recv_sems.at[1],
    )
    z_src[...] = jnp.sum(y_buf[...].astype(jnp.float32), axis=0).astype(z_src.dtype)
    run_phase(
        Z_CHIPS, z_place, lane_blocks(Z_CHIPS), z_src, z_buf,
        local_sems.at[2], send_sems.at[2], recv_sems.at[2],
    )
    d_src[0] = jnp.sum(z_buf[...].astype(jnp.float32), axis=0).astype(d_src.dtype)
    run_phase(groups, group_place, whole, d_src, out_ref, local_sems.at[3], send_sems.at[3], recv_sems.at[3])


def reduce_chain(x, stencil, y_rows, side, y_chips, groups, collective_id):
    _, rows, width = x.shape
    band = width // (y_chips * Z_CHIPS)
    wide = 8
    depth = stencil[0].shape[1]
    return pl.pallas_call(
        functools.partial(reduce_chain_kernel, y_chips, groups),
        out_shape=[
            jax.ShapeDtypeStruct((groups, rows, band), jnp.bfloat16),
            jax.ShapeDtypeStruct((y_rows, depth), jnp.bfloat16),
            jax.ShapeDtypeStruct((depth, side), jnp.bfloat16),
        ],
        in_specs=[pl.BlockSpec(memory_space=pltpu.VMEM)] * 5,
        out_specs=[pl.BlockSpec(memory_space=pltpu.VMEM)] * 3,
        scratch_shapes=[
            pltpu.VMEM((2, rows, width), x.dtype),
            pltpu.VMEM((rows, width), jnp.bfloat16),
            pltpu.VMEM((y_chips, rows, width // y_chips), jnp.bfloat16),
            pltpu.VMEM((rows, width // y_chips), jnp.bfloat16),
            pltpu.VMEM((Z_CHIPS, rows, band), jnp.bfloat16),
            pltpu.VMEM((1, rows, band), jnp.bfloat16),
            pltpu.SemaphoreType.DMA((4,)),
            pltpu.SemaphoreType.DMA((4, wide)),
            pltpu.SemaphoreType.DMA((4, wide)),
        ],
        compiler_params=pltpu.CompilerParams(collective_id=collective_id, has_side_effects=True),
    )(x, *stencil)


def phase_kernel(cos_b, sin_b, cos_l, sin_l, phase_ref):
    half = phase_ref.shape[1] // 2
    lanes = cos_l.shape[1]
    c_l, s_l = cos_l[...], sin_l[...]
    for q in range(cos_b.shape[1]):
        c_b, s_b = cos_b[:, q : q + 1], sin_b[:, q : q + 1]
        phase_ref[:, q * lanes : (q + 1) * lanes] = (c_b * c_l - s_b * s_l).astype(phase_ref.dtype)
        phase_ref[:, half + q * lanes : half + (q + 1) * lanes] = (s_b * c_l + c_b * s_l).astype(
            phase_ref.dtype
        )


def gather_chain_kernel(y_chips, x_ref, cos_b, sin_b, cos_l, sin_l, out_ref, phase_ref, z_buf, y_buf,
                        local_sems, send_sems, recv_sems):
    arrive = signal_all(peers(Z_CHIPS, z_place) + peers(y_chips, y_place) + peers(2, core_place))
    phase_kernel(cos_b, sin_b, cos_l, sin_l, phase_ref)
    arrive()
    run_phase(Z_CHIPS, z_place, whole, x_ref, z_buf, local_sems.at[0], send_sems.at[0], recv_sems.at[0])
    run_phase(y_chips, y_place, entire, z_buf, y_buf, local_sems.at[1], send_sems.at[1], recv_sems.at[1])
    run_phase(2, core_place, entire, y_buf, out_ref, local_sems.at[2], send_sems.at[2], recv_sems.at[2])


def gather_chain(x, trig, y_chips, collective_id):
    _, rows, lanes = x.shape
    shifts = trig[0].shape[0]
    table = 2 * trig[0].shape[1] * trig[2].shape[1]
    return pl.pallas_call(
        functools.partial(gather_chain_kernel, y_chips),
        out_shape=[
            jax.ShapeDtypeStruct((2, y_chips, Z_CHIPS, rows, lanes), x.dtype),
            jax.ShapeDtypeStruct((shifts, table), jnp.bfloat16),
        ],
        in_specs=[pl.BlockSpec(memory_space=pltpu.VMEM)] * 5,
        out_specs=[pl.BlockSpec(memory_space=pltpu.VMEM)] * 2,
        scratch_shapes=[
            pltpu.VMEM((Z_CHIPS, rows, lanes), x.dtype),
            pltpu.VMEM((y_chips, Z_CHIPS, rows, lanes), x.dtype),
            pltpu.SemaphoreType.DMA((3,)),
            pltpu.SemaphoreType.DMA((3, Z_CHIPS)),
            pltpu.SemaphoreType.DMA((3, Z_CHIPS)),
        ],
        compiler_params=pltpu.CompilerParams(collective_id=collective_id, has_side_effects=True),
    )(x, *trig)


def align_frames(frames, ctf_rows, ref_re, ref_im, phase, score_scale):
    pixels = ctf_rows.shape[1]
    frame_re = frames[:, :pixels].astype(jnp.float32)
    frame_im = frames[:, pixels:].astype(jnp.float32)
    ref_re = ref_re.astype(jnp.float32)
    ref_im = ref_im.astype(jnp.float32)
    weight = ctf_rows.astype(jnp.float32)
    cross_terms = jnp.concatenate(
        [
            weight * (ref_re * frame_re + ref_im * frame_im),
            weight * (ref_re * frame_im - ref_im * frame_re),
        ],
        axis=1,
    ).astype(jnp.bfloat16)
    scores = score_scale * jnp.einsum(
        "np,sp->ns", cross_terms, phase, preferred_element_type=jnp.float32
    )
    shift_probs = jax.nn.softmax(scores, axis=1).astype(jnp.bfloat16)
    shift_mix = jnp.dot(shift_probs, phase, preferred_element_type=jnp.float32)
    mix_re = shift_mix[:, :pixels]
    mix_im = shift_mix[:, pixels:]
    return jnp.concatenate(
        [
            weight * (frame_re * mix_re + frame_im * mix_im),
            weight * (frame_im * mix_re - frame_re * mix_im),
        ],
        axis=1,
    )


def stencil_weights(base_cell, fraction, side_cells):
    cell_ids = jnp.arange(side_cells, dtype=jnp.int32)
    dense_weight = jnp.where(
        cell_ids[None, None, :] == base_cell[:, :, None], (1.0 - fraction)[:, :, None], 0.0
    )
    dense_weight = dense_weight + jnp.where(
        cell_ids[None, None, :] == base_cell[:, :, None] + 1, fraction[:, :, None], 0.0
    )
    return dense_weight.astype(jnp.bfloat16)


def local(
    images,
    image_class,
    image_ctf,
    class_owner,
    references,
    ctf_table,
    x_base,
    y_base,
    x_frac,
    y_frac,
    z_offset,
    z_frac,
):
    slab_count = lax.axis_size("slab")
    group_count = lax.axis_size("grp")
    frame_count = images.shape[0]
    pixels = ctf_table.shape[1]
    groups_ctf = ctf_table.shape[0]
    row_count = z_offset.shape[1]
    half_cols = x_base.shape[1]
    class_count = class_owner.shape[0]
    side_cells = 2 * row_count
    band_rows = row_count // slab_count
    band_pixels = band_rows * half_cols
    z_dev = 2 * band_rows
    score_scale = 2.0 / math.sqrt(2.0 * pixels)
    channel_scale = jnp.array(
        [
            1.0 / math.sqrt(frame_count * group_count),
            1.0 / math.sqrt(frame_count * group_count),
            1.0 / (frame_count * group_count),
        ],
        jnp.float32,
    )
    lanes = 128
    core = lax.rem(lax.axis_index("grp"), 2)
    ref_halves = references.reshape(2, -1, lanes)
    my_half = lax.dynamic_slice_in_dim(ref_halves, core, 1, 0)
    y_chips = slab_count // Z_CHIPS
    gathered, phase = gather_chain(my_half, phase_factors(row_count, half_cols), y_chips, 0)
    both_halves = gathered.reshape(2, slab_count, pixels)
    class_ids = jnp.arange(class_count, dtype=jnp.int32)
    owner_of = jnp.sum(
        jnp.where(image_class[:, None] == class_ids[None, :], class_owner[None, :], 0), axis=1
    )
    pick_ref = (owner_of[:, None] == jnp.arange(slab_count, dtype=jnp.int32)[None, :]).astype(
        jnp.bfloat16
    )
    ref_re = jnp.dot(pick_ref, both_halves[0], preferred_element_type=jnp.float32).astype(
        jnp.bfloat16
    )
    ref_im = jnp.dot(pick_ref, both_halves[1], preferred_element_type=jnp.float32).astype(
        jnp.bfloat16
    )
    pick_ctf = (image_ctf[:, None] == jnp.arange(groups_ctf, dtype=jnp.int32)[None, :]).astype(
        jnp.bfloat16
    )
    ctf_rows = jnp.dot(pick_ctf, ctf_table, preferred_element_type=jnp.float32).astype(
        jnp.bfloat16
    )
    stacked = align_frames(images, ctf_rows, ref_re, ref_im, phase, score_scale)
    member = (class_ids[:, None] == image_class[None, :]).astype(jnp.float32)
    partial = jnp.dot(
        member, stacked, precision=lax.Precision.HIGHEST, preferred_element_type=jnp.float32
    ) * channel_scale[0]
    half_rows = class_count // 2 * 2
    class_hits = (class_ids[:, None] == image_class[None, :]).astype(jnp.bfloat16)
    ctf_hits = (image_ctf[:, None] == jnp.arange(groups_ctf, dtype=jnp.int32)[None, :]).astype(
        jnp.bfloat16
    )
    counts = jnp.dot(class_hits, ctf_hits, preferred_element_type=jnp.float32)
    count_rows = class_count * groups_ctf // band_pixels
    tiled_counts = jnp.tile(counts.reshape(count_rows, band_pixels), (1, slab_count))
    rows = half_rows + count_rows
    by_half = jnp.concatenate(
        [partial.reshape(2, half_rows, pixels), jnp.broadcast_to(tiled_counts, (2, count_rows, pixels))],
        axis=1,
    )
    y_rows = side_cells // group_count
    flat = class_count * half_cols
    stencil = (
        y_base.reshape(1, flat),
        y_frac.reshape(1, flat),
        x_base.reshape(flat, 1),
        x_frac.reshape(flat, 1),
    )
    groups, row_weights, col_weights = reduce_chain(
        by_half, stencil, y_rows, side_cells, slab_count // Z_CHIPS, group_count, 1
    )
    groups = groups.astype(jnp.float32).reshape(group_count // 2, 2, rows, band_pixels)
    band = jnp.sum(groups[:, :, :half_rows], axis=0).reshape(class_count, 2, band_rows, half_cols)
    total_counts = jnp.sum(groups[:, 0, half_rows:], axis=0).reshape(class_count, groups_ctf)
    up = [(i, i + 1) for i in range(slab_count - 1)]
    down = [(i + 1, i) for i in range(slab_count - 1)]
    from_below = lax.ppermute(band[:, :, band_rows - 1 :], "slab", up)
    from_above = lax.ppermute(band[:, :, :1], "slab", down)
    data_bands = jnp.concatenate([from_below, band, from_above], axis=2)
    slab_index = lax.axis_index("slab")
    ctf_sq = jnp.pad(
        jnp.square(ctf_table.astype(jnp.float32)), ((0, 0), (half_cols, half_cols))
    )
    window = lax.dynamic_slice_in_dim(
        ctf_sq, slab_index * band_pixels, band_pixels + 2 * half_cols, 1
    )
    weight_rows = jnp.dot(
        total_counts, window, precision=lax.Precision.HIGHEST, preferred_element_type=jnp.float32
    ) * channel_scale[2]
    class_bands = jnp.concatenate(
        [data_bands, weight_rows.reshape(class_count, 1, band_rows + 2, half_cols)], axis=1
    )
    group_index = lax.axis_index("grp")
    offset_pad = jnp.pad(z_offset, ((0, 0), (1, 1)))
    frac_pad = jnp.pad(z_frac, ((0, 0), (1, 1)))
    rows_held = band_rows + 2
    local_offset = lax.dynamic_slice_in_dim(offset_pad, slab_index * band_rows, rows_held, 1)
    local_frac = lax.dynamic_slice_in_dim(frac_pad, slab_index * band_rows, rows_held, 1)
    row_ids = jnp.arange(rows_held, dtype=jnp.int32) + (band_rows - 1)
    band_shift = (row_ids // band_rows - 1) * z_dev - 1
    target = 2 * (row_ids % band_rows)[None, :] + local_offset + 1 + band_shift[None, :]
    plane_ids = jnp.arange(z_dev, dtype=jnp.int32)
    depth_weight = jnp.where(
        plane_ids[None, None, :] == target[:, :, None], (1.0 - local_frac)[:, :, None], 0.0
    )
    depth_weight = depth_weight + jnp.where(
        plane_ids[None, None, :] == target[:, :, None] + 1, local_frac[:, :, None], 0.0
    )
    sectioned = jnp.einsum(
        "ckra,crz->kzca",
        class_bands,
        depth_weight,
        precision=lax.Precision.HIGHEST,
    ).reshape(3 * z_dev, class_count * half_cols)
    inserted = insert_planes(row_weights, sectioned, col_weights)
    return inserted.reshape(3, z_dev, y_rows, side_cells)


def insert_kernel(rows_ref, sec_ref, cols_ref, out_ref, lifted_ref):
    y_rows = rows_ref.shape[0]

    def body(i, carry):
        start = pl.multiple_of(i * y_rows, y_rows)
        lifted_ref[pl.ds(start, y_rows), :] = (
            rows_ref[...].astype(jnp.float32) * sec_ref[pl.ds(i, 1), :]
        ).astype(jnp.bfloat16)
        return carry

    lax.fori_loop(0, sec_ref.shape[0], body, 0)
    out_ref[...] = jnp.dot(lifted_ref[...], cols_ref[...], preferred_element_type=jnp.float32)


def insert_planes(row_weights, sectioned, col_weights):
    planes = sectioned.shape[0]
    y_rows, depth = row_weights.shape
    side = col_weights.shape[1]
    return pl.pallas_call(
        insert_kernel,
        out_shape=jax.ShapeDtypeStruct((planes * y_rows, side), jnp.float32),
        in_specs=[pl.BlockSpec(memory_space=pltpu.VMEM)] * 3,
        out_specs=pl.BlockSpec(memory_space=pltpu.VMEM),
        scratch_shapes=[pltpu.VMEM((planes * y_rows, depth), jnp.bfloat16)],
        cost_estimate=pl.CostEstimate(
            flops=2 * planes * y_rows * depth * side,
            transcendentals=0,
            bytes_accessed=2 * y_rows * depth + 4 * planes * depth + 2 * depth * side
            + 4 * planes * y_rows * side,
        ),
    )(row_weights, sectioned, col_weights)


def solution(mesh):
    in_specs = (
        P(("grp", "slab"), None),
        P(("grp", "slab")),
        P(("grp", "slab")),
        P(),
        P("slab", None),
        P(),
        P(),
        P(),
        P(),
        P(),
        P(),
        P(),
    )
    out_specs = P(None, "slab", "grp", None)
    return jax.shard_map(local, mesh=mesh, in_specs=in_specs, out_specs=out_specs, check_vma=False)
```

```python
import functools
import math

import jax
import jax.numpy as jnp
from jax import lax
from jax.experimental import pallas as pl
from jax.experimental.pallas import tpu as pltpu
from jax.sharding import PartitionSpec as P

SHIFTS = 128
Z_CHIPS = 8


def phase_factors(row_count, half_cols):
    shift_ids = jnp.arange(SHIFTS)
    shift_rows = (shift_ids // 8 - SHIFTS // 16).astype(jnp.float32)
    shift_cols = (shift_ids % 8 - 4).astype(jnp.float32)
    lanes = 128
    per_lane_row = lanes // half_cols
    blocks = row_count * half_cols // lanes
    block_rows = (jnp.arange(blocks) * per_lane_row - row_count // 2).astype(jnp.float32)
    lane_ids = jnp.arange(lanes)
    lane_rows = (lane_ids // half_cols).astype(jnp.float32)
    lane_cols = (lane_ids % half_cols).astype(jnp.float32)
    step = 2.0 * math.pi / row_count
    block_angle = shift_rows[:, None] * block_rows[None, :] * step
    lane_angle = (
        shift_rows[:, None] * lane_rows[None, :] + shift_cols[:, None] * lane_cols[None, :]
    ) * step
    return (jnp.cos(block_angle), jnp.sin(block_angle), jnp.cos(lane_angle), jnp.sin(lane_angle))


def exchange_kernel(count, place, picks, *refs):
    parts = len(picks)
    x_refs, out_refs = refs[:parts], refs[parts : 2 * parts]
    local_sems, send_sems, recv_sems = refs[2 * parts :]
    me, device = place()
    barrier = pltpu.get_barrier_semaphore()
    for k in range(1, count):
        pl.semaphore_signal(
            barrier,
            1,
            device_id=device(lax.rem(me + k, count)),
            device_id_type=pl.DeviceIdType.MESH,
        )
    pl.semaphore_wait(barrier, count - 1)
    owns, copies = [], []
    for part, (pick, x_ref, out_ref) in enumerate(zip(picks, x_refs, out_refs)):
        own = pltpu.make_async_copy(pick(x_ref, me), out_ref.at[me], local_sems.at[part])
        own.start()
        owns.append(own)
        for k in range(1, count):
            peer = lax.rem(me + k, count)
            copy = pltpu.make_async_remote_copy(
                src_ref=pick(x_ref, peer),
                dst_ref=out_ref.at[me],
                send_sem=send_sems.at[part, k],
                recv_sem=recv_sems.at[part, k],
                device_id=device(peer),
                device_id_type=pl.DeviceIdType.MESH,
            )
            copy.start()
            copies.append(copy)
    for own in owns:
        own.wait()
    for copy in copies:
        copy.wait_send()
        copy.wait_recv()


def slab_place():
    group = lax.axis_index("grp")
    return lax.axis_index("slab"), lambda peer: (group, peer)


def core_place():
    group, slab = lax.axis_index("grp"), lax.axis_index("slab")
    return lax.rem(group, 2), lambda peer: (group - lax.rem(group, 2) + peer, slab)


def z_place():
    group, slab = lax.axis_index("grp"), lax.axis_index("slab")
    z = lax.rem(slab, Z_CHIPS)
    return z, lambda peer: (group, slab - z + peer)


def y_place():
    group, slab = lax.axis_index("grp"), lax.axis_index("slab")
    z = lax.rem(slab, Z_CHIPS)
    return slab // Z_CHIPS, lambda peer: (group, peer * Z_CHIPS + z)


def group_place():
    slab = lax.axis_index("slab")
    return lax.axis_index("grp"), lambda peer: (peer, slab)


def whole(x_ref, peer):
    return x_ref.at[0]


def entire(x_ref, peer):
    return x_ref


def row_block(x_ref, peer):
    return x_ref.at[peer]


def lane_blocks(count):
    def pick(x_ref, peer):
        width = x_ref.shape[1] // count
        return x_ref.at[:, pl.ds(pl.multiple_of(peer * width, width), width)]

    return pick


def exchange_many(xs, count, place, picks, collective_id, block_shapes):
    parts = len(xs)
    return pl.pallas_call(
        functools.partial(exchange_kernel, count, place, tuple(picks)),
        out_shape=[
            jax.ShapeDtypeStruct((count,) + shape, x.dtype) for x, shape in zip(xs, block_shapes)
        ],
        in_specs=[pl.BlockSpec(memory_space=pltpu.VMEM)] * parts,
        out_specs=[pl.BlockSpec(memory_space=pltpu.VMEM)] * parts,
        scratch_shapes=[
            pltpu.SemaphoreType.DMA((parts,)),
            pltpu.SemaphoreType.DMA((parts, count)),
            pltpu.SemaphoreType.DMA((parts, count)),
        ],
        compiler_params=pltpu.CompilerParams(collective_id=collective_id, has_side_effects=True),
    )(*xs)


def exchange(x, count, place, pick, collective_id, block_shape):
    return exchange_many([x], count, place, [pick], collective_id, [block_shape])[0]


def signal_all(devices):
    barrier = pltpu.get_barrier_semaphore()
    for device in devices:
        pl.semaphore_signal(barrier, 1, device_id=device, device_id_type=pl.DeviceIdType.MESH)
    return lambda: pl.semaphore_wait(barrier, len(devices))


def run_phase(count, place, pick, x_ref, out_ref, local_sem, send_sems, recv_sems):
    me, device = place()
    own = pltpu.make_async_copy(pick(x_ref, me), out_ref.at[me], local_sem)
    own.start()
    copies = []
    for k in range(1, count):
        peer = lax.rem(me + k, count)
        copy = pltpu.make_async_remote_copy(
            src_ref=pick(x_ref, peer),
            dst_ref=out_ref.at[me],
            send_sem=send_sems.at[k],
            recv_sem=recv_sems.at[k],
            device_id=device(peer),
            device_id_type=pl.DeviceIdType.MESH,
        )
        copy.start()
        copies.append(copy)
    own.wait()
    for copy in copies:
        copy.wait_send()
        copy.wait_recv()


def peers(count, place):
    me, device = place()
    return [device(lax.rem(me + k, count)) for k in range(1, count)]


def stencil_kernel(base_ref, frac_ref, rows_ref, cols_ref):
    y_rows = rows_ref.shape[0]
    y_ids = lax.axis_index("grp") * y_rows + lax.broadcasted_iota(jnp.int32, rows_ref.shape, 0)
    y_base, y_frac = base_ref[0:1, :], frac_ref[0:1, :]
    rows = jnp.where(y_ids == y_base, 1.0 - y_frac, 0.0) + jnp.where(y_ids == y_base + 1, y_frac, 0.0)
    rows_ref[...] = rows.astype(rows_ref.dtype)
    x_ids = lax.broadcasted_iota(jnp.int32, cols_ref.shape, 0)
    x_base, x_frac = base_ref[1:2, :], frac_ref[1:2, :]
    cols = jnp.where(x_ids == x_base, 1.0 - x_frac, 0.0) + jnp.where(x_ids == x_base + 1, x_frac, 0.0)
    cols_ref[...] = cols.astype(cols_ref.dtype)


def neighbour_place():
    group, slab = lax.axis_index("grp"), lax.axis_index("slab")
    count = lax.axis_size("slab")
    return [(group, lax.rem(slab + 1, count)), (group, lax.rem(slab + count - 1, count))]


def reduce_chain_kernel(y_chips, groups, x_ref, base_ref, frac_ref,
                        total_ref, halo_ref, rows_ref, cols_ref, core_buf, y_src, y_buf, z_src, z_buf,
                        d_src, d_buf, local_sems, send_sems, recv_sems, halo_send, halo_recv):
    arrive = signal_all(
        peers(2, core_place)
        + peers(y_chips, y_place)
        + peers(Z_CHIPS, z_place)
        + peers(groups, group_place)
        + neighbour_place()
    )
    stencil_kernel(base_ref, frac_ref, rows_ref, cols_ref)
    arrive()
    run_phase(2, core_place, row_block, x_ref, core_buf, local_sems.at[0], send_sems.at[0], recv_sems.at[0])
    y_src[...] = (core_buf[0] + core_buf[1]).astype(y_src.dtype)
    run_phase(
        y_chips, y_place, lane_blocks(y_chips), y_src, y_buf,
        local_sems.at[1], send_sems.at[1], recv_sems.at[1],
    )
    z_src[...] = jnp.sum(y_buf[...].astype(jnp.float32), axis=0).astype(z_src.dtype)
    run_phase(
        Z_CHIPS, z_place, lane_blocks(Z_CHIPS), z_src, z_buf,
        local_sems.at[2], send_sems.at[2], recv_sems.at[2],
    )
    d_src[0] = jnp.sum(z_buf[...].astype(jnp.float32), axis=0).astype(d_src.dtype)
    run_phase(groups, group_place, whole, d_src, d_buf, local_sems.at[3], send_sems.at[3], recv_sems.at[3])
    for half in range(2):
        total_ref[half] = jnp.sum(
            jnp.stack([d_buf[j].astype(jnp.float32) for j in range(half, groups, 2)]), axis=0
        )
    copies = []
    for side, device in enumerate(neighbour_place()):
        copy = pltpu.make_async_remote_copy(
            src_ref=total_ref,
            dst_ref=halo_ref.at[side],
            send_sem=halo_send.at[side],
            recv_sem=halo_recv.at[side],
            device_id=device,
            device_id_type=pl.DeviceIdType.MESH,
        )
        copy.start()
        copies.append(copy)
    for copy in copies:
        copy.wait_send()
        copy.wait_recv()


def reduce_chain(x, stencil, y_rows, side, y_chips, groups, collective_id):
    _, rows, width = x.shape
    band = width // (y_chips * Z_CHIPS)
    wide = 8
    depth = stencil[0].shape[1]
    return pl.pallas_call(
        functools.partial(reduce_chain_kernel, y_chips, groups),
        out_shape=[
            jax.ShapeDtypeStruct((2, rows, band), jnp.float32),
            jax.ShapeDtypeStruct((2, 2, rows, band), jnp.float32),
            jax.ShapeDtypeStruct((y_rows, depth), jnp.bfloat16),
            jax.ShapeDtypeStruct((side, depth), jnp.bfloat16),
        ],
        in_specs=[pl.BlockSpec(memory_space=pltpu.VMEM)] * 3,
        out_specs=[pl.BlockSpec(memory_space=pltpu.VMEM)] * 4,
        scratch_shapes=[
            pltpu.VMEM((2, rows, width), x.dtype),
            pltpu.VMEM((rows, width), jnp.bfloat16),
            pltpu.VMEM((y_chips, rows, width // y_chips), jnp.bfloat16),
            pltpu.VMEM((rows, width // y_chips), jnp.bfloat16),
            pltpu.VMEM((Z_CHIPS, rows, band), jnp.bfloat16),
            pltpu.VMEM((1, rows, band), jnp.bfloat16),
            pltpu.VMEM((groups, rows, band), jnp.bfloat16),
            pltpu.SemaphoreType.DMA((4,)),
            pltpu.SemaphoreType.DMA((4, wide)),
            pltpu.SemaphoreType.DMA((4, wide)),
            pltpu.SemaphoreType.DMA((2,)),
            pltpu.SemaphoreType.DMA((2,)),
        ],
        compiler_params=pltpu.CompilerParams(collective_id=collective_id, has_side_effects=True),
    )(x, *stencil)


def phase_kernel(cos_b, sin_b, cos_l, sin_l, phase_ref):
    half = phase_ref.shape[1] // 2
    lanes = cos_l.shape[1]
    c_l, s_l = cos_l[...], sin_l[...]
    for q in range(cos_b.shape[1]):
        c_b, s_b = cos_b[:, q : q + 1], sin_b[:, q : q + 1]
        phase_ref[:, q * lanes : (q + 1) * lanes] = (c_b * c_l - s_b * s_l).astype(phase_ref.dtype)
        phase_ref[:, half + q * lanes : half + (q + 1) * lanes] = (s_b * c_l + c_b * s_l).astype(
            phase_ref.dtype
        )


def gather_chain_kernel(y_chips, x_ref, cos_b, sin_b, cos_l, sin_l, out_ref, phase_ref, z_buf, y_buf,
                        local_sems, send_sems, recv_sems):
    arrive = signal_all(peers(Z_CHIPS, z_place) + peers(y_chips, y_place) + peers(2, core_place))
    phase_kernel(cos_b, sin_b, cos_l, sin_l, phase_ref)
    arrive()
    run_phase(Z_CHIPS, z_place, whole, x_ref, z_buf, local_sems.at[0], send_sems.at[0], recv_sems.at[0])
    run_phase(y_chips, y_place, entire, z_buf, y_buf, local_sems.at[1], send_sems.at[1], recv_sems.at[1])
    run_phase(2, core_place, entire, y_buf, out_ref, local_sems.at[2], send_sems.at[2], recv_sems.at[2])


def gather_chain(x, trig, y_chips, collective_id):
    _, rows, lanes = x.shape
    shifts = trig[0].shape[0]
    table = 2 * trig[0].shape[1] * trig[2].shape[1]
    return pl.pallas_call(
        functools.partial(gather_chain_kernel, y_chips),
        out_shape=[
            jax.ShapeDtypeStruct((2, y_chips, Z_CHIPS, rows, lanes), x.dtype),
            jax.ShapeDtypeStruct((shifts, table), jnp.bfloat16),
        ],
        in_specs=[pl.BlockSpec(memory_space=pltpu.VMEM)] * 5,
        out_specs=[pl.BlockSpec(memory_space=pltpu.VMEM)] * 2,
        scratch_shapes=[
            pltpu.VMEM((Z_CHIPS, rows, lanes), x.dtype),
            pltpu.VMEM((y_chips, Z_CHIPS, rows, lanes), x.dtype),
            pltpu.SemaphoreType.DMA((3,)),
            pltpu.SemaphoreType.DMA((3, Z_CHIPS)),
            pltpu.SemaphoreType.DMA((3, Z_CHIPS)),
        ],
        compiler_params=pltpu.CompilerParams(collective_id=collective_id, has_side_effects=True),
    )(x, *trig)


def align_frames(frames, ctf_rows, ref_re, ref_im, phase, score_scale):
    pixels = ctf_rows.shape[1]
    frame_re = frames[:, :pixels].astype(jnp.float32)
    frame_im = frames[:, pixels:].astype(jnp.float32)
    ref_re = ref_re.astype(jnp.float32)
    ref_im = ref_im.astype(jnp.float32)
    weight = ctf_rows.astype(jnp.float32)
    cross_terms = jnp.concatenate(
        [
            weight * (ref_re * frame_re + ref_im * frame_im),
            weight * (ref_re * frame_im - ref_im * frame_re),
        ],
        axis=1,
    ).astype(jnp.bfloat16)
    scores = score_scale * jnp.einsum(
        "np,sp->ns", cross_terms, phase, preferred_element_type=jnp.float32
    )
    shift_probs = jax.nn.softmax(scores, axis=1).astype(jnp.bfloat16)
    shift_mix = jnp.dot(shift_probs, phase, preferred_element_type=jnp.float32)
    mix_re = shift_mix[:, :pixels]
    mix_im = shift_mix[:, pixels:]
    return jnp.concatenate(
        [
            weight * (frame_re * mix_re + frame_im * mix_im),
            weight * (frame_im * mix_re - frame_re * mix_im),
        ],
        axis=1,
    )


def stencil_weights(base_cell, fraction, side_cells):
    cell_ids = jnp.arange(side_cells, dtype=jnp.int32)
    dense_weight = jnp.where(
        cell_ids[None, None, :] == base_cell[:, :, None], (1.0 - fraction)[:, :, None], 0.0
    )
    dense_weight = dense_weight + jnp.where(
        cell_ids[None, None, :] == base_cell[:, :, None] + 1, fraction[:, :, None], 0.0
    )
    return dense_weight.astype(jnp.bfloat16)


def local(
    images,
    image_class,
    image_ctf,
    class_owner,
    references,
    ctf_table,
    x_base,
    y_base,
    x_frac,
    y_frac,
    z_offset,
    z_frac,
):
    slab_count = lax.axis_size("slab")
    group_count = lax.axis_size("grp")
    frame_count = images.shape[0]
    pixels = ctf_table.shape[1]
    groups_ctf = ctf_table.shape[0]
    row_count = z_offset.shape[1]
    half_cols = x_base.shape[1]
    class_count = class_owner.shape[0]
    side_cells = 2 * row_count
    band_rows = row_count // slab_count
    band_pixels = band_rows * half_cols
    z_dev = 2 * band_rows
    score_scale = 2.0 / math.sqrt(2.0 * pixels)
    channel_scale = jnp.array(
        [
            1.0 / math.sqrt(frame_count * group_count),
            1.0 / math.sqrt(frame_count * group_count),
            1.0 / (frame_count * group_count),
        ],
        jnp.float32,
    )
    lanes = 128
    core = lax.rem(lax.axis_index("grp"), 2)
    ref_halves = references.reshape(2, -1, lanes)
    my_half = lax.dynamic_slice_in_dim(ref_halves, core, 1, 0)
    y_chips = slab_count // Z_CHIPS
    gathered, phase = gather_chain(my_half, phase_factors(row_count, half_cols), y_chips, 0)
    both_halves = gathered.reshape(2, slab_count, pixels)
    class_ids = jnp.arange(class_count, dtype=jnp.int32)
    owner_of = jnp.sum(
        jnp.where(image_class[:, None] == class_ids[None, :], class_owner[None, :], 0), axis=1
    )
    pick_ref = (owner_of[:, None] == jnp.arange(slab_count, dtype=jnp.int32)[None, :]).astype(
        jnp.bfloat16
    )
    ref_re = jnp.dot(pick_ref, both_halves[0], preferred_element_type=jnp.float32).astype(
        jnp.bfloat16
    )
    ref_im = jnp.dot(pick_ref, both_halves[1], preferred_element_type=jnp.float32).astype(
        jnp.bfloat16
    )
    pick_ctf = (image_ctf[:, None] == jnp.arange(groups_ctf, dtype=jnp.int32)[None, :]).astype(
        jnp.bfloat16
    )
    ctf_rows = jnp.dot(pick_ctf, ctf_table, preferred_element_type=jnp.float32).astype(
        jnp.bfloat16
    )
    stacked = align_frames(images, ctf_rows, ref_re, ref_im, phase, score_scale)
    member = (class_ids[:, None] == image_class[None, :]).astype(jnp.float32)
    partial = jnp.dot(
        member, stacked, precision=lax.Precision.HIGHEST, preferred_element_type=jnp.float32
    ) * channel_scale[0]
    half_rows = class_count // 2 * 2
    class_hits = (class_ids[:, None] == image_class[None, :]).astype(jnp.bfloat16)
    ctf_hits = (image_ctf[:, None] == jnp.arange(groups_ctf, dtype=jnp.int32)[None, :]).astype(
        jnp.bfloat16
    )
    counts = jnp.dot(class_hits, ctf_hits, preferred_element_type=jnp.float32)
    count_rows = class_count * groups_ctf // band_pixels
    tiled_counts = jnp.tile(counts.reshape(count_rows, band_pixels), (1, slab_count))
    rows = half_rows + count_rows
    by_half = jnp.concatenate(
        [partial.reshape(2, half_rows, pixels), jnp.broadcast_to(tiled_counts, (2, count_rows, pixels))],
        axis=1,
    )
    y_rows = side_cells // group_count
    flat = class_count * half_cols
    stencil = (
        jnp.stack([y_base.reshape(flat), x_base.reshape(flat)]),
        jnp.stack([y_frac.reshape(flat), x_frac.reshape(flat)]),
    )
    total, halo, row_weights, col_weights = reduce_chain(
        by_half, stencil, y_rows, side_cells, slab_count // Z_CHIPS, group_count, 1
    )
    band = total[:, :half_rows].reshape(class_count, 2, band_rows, half_cols)
    total_counts = total[0, half_rows:].reshape(class_count, groups_ctf)
    halo = halo[:, :, :half_rows].reshape(2, class_count, 2, band_rows, half_cols)
    slab_index = lax.axis_index("slab")
    from_below = jnp.where(slab_index > 0, halo[0][:, :, band_rows - 1 :], 0.0)
    from_above = jnp.where(slab_index < slab_count - 1, halo[1][:, :, :1], 0.0)
    data_bands = jnp.concatenate([from_below, band, from_above], axis=2)
    slab_index = lax.axis_index("slab")
    ctf_sq = jnp.pad(
        jnp.square(ctf_table.astype(jnp.float32)), ((0, 0), (half_cols, half_cols))
    )
    window = lax.dynamic_slice_in_dim(
        ctf_sq, slab_index * band_pixels, band_pixels + 2 * half_cols, 1
    )
    weight_rows = jnp.dot(
        total_counts, window, precision=lax.Precision.HIGHEST, preferred_element_type=jnp.float32
    ) * channel_scale[2]
    class_bands = jnp.concatenate(
        [data_bands, weight_rows.reshape(class_count, 1, band_rows + 2, half_cols)], axis=1
    )
    group_index = lax.axis_index("grp")
    offset_pad = jnp.pad(z_offset, ((0, 0), (1, 1)))
    frac_pad = jnp.pad(z_frac, ((0, 0), (1, 1)))
    rows_held = band_rows + 2
    local_offset = lax.dynamic_slice_in_dim(offset_pad, slab_index * band_rows, rows_held, 1)
    local_frac = lax.dynamic_slice_in_dim(frac_pad, slab_index * band_rows, rows_held, 1)
    row_ids = jnp.arange(rows_held, dtype=jnp.int32) + (band_rows - 1)
    band_shift = (row_ids // band_rows - 1) * z_dev - 1
    target = 2 * (row_ids % band_rows)[None, :] + local_offset + 1 + band_shift[None, :]
    plane_ids = jnp.arange(z_dev, dtype=jnp.int32)
    depth_weight = jnp.where(
        plane_ids[None, None, :] == target[:, :, None], (1.0 - local_frac)[:, :, None], 0.0
    )
    depth_weight = depth_weight + jnp.where(
        plane_ids[None, None, :] == target[:, :, None] + 1, local_frac[:, :, None], 0.0
    )
    sectioned = jnp.einsum(
        "ckra,crz->kzca",
        class_bands,
        depth_weight,
        precision=lax.Precision.HIGHEST,
    ).reshape(3 * z_dev, class_count * half_cols)
    inserted = insert_planes(row_weights, sectioned, col_weights)
    return inserted.reshape(3, z_dev, y_rows, side_cells)


def insert_kernel(rows_ref, sec_ref, cols_ref, out_ref, lifted_ref):
    y_rows = rows_ref.shape[0]

    def body(i, carry):
        start = pl.multiple_of(i * y_rows, y_rows)
        lifted_ref[pl.ds(start, y_rows), :] = (
            rows_ref[...].astype(jnp.float32) * sec_ref[pl.ds(i, 1), :]
        ).astype(jnp.bfloat16)
        return carry

    lax.fori_loop(0, sec_ref.shape[0], body, 0)
    out_ref[...] = lax.dot_general(
        lifted_ref[...], cols_ref[...], (((1,), (1,)), ((), ())), preferred_element_type=jnp.float32
    )


def insert_planes(row_weights, sectioned, col_weights):
    planes = sectioned.shape[0]
    y_rows, depth = row_weights.shape
    side = col_weights.shape[0]
    return pl.pallas_call(
        insert_kernel,
        out_shape=jax.ShapeDtypeStruct((planes * y_rows, side), jnp.float32),
        in_specs=[pl.BlockSpec(memory_space=pltpu.VMEM)] * 3,
        out_specs=pl.BlockSpec(memory_space=pltpu.VMEM),
        scratch_shapes=[pltpu.VMEM((planes * y_rows, depth), jnp.bfloat16)],
        cost_estimate=pl.CostEstimate(
            flops=2 * planes * y_rows * depth * side,
            transcendentals=0,
            bytes_accessed=2 * y_rows * depth + 4 * planes * depth + 2 * depth * side
            + 4 * planes * y_rows * side,
        ),
    )(row_weights, sectioned, col_weights)


def solution(mesh):
    in_specs = (
        P(("grp", "slab"), None),
        P(("grp", "slab")),
        P(("grp", "slab")),
        P(),
        P("slab", None),
        P(),
        P(),
        P(),
        P(),
        P(),
        P(),
        P(),
    )
    out_specs = P(None, "slab", "grp", None)
    return jax.shard_map(local, mesh=mesh, in_specs=in_specs, out_specs=out_specs, check_vma=False)
```

```python
import functools
import math

import jax
import jax.numpy as jnp
from jax import lax
from jax.experimental import pallas as pl
from jax.experimental.pallas import tpu as pltpu
from jax.sharding import PartitionSpec as P

SHIFTS = 128
Z_CHIPS = 8


def phase_factors(row_count, half_cols):
    shift_ids = jnp.arange(SHIFTS)
    shift_rows = (shift_ids // 8 - SHIFTS // 16).astype(jnp.float32)
    shift_cols = (shift_ids % 8 - 4).astype(jnp.float32)
    lanes = 128
    per_lane_row = lanes // half_cols
    blocks = row_count * half_cols // lanes
    block_rows = (jnp.arange(blocks) * per_lane_row - row_count // 2).astype(jnp.float32)
    lane_ids = jnp.arange(lanes)
    lane_rows = (lane_ids // half_cols).astype(jnp.float32)
    lane_cols = (lane_ids % half_cols).astype(jnp.float32)
    step = 2.0 * math.pi / row_count
    block_angle = shift_rows[:, None] * block_rows[None, :] * step
    lane_angle = (
        shift_rows[:, None] * lane_rows[None, :] + shift_cols[:, None] * lane_cols[None, :]
    ) * step
    return (jnp.cos(block_angle), jnp.sin(block_angle), jnp.cos(lane_angle), jnp.sin(lane_angle))


def exchange_kernel(count, place, picks, *refs):
    parts = len(picks)
    x_refs, out_refs = refs[:parts], refs[parts : 2 * parts]
    local_sems, send_sems, recv_sems = refs[2 * parts :]
    me, device = place()
    barrier = pltpu.get_barrier_semaphore()
    for k in range(1, count):
        pl.semaphore_signal(
            barrier,
            1,
            device_id=device(lax.rem(me + k, count)),
            device_id_type=pl.DeviceIdType.MESH,
        )
    pl.semaphore_wait(barrier, count - 1)
    owns, copies = [], []
    for part, (pick, x_ref, out_ref) in enumerate(zip(picks, x_refs, out_refs)):
        own = pltpu.make_async_copy(pick(x_ref, me), out_ref.at[me], local_sems.at[part])
        own.start()
        owns.append(own)
        for k in range(1, count):
            peer = lax.rem(me + k, count)
            copy = pltpu.make_async_remote_copy(
                src_ref=pick(x_ref, peer),
                dst_ref=out_ref.at[me],
                send_sem=send_sems.at[part, k],
                recv_sem=recv_sems.at[part, k],
                device_id=device(peer),
                device_id_type=pl.DeviceIdType.MESH,
            )
            copy.start()
            copies.append(copy)
    for own in owns:
        own.wait()
    for copy in copies:
        copy.wait_send()
        copy.wait_recv()


def slab_place():
    group = lax.axis_index("grp")
    return lax.axis_index("slab"), lambda peer: (group, peer)


def core_place():
    group, slab = lax.axis_index("grp"), lax.axis_index("slab")
    return lax.rem(group, 2), lambda peer: (group - lax.rem(group, 2) + peer, slab)


def z_place():
    group, slab = lax.axis_index("grp"), lax.axis_index("slab")
    z = lax.rem(slab, Z_CHIPS)
    return z, lambda peer: (group, slab - z + peer)


def y_place():
    group, slab = lax.axis_index("grp"), lax.axis_index("slab")
    z = lax.rem(slab, Z_CHIPS)
    return slab // Z_CHIPS, lambda peer: (group, peer * Z_CHIPS + z)


def group_place():
    slab = lax.axis_index("slab")
    return lax.axis_index("grp"), lambda peer: (peer, slab)


def whole(x_ref, peer):
    return x_ref.at[0]


def entire(x_ref, peer):
    return x_ref


def row_block(x_ref, peer):
    return x_ref.at[peer]


def lane_blocks(count):
    def pick(x_ref, peer):
        width = x_ref.shape[1] // count
        return x_ref.at[:, pl.ds(pl.multiple_of(peer * width, width), width)]

    return pick


def exchange_many(xs, count, place, picks, collective_id, block_shapes):
    parts = len(xs)
    return pl.pallas_call(
        functools.partial(exchange_kernel, count, place, tuple(picks)),
        out_shape=[
            jax.ShapeDtypeStruct((count,) + shape, x.dtype) for x, shape in zip(xs, block_shapes)
        ],
        in_specs=[pl.BlockSpec(memory_space=pltpu.VMEM)] * parts,
        out_specs=[pl.BlockSpec(memory_space=pltpu.VMEM)] * parts,
        scratch_shapes=[
            pltpu.SemaphoreType.DMA((parts,)),
            pltpu.SemaphoreType.DMA((parts, count)),
            pltpu.SemaphoreType.DMA((parts, count)),
        ],
        compiler_params=pltpu.CompilerParams(collective_id=collective_id, has_side_effects=True),
    )(*xs)


def exchange(x, count, place, pick, collective_id, block_shape):
    return exchange_many([x], count, place, [pick], collective_id, [block_shape])[0]


def signal_all(devices):
    barrier = pltpu.get_barrier_semaphore()
    for device in devices:
        pl.semaphore_signal(barrier, 1, device_id=device, device_id_type=pl.DeviceIdType.MESH)
    return lambda: pl.semaphore_wait(barrier, len(devices))


def run_phase(count, place, pick, x_ref, out_ref, local_sem, send_sems, recv_sems):
    me, device = place()
    own = pltpu.make_async_copy(pick(x_ref, me), out_ref.at[me], local_sem)
    own.start()
    copies = []
    for k in range(1, count):
        peer = lax.rem(me + k, count)
        copy = pltpu.make_async_remote_copy(
            src_ref=pick(x_ref, peer),
            dst_ref=out_ref.at[me],
            send_sem=send_sems.at[k],
            recv_sem=recv_sems.at[k],
            device_id=device(peer),
            device_id_type=pl.DeviceIdType.MESH,
        )
        copy.start()
        copies.append(copy)
    own.wait()
    for copy in copies:
        copy.wait_send()
        copy.wait_recv()


def peers(count, place):
    me, device = place()
    return [device(lax.rem(me + k, count)) for k in range(1, count)]


def stencil_kernel(base_ref, frac_ref, rows_ref, cols_ref):
    y_rows = rows_ref.shape[0]
    y_ids = lax.axis_index("grp") * y_rows + lax.broadcasted_iota(jnp.int32, rows_ref.shape, 0)
    y_base, y_frac = base_ref[0:1, :], frac_ref[0:1, :]
    rows = jnp.where(y_ids == y_base, 1.0 - y_frac, 0.0) + jnp.where(y_ids == y_base + 1, y_frac, 0.0)
    rows_ref[...] = rows.astype(rows_ref.dtype)
    x_ids = lax.broadcasted_iota(jnp.int32, cols_ref.shape, 0)
    x_base, x_frac = base_ref[1:2, :], frac_ref[1:2, :]
    cols = jnp.where(x_ids == x_base, 1.0 - x_frac, 0.0) + jnp.where(x_ids == x_base + 1, x_frac, 0.0)
    cols_ref[...] = cols.astype(cols_ref.dtype)


def neighbour_place():
    group, slab = lax.axis_index("grp"), lax.axis_index("slab")
    count = lax.axis_size("slab")
    return [(group, lax.rem(slab + 1, count)), (group, lax.rem(slab + count - 1, count))]


def reduce_chain_kernel(y_chips, groups, x_ref, base_ref, frac_ref,
                        total_ref, halo_ref, rows_ref, cols_ref, core_buf, y_src, y_buf, z_src, z_buf,
                        d_src, d_buf, local_sems, send_sems, recv_sems, halo_send, halo_recv):
    arrive = signal_all(
        peers(2, core_place)
        + peers(y_chips, y_place)
        + peers(Z_CHIPS, z_place)
        + peers(groups, group_place)
        + neighbour_place()
    )
    stencil_kernel(base_ref, frac_ref, rows_ref, cols_ref)
    arrive()
    run_phase(2, core_place, row_block, x_ref, core_buf, local_sems.at[0], send_sems.at[0], recv_sems.at[0])
    y_src[...] = (core_buf[0].astype(jnp.float32) + core_buf[1].astype(jnp.float32)).astype(y_src.dtype)
    run_phase(
        y_chips, y_place, lane_blocks(y_chips), y_src, y_buf,
        local_sems.at[1], send_sems.at[1], recv_sems.at[1],
    )
    z_src[...] = jnp.sum(y_buf[...].astype(jnp.float32), axis=0).astype(z_src.dtype)
    run_phase(
        Z_CHIPS, z_place, lane_blocks(Z_CHIPS), z_src, z_buf,
        local_sems.at[2], send_sems.at[2], recv_sems.at[2],
    )
    d_src[0] = jnp.sum(z_buf[...].astype(jnp.float32), axis=0).astype(d_src.dtype)
    run_phase(groups, group_place, whole, d_src, d_buf, local_sems.at[3], send_sems.at[3], recv_sems.at[3])
    for half in range(2):
        total_ref[half] = jnp.sum(
            jnp.stack([d_buf[j].astype(jnp.float32) for j in range(half, groups, 2)]), axis=0
        )
    copies = []
    for side, device in enumerate(neighbour_place()):
        copy = pltpu.make_async_remote_copy(
            src_ref=total_ref,
            dst_ref=halo_ref.at[side],
            send_sem=halo_send.at[side],
            recv_sem=halo_recv.at[side],
            device_id=device,
            device_id_type=pl.DeviceIdType.MESH,
        )
        copy.start()
        copies.append(copy)
    for copy in copies:
        copy.wait_send()
        copy.wait_recv()


def reduce_chain(x, stencil, y_rows, side, y_chips, groups, collective_id):
    _, rows, width = x.shape
    band = width // (y_chips * Z_CHIPS)
    wide = 8
    depth = stencil[0].shape[1]
    return pl.pallas_call(
        functools.partial(reduce_chain_kernel, y_chips, groups),
        out_shape=[
            jax.ShapeDtypeStruct((2, rows, band), jnp.float32),
            jax.ShapeDtypeStruct((2, 2, rows, band), jnp.float32),
            jax.ShapeDtypeStruct((y_rows, depth), jnp.bfloat16),
            jax.ShapeDtypeStruct((side, depth), jnp.bfloat16),
        ],
        in_specs=[pl.BlockSpec(memory_space=pltpu.VMEM)] * 3,
        out_specs=[pl.BlockSpec(memory_space=pltpu.VMEM)] * 4,
        scratch_shapes=[
            pltpu.VMEM((2, rows, width), x.dtype),
            pltpu.VMEM((rows, width), jnp.bfloat16),
            pltpu.VMEM((y_chips, rows, width // y_chips), jnp.bfloat16),
            pltpu.VMEM((rows, width // y_chips), jnp.bfloat16),
            pltpu.VMEM((Z_CHIPS, rows, band), jnp.bfloat16),
            pltpu.VMEM((1, rows, band), jnp.bfloat16),
            pltpu.VMEM((groups, rows, band), jnp.bfloat16),
            pltpu.SemaphoreType.DMA((4,)),
            pltpu.SemaphoreType.DMA((4, wide)),
            pltpu.SemaphoreType.DMA((4, wide)),
            pltpu.SemaphoreType.DMA((2,)),
            pltpu.SemaphoreType.DMA((2,)),
        ],
        compiler_params=pltpu.CompilerParams(collective_id=collective_id, has_side_effects=True),
    )(x, *stencil)


def phase_kernel(cos_b, sin_b, cos_l, sin_l, phase_ref):
    half = phase_ref.shape[1] // 2
    lanes = cos_l.shape[1]
    c_l, s_l = cos_l[...], sin_l[...]
    for q in range(cos_b.shape[1]):
        c_b, s_b = cos_b[:, q : q + 1], sin_b[:, q : q + 1]
        phase_ref[:, q * lanes : (q + 1) * lanes] = (c_b * c_l - s_b * s_l).astype(phase_ref.dtype)
        phase_ref[:, half + q * lanes : half + (q + 1) * lanes] = (s_b * c_l + c_b * s_l).astype(
            phase_ref.dtype
        )


def gather_chain_kernel(y_chips, x_ref, cos_b, sin_b, cos_l, sin_l, out_ref, phase_ref, z_buf, y_buf,
                        local_sems, send_sems, recv_sems):
    arrive = signal_all(peers(Z_CHIPS, z_place) + peers(y_chips, y_place) + peers(2, core_place))
    phase_kernel(cos_b, sin_b, cos_l, sin_l, phase_ref)
    arrive()
    run_phase(Z_CHIPS, z_place, whole, x_ref, z_buf, local_sems.at[0], send_sems.at[0], recv_sems.at[0])
    run_phase(y_chips, y_place, entire, z_buf, y_buf, local_sems.at[1], send_sems.at[1], recv_sems.at[1])
    run_phase(2, core_place, entire, y_buf, out_ref, local_sems.at[2], send_sems.at[2], recv_sems.at[2])


def gather_chain(x, trig, y_chips, collective_id):
    _, rows, lanes = x.shape
    shifts = trig[0].shape[0]
    table = 2 * trig[0].shape[1] * trig[2].shape[1]
    return pl.pallas_call(
        functools.partial(gather_chain_kernel, y_chips),
        out_shape=[
            jax.ShapeDtypeStruct((2, y_chips, Z_CHIPS, rows, lanes), x.dtype),
            jax.ShapeDtypeStruct((shifts, table), jnp.bfloat16),
        ],
        in_specs=[pl.BlockSpec(memory_space=pltpu.VMEM)] * 5,
        out_specs=[pl.BlockSpec(memory_space=pltpu.VMEM)] * 2,
        scratch_shapes=[
            pltpu.VMEM((Z_CHIPS, rows, lanes), x.dtype),
            pltpu.VMEM((y_chips, Z_CHIPS, rows, lanes), x.dtype),
            pltpu.SemaphoreType.DMA((3,)),
            pltpu.SemaphoreType.DMA((3, Z_CHIPS)),
            pltpu.SemaphoreType.DMA((3, Z_CHIPS)),
        ],
        compiler_params=pltpu.CompilerParams(collective_id=collective_id, has_side_effects=True),
    )(x, *trig)


def align_frames(frames, ctf_rows, ref_re, ref_im, phase, score_scale):
    pixels = ctf_rows.shape[1]
    frame_re = frames[:, :pixels].astype(jnp.float32)
    frame_im = frames[:, pixels:].astype(jnp.float32)
    ref_re = ref_re.astype(jnp.float32)
    ref_im = ref_im.astype(jnp.float32)
    weight = ctf_rows.astype(jnp.float32)
    cross_terms = jnp.concatenate(
        [
            weight * (ref_re * frame_re + ref_im * frame_im),
            weight * (ref_re * frame_im - ref_im * frame_re),
        ],
        axis=1,
    ).astype(jnp.bfloat16)
    scores = score_scale * jnp.einsum(
        "np,sp->ns", cross_terms, phase, preferred_element_type=jnp.float32
    )
    shift_probs = jax.nn.softmax(scores, axis=1).astype(jnp.bfloat16)
    shift_mix = jnp.dot(shift_probs, phase, preferred_element_type=jnp.float32)
    mix_re = shift_mix[:, :pixels]
    mix_im = shift_mix[:, pixels:]
    return (
        weight * (frame_re * mix_re + frame_im * mix_im),
        weight * (frame_im * mix_re - frame_re * mix_im),
    )


def stencil_weights(base_cell, fraction, side_cells):
    cell_ids = jnp.arange(side_cells, dtype=jnp.int32)
    dense_weight = jnp.where(
        cell_ids[None, None, :] == base_cell[:, :, None], (1.0 - fraction)[:, :, None], 0.0
    )
    dense_weight = dense_weight + jnp.where(
        cell_ids[None, None, :] == base_cell[:, :, None] + 1, fraction[:, :, None], 0.0
    )
    return dense_weight.astype(jnp.bfloat16)


def local(
    images,
    image_class,
    image_ctf,
    class_owner,
    references,
    ctf_table,
    x_base,
    y_base,
    x_frac,
    y_frac,
    z_offset,
    z_frac,
):
    slab_count = lax.axis_size("slab")
    group_count = lax.axis_size("grp")
    frame_count = images.shape[0]
    pixels = ctf_table.shape[1]
    groups_ctf = ctf_table.shape[0]
    row_count = z_offset.shape[1]
    half_cols = x_base.shape[1]
    class_count = class_owner.shape[0]
    side_cells = 2 * row_count
    band_rows = row_count // slab_count
    band_pixels = band_rows * half_cols
    z_dev = 2 * band_rows
    score_scale = 2.0 / math.sqrt(2.0 * pixels)
    channel_scale = jnp.array(
        [
            1.0 / math.sqrt(frame_count * group_count),
            1.0 / math.sqrt(frame_count * group_count),
            1.0 / (frame_count * group_count),
        ],
        jnp.float32,
    )
    lanes = 128
    core = lax.rem(lax.axis_index("grp"), 2)
    ref_halves = references.reshape(2, -1, lanes)
    my_half = lax.dynamic_slice_in_dim(ref_halves, core, 1, 0)
    y_chips = slab_count // Z_CHIPS
    gathered, phase = gather_chain(my_half, phase_factors(row_count, half_cols), y_chips, 0)
    both_halves = gathered.reshape(2, slab_count, pixels)
    class_ids = jnp.arange(class_count, dtype=jnp.int32)
    owner_of = jnp.sum(
        jnp.where(image_class[:, None] == class_ids[None, :], class_owner[None, :], 0), axis=1
    )
    pick_ref = (owner_of[:, None] == jnp.arange(slab_count, dtype=jnp.int32)[None, :]).astype(
        jnp.bfloat16
    )
    ref_re = jnp.dot(pick_ref, both_halves[0], preferred_element_type=jnp.float32).astype(
        jnp.bfloat16
    )
    ref_im = jnp.dot(pick_ref, both_halves[1], preferred_element_type=jnp.float32).astype(
        jnp.bfloat16
    )
    pick_ctf = (image_ctf[:, None] == jnp.arange(groups_ctf, dtype=jnp.int32)[None, :]).astype(
        jnp.bfloat16
    )
    ctf_rows = jnp.dot(pick_ctf, ctf_table, preferred_element_type=jnp.float32).astype(
        jnp.bfloat16
    )
    stacked = align_frames(images, ctf_rows, ref_re, ref_im, phase, score_scale)
    member = (class_ids[:, None] == image_class[None, :]).astype(jnp.float32)
    aligned_re, aligned_im = stacked
    partial_re, partial_im = (
        jnp.dot(
            member, part, precision=lax.Precision.HIGHEST, preferred_element_type=jnp.float32
        ) * channel_scale[0]
        for part in (aligned_re, aligned_im)
    )
    half_classes = class_count // 2
    half_rows = half_classes * 2
    class_hits = (class_ids[:, None] == image_class[None, :]).astype(jnp.bfloat16)
    ctf_hits = (image_ctf[:, None] == jnp.arange(groups_ctf, dtype=jnp.int32)[None, :]).astype(
        jnp.bfloat16
    )
    counts = jnp.dot(class_hits, ctf_hits, preferred_element_type=jnp.float32)
    count_rows = class_count * groups_ctf // band_pixels
    tiled_counts = jnp.tile(counts.reshape(count_rows, band_pixels), (1, slab_count))
    rows = half_rows + count_rows
    by_half = jnp.stack(
        [
            jnp.concatenate(
                [
                    partial_re[h * half_classes : (h + 1) * half_classes],
                    partial_im[h * half_classes : (h + 1) * half_classes],
                    tiled_counts,
                ],
                axis=0,
            )
            for h in range(2)
        ]
    ).astype(jnp.bfloat16)
    y_rows = side_cells // group_count
    flat = class_count * half_cols
    stencil = (
        jnp.stack([y_base.reshape(flat), x_base.reshape(flat)]),
        jnp.stack([y_frac.reshape(flat), x_frac.reshape(flat)]),
    )
    total, halo, row_weights, col_weights = reduce_chain(
        by_half, stencil, y_rows, side_cells, slab_count // Z_CHIPS, group_count, 1
    )
    band = total[:, :half_rows].reshape(2, 2, half_classes, band_rows, half_cols)
    band = band.transpose(0, 2, 1, 3, 4).reshape(class_count, 2, band_rows, half_cols)
    total_counts = total[0, half_rows:].reshape(class_count, groups_ctf)
    halo = halo[:, :, :half_rows].reshape(2, 2, 2, half_classes, band_rows, half_cols)
    halo = halo.transpose(0, 1, 3, 2, 4, 5).reshape(2, class_count, 2, band_rows, half_cols)
    slab_index = lax.axis_index("slab")
    from_below = jnp.where(slab_index > 0, halo[0][:, :, band_rows - 1 :], 0.0)
    from_above = jnp.where(slab_index < slab_count - 1, halo[1][:, :, :1], 0.0)
    data_bands = jnp.concatenate([from_below, band, from_above], axis=2)
    slab_index = lax.axis_index("slab")
    ctf_sq = jnp.pad(
        jnp.square(ctf_table.astype(jnp.float32)), ((0, 0), (half_cols, half_cols))
    )
    window = lax.dynamic_slice_in_dim(
        ctf_sq, slab_index * band_pixels, band_pixels + 2 * half_cols, 1
    )
    weight_rows = jnp.dot(
        total_counts, window, precision=lax.Precision.HIGHEST, preferred_element_type=jnp.float32
    ) * channel_scale[2]
    class_bands = jnp.concatenate(
        [data_bands, weight_rows.reshape(class_count, 1, band_rows + 2, half_cols)], axis=1
    )
    group_index = lax.axis_index("grp")
    offset_pad = jnp.pad(z_offset, ((0, 0), (1, 1)))
    frac_pad = jnp.pad(z_frac, ((0, 0), (1, 1)))
    rows_held = band_rows + 2
    local_offset = lax.dynamic_slice_in_dim(offset_pad, slab_index * band_rows, rows_held, 1)
    local_frac = lax.dynamic_slice_in_dim(frac_pad, slab_index * band_rows, rows_held, 1)
    row_ids = jnp.arange(rows_held, dtype=jnp.int32) + (band_rows - 1)
    band_shift = (row_ids // band_rows - 1) * z_dev - 1
    target = 2 * (row_ids % band_rows)[None, :] + local_offset + 1 + band_shift[None, :]
    plane_ids = jnp.arange(z_dev, dtype=jnp.int32)
    depth_weight = jnp.where(
        plane_ids[None, None, :] == target[:, :, None], (1.0 - local_frac)[:, :, None], 0.0
    )
    depth_weight = depth_weight + jnp.where(
        plane_ids[None, None, :] == target[:, :, None] + 1, local_frac[:, :, None], 0.0
    )
    sectioned = jnp.einsum(
        "ckra,crz->kzca",
        class_bands,
        depth_weight,
        precision=lax.Precision.HIGHEST,
    ).reshape(3 * z_dev, class_count * half_cols)
    inserted = insert_planes(row_weights, sectioned, col_weights)
    return inserted.reshape(3, z_dev, y_rows, side_cells)


def insert_kernel(rows_ref, sec_ref, cols_ref, out_ref, lifted_ref):
    y_rows = rows_ref.shape[0]

    def body(i, carry):
        start = pl.multiple_of(i * y_rows, y_rows)
        lifted_ref[pl.ds(start, y_rows), :] = (
            rows_ref[...].astype(jnp.float32) * sec_ref[pl.ds(i, 1), :]
        ).astype(jnp.bfloat16)
        return carry

    lax.fori_loop(0, sec_ref.shape[0], body, 0)
    out_ref[...] = lax.dot_general(
        lifted_ref[...], cols_ref[...], (((1,), (1,)), ((), ())), preferred_element_type=jnp.float32
    )


def insert_planes(row_weights, sectioned, col_weights):
    planes = sectioned.shape[0]
    y_rows, depth = row_weights.shape
    side = col_weights.shape[0]
    return pl.pallas_call(
        insert_kernel,
        out_shape=jax.ShapeDtypeStruct((planes * y_rows, side), jnp.float32),
        in_specs=[pl.BlockSpec(memory_space=pltpu.VMEM)] * 3,
        out_specs=pl.BlockSpec(memory_space=pltpu.VMEM),
        scratch_shapes=[pltpu.VMEM((planes * y_rows, depth), jnp.bfloat16)],
        cost_estimate=pl.CostEstimate(
            flops=2 * planes * y_rows * depth * side,
            transcendentals=0,
            bytes_accessed=2 * y_rows * depth + 4 * planes * depth + 2 * depth * side
            + 4 * planes * y_rows * side,
        ),
    )(row_weights, sectioned, col_weights)


def solution(mesh):
    in_specs = (
        P(("grp", "slab"), None),
        P(("grp", "slab")),
        P(("grp", "slab")),
        P(),
        P("slab", None),
        P(),
        P(),
        P(),
        P(),
        P(),
        P(),
        P(),
    )
    out_specs = P(None, "slab", "grp", None)
    return jax.shard_map(local, mesh=mesh, in_specs=in_specs, out_specs=out_specs, check_vma=False)
```

```python
import functools
import math

import jax
import jax.numpy as jnp
from jax import lax
from jax.experimental import pallas as pl
from jax.experimental.pallas import tpu as pltpu
from jax.sharding import PartitionSpec as P

SHIFTS = 128
Z_CHIPS = 8


def exchange_kernel(count, place, picks, *refs):
    parts = len(picks)
    x_refs, out_refs = refs[:parts], refs[parts : 2 * parts]
    local_sems, send_sems, recv_sems = refs[2 * parts :]
    me, device = place()
    barrier = pltpu.get_barrier_semaphore()
    for k in range(1, count):
        pl.semaphore_signal(
            barrier,
            1,
            device_id=device(lax.rem(me + k, count)),
            device_id_type=pl.DeviceIdType.MESH,
        )
    pl.semaphore_wait(barrier, count - 1)
    owns, copies = [], []
    for part, (pick, x_ref, out_ref) in enumerate(zip(picks, x_refs, out_refs)):
        own = pltpu.make_async_copy(pick(x_ref, me), out_ref.at[me], local_sems.at[part])
        own.start()
        owns.append(own)
        for k in range(1, count):
            peer = lax.rem(me + k, count)
            copy = pltpu.make_async_remote_copy(
                src_ref=pick(x_ref, peer),
                dst_ref=out_ref.at[me],
                send_sem=send_sems.at[part, k],
                recv_sem=recv_sems.at[part, k],
                device_id=device(peer),
                device_id_type=pl.DeviceIdType.MESH,
            )
            copy.start()
            copies.append(copy)
    for own in owns:
        own.wait()
    for copy in copies:
        copy.wait_send()
        copy.wait_recv()


def slab_place():
    group = lax.axis_index("grp")
    return lax.axis_index("slab"), lambda peer: (group, peer)


def core_place():
    group, slab = lax.axis_index("grp"), lax.axis_index("slab")
    return lax.rem(group, 2), lambda peer: (group - lax.rem(group, 2) + peer, slab)


def z_place():
    group, slab = lax.axis_index("grp"), lax.axis_index("slab")
    z = lax.rem(slab, Z_CHIPS)
    return z, lambda peer: (group, slab - z + peer)


def y_place():
    group, slab = lax.axis_index("grp"), lax.axis_index("slab")
    z = lax.rem(slab, Z_CHIPS)
    return slab // Z_CHIPS, lambda peer: (group, peer * Z_CHIPS + z)


def group_place():
    slab = lax.axis_index("slab")
    return lax.axis_index("grp"), lambda peer: (peer, slab)


def whole(x_ref, peer):
    return x_ref.at[0]


def entire(x_ref, peer):
    return x_ref


def row_block(x_ref, peer):
    return x_ref.at[peer]


def lane_blocks(count):
    def pick(x_ref, peer):
        width = x_ref.shape[1] // count
        return x_ref.at[:, pl.ds(pl.multiple_of(peer * width, width), width)]

    return pick


def exchange_many(xs, count, place, picks, collective_id, block_shapes):
    parts = len(xs)
    return pl.pallas_call(
        functools.partial(exchange_kernel, count, place, tuple(picks)),
        out_shape=[
            jax.ShapeDtypeStruct((count,) + shape, x.dtype) for x, shape in zip(xs, block_shapes)
        ],
        in_specs=[pl.BlockSpec(memory_space=pltpu.VMEM)] * parts,
        out_specs=[pl.BlockSpec(memory_space=pltpu.VMEM)] * parts,
        scratch_shapes=[
            pltpu.SemaphoreType.DMA((parts,)),
            pltpu.SemaphoreType.DMA((parts, count)),
            pltpu.SemaphoreType.DMA((parts, count)),
        ],
        compiler_params=pltpu.CompilerParams(collective_id=collective_id, has_side_effects=True),
    )(*xs)


def exchange(x, count, place, pick, collective_id, block_shape):
    return exchange_many([x], count, place, [pick], collective_id, [block_shape])[0]


def signal_all(devices):
    barrier = pltpu.get_barrier_semaphore()
    for device in devices:
        pl.semaphore_signal(barrier, 1, device_id=device, device_id_type=pl.DeviceIdType.MESH)
    return lambda: pl.semaphore_wait(barrier, len(devices))


def run_phase(count, place, pick, x_ref, out_ref, local_sem, send_sems, recv_sems):
    me, device = place()
    own = pltpu.make_async_copy(pick(x_ref, me), out_ref.at[me], local_sem)
    own.start()
    copies = []
    for k in range(1, count):
        peer = lax.rem(me + k, count)
        copy = pltpu.make_async_remote_copy(
            src_ref=pick(x_ref, peer),
            dst_ref=out_ref.at[me],
            send_sem=send_sems.at[k],
            recv_sem=recv_sems.at[k],
            device_id=device(peer),
            device_id_type=pl.DeviceIdType.MESH,
        )
        copy.start()
        copies.append(copy)
    own.wait()
    for copy in copies:
        copy.wait_send()
        copy.wait_recv()


def peers(count, place):
    me, device = place()
    return [device(lax.rem(me + k, count)) for k in range(1, count)]


def stencil_kernel(base_ref, frac_ref, rows_ref, cols_ref):
    y_rows = rows_ref.shape[0]
    y_ids = lax.axis_index("grp") * y_rows + lax.broadcasted_iota(jnp.int32, rows_ref.shape, 0)
    y_base, y_frac = base_ref[0:1, :], frac_ref[0:1, :]
    rows = jnp.where(y_ids == y_base, 1.0 - y_frac, 0.0) + jnp.where(y_ids == y_base + 1, y_frac, 0.0)
    rows_ref[...] = rows.astype(rows_ref.dtype)
    x_ids = lax.broadcasted_iota(jnp.int32, cols_ref.shape, 0)
    x_base, x_frac = base_ref[1:2, :], frac_ref[1:2, :]
    cols = jnp.where(x_ids == x_base, 1.0 - x_frac, 0.0) + jnp.where(x_ids == x_base + 1, x_frac, 0.0)
    cols_ref[...] = cols.astype(cols_ref.dtype)


def neighbour_place():
    group, slab = lax.axis_index("grp"), lax.axis_index("slab")
    count = lax.axis_size("slab")
    return [(group, lax.rem(slab + 1, count)), (group, lax.rem(slab + count - 1, count))]


def reduce_chain_kernel(y_chips, groups, x_ref, base_ref, frac_ref,
                        total_ref, halo_ref, rows_ref, cols_ref, core_buf, y_src, y_buf, z_src, z_buf,
                        d_src, d_buf, local_sems, send_sems, recv_sems, halo_send, halo_recv):
    arrive = signal_all(
        peers(2, core_place)
        + peers(y_chips, y_place)
        + peers(Z_CHIPS, z_place)
        + peers(groups, group_place)
        + neighbour_place()
    )
    stencil_kernel(base_ref, frac_ref, rows_ref, cols_ref)
    arrive()
    run_phase(2, core_place, row_block, x_ref, core_buf, local_sems.at[0], send_sems.at[0], recv_sems.at[0])
    y_src[...] = (core_buf[0].astype(jnp.float32) + core_buf[1].astype(jnp.float32)).astype(y_src.dtype)
    run_phase(
        y_chips, y_place, lane_blocks(y_chips), y_src, y_buf,
        local_sems.at[1], send_sems.at[1], recv_sems.at[1],
    )
    z_src[...] = jnp.sum(y_buf[...].astype(jnp.float32), axis=0).astype(z_src.dtype)
    run_phase(
        Z_CHIPS, z_place, lane_blocks(Z_CHIPS), z_src, z_buf,
        local_sems.at[2], send_sems.at[2], recv_sems.at[2],
    )
    d_src[0] = jnp.sum(z_buf[...].astype(jnp.float32), axis=0).astype(d_src.dtype)
    run_phase(groups, group_place, whole, d_src, d_buf, local_sems.at[3], send_sems.at[3], recv_sems.at[3])
    for half in range(2):
        total_ref[half] = jnp.sum(
            jnp.stack([d_buf[j].astype(jnp.float32) for j in range(half, groups, 2)]), axis=0
        )
    copies = []
    for side, device in enumerate(neighbour_place()):
        copy = pltpu.make_async_remote_copy(
            src_ref=total_ref,
            dst_ref=halo_ref.at[side],
            send_sem=halo_send.at[side],
            recv_sem=halo_recv.at[side],
            device_id=device,
            device_id_type=pl.DeviceIdType.MESH,
        )
        copy.start()
        copies.append(copy)
    for copy in copies:
        copy.wait_send()
        copy.wait_recv()


def reduce_chain(x, stencil, y_rows, side, y_chips, groups, collective_id):
    _, rows, width = x.shape
    band = width // (y_chips * Z_CHIPS)
    wide = 8
    depth = stencil[0].shape[1]
    return pl.pallas_call(
        functools.partial(reduce_chain_kernel, y_chips, groups),
        out_shape=[
            jax.ShapeDtypeStruct((2, rows, band), jnp.float32),
            jax.ShapeDtypeStruct((2, 2, rows, band), jnp.float32),
            jax.ShapeDtypeStruct((y_rows, depth), jnp.bfloat16),
            jax.ShapeDtypeStruct((side, depth), jnp.bfloat16),
        ],
        in_specs=[pl.BlockSpec(memory_space=pltpu.VMEM)] * 3,
        out_specs=[pl.BlockSpec(memory_space=pltpu.VMEM)] * 4,
        scratch_shapes=[
            pltpu.VMEM((2, rows, width), x.dtype),
            pltpu.VMEM((rows, width), jnp.bfloat16),
            pltpu.VMEM((y_chips, rows, width // y_chips), jnp.bfloat16),
            pltpu.VMEM((rows, width // y_chips), jnp.bfloat16),
            pltpu.VMEM((Z_CHIPS, rows, band), jnp.bfloat16),
            pltpu.VMEM((1, rows, band), jnp.bfloat16),
            pltpu.VMEM((groups, rows, band), jnp.bfloat16),
            pltpu.SemaphoreType.DMA((4,)),
            pltpu.SemaphoreType.DMA((4, wide)),
            pltpu.SemaphoreType.DMA((4, wide)),
            pltpu.SemaphoreType.DMA((2,)),
            pltpu.SemaphoreType.DMA((2,)),
        ],
        compiler_params=pltpu.CompilerParams(collective_id=collective_id, has_side_effects=True),
    )(x, *stencil)


def phase_kernel(row_count, half_cols, phase_ref):
    half = phase_ref.shape[1] // 2
    lanes = 128
    blocks = half // lanes
    shifts = phase_ref.shape[0]
    step = 2.0 * math.pi / row_count
    t_b = lax.broadcasted_iota(jnp.int32, (shifts, blocks), 0)
    q_b = lax.broadcasted_iota(jnp.int32, (shifts, blocks), 1)
    shift_rows_b = (t_b // 8 - SHIFTS // 16).astype(jnp.float32)
    block_rows = (q_b * (lanes // half_cols) - row_count // 2).astype(jnp.float32)
    block_angle = shift_rows_b * block_rows * step
    t_l = lax.broadcasted_iota(jnp.int32, (shifts, lanes), 0)
    l_l = lax.broadcasted_iota(jnp.int32, (shifts, lanes), 1)
    shift_rows_l = (t_l // 8 - SHIFTS // 16).astype(jnp.float32)
    shift_cols_l = (t_l % 8 - 4).astype(jnp.float32)
    lane_angle = (
        shift_rows_l * (l_l // half_cols).astype(jnp.float32)
        + shift_cols_l * (l_l % half_cols).astype(jnp.float32)
    ) * step
    cos_b, sin_b = jnp.cos(block_angle), jnp.sin(block_angle)
    c_l, s_l = jnp.cos(lane_angle), jnp.sin(lane_angle)
    for q in range(blocks):
        c_b, s_b = cos_b[:, q : q + 1], sin_b[:, q : q + 1]
        phase_ref[:, q * lanes : (q + 1) * lanes] = (c_b * c_l - s_b * s_l).astype(phase_ref.dtype)
        phase_ref[:, half + q * lanes : half + (q + 1) * lanes] = (s_b * c_l + c_b * s_l).astype(
            phase_ref.dtype
        )


def gather_chain_kernel(y_chips, row_count, half_cols, x_ref, out_ref, phase_ref, z_buf, y_buf,
                        local_sems, send_sems, recv_sems):
    arrive = signal_all(peers(Z_CHIPS, z_place) + peers(y_chips, y_place) + peers(2, core_place))
    phase_kernel(row_count, half_cols, phase_ref)
    arrive()
    run_phase(Z_CHIPS, z_place, whole, x_ref, z_buf, local_sems.at[0], send_sems.at[0], recv_sems.at[0])
    run_phase(y_chips, y_place, entire, z_buf, y_buf, local_sems.at[1], send_sems.at[1], recv_sems.at[1])
    run_phase(2, core_place, entire, y_buf, out_ref, local_sems.at[2], send_sems.at[2], recv_sems.at[2])


def gather_chain(x, row_count, half_cols, y_chips, collective_id):
    _, rows, lanes = x.shape
    shifts = SHIFTS
    table = 2 * row_count * half_cols
    return pl.pallas_call(
        functools.partial(gather_chain_kernel, y_chips, row_count, half_cols),
        out_shape=[
            jax.ShapeDtypeStruct((2, y_chips, Z_CHIPS, rows, lanes), x.dtype),
            jax.ShapeDtypeStruct((shifts, table), jnp.bfloat16),
        ],
        in_specs=[pl.BlockSpec(memory_space=pltpu.VMEM)],
        out_specs=[pl.BlockSpec(memory_space=pltpu.VMEM)] * 2,
        scratch_shapes=[
            pltpu.VMEM((Z_CHIPS, rows, lanes), x.dtype),
            pltpu.VMEM((y_chips, Z_CHIPS, rows, lanes), x.dtype),
            pltpu.SemaphoreType.DMA((3,)),
            pltpu.SemaphoreType.DMA((3, Z_CHIPS)),
            pltpu.SemaphoreType.DMA((3, Z_CHIPS)),
        ],
        compiler_params=pltpu.CompilerParams(collective_id=collective_id, has_side_effects=True),
    )(x)


def align_frames(frames, ctf_rows, ref_re, ref_im, phase, score_scale):
    pixels = ctf_rows.shape[1]
    frame_re = frames[:, :pixels].astype(jnp.float32)
    frame_im = frames[:, pixels:].astype(jnp.float32)
    ref_re = ref_re.astype(jnp.float32)
    ref_im = ref_im.astype(jnp.float32)
    weight = ctf_rows.astype(jnp.float32)
    cross_terms = jnp.concatenate(
        [
            weight * (ref_re * frame_re + ref_im * frame_im),
            weight * (ref_re * frame_im - ref_im * frame_re),
        ],
        axis=1,
    ).astype(jnp.bfloat16)
    scores = score_scale * jnp.einsum(
        "np,sp->ns", cross_terms, phase, preferred_element_type=jnp.float32
    )
    shift_probs = jax.nn.softmax(scores, axis=1).astype(jnp.bfloat16)
    shift_mix = jnp.dot(shift_probs, phase, preferred_element_type=jnp.float32)
    mix_re = shift_mix[:, :pixels]
    mix_im = shift_mix[:, pixels:]
    return (
        weight * (frame_re * mix_re + frame_im * mix_im),
        weight * (frame_im * mix_re - frame_re * mix_im),
    )


def stencil_weights(base_cell, fraction, side_cells):
    cell_ids = jnp.arange(side_cells, dtype=jnp.int32)
    dense_weight = jnp.where(
        cell_ids[None, None, :] == base_cell[:, :, None], (1.0 - fraction)[:, :, None], 0.0
    )
    dense_weight = dense_weight + jnp.where(
        cell_ids[None, None, :] == base_cell[:, :, None] + 1, fraction[:, :, None], 0.0
    )
    return dense_weight.astype(jnp.bfloat16)


def local(
    images,
    image_class,
    image_ctf,
    class_owner,
    references,
    ctf_table,
    x_base,
    y_base,
    x_frac,
    y_frac,
    z_offset,
    z_frac,
):
    slab_count = lax.axis_size("slab")
    group_count = lax.axis_size("grp")
    frame_count = images.shape[0]
    pixels = ctf_table.shape[1]
    groups_ctf = ctf_table.shape[0]
    row_count = z_offset.shape[1]
    half_cols = x_base.shape[1]
    class_count = class_owner.shape[0]
    side_cells = 2 * row_count
    band_rows = row_count // slab_count
    band_pixels = band_rows * half_cols
    z_dev = 2 * band_rows
    score_scale = 2.0 / math.sqrt(2.0 * pixels)
    channel_scale = jnp.array(
        [
            1.0 / math.sqrt(frame_count * group_count),
            1.0 / math.sqrt(frame_count * group_count),
            1.0 / (frame_count * group_count),
        ],
        jnp.float32,
    )
    lanes = 128
    core = lax.rem(lax.axis_index("grp"), 2)
    ref_halves = references.reshape(2, -1, lanes)
    my_half = lax.dynamic_slice_in_dim(ref_halves, core, 1, 0)
    y_chips = slab_count // Z_CHIPS
    gathered, phase = gather_chain(my_half, row_count, half_cols, y_chips, 0)
    both_halves = gathered.reshape(2, slab_count, pixels)
    class_ids = jnp.arange(class_count, dtype=jnp.int32)
    owner_of = jnp.sum(
        jnp.where(image_class[:, None] == class_ids[None, :], class_owner[None, :], 0), axis=1
    )
    pick_ref = (owner_of[:, None] == jnp.arange(slab_count, dtype=jnp.int32)[None, :]).astype(
        jnp.bfloat16
    )
    ref_re = jnp.dot(pick_ref, both_halves[0], preferred_element_type=jnp.float32).astype(
        jnp.bfloat16
    )
    ref_im = jnp.dot(pick_ref, both_halves[1], preferred_element_type=jnp.float32).astype(
        jnp.bfloat16
    )
    pick_ctf = (image_ctf[:, None] == jnp.arange(groups_ctf, dtype=jnp.int32)[None, :]).astype(
        jnp.bfloat16
    )
    ctf_rows = jnp.dot(pick_ctf, ctf_table, preferred_element_type=jnp.float32).astype(
        jnp.bfloat16
    )
    stacked = align_frames(images, ctf_rows, ref_re, ref_im, phase, score_scale)
    member = (class_ids[:, None] == image_class[None, :]).astype(jnp.float32)
    aligned_re, aligned_im = stacked
    partial_re, partial_im = (
        jnp.dot(
            member, part, precision=lax.Precision.HIGHEST, preferred_element_type=jnp.float32
        ) * channel_scale[0]
        for part in (aligned_re, aligned_im)
    )
    half_classes = class_count // 2
    half_rows = half_classes * 2
    class_hits = (class_ids[:, None] == image_class[None, :]).astype(jnp.bfloat16)
    ctf_hits = (image_ctf[:, None] == jnp.arange(groups_ctf, dtype=jnp.int32)[None, :]).astype(
        jnp.bfloat16
    )
    counts = jnp.dot(class_hits, ctf_hits, preferred_element_type=jnp.float32)
    count_rows = class_count * groups_ctf // band_pixels
    tiled_counts = jnp.tile(counts.reshape(count_rows, band_pixels), (1, slab_count))
    rows = half_rows + count_rows
    by_half = jnp.stack(
        [
            jnp.concatenate(
                [
                    partial_re[h * half_classes : (h + 1) * half_classes],
                    partial_im[h * half_classes : (h + 1) * half_classes],
                    tiled_counts,
                ],
                axis=0,
            )
            for h in range(2)
        ]
    ).astype(jnp.bfloat16)
    y_rows = side_cells // group_count
    flat = class_count * half_cols
    stencil = (
        jnp.stack([y_base.reshape(flat), x_base.reshape(flat)]),
        jnp.stack([y_frac.reshape(flat), x_frac.reshape(flat)]),
    )
    total, halo, row_weights, col_weights = reduce_chain(
        by_half, stencil, y_rows, side_cells, slab_count // Z_CHIPS, group_count, 1
    )
    band = total[:, :half_rows].reshape(2, 2, half_classes, band_rows, half_cols)
    band = band.transpose(0, 2, 1, 3, 4).reshape(class_count, 2, band_rows, half_cols)
    total_counts = total[0, half_rows:].reshape(class_count, groups_ctf)
    halo = halo[:, :, :half_rows].reshape(2, 2, 2, half_classes, band_rows, half_cols)
    halo = halo.transpose(0, 1, 3, 2, 4, 5).reshape(2, class_count, 2, band_rows, half_cols)
    slab_index = lax.axis_index("slab")
    from_below = jnp.where(slab_index > 0, halo[0][:, :, band_rows - 1 :], 0.0)
    from_above = jnp.where(slab_index < slab_count - 1, halo[1][:, :, :1], 0.0)
    data_bands = jnp.concatenate([from_below, band, from_above], axis=2)
    slab_index = lax.axis_index("slab")
    ctf_sq = jnp.pad(
        jnp.square(ctf_table.astype(jnp.float32)), ((0, 0), (half_cols, half_cols))
    )
    window = lax.dynamic_slice_in_dim(
        ctf_sq, slab_index * band_pixels, band_pixels + 2 * half_cols, 1
    )
    weight_rows = jnp.dot(
        total_counts, window, precision=lax.Precision.HIGHEST, preferred_element_type=jnp.float32
    ) * channel_scale[2]
    class_bands = jnp.concatenate(
        [data_bands, weight_rows.reshape(class_count, 1, band_rows + 2, half_cols)], axis=1
    )
    group_index = lax.axis_index("grp")
    offset_pad = jnp.pad(z_offset, ((0, 0), (1, 1)))
    frac_pad = jnp.pad(z_frac, ((0, 0), (1, 1)))
    rows_held = band_rows + 2
    local_offset = lax.dynamic_slice_in_dim(offset_pad, slab_index * band_rows, rows_held, 1)
    local_frac = lax.dynamic_slice_in_dim(frac_pad, slab_index * band_rows, rows_held, 1)
    row_ids = jnp.arange(rows_held, dtype=jnp.int32) + (band_rows - 1)
    band_shift = (row_ids // band_rows - 1) * z_dev - 1
    target = 2 * (row_ids % band_rows)[None, :] + local_offset + 1 + band_shift[None, :]
    plane_ids = jnp.arange(z_dev, dtype=jnp.int32)
    depth_weight = jnp.where(
        plane_ids[None, None, :] == target[:, :, None], (1.0 - local_frac)[:, :, None], 0.0
    )
    depth_weight = depth_weight + jnp.where(
        plane_ids[None, None, :] == target[:, :, None] + 1, local_frac[:, :, None], 0.0
    )
    sectioned = jnp.einsum(
        "ckra,crz->kzca",
        class_bands,
        depth_weight,
        precision=lax.Precision.HIGHEST,
    ).reshape(3 * z_dev, class_count * half_cols)
    inserted = insert_planes(row_weights, sectioned, col_weights)
    return inserted.reshape(3, z_dev, y_rows, side_cells)


def insert_kernel(rows_ref, sec_ref, cols_ref, out_ref, lifted_ref):
    y_rows = rows_ref.shape[0]

    def body(i, carry):
        start = pl.multiple_of(i * y_rows, y_rows)
        lifted_ref[pl.ds(start, y_rows), :] = (
            rows_ref[...].astype(jnp.float32) * sec_ref[pl.ds(i, 1), :]
        ).astype(jnp.bfloat16)
        return carry

    lax.fori_loop(0, sec_ref.shape[0], body, 0)
    out_ref[...] = lax.dot_general(
        lifted_ref[...], cols_ref[...], (((1,), (1,)), ((), ())), preferred_element_type=jnp.float32
    )


def insert_planes(row_weights, sectioned, col_weights):
    planes = sectioned.shape[0]
    y_rows, depth = row_weights.shape
    side = col_weights.shape[0]
    return pl.pallas_call(
        insert_kernel,
        out_shape=jax.ShapeDtypeStruct((planes * y_rows, side), jnp.float32),
        in_specs=[pl.BlockSpec(memory_space=pltpu.VMEM)] * 3,
        out_specs=pl.BlockSpec(memory_space=pltpu.VMEM),
        scratch_shapes=[pltpu.VMEM((planes * y_rows, depth), jnp.bfloat16)],
        cost_estimate=pl.CostEstimate(
            flops=2 * planes * y_rows * depth * side,
            transcendentals=0,
            bytes_accessed=2 * y_rows * depth + 4 * planes * depth + 2 * depth * side
            + 4 * planes * y_rows * side,
        ),
    )(row_weights, sectioned, col_weights)


def solution(mesh):
    in_specs = (
        P(("grp", "slab"), None),
        P(("grp", "slab")),
        P(("grp", "slab")),
        P(),
        P("slab", None),
        P(),
        P(),
        P(),
        P(),
        P(),
        P(),
        P(),
    )
    out_specs = P(None, "slab", "grp", None)
    return jax.shard_map(local, mesh=mesh, in_specs=in_specs, out_specs=out_specs, check_vma=False)
```

```python
import functools
import math

import jax
import jax.numpy as jnp
from jax import lax
from jax.experimental import pallas as pl
from jax.experimental.pallas import tpu as pltpu
from jax.sharding import PartitionSpec as P

SHIFTS = 128
Z_CHIPS = 8


def exchange_kernel(count, place, picks, *refs):
    parts = len(picks)
    x_refs, out_refs = refs[:parts], refs[parts : 2 * parts]
    local_sems, send_sems, recv_sems = refs[2 * parts :]
    me, device = place()
    barrier = pltpu.get_barrier_semaphore()
    for k in range(1, count):
        pl.semaphore_signal(
            barrier,
            1,
            device_id=device(lax.rem(me + k, count)),
            device_id_type=pl.DeviceIdType.MESH,
        )
    pl.semaphore_wait(barrier, count - 1)
    owns, copies = [], []
    for part, (pick, x_ref, out_ref) in enumerate(zip(picks, x_refs, out_refs)):
        own = pltpu.make_async_copy(pick(x_ref, me), out_ref.at[me], local_sems.at[part])
        own.start()
        owns.append(own)
        for k in range(1, count):
            peer = lax.rem(me + k, count)
            copy = pltpu.make_async_remote_copy(
                src_ref=pick(x_ref, peer),
                dst_ref=out_ref.at[me],
                send_sem=send_sems.at[part, k],
                recv_sem=recv_sems.at[part, k],
                device_id=device(peer),
                device_id_type=pl.DeviceIdType.MESH,
            )
            copy.start()
            copies.append(copy)
    for own in owns:
        own.wait()
    for copy in copies:
        copy.wait_send()
        copy.wait_recv()


def slab_place():
    group = lax.axis_index("grp")
    return lax.axis_index("slab"), lambda peer: (group, peer)


def core_place():
    group, slab = lax.axis_index("grp"), lax.axis_index("slab")
    return lax.rem(group, 2), lambda peer: (group - lax.rem(group, 2) + peer, slab)


def z_place():
    group, slab = lax.axis_index("grp"), lax.axis_index("slab")
    z = lax.rem(slab, Z_CHIPS)
    return z, lambda peer: (group, slab - z + peer)


def y_place():
    group, slab = lax.axis_index("grp"), lax.axis_index("slab")
    z = lax.rem(slab, Z_CHIPS)
    return slab // Z_CHIPS, lambda peer: (group, peer * Z_CHIPS + z)


def group_place():
    slab = lax.axis_index("slab")
    return lax.axis_index("grp"), lambda peer: (peer, slab)


def whole(x_ref, peer):
    return x_ref.at[0]


def entire(x_ref, peer):
    return x_ref


def row_block(x_ref, peer):
    return x_ref.at[peer]


def lane_blocks(count):
    def pick(x_ref, peer):
        width = x_ref.shape[1] // count
        return x_ref.at[:, pl.ds(pl.multiple_of(peer * width, width), width)]

    return pick


def exchange_many(xs, count, place, picks, collective_id, block_shapes):
    parts = len(xs)
    return pl.pallas_call(
        functools.partial(exchange_kernel, count, place, tuple(picks)),
        out_shape=[
            jax.ShapeDtypeStruct((count,) + shape, x.dtype) for x, shape in zip(xs, block_shapes)
        ],
        in_specs=[pl.BlockSpec(memory_space=pltpu.VMEM)] * parts,
        out_specs=[pl.BlockSpec(memory_space=pltpu.VMEM)] * parts,
        scratch_shapes=[
            pltpu.SemaphoreType.DMA((parts,)),
            pltpu.SemaphoreType.DMA((parts, count)),
            pltpu.SemaphoreType.DMA((parts, count)),
        ],
        compiler_params=pltpu.CompilerParams(collective_id=collective_id, has_side_effects=True),
    )(*xs)


def exchange(x, count, place, pick, collective_id, block_shape):
    return exchange_many([x], count, place, [pick], collective_id, [block_shape])[0]


def signal_all(devices):
    barrier = pltpu.get_barrier_semaphore()
    for device in devices:
        pl.semaphore_signal(barrier, 1, device_id=device, device_id_type=pl.DeviceIdType.MESH)
    return lambda: pl.semaphore_wait(barrier, len(devices))


def run_phase(count, place, pick, x_ref, out_ref, local_sem, send_sems, recv_sems, cover=None):
    me, device = place()
    own = pltpu.make_async_copy(pick(x_ref, me), out_ref.at[me], local_sem)
    own.start()
    copies = []
    for k in range(1, count):
        peer = lax.rem(me + k, count)
        copy = pltpu.make_async_remote_copy(
            src_ref=pick(x_ref, peer),
            dst_ref=out_ref.at[me],
            send_sem=send_sems.at[k],
            recv_sem=recv_sems.at[k],
            device_id=device(peer),
            device_id_type=pl.DeviceIdType.MESH,
        )
        copy.start()
        copies.append(copy)
    if cover is not None:
        cover()
    own.wait()
    for copy in copies:
        copy.wait_send()
        copy.wait_recv()


def peers(count, place):
    me, device = place()
    return [device(lax.rem(me + k, count)) for k in range(1, count)]


def stencil_kernel(base_ref, frac_ref, rows_ref, cols_ref):
    y_rows = rows_ref.shape[0]
    y_ids = lax.axis_index("grp") * y_rows + lax.broadcasted_iota(jnp.int32, rows_ref.shape, 0)
    y_base, y_frac = base_ref[0:1, :], frac_ref[0:1, :]
    rows = jnp.where(y_ids == y_base, 1.0 - y_frac, 0.0) + jnp.where(y_ids == y_base + 1, y_frac, 0.0)
    rows_ref[...] = rows.astype(rows_ref.dtype)
    x_ids = lax.broadcasted_iota(jnp.int32, cols_ref.shape, 0)
    x_base, x_frac = base_ref[1:2, :], frac_ref[1:2, :]
    cols = jnp.where(x_ids == x_base, 1.0 - x_frac, 0.0) + jnp.where(x_ids == x_base + 1, x_frac, 0.0)
    cols_ref[...] = cols.astype(cols_ref.dtype)


def neighbour_place():
    group, slab = lax.axis_index("grp"), lax.axis_index("slab")
    count = lax.axis_size("slab")
    return [(group, lax.rem(slab + 1, count)), (group, lax.rem(slab + count - 1, count))]


def reduce_chain_kernel(y_chips, groups, x_ref, base_ref, frac_ref,
                        total_ref, halo_ref, rows_ref, cols_ref, core_buf, y_src, y_buf, z_src, z_buf,
                        d_src, d_buf, local_sems, send_sems, recv_sems, halo_send, halo_recv):
    arrive = signal_all(
        peers(2, core_place)
        + peers(y_chips, y_place)
        + peers(Z_CHIPS, z_place)
        + peers(groups, group_place)
        + neighbour_place()
    )
    arrive()
    run_phase(2, core_place, row_block, x_ref, core_buf, local_sems.at[0], send_sems.at[0], recv_sems.at[0],
              lambda: stencil_kernel(base_ref, frac_ref, rows_ref, cols_ref))
    y_src[...] = (core_buf[0].astype(jnp.float32) + core_buf[1].astype(jnp.float32)).astype(y_src.dtype)
    run_phase(
        y_chips, y_place, lane_blocks(y_chips), y_src, y_buf,
        local_sems.at[1], send_sems.at[1], recv_sems.at[1],
    )
    z_src[...] = jnp.sum(y_buf[...].astype(jnp.float32), axis=0).astype(z_src.dtype)
    run_phase(
        Z_CHIPS, z_place, lane_blocks(Z_CHIPS), z_src, z_buf,
        local_sems.at[2], send_sems.at[2], recv_sems.at[2],
    )
    d_src[0] = jnp.sum(z_buf[...].astype(jnp.float32), axis=0).astype(d_src.dtype)
    run_phase(groups, group_place, whole, d_src, d_buf, local_sems.at[3], send_sems.at[3], recv_sems.at[3])
    for half in range(2):
        total_ref[half] = jnp.sum(
            jnp.stack([d_buf[j].astype(jnp.float32) for j in range(half, groups, 2)]), axis=0
        )
    copies = []
    for side, device in enumerate(neighbour_place()):
        copy = pltpu.make_async_remote_copy(
            src_ref=total_ref,
            dst_ref=halo_ref.at[side],
            send_sem=halo_send.at[side],
            recv_sem=halo_recv.at[side],
            device_id=device,
            device_id_type=pl.DeviceIdType.MESH,
        )
        copy.start()
        copies.append(copy)
    for copy in copies:
        copy.wait_send()
        copy.wait_recv()


def reduce_chain(x, stencil, y_rows, side, y_chips, groups, collective_id):
    _, rows, width = x.shape
    band = width // (y_chips * Z_CHIPS)
    wide = 8
    depth = stencil[0].shape[1]
    return pl.pallas_call(
        functools.partial(reduce_chain_kernel, y_chips, groups),
        out_shape=[
            jax.ShapeDtypeStruct((2, rows, band), jnp.float32),
            jax.ShapeDtypeStruct((2, 2, rows, band), jnp.float32),
            jax.ShapeDtypeStruct((y_rows, depth), jnp.bfloat16),
            jax.ShapeDtypeStruct((side, depth), jnp.bfloat16),
        ],
        in_specs=[pl.BlockSpec(memory_space=pltpu.VMEM)] * 3,
        out_specs=[pl.BlockSpec(memory_space=pltpu.VMEM)] * 4,
        scratch_shapes=[
            pltpu.VMEM((2, rows, width), x.dtype),
            pltpu.VMEM((rows, width), jnp.bfloat16),
            pltpu.VMEM((y_chips, rows, width // y_chips), jnp.bfloat16),
            pltpu.VMEM((rows, width // y_chips), jnp.bfloat16),
            pltpu.VMEM((Z_CHIPS, rows, band), jnp.bfloat16),
            pltpu.VMEM((1, rows, band), jnp.bfloat16),
            pltpu.VMEM((groups, rows, band), jnp.bfloat16),
            pltpu.SemaphoreType.DMA((4,)),
            pltpu.SemaphoreType.DMA((4, wide)),
            pltpu.SemaphoreType.DMA((4, wide)),
            pltpu.SemaphoreType.DMA((2,)),
            pltpu.SemaphoreType.DMA((2,)),
        ],
        compiler_params=pltpu.CompilerParams(collective_id=collective_id, has_side_effects=True),
    )(x, *stencil)


def phase_kernel(row_count, half_cols, phase_ref, parts):
    half = phase_ref.shape[1] // 2
    lanes = 128
    blocks = half // lanes
    shifts = phase_ref.shape[0]
    step = 2.0 * math.pi / row_count
    t_b = lax.broadcasted_iota(jnp.int32, (shifts, blocks), 0)
    q_b = lax.broadcasted_iota(jnp.int32, (shifts, blocks), 1)
    shift_rows_b = (t_b // 8 - SHIFTS // 16).astype(jnp.float32)
    block_rows = (q_b * (lanes // half_cols) - row_count // 2).astype(jnp.float32)
    block_angle = shift_rows_b * block_rows * step
    t_l = lax.broadcasted_iota(jnp.int32, (shifts, lanes), 0)
    l_l = lax.broadcasted_iota(jnp.int32, (shifts, lanes), 1)
    shift_rows_l = (t_l // 8 - SHIFTS // 16).astype(jnp.float32)
    shift_cols_l = (t_l % 8 - 4).astype(jnp.float32)
    lane_angle = (
        shift_rows_l * (l_l // half_cols).astype(jnp.float32)
        + shift_cols_l * (l_l % half_cols).astype(jnp.float32)
    ) * step

    def part(first, last):
        def fill():
            cos_b, sin_b = jnp.cos(block_angle), jnp.sin(block_angle)
            c_l, s_l = jnp.cos(lane_angle), jnp.sin(lane_angle)
            for q in range(first, last):
                c_b, s_b = cos_b[:, q : q + 1], sin_b[:, q : q + 1]
                phase_ref[:, q * lanes : (q + 1) * lanes] = (c_b * c_l - s_b * s_l).astype(
                    phase_ref.dtype
                )
                phase_ref[:, half + q * lanes : half + (q + 1) * lanes] = (
                    s_b * c_l + c_b * s_l
                ).astype(phase_ref.dtype)

        return fill

    edges = [blocks * i // parts for i in range(parts + 1)]
    return [part(edges[i], edges[i + 1]) for i in range(parts)]


def gather_chain_kernel(y_chips, row_count, half_cols, x_ref, out_ref, phase_ref, z_buf, y_buf,
                        local_sems, send_sems, recv_sems):
    arrive = signal_all(peers(Z_CHIPS, z_place) + peers(y_chips, y_place) + peers(2, core_place))
    fills = phase_kernel(row_count, half_cols, phase_ref, 3)
    arrive()
    run_phase(Z_CHIPS, z_place, whole, x_ref, z_buf, local_sems.at[0], send_sems.at[0], recv_sems.at[0],
              fills[0])
    run_phase(y_chips, y_place, entire, z_buf, y_buf, local_sems.at[1], send_sems.at[1], recv_sems.at[1],
              fills[1])
    run_phase(2, core_place, entire, y_buf, out_ref, local_sems.at[2], send_sems.at[2], recv_sems.at[2],
              fills[2])


def gather_chain(x, row_count, half_cols, y_chips, collective_id):
    _, rows, lanes = x.shape
    shifts = SHIFTS
    table = 2 * row_count * half_cols
    return pl.pallas_call(
        functools.partial(gather_chain_kernel, y_chips, row_count, half_cols),
        out_shape=[
            jax.ShapeDtypeStruct((2, y_chips, Z_CHIPS, rows, lanes), x.dtype),
            jax.ShapeDtypeStruct((shifts, table), jnp.bfloat16),
        ],
        in_specs=[pl.BlockSpec(memory_space=pltpu.VMEM)],
        out_specs=[pl.BlockSpec(memory_space=pltpu.VMEM)] * 2,
        scratch_shapes=[
            pltpu.VMEM((Z_CHIPS, rows, lanes), x.dtype),
            pltpu.VMEM((y_chips, Z_CHIPS, rows, lanes), x.dtype),
            pltpu.SemaphoreType.DMA((3,)),
            pltpu.SemaphoreType.DMA((3, Z_CHIPS)),
            pltpu.SemaphoreType.DMA((3, Z_CHIPS)),
        ],
        compiler_params=pltpu.CompilerParams(collective_id=collective_id, has_side_effects=True),
    )(x)


def align_frames(frames, ctf_rows, ref_re, ref_im, phase, score_scale):
    pixels = ctf_rows.shape[1]
    frame_re = frames[:, :pixels].astype(jnp.float32)
    frame_im = frames[:, pixels:].astype(jnp.float32)
    ref_re = ref_re.astype(jnp.float32)
    ref_im = ref_im.astype(jnp.float32)
    weight = ctf_rows.astype(jnp.float32)
    cross_terms = jnp.concatenate(
        [
            weight * (ref_re * frame_re + ref_im * frame_im),
            weight * (ref_re * frame_im - ref_im * frame_re),
        ],
        axis=1,
    ).astype(jnp.bfloat16)
    scores = score_scale * jnp.einsum(
        "np,sp->ns", cross_terms, phase, preferred_element_type=jnp.float32
    )
    shift_probs = jax.nn.softmax(scores, axis=1).astype(jnp.bfloat16)
    shift_mix = jnp.dot(shift_probs, phase, preferred_element_type=jnp.float32)
    mix_re = shift_mix[:, :pixels]
    mix_im = shift_mix[:, pixels:]
    return (
        weight * (frame_re * mix_re + frame_im * mix_im),
        weight * (frame_im * mix_re - frame_re * mix_im),
    )


def stencil_weights(base_cell, fraction, side_cells):
    cell_ids = jnp.arange(side_cells, dtype=jnp.int32)
    dense_weight = jnp.where(
        cell_ids[None, None, :] == base_cell[:, :, None], (1.0 - fraction)[:, :, None], 0.0
    )
    dense_weight = dense_weight + jnp.where(
        cell_ids[None, None, :] == base_cell[:, :, None] + 1, fraction[:, :, None], 0.0
    )
    return dense_weight.astype(jnp.bfloat16)


def local(
    images,
    image_class,
    image_ctf,
    class_owner,
    references,
    ctf_table,
    x_base,
    y_base,
    x_frac,
    y_frac,
    z_offset,
    z_frac,
):
    slab_count = lax.axis_size("slab")
    group_count = lax.axis_size("grp")
    frame_count = images.shape[0]
    pixels = ctf_table.shape[1]
    groups_ctf = ctf_table.shape[0]
    row_count = z_offset.shape[1]
    half_cols = x_base.shape[1]
    class_count = class_owner.shape[0]
    side_cells = 2 * row_count
    band_rows = row_count // slab_count
    band_pixels = band_rows * half_cols
    z_dev = 2 * band_rows
    score_scale = 2.0 / math.sqrt(2.0 * pixels)
    channel_scale = jnp.array(
        [
            1.0 / math.sqrt(frame_count * group_count),
            1.0 / math.sqrt(frame_count * group_count),
            1.0 / (frame_count * group_count),
        ],
        jnp.float32,
    )
    lanes = 128
    core = lax.rem(lax.axis_index("grp"), 2)
    ref_halves = references.reshape(2, -1, lanes)
    my_half = lax.dynamic_slice_in_dim(ref_halves, core, 1, 0)
    y_chips = slab_count // Z_CHIPS
    gathered, phase = gather_chain(my_half, row_count, half_cols, y_chips, 0)
    both_halves = gathered.reshape(2, slab_count, pixels)
    class_ids = jnp.arange(class_count, dtype=jnp.int32)
    owner_of = jnp.sum(
        jnp.where(image_class[:, None] == class_ids[None, :], class_owner[None, :], 0), axis=1
    )
    pick_ref = (owner_of[:, None] == jnp.arange(slab_count, dtype=jnp.int32)[None, :]).astype(
        jnp.bfloat16
    )
    ref_re = jnp.dot(pick_ref, both_halves[0], preferred_element_type=jnp.float32).astype(
        jnp.bfloat16
    )
    ref_im = jnp.dot(pick_ref, both_halves[1], preferred_element_type=jnp.float32).astype(
        jnp.bfloat16
    )
    pick_ctf = (image_ctf[:, None] == jnp.arange(groups_ctf, dtype=jnp.int32)[None, :]).astype(
        jnp.bfloat16
    )
    ctf_rows = jnp.dot(pick_ctf, ctf_table, preferred_element_type=jnp.float32).astype(
        jnp.bfloat16
    )
    stacked = align_frames(images, ctf_rows, ref_re, ref_im, phase, score_scale)
    member = (class_ids[:, None] == image_class[None, :]).astype(jnp.float32)
    aligned_re, aligned_im = stacked
    partial_re, partial_im = (
        jnp.dot(
            member, part, precision=lax.Precision.HIGHEST, preferred_element_type=jnp.float32
        ) * channel_scale[0]
        for part in (aligned_re, aligned_im)
    )
    half_classes = class_count // 2
    half_rows = half_classes * 2
    class_hits = (class_ids[:, None] == image_class[None, :]).astype(jnp.bfloat16)
    ctf_hits = (image_ctf[:, None] == jnp.arange(groups_ctf, dtype=jnp.int32)[None, :]).astype(
        jnp.bfloat16
    )
    counts = jnp.dot(class_hits, ctf_hits, preferred_element_type=jnp.float32)
    count_rows = class_count * groups_ctf // band_pixels
    tiled_counts = jnp.tile(counts.reshape(count_rows, band_pixels), (1, slab_count))
    rows = half_rows + count_rows
    by_half = jnp.stack(
        [
            jnp.concatenate(
                [
                    partial_re[h * half_classes : (h + 1) * half_classes],
                    partial_im[h * half_classes : (h + 1) * half_classes],
                    tiled_counts,
                ],
                axis=0,
            )
            for h in range(2)
        ]
    ).astype(jnp.bfloat16)
    y_rows = side_cells // group_count
    flat = class_count * half_cols
    stencil = (
        jnp.stack([y_base.reshape(flat), x_base.reshape(flat)]),
        jnp.stack([y_frac.reshape(flat), x_frac.reshape(flat)]),
    )
    total, halo, row_weights, col_weights = reduce_chain(
        by_half, stencil, y_rows, side_cells, slab_count // Z_CHIPS, group_count, 1
    )
    band = total[:, :half_rows].reshape(2, 2, half_classes, band_rows, half_cols)
    band = band.transpose(0, 2, 1, 3, 4).reshape(class_count, 2, band_rows, half_cols)
    total_counts = total[0, half_rows:].reshape(class_count, groups_ctf)
    halo = halo[:, :, :half_rows].reshape(2, 2, 2, half_classes, band_rows, half_cols)
    halo = halo.transpose(0, 1, 3, 2, 4, 5).reshape(2, class_count, 2, band_rows, half_cols)
    slab_index = lax.axis_index("slab")
    from_below = jnp.where(slab_index > 0, halo[0][:, :, band_rows - 1 :], 0.0)
    from_above = jnp.where(slab_index < slab_count - 1, halo[1][:, :, :1], 0.0)
    data_bands = jnp.concatenate([from_below, band, from_above], axis=2)
    slab_index = lax.axis_index("slab")
    ctf_sq = jnp.pad(
        jnp.square(ctf_table.astype(jnp.float32)), ((0, 0), (half_cols, half_cols))
    )
    window = lax.dynamic_slice_in_dim(
        ctf_sq, slab_index * band_pixels, band_pixels + 2 * half_cols, 1
    )
    weight_rows = jnp.dot(
        total_counts, window, precision=lax.Precision.HIGHEST, preferred_element_type=jnp.float32
    ) * channel_scale[2]
    class_bands = jnp.concatenate(
        [data_bands, weight_rows.reshape(class_count, 1, band_rows + 2, half_cols)], axis=1
    )
    group_index = lax.axis_index("grp")
    offset_pad = jnp.pad(z_offset, ((0, 0), (1, 1)))
    frac_pad = jnp.pad(z_frac, ((0, 0), (1, 1)))
    rows_held = band_rows + 2
    local_offset = lax.dynamic_slice_in_dim(offset_pad, slab_index * band_rows, rows_held, 1)
    local_frac = lax.dynamic_slice_in_dim(frac_pad, slab_index * band_rows, rows_held, 1)
    row_ids = jnp.arange(rows_held, dtype=jnp.int32) + (band_rows - 1)
    band_shift = (row_ids // band_rows - 1) * z_dev - 1
    target = 2 * (row_ids % band_rows)[None, :] + local_offset + 1 + band_shift[None, :]
    plane_ids = jnp.arange(z_dev, dtype=jnp.int32)
    depth_weight = jnp.where(
        plane_ids[None, None, :] == target[:, :, None], (1.0 - local_frac)[:, :, None], 0.0
    )
    depth_weight = depth_weight + jnp.where(
        plane_ids[None, None, :] == target[:, :, None] + 1, local_frac[:, :, None], 0.0
    )
    sectioned = jnp.einsum(
        "ckra,crz->kzca",
        class_bands,
        depth_weight,
        precision=lax.Precision.HIGHEST,
    ).reshape(3 * z_dev, class_count * half_cols)
    inserted = insert_planes(row_weights, sectioned, col_weights)
    return inserted.reshape(3, z_dev, y_rows, side_cells)


def insert_kernel(rows_ref, sec_ref, cols_ref, out_ref, lifted_ref):
    y_rows = rows_ref.shape[0]

    def body(i, carry):
        start = pl.multiple_of(i * y_rows, y_rows)
        lifted_ref[pl.ds(start, y_rows), :] = (
            rows_ref[...].astype(jnp.float32) * sec_ref[pl.ds(i, 1), :]
        ).astype(jnp.bfloat16)
        return carry

    lax.fori_loop(0, sec_ref.shape[0], body, 0)
    out_ref[...] = lax.dot_general(
        lifted_ref[...], cols_ref[...], (((1,), (1,)), ((), ())), preferred_element_type=jnp.float32
    )


def insert_planes(row_weights, sectioned, col_weights):
    planes = sectioned.shape[0]
    y_rows, depth = row_weights.shape
    side = col_weights.shape[0]
    return pl.pallas_call(
        insert_kernel,
        out_shape=jax.ShapeDtypeStruct((planes * y_rows, side), jnp.float32),
        in_specs=[pl.BlockSpec(memory_space=pltpu.VMEM)] * 3,
        out_specs=pl.BlockSpec(memory_space=pltpu.VMEM),
        scratch_shapes=[pltpu.VMEM((planes * y_rows, depth), jnp.bfloat16)],
        cost_estimate=pl.CostEstimate(
            flops=2 * planes * y_rows * depth * side,
            transcendentals=0,
            bytes_accessed=2 * y_rows * depth + 4 * planes * depth + 2 * depth * side
            + 4 * planes * y_rows * side,
        ),
    )(row_weights, sectioned, col_weights)


def solution(mesh):
    in_specs = (
        P(("grp", "slab"), None),
        P(("grp", "slab")),
        P(("grp", "slab")),
        P(),
        P("slab", None),
        P(),
        P(),
        P(),
        P(),
        P(),
        P(),
        P(),
    )
    out_specs = P(None, "slab", "grp", None)
    return jax.shard_map(local, mesh=mesh, in_specs=in_specs, out_specs=out_specs, check_vma=False)
```

```python
import functools
import math

import jax
import jax.numpy as jnp
from jax import lax
from jax.experimental import pallas as pl
from jax.experimental.pallas import tpu as pltpu
from jax.sharding import PartitionSpec as P

SHIFTS = 128
Z_CHIPS = 8


def exchange_kernel(count, place, picks, *refs):
    parts = len(picks)
    x_refs, out_refs = refs[:parts], refs[parts : 2 * parts]
    local_sems, send_sems, recv_sems = refs[2 * parts :]
    me, device = place()
    barrier = pltpu.get_barrier_semaphore()
    for k in range(1, count):
        pl.semaphore_signal(
            barrier,
            1,
            device_id=device(lax.rem(me + k, count)),
            device_id_type=pl.DeviceIdType.MESH,
        )
    pl.semaphore_wait(barrier, count - 1)
    owns, copies = [], []
    for part, (pick, x_ref, out_ref) in enumerate(zip(picks, x_refs, out_refs)):
        own = pltpu.make_async_copy(pick(x_ref, me), out_ref.at[me], local_sems.at[part])
        own.start()
        owns.append(own)
        for k in range(1, count):
            peer = lax.rem(me + k, count)
            copy = pltpu.make_async_remote_copy(
                src_ref=pick(x_ref, peer),
                dst_ref=out_ref.at[me],
                send_sem=send_sems.at[part, k],
                recv_sem=recv_sems.at[part, k],
                device_id=device(peer),
                device_id_type=pl.DeviceIdType.MESH,
            )
            copy.start()
            copies.append(copy)
    for own in owns:
        own.wait()
    for copy in copies:
        copy.wait_send()
        copy.wait_recv()


def slab_place():
    group = lax.axis_index("grp")
    return lax.axis_index("slab"), lambda peer: (group, peer)


def core_place():
    group, slab = lax.axis_index("grp"), lax.axis_index("slab")
    return lax.rem(group, 2), lambda peer: (group - lax.rem(group, 2) + peer, slab)


def z_place():
    group, slab = lax.axis_index("grp"), lax.axis_index("slab")
    z = lax.rem(slab, Z_CHIPS)
    return z, lambda peer: (group, slab - z + peer)


def y_place():
    group, slab = lax.axis_index("grp"), lax.axis_index("slab")
    z = lax.rem(slab, Z_CHIPS)
    return slab // Z_CHIPS, lambda peer: (group, peer * Z_CHIPS + z)


def group_place():
    slab = lax.axis_index("slab")
    return lax.axis_index("grp"), lambda peer: (peer, slab)


def whole(x_ref, peer):
    return x_ref.at[0]


def entire(x_ref, peer):
    return x_ref


def row_block(x_ref, peer):
    return x_ref.at[peer]


def lane_blocks(count):
    def pick(x_ref, peer):
        width = x_ref.shape[1] // count
        return x_ref.at[:, pl.ds(pl.multiple_of(peer * width, width), width)]

    return pick


def exchange_many(xs, count, place, picks, collective_id, block_shapes):
    parts = len(xs)
    return pl.pallas_call(
        functools.partial(exchange_kernel, count, place, tuple(picks)),
        out_shape=[
            jax.ShapeDtypeStruct((count,) + shape, x.dtype) for x, shape in zip(xs, block_shapes)
        ],
        in_specs=[pl.BlockSpec(memory_space=pltpu.VMEM)] * parts,
        out_specs=[pl.BlockSpec(memory_space=pltpu.VMEM)] * parts,
        scratch_shapes=[
            pltpu.SemaphoreType.DMA((parts,)),
            pltpu.SemaphoreType.DMA((parts, count)),
            pltpu.SemaphoreType.DMA((parts, count)),
        ],
        compiler_params=pltpu.CompilerParams(collective_id=collective_id, has_side_effects=True),
    )(*xs)


def exchange(x, count, place, pick, collective_id, block_shape):
    return exchange_many([x], count, place, [pick], collective_id, [block_shape])[0]


def signal_all(devices):
    barrier = pltpu.get_barrier_semaphore()
    for device in devices:
        pl.semaphore_signal(barrier, 1, device_id=device, device_id_type=pl.DeviceIdType.MESH)
    return lambda: pl.semaphore_wait(barrier, len(devices))


def run_phase(count, place, pick, x_ref, out_ref, local_sem, send_sems, recv_sems):
    me, device = place()
    own = pltpu.make_async_copy(pick(x_ref, me), out_ref.at[me], local_sem)
    own.start()
    copies = []
    for k in range(1, count):
        peer = lax.rem(me + k, count)
        copy = pltpu.make_async_remote_copy(
            src_ref=pick(x_ref, peer),
            dst_ref=out_ref.at[me],
            send_sem=send_sems.at[k],
            recv_sem=recv_sems.at[k],
            device_id=device(peer),
            device_id_type=pl.DeviceIdType.MESH,
        )
        copy.start()
        copies.append(copy)
    own.wait()
    for copy in copies:
        copy.wait_send()
        copy.wait_recv()


def peers(count, place):
    me, device = place()
    return [device(lax.rem(me + k, count)) for k in range(1, count)]


def stencil_kernel(base_ref, frac_ref, rows_ref, cols_ref):
    y_rows = rows_ref.shape[0]
    y_ids = lax.axis_index("grp") * y_rows + lax.broadcasted_iota(jnp.int32, rows_ref.shape, 0)
    y_base, y_frac = base_ref[0:1, :], frac_ref[0:1, :]
    rows = jnp.where(y_ids == y_base, 1.0 - y_frac, 0.0) + jnp.where(y_ids == y_base + 1, y_frac, 0.0)
    rows_ref[...] = rows.astype(rows_ref.dtype)
    x_ids = lax.broadcasted_iota(jnp.int32, cols_ref.shape, 0)
    x_base, x_frac = base_ref[1:2, :], frac_ref[1:2, :]
    cols = jnp.where(x_ids == x_base, 1.0 - x_frac, 0.0) + jnp.where(x_ids == x_base + 1, x_frac, 0.0)
    cols_ref[...] = cols.astype(cols_ref.dtype)


def neighbour_place(groups):
    slab = lax.axis_index("slab")
    count = lax.axis_size("slab")
    return [
        (peer, lax.rem(slab + step, count))
        for step in (1, count - 1)
        for peer in range(groups)
    ]


def reduce_chain_kernel(y_chips, groups, x_ref, base_ref, frac_ref,
                        total_ref, halo_ref, rows_ref, cols_ref, core_buf, y_src, y_buf, z_src, z_buf,
                        d_src, d_buf, edge_buf, local_sems, send_sems, recv_sems, halo_send, halo_recv):
    arrive = signal_all(
        peers(2, core_place)
        + peers(y_chips, y_place)
        + peers(Z_CHIPS, z_place)
        + peers(groups, group_place)
        + neighbour_place(groups)
    )
    stencil_kernel(base_ref, frac_ref, rows_ref, cols_ref)
    arrive()
    run_phase(2, core_place, row_block, x_ref, core_buf, local_sems.at[0], send_sems.at[0], recv_sems.at[0])
    y_src[...] = (core_buf[0].astype(jnp.float32) + core_buf[1].astype(jnp.float32)).astype(y_src.dtype)
    run_phase(
        y_chips, y_place, lane_blocks(y_chips), y_src, y_buf,
        local_sems.at[1], send_sems.at[1], recv_sems.at[1],
    )
    z_src[...] = jnp.sum(y_buf[...].astype(jnp.float32), axis=0).astype(z_src.dtype)
    run_phase(
        Z_CHIPS, z_place, lane_blocks(Z_CHIPS), z_src, z_buf,
        local_sems.at[2], send_sems.at[2], recv_sems.at[2],
    )
    d_src[0] = jnp.sum(z_buf[...].astype(jnp.float32), axis=0).astype(d_src.dtype)
    group = lax.axis_index("grp")
    edge_copies = []
    for index, device in enumerate(neighbour_place(groups)):
        side, peer = divmod(index, groups)
        copy = pltpu.make_async_remote_copy(
            src_ref=d_src.at[0],
            dst_ref=edge_buf.at[side, group],
            send_sem=halo_send.at[side, peer],
            recv_sem=halo_recv.at[side, group],
            device_id=device,
            device_id_type=pl.DeviceIdType.MESH,
        )
        copy.start()
        edge_copies.append(copy)
    run_phase(groups, group_place, whole, d_src, d_buf, local_sems.at[3], send_sems.at[3], recv_sems.at[3])
    for copy in edge_copies:
        copy.wait_send()
    slab, count = lax.axis_index("slab"), lax.axis_size("slab")
    for side, step in enumerate((count - 1, 1)):
        for peer in range(groups):
            pltpu.make_async_remote_copy(
                src_ref=d_src.at[0],
                dst_ref=edge_buf.at[side, peer],
                send_sem=halo_send.at[side, peer],
                recv_sem=halo_recv.at[side, peer],
                device_id=(peer, lax.rem(slab + step, count)),
                device_id_type=pl.DeviceIdType.MESH,
            ).wait_recv()
    for half in range(2):
        total_ref[half] = jnp.sum(
            jnp.stack([d_buf[j].astype(jnp.float32) for j in range(half, groups, 2)]), axis=0
        )
        for side in range(2):
            halo_ref[side, half] = jnp.sum(
                jnp.stack([edge_buf[side, j].astype(jnp.float32) for j in range(half, groups, 2)]),
                axis=0,
            )


def reduce_chain(x, stencil, y_rows, side, y_chips, groups, collective_id):
    _, rows, width = x.shape
    band = width // (y_chips * Z_CHIPS)
    wide = 8
    depth = stencil[0].shape[1]
    return pl.pallas_call(
        functools.partial(reduce_chain_kernel, y_chips, groups),
        out_shape=[
            jax.ShapeDtypeStruct((2, rows, band), jnp.float32),
            jax.ShapeDtypeStruct((2, 2, rows, band), jnp.float32),
            jax.ShapeDtypeStruct((y_rows, depth), jnp.bfloat16),
            jax.ShapeDtypeStruct((side, depth), jnp.bfloat16),
        ],
        in_specs=[pl.BlockSpec(memory_space=pltpu.VMEM)] * 3,
        out_specs=[pl.BlockSpec(memory_space=pltpu.VMEM)] * 4,
        scratch_shapes=[
            pltpu.VMEM((2, rows, width), x.dtype),
            pltpu.VMEM((rows, width), jnp.bfloat16),
            pltpu.VMEM((y_chips, rows, width // y_chips), jnp.bfloat16),
            pltpu.VMEM((rows, width // y_chips), jnp.bfloat16),
            pltpu.VMEM((Z_CHIPS, rows, band), jnp.bfloat16),
            pltpu.VMEM((1, rows, band), jnp.bfloat16),
            pltpu.VMEM((groups, rows, band), jnp.bfloat16),
            pltpu.VMEM((2, groups, rows, band), jnp.bfloat16),
            pltpu.SemaphoreType.DMA((4,)),
            pltpu.SemaphoreType.DMA((4, wide)),
            pltpu.SemaphoreType.DMA((4, wide)),
            pltpu.SemaphoreType.DMA((2, groups)),
            pltpu.SemaphoreType.DMA((2, groups)),
        ],
        compiler_params=pltpu.CompilerParams(collective_id=collective_id, has_side_effects=True),
    )(x, *stencil)


def phase_kernel(row_count, half_cols, phase_ref):
    half = phase_ref.shape[1] // 2
    lanes = 128
    blocks = half // lanes
    shifts = phase_ref.shape[0]
    step = 2.0 * math.pi / row_count
    t_b = lax.broadcasted_iota(jnp.int32, (shifts, blocks), 0)
    q_b = lax.broadcasted_iota(jnp.int32, (shifts, blocks), 1)
    shift_rows_b = (t_b // 8 - SHIFTS // 16).astype(jnp.float32)
    block_rows = (q_b * (lanes // half_cols) - row_count // 2).astype(jnp.float32)
    block_angle = shift_rows_b * block_rows * step
    t_l = lax.broadcasted_iota(jnp.int32, (shifts, lanes), 0)
    l_l = lax.broadcasted_iota(jnp.int32, (shifts, lanes), 1)
    shift_rows_l = (t_l // 8 - SHIFTS // 16).astype(jnp.float32)
    shift_cols_l = (t_l % 8 - 4).astype(jnp.float32)
    lane_angle = (
        shift_rows_l * (l_l // half_cols).astype(jnp.float32)
        + shift_cols_l * (l_l % half_cols).astype(jnp.float32)
    ) * step
    cos_b, sin_b = jnp.cos(block_angle), jnp.sin(block_angle)
    c_l, s_l = jnp.cos(lane_angle), jnp.sin(lane_angle)
    for q in range(blocks):
        c_b, s_b = cos_b[:, q : q + 1], sin_b[:, q : q + 1]
        phase_ref[:, q * lanes : (q + 1) * lanes] = (c_b * c_l - s_b * s_l).astype(phase_ref.dtype)
        phase_ref[:, half + q * lanes : half + (q + 1) * lanes] = (s_b * c_l + c_b * s_l).astype(
            phase_ref.dtype
        )


def gather_chain_kernel(y_chips, row_count, half_cols, x_ref, out_ref, phase_ref, z_buf, y_buf,
                        local_sems, send_sems, recv_sems):
    arrive = signal_all(peers(Z_CHIPS, z_place) + peers(y_chips, y_place) + peers(2, core_place))
    phase_kernel(row_count, half_cols, phase_ref)
    arrive()
    run_phase(Z_CHIPS, z_place, whole, x_ref, z_buf, local_sems.at[0], send_sems.at[0], recv_sems.at[0])
    run_phase(y_chips, y_place, entire, z_buf, y_buf, local_sems.at[1], send_sems.at[1], recv_sems.at[1])
    run_phase(2, core_place, entire, y_buf, out_ref, local_sems.at[2], send_sems.at[2], recv_sems.at[2])


def gather_chain(x, row_count, half_cols, y_chips, collective_id):
    _, rows, lanes = x.shape
    shifts = SHIFTS
    table = 2 * row_count * half_cols
    return pl.pallas_call(
        functools.partial(gather_chain_kernel, y_chips, row_count, half_cols),
        out_shape=[
            jax.ShapeDtypeStruct((2, y_chips, Z_CHIPS, rows, lanes), x.dtype),
            jax.ShapeDtypeStruct((shifts, table), jnp.bfloat16),
        ],
        in_specs=[pl.BlockSpec(memory_space=pltpu.VMEM)],
        out_specs=[pl.BlockSpec(memory_space=pltpu.VMEM)] * 2,
        scratch_shapes=[
            pltpu.VMEM((Z_CHIPS, rows, lanes), x.dtype),
            pltpu.VMEM((y_chips, Z_CHIPS, rows, lanes), x.dtype),
            pltpu.SemaphoreType.DMA((3,)),
            pltpu.SemaphoreType.DMA((3, Z_CHIPS)),
            pltpu.SemaphoreType.DMA((3, Z_CHIPS)),
        ],
        compiler_params=pltpu.CompilerParams(collective_id=collective_id, has_side_effects=True),
    )(x)


def align_frames(frames, ctf_rows, ref_re, ref_im, phase, score_scale):
    pixels = ctf_rows.shape[1]
    frame_re = frames[:, :pixels].astype(jnp.float32)
    frame_im = frames[:, pixels:].astype(jnp.float32)
    ref_re = ref_re.astype(jnp.float32)
    ref_im = ref_im.astype(jnp.float32)
    weight = ctf_rows.astype(jnp.float32)
    cross_terms = jnp.concatenate(
        [
            weight * (ref_re * frame_re + ref_im * frame_im),
            weight * (ref_re * frame_im - ref_im * frame_re),
        ],
        axis=1,
    ).astype(jnp.bfloat16)
    scores = score_scale * jnp.einsum(
        "np,sp->ns", cross_terms, phase, preferred_element_type=jnp.float32
    )
    shift_probs = jax.nn.softmax(scores, axis=1).astype(jnp.bfloat16)
    shift_mix = jnp.dot(shift_probs, phase, preferred_element_type=jnp.float32)
    mix_re = shift_mix[:, :pixels]
    mix_im = shift_mix[:, pixels:]
    return (
        weight * (frame_re * mix_re + frame_im * mix_im),
        weight * (frame_im * mix_re - frame_re * mix_im),
    )


def stencil_weights(base_cell, fraction, side_cells):
    cell_ids = jnp.arange(side_cells, dtype=jnp.int32)
    dense_weight = jnp.where(
        cell_ids[None, None, :] == base_cell[:, :, None], (1.0 - fraction)[:, :, None], 0.0
    )
    dense_weight = dense_weight + jnp.where(
        cell_ids[None, None, :] == base_cell[:, :, None] + 1, fraction[:, :, None], 0.0
    )
    return dense_weight.astype(jnp.bfloat16)


def local(
    images,
    image_class,
    image_ctf,
    class_owner,
    references,
    ctf_table,
    x_base,
    y_base,
    x_frac,
    y_frac,
    z_offset,
    z_frac,
):
    slab_count = lax.axis_size("slab")
    group_count = lax.axis_size("grp")
    frame_count = images.shape[0]
    pixels = ctf_table.shape[1]
    groups_ctf = ctf_table.shape[0]
    row_count = z_offset.shape[1]
    half_cols = x_base.shape[1]
    class_count = class_owner.shape[0]
    side_cells = 2 * row_count
    band_rows = row_count // slab_count
    band_pixels = band_rows * half_cols
    z_dev = 2 * band_rows
    score_scale = 2.0 / math.sqrt(2.0 * pixels)
    channel_scale = jnp.array(
        [
            1.0 / math.sqrt(frame_count * group_count),
            1.0 / math.sqrt(frame_count * group_count),
            1.0 / (frame_count * group_count),
        ],
        jnp.float32,
    )
    lanes = 128
    core = lax.rem(lax.axis_index("grp"), 2)
    ref_halves = references.reshape(2, -1, lanes)
    my_half = lax.dynamic_slice_in_dim(ref_halves, core, 1, 0)
    y_chips = slab_count // Z_CHIPS
    gathered, phase = gather_chain(my_half, row_count, half_cols, y_chips, 0)
    both_halves = gathered.reshape(2, slab_count, pixels)
    class_ids = jnp.arange(class_count, dtype=jnp.int32)
    owner_of = jnp.sum(
        jnp.where(image_class[:, None] == class_ids[None, :], class_owner[None, :], 0), axis=1
    )
    pick_ref = (owner_of[:, None] == jnp.arange(slab_count, dtype=jnp.int32)[None, :]).astype(
        jnp.bfloat16
    )
    ref_re = jnp.dot(pick_ref, both_halves[0], preferred_element_type=jnp.float32).astype(
        jnp.bfloat16
    )
    ref_im = jnp.dot(pick_ref, both_halves[1], preferred_element_type=jnp.float32).astype(
        jnp.bfloat16
    )
    pick_ctf = (image_ctf[:, None] == jnp.arange(groups_ctf, dtype=jnp.int32)[None, :]).astype(
        jnp.bfloat16
    )
    ctf_rows = jnp.dot(pick_ctf, ctf_table, preferred_element_type=jnp.float32).astype(
        jnp.bfloat16
    )
    stacked = align_frames(images, ctf_rows, ref_re, ref_im, phase, score_scale)
    member = (class_ids[:, None] == image_class[None, :]).astype(jnp.float32)
    aligned_re, aligned_im = stacked
    partial_re, partial_im = (
        jnp.dot(
            member, part, precision=lax.Precision.HIGHEST, preferred_element_type=jnp.float32
        ) * channel_scale[0]
        for part in (aligned_re, aligned_im)
    )
    half_classes = class_count // 2
    half_rows = half_classes * 2
    class_hits = (class_ids[:, None] == image_class[None, :]).astype(jnp.bfloat16)
    ctf_hits = (image_ctf[:, None] == jnp.arange(groups_ctf, dtype=jnp.int32)[None, :]).astype(
        jnp.bfloat16
    )
    counts = jnp.dot(class_hits, ctf_hits, preferred_element_type=jnp.float32)
    count_rows = class_count * groups_ctf // band_pixels
    tiled_counts = jnp.tile(counts.reshape(count_rows, band_pixels), (1, slab_count))
    rows = half_rows + count_rows
    by_half = jnp.stack(
        [
            jnp.concatenate(
                [
                    partial_re[h * half_classes : (h + 1) * half_classes],
                    partial_im[h * half_classes : (h + 1) * half_classes],
                    tiled_counts,
                ],
                axis=0,
            )
            for h in range(2)
        ]
    ).astype(jnp.bfloat16)
    y_rows = side_cells // group_count
    flat = class_count * half_cols
    stencil = (
        jnp.stack([y_base.reshape(flat), x_base.reshape(flat)]),
        jnp.stack([y_frac.reshape(flat), x_frac.reshape(flat)]),
    )
    total, halo, row_weights, col_weights = reduce_chain(
        by_half, stencil, y_rows, side_cells, slab_count // Z_CHIPS, group_count, 1
    )
    band = total[:, :half_rows].reshape(2, 2, half_classes, band_rows, half_cols)
    band = band.transpose(0, 2, 1, 3, 4).reshape(class_count, 2, band_rows, half_cols)
    total_counts = total[0, half_rows:].reshape(class_count, groups_ctf)
    halo = halo[:, :, :half_rows].reshape(2, 2, 2, half_classes, band_rows, half_cols)
    halo = halo.transpose(0, 1, 3, 2, 4, 5).reshape(2, class_count, 2, band_rows, half_cols)
    slab_index = lax.axis_index("slab")
    from_below = jnp.where(slab_index > 0, halo[0][:, :, band_rows - 1 :], 0.0)
    from_above = jnp.where(slab_index < slab_count - 1, halo[1][:, :, :1], 0.0)
    data_bands = jnp.concatenate([from_below, band, from_above], axis=2)
    slab_index = lax.axis_index("slab")
    ctf_sq = jnp.pad(
        jnp.square(ctf_table.astype(jnp.float32)), ((0, 0), (half_cols, half_cols))
    )
    window = lax.dynamic_slice_in_dim(
        ctf_sq, slab_index * band_pixels, band_pixels + 2 * half_cols, 1
    )
    weight_rows = jnp.dot(
        total_counts, window, precision=lax.Precision.HIGHEST, preferred_element_type=jnp.float32
    ) * channel_scale[2]
    class_bands = jnp.concatenate(
        [data_bands, weight_rows.reshape(class_count, 1, band_rows + 2, half_cols)], axis=1
    )
    group_index = lax.axis_index("grp")
    offset_pad = jnp.pad(z_offset, ((0, 0), (1, 1)))
    frac_pad = jnp.pad(z_frac, ((0, 0), (1, 1)))
    rows_held = band_rows + 2
    local_offset = lax.dynamic_slice_in_dim(offset_pad, slab_index * band_rows, rows_held, 1)
    local_frac = lax.dynamic_slice_in_dim(frac_pad, slab_index * band_rows, rows_held, 1)
    row_ids = jnp.arange(rows_held, dtype=jnp.int32) + (band_rows - 1)
    band_shift = (row_ids // band_rows - 1) * z_dev - 1
    target = 2 * (row_ids % band_rows)[None, :] + local_offset + 1 + band_shift[None, :]
    plane_ids = jnp.arange(z_dev, dtype=jnp.int32)
    depth_weight = jnp.where(
        plane_ids[None, None, :] == target[:, :, None], (1.0 - local_frac)[:, :, None], 0.0
    )
    depth_weight = depth_weight + jnp.where(
        plane_ids[None, None, :] == target[:, :, None] + 1, local_frac[:, :, None], 0.0
    )
    sectioned = jnp.einsum(
        "ckra,crz->kzca",
        class_bands,
        depth_weight,
        precision=lax.Precision.HIGHEST,
    ).reshape(3 * z_dev, class_count * half_cols)
    inserted = insert_planes(row_weights, sectioned, col_weights)
    return inserted.reshape(3, z_dev, y_rows, side_cells)


def insert_kernel(rows_ref, sec_ref, cols_ref, out_ref, lifted_ref):
    y_rows = rows_ref.shape[0]

    def body(i, carry):
        start = pl.multiple_of(i * y_rows, y_rows)
        lifted_ref[pl.ds(start, y_rows), :] = (
            rows_ref[...].astype(jnp.float32) * sec_ref[pl.ds(i, 1), :]
        ).astype(jnp.bfloat16)
        return carry

    lax.fori_loop(0, sec_ref.shape[0], body, 0)
    out_ref[...] = lax.dot_general(
        lifted_ref[...], cols_ref[...], (((1,), (1,)), ((), ())), preferred_element_type=jnp.float32
    )


def insert_planes(row_weights, sectioned, col_weights):
    planes = sectioned.shape[0]
    y_rows, depth = row_weights.shape
    side = col_weights.shape[0]
    return pl.pallas_call(
        insert_kernel,
        out_shape=jax.ShapeDtypeStruct((planes * y_rows, side), jnp.float32),
        in_specs=[pl.BlockSpec(memory_space=pltpu.VMEM)] * 3,
        out_specs=pl.BlockSpec(memory_space=pltpu.VMEM),
        scratch_shapes=[pltpu.VMEM((planes * y_rows, depth), jnp.bfloat16)],
        cost_estimate=pl.CostEstimate(
            flops=2 * planes * y_rows * depth * side,
            transcendentals=0,
            bytes_accessed=2 * y_rows * depth + 4 * planes * depth + 2 * depth * side
            + 4 * planes * y_rows * side,
        ),
    )(row_weights, sectioned, col_weights)


def solution(mesh):
    in_specs = (
        P(("grp", "slab"), None),
        P(("grp", "slab")),
        P(("grp", "slab")),
        P(),
        P("slab", None),
        P(),
        P(),
        P(),
        P(),
        P(),
        P(),
        P(),
    )
    out_specs = P(None, "slab", "grp", None)
    return jax.shard_map(local, mesh=mesh, in_specs=in_specs, out_specs=out_specs, check_vma=False)
```

```python
import functools
import math

import jax
import jax.numpy as jnp
from jax import lax
from jax.experimental import pallas as pl
from jax.experimental.pallas import tpu as pltpu
from jax.sharding import PartitionSpec as P

SHIFTS = 128
Z_CHIPS = 8


def exchange_kernel(count, place, picks, *refs):
    parts = len(picks)
    x_refs, out_refs = refs[:parts], refs[parts : 2 * parts]
    local_sems, send_sems, recv_sems = refs[2 * parts :]
    me, device = place()
    barrier = pltpu.get_barrier_semaphore()
    for k in range(1, count):
        pl.semaphore_signal(
            barrier,
            1,
            device_id=device(lax.rem(me + k, count)),
            device_id_type=pl.DeviceIdType.MESH,
        )
    pl.semaphore_wait(barrier, count - 1)
    owns, copies = [], []
    for part, (pick, x_ref, out_ref) in enumerate(zip(picks, x_refs, out_refs)):
        own = pltpu.make_async_copy(pick(x_ref, me), out_ref.at[me], local_sems.at[part])
        own.start()
        owns.append(own)
        for k in range(1, count):
            peer = lax.rem(me + k, count)
            copy = pltpu.make_async_remote_copy(
                src_ref=pick(x_ref, peer),
                dst_ref=out_ref.at[me],
                send_sem=send_sems.at[part, k],
                recv_sem=recv_sems.at[part, k],
                device_id=device(peer),
                device_id_type=pl.DeviceIdType.MESH,
            )
            copy.start()
            copies.append(copy)
    for own in owns:
        own.wait()
    for copy in copies:
        copy.wait_send()
        copy.wait_recv()


def slab_place():
    group = lax.axis_index("grp")
    return lax.axis_index("slab"), lambda peer: (group, peer)


def core_place():
    group, slab = lax.axis_index("grp"), lax.axis_index("slab")
    return lax.rem(group, 2), lambda peer: (group - lax.rem(group, 2) + peer, slab)


def z_place():
    group, slab = lax.axis_index("grp"), lax.axis_index("slab")
    z = lax.rem(slab, Z_CHIPS)
    return z, lambda peer: (group, slab - z + peer)


def y_place():
    group, slab = lax.axis_index("grp"), lax.axis_index("slab")
    z = lax.rem(slab, Z_CHIPS)
    return slab // Z_CHIPS, lambda peer: (group, peer * Z_CHIPS + z)


def column_place():
    group, slab = lax.axis_index("grp"), lax.axis_index("slab")
    core, z = lax.rem(group, 2), lax.rem(slab, Z_CHIPS)
    me = core * (lax.axis_size("slab") // Z_CHIPS) + slab // Z_CHIPS
    y_chips = lax.axis_size("slab") // Z_CHIPS
    return me, lambda peer: (group - core + peer // y_chips, lax.rem(peer, y_chips) * Z_CHIPS + z)


def group_place():
    slab = lax.axis_index("slab")
    return lax.axis_index("grp"), lambda peer: (peer, slab)


def whole(x_ref, peer):
    return x_ref.at[0]


def entire(x_ref, peer):
    return x_ref


def row_block(x_ref, peer):
    return x_ref.at[peer]


def lane_blocks(count):
    def pick(x_ref, peer):
        width = x_ref.shape[1] // count
        return x_ref.at[:, pl.ds(pl.multiple_of(peer * width, width), width)]

    return pick


def exchange_many(xs, count, place, picks, collective_id, block_shapes):
    parts = len(xs)
    return pl.pallas_call(
        functools.partial(exchange_kernel, count, place, tuple(picks)),
        out_shape=[
            jax.ShapeDtypeStruct((count,) + shape, x.dtype) for x, shape in zip(xs, block_shapes)
        ],
        in_specs=[pl.BlockSpec(memory_space=pltpu.VMEM)] * parts,
        out_specs=[pl.BlockSpec(memory_space=pltpu.VMEM)] * parts,
        scratch_shapes=[
            pltpu.SemaphoreType.DMA((parts,)),
            pltpu.SemaphoreType.DMA((parts, count)),
            pltpu.SemaphoreType.DMA((parts, count)),
        ],
        compiler_params=pltpu.CompilerParams(collective_id=collective_id, has_side_effects=True),
    )(*xs)


def exchange(x, count, place, pick, collective_id, block_shape):
    return exchange_many([x], count, place, [pick], collective_id, [block_shape])[0]


def signal_all(devices):
    barrier = pltpu.get_barrier_semaphore()
    for device in devices:
        pl.semaphore_signal(barrier, 1, device_id=device, device_id_type=pl.DeviceIdType.MESH)
    return lambda: pl.semaphore_wait(barrier, len(devices))


def run_phase(count, place, pick, x_ref, out_ref, local_sem, send_sems, recv_sems):
    me, device = place()
    own = pltpu.make_async_copy(pick(x_ref, me), out_ref.at[me], local_sem)
    own.start()
    copies = []
    for k in range(1, count):
        peer = lax.rem(me + k, count)
        copy = pltpu.make_async_remote_copy(
            src_ref=pick(x_ref, peer),
            dst_ref=out_ref.at[me],
            send_sem=send_sems.at[k],
            recv_sem=recv_sems.at[k],
            device_id=device(peer),
            device_id_type=pl.DeviceIdType.MESH,
        )
        copy.start()
        copies.append(copy)
    own.wait()
    for copy in copies:
        copy.wait_send()
        copy.wait_recv()


def peers(count, place):
    me, device = place()
    return [device(lax.rem(me + k, count)) for k in range(1, count)]


def stencil_kernel(base_ref, frac_ref, rows_ref, cols_ref):
    y_rows = rows_ref.shape[0]
    y_ids = lax.axis_index("grp") * y_rows + lax.broadcasted_iota(jnp.int32, rows_ref.shape, 0)
    y_base, y_frac = base_ref[0:1, :], frac_ref[0:1, :]
    rows = jnp.where(y_ids == y_base, 1.0 - y_frac, 0.0) + jnp.where(y_ids == y_base + 1, y_frac, 0.0)
    rows_ref[...] = rows.astype(rows_ref.dtype)
    x_ids = lax.broadcasted_iota(jnp.int32, cols_ref.shape, 0)
    x_base, x_frac = base_ref[1:2, :], frac_ref[1:2, :]
    cols = jnp.where(x_ids == x_base, 1.0 - x_frac, 0.0) + jnp.where(x_ids == x_base + 1, x_frac, 0.0)
    cols_ref[...] = cols.astype(cols_ref.dtype)


def neighbour_place(groups):
    slab = lax.axis_index("slab")
    count = lax.axis_size("slab")
    return [
        (peer, lax.rem(slab + step, count))
        for step in (1, count - 1)
        for peer in range(groups)
    ]


def reduce_chain_kernel(y_chips, groups, x_ref, base_ref, frac_ref,
                        total_ref, halo_ref, rows_ref, cols_ref, core_buf, y_src, y_buf, z_src, z_buf,
                        d_src, d_buf, edge_buf, local_sems, send_sems, recv_sems, halo_send, halo_recv):
    arrive = signal_all(
        peers(2, core_place)
        + peers(y_chips, y_place)
        + peers(Z_CHIPS, z_place)
        + peers(groups, group_place)
        + neighbour_place(groups)
    )
    stencil_kernel(base_ref, frac_ref, rows_ref, cols_ref)
    arrive()
    run_phase(2, core_place, row_block, x_ref, core_buf, local_sems.at[0], send_sems.at[0], recv_sems.at[0])
    y_src[...] = (core_buf[0].astype(jnp.float32) + core_buf[1].astype(jnp.float32)).astype(y_src.dtype)
    run_phase(
        y_chips, y_place, lane_blocks(y_chips), y_src, y_buf,
        local_sems.at[1], send_sems.at[1], recv_sems.at[1],
    )
    z_src[...] = jnp.sum(y_buf[...].astype(jnp.float32), axis=0).astype(z_src.dtype)
    run_phase(
        Z_CHIPS, z_place, lane_blocks(Z_CHIPS), z_src, z_buf,
        local_sems.at[2], send_sems.at[2], recv_sems.at[2],
    )
    d_src[0] = jnp.sum(z_buf[...].astype(jnp.float32), axis=0).astype(d_src.dtype)
    group = lax.axis_index("grp")
    edge_copies = []
    for index, device in enumerate(neighbour_place(groups)):
        side, peer = divmod(index, groups)
        copy = pltpu.make_async_remote_copy(
            src_ref=d_src.at[0],
            dst_ref=edge_buf.at[side, group],
            send_sem=halo_send.at[side, peer],
            recv_sem=halo_recv.at[side, group],
            device_id=device,
            device_id_type=pl.DeviceIdType.MESH,
        )
        copy.start()
        edge_copies.append(copy)
    run_phase(groups, group_place, whole, d_src, d_buf, local_sems.at[3], send_sems.at[3], recv_sems.at[3])
    for copy in edge_copies:
        copy.wait_send()
    slab, count = lax.axis_index("slab"), lax.axis_size("slab")
    for side, step in enumerate((count - 1, 1)):
        for peer in range(groups):
            pltpu.make_async_remote_copy(
                src_ref=d_src.at[0],
                dst_ref=edge_buf.at[side, peer],
                send_sem=halo_send.at[side, peer],
                recv_sem=halo_recv.at[side, peer],
                device_id=(peer, lax.rem(slab + step, count)),
                device_id_type=pl.DeviceIdType.MESH,
            ).wait_recv()
    for half in range(2):
        total_ref[half] = jnp.sum(
            jnp.stack([d_buf[j].astype(jnp.float32) for j in range(half, groups, 2)]), axis=0
        )
        for side in range(2):
            halo_ref[side, half] = jnp.sum(
                jnp.stack([edge_buf[side, j].astype(jnp.float32) for j in range(half, groups, 2)]),
                axis=0,
            )


def reduce_chain(x, stencil, y_rows, side, y_chips, groups, collective_id):
    _, rows, width = x.shape
    band = width // (y_chips * Z_CHIPS)
    wide = 8
    depth = stencil[0].shape[1]
    return pl.pallas_call(
        functools.partial(reduce_chain_kernel, y_chips, groups),
        out_shape=[
            jax.ShapeDtypeStruct((2, rows, band), jnp.float32),
            jax.ShapeDtypeStruct((2, 2, rows, band), jnp.float32),
            jax.ShapeDtypeStruct((y_rows, depth), jnp.bfloat16),
            jax.ShapeDtypeStruct((side, depth), jnp.bfloat16),
        ],
        in_specs=[pl.BlockSpec(memory_space=pltpu.VMEM)] * 3,
        out_specs=[pl.BlockSpec(memory_space=pltpu.VMEM)] * 4,
        scratch_shapes=[
            pltpu.VMEM((2, rows, width), x.dtype),
            pltpu.VMEM((rows, width), jnp.bfloat16),
            pltpu.VMEM((y_chips, rows, width // y_chips), jnp.bfloat16),
            pltpu.VMEM((rows, width // y_chips), jnp.bfloat16),
            pltpu.VMEM((Z_CHIPS, rows, band), jnp.bfloat16),
            pltpu.VMEM((1, rows, band), jnp.bfloat16),
            pltpu.VMEM((groups, rows, band), jnp.bfloat16),
            pltpu.VMEM((2, groups, rows, band), jnp.bfloat16),
            pltpu.SemaphoreType.DMA((4,)),
            pltpu.SemaphoreType.DMA((4, wide)),
            pltpu.SemaphoreType.DMA((4, wide)),
            pltpu.SemaphoreType.DMA((2, groups)),
            pltpu.SemaphoreType.DMA((2, groups)),
        ],
        compiler_params=pltpu.CompilerParams(collective_id=collective_id, has_side_effects=True),
    )(x, *stencil)


def phase_kernel(row_count, half_cols, phase_ref):
    half = phase_ref.shape[1] // 2
    lanes = 128
    blocks = half // lanes
    shifts = phase_ref.shape[0]
    step = 2.0 * math.pi / row_count
    t_b = lax.broadcasted_iota(jnp.int32, (shifts, blocks), 0)
    q_b = lax.broadcasted_iota(jnp.int32, (shifts, blocks), 1)
    shift_rows_b = (t_b // 8 - SHIFTS // 16).astype(jnp.float32)
    block_rows = (q_b * (lanes // half_cols) - row_count // 2).astype(jnp.float32)
    block_angle = shift_rows_b * block_rows * step
    t_l = lax.broadcasted_iota(jnp.int32, (shifts, lanes), 0)
    l_l = lax.broadcasted_iota(jnp.int32, (shifts, lanes), 1)
    shift_rows_l = (t_l // 8 - SHIFTS // 16).astype(jnp.float32)
    shift_cols_l = (t_l % 8 - 4).astype(jnp.float32)
    lane_angle = (
        shift_rows_l * (l_l // half_cols).astype(jnp.float32)
        + shift_cols_l * (l_l % half_cols).astype(jnp.float32)
    ) * step
    cos_b, sin_b = jnp.cos(block_angle), jnp.sin(block_angle)
    c_l, s_l = jnp.cos(lane_angle), jnp.sin(lane_angle)
    for q in range(blocks):
        c_b, s_b = cos_b[:, q : q + 1], sin_b[:, q : q + 1]
        phase_ref[:, q * lanes : (q + 1) * lanes] = (c_b * c_l - s_b * s_l).astype(phase_ref.dtype)
        phase_ref[:, half + q * lanes : half + (q + 1) * lanes] = (s_b * c_l + c_b * s_l).astype(
            phase_ref.dtype
        )


def gather_chain_kernel(y_chips, row_count, half_cols, x_ref, out_ref, phase_ref, z_buf,
                        local_sems, send_sems, recv_sems):
    arrive = signal_all(peers(Z_CHIPS, z_place) + peers(2 * y_chips, column_place))
    phase_kernel(row_count, half_cols, phase_ref)
    arrive()
    run_phase(Z_CHIPS, z_place, whole, x_ref, z_buf, local_sems.at[0], send_sems.at[0], recv_sems.at[0])
    run_phase(2 * y_chips, column_place, entire, z_buf, out_ref,
              local_sems.at[1], send_sems.at[1], recv_sems.at[1])


def gather_chain(x, row_count, half_cols, y_chips, collective_id):
    _, rows, lanes = x.shape
    shifts = SHIFTS
    table = 2 * row_count * half_cols
    return pl.pallas_call(
        functools.partial(gather_chain_kernel, y_chips, row_count, half_cols),
        out_shape=[
            jax.ShapeDtypeStruct((2 * y_chips, Z_CHIPS, rows, lanes), x.dtype),
            jax.ShapeDtypeStruct((shifts, table), jnp.bfloat16),
        ],
        in_specs=[pl.BlockSpec(memory_space=pltpu.VMEM)],
        out_specs=[pl.BlockSpec(memory_space=pltpu.VMEM)] * 2,
        scratch_shapes=[
            pltpu.VMEM((Z_CHIPS, rows, lanes), x.dtype),
            pltpu.SemaphoreType.DMA((2,)),
            pltpu.SemaphoreType.DMA((2, 2 * y_chips)),
            pltpu.SemaphoreType.DMA((2, 2 * y_chips)),
        ],
        compiler_params=pltpu.CompilerParams(collective_id=collective_id, has_side_effects=True),
    )(x)


def align_frames(frames, ctf_rows, ref_re, ref_im, phase, score_scale):
    pixels = ctf_rows.shape[1]
    frame_re = frames[:, :pixels].astype(jnp.float32)
    frame_im = frames[:, pixels:].astype(jnp.float32)
    ref_re = ref_re.astype(jnp.float32)
    ref_im = ref_im.astype(jnp.float32)
    weight = ctf_rows.astype(jnp.float32)
    cross_terms = jnp.concatenate(
        [
            weight * (ref_re * frame_re + ref_im * frame_im),
            weight * (ref_re * frame_im - ref_im * frame_re),
        ],
        axis=1,
    ).astype(jnp.bfloat16)
    scores = score_scale * jnp.einsum(
        "np,sp->ns", cross_terms, phase, preferred_element_type=jnp.float32
    )
    shift_probs = jax.nn.softmax(scores, axis=1).astype(jnp.bfloat16)
    shift_mix = jnp.dot(shift_probs, phase, preferred_element_type=jnp.float32)
    mix_re = shift_mix[:, :pixels]
    mix_im = shift_mix[:, pixels:]
    return (
        weight * (frame_re * mix_re + frame_im * mix_im),
        weight * (frame_im * mix_re - frame_re * mix_im),
    )


def stencil_weights(base_cell, fraction, side_cells):
    cell_ids = jnp.arange(side_cells, dtype=jnp.int32)
    dense_weight = jnp.where(
        cell_ids[None, None, :] == base_cell[:, :, None], (1.0 - fraction)[:, :, None], 0.0
    )
    dense_weight = dense_weight + jnp.where(
        cell_ids[None, None, :] == base_cell[:, :, None] + 1, fraction[:, :, None], 0.0
    )
    return dense_weight.astype(jnp.bfloat16)


def local(
    images,
    image_class,
    image_ctf,
    class_owner,
    references,
    ctf_table,
    x_base,
    y_base,
    x_frac,
    y_frac,
    z_offset,
    z_frac,
):
    slab_count = lax.axis_size("slab")
    group_count = lax.axis_size("grp")
    frame_count = images.shape[0]
    pixels = ctf_table.shape[1]
    groups_ctf = ctf_table.shape[0]
    row_count = z_offset.shape[1]
    half_cols = x_base.shape[1]
    class_count = class_owner.shape[0]
    side_cells = 2 * row_count
    band_rows = row_count // slab_count
    band_pixels = band_rows * half_cols
    z_dev = 2 * band_rows
    score_scale = 2.0 / math.sqrt(2.0 * pixels)
    channel_scale = jnp.array(
        [
            1.0 / math.sqrt(frame_count * group_count),
            1.0 / math.sqrt(frame_count * group_count),
            1.0 / (frame_count * group_count),
        ],
        jnp.float32,
    )
    lanes = 128
    core = lax.rem(lax.axis_index("grp"), 2)
    ref_halves = references.reshape(2, -1, lanes)
    my_half = lax.dynamic_slice_in_dim(ref_halves, core, 1, 0)
    y_chips = slab_count // Z_CHIPS
    gathered, phase = gather_chain(my_half, row_count, half_cols, y_chips, 0)
    both_halves = gathered.reshape(2, slab_count, pixels)
    class_ids = jnp.arange(class_count, dtype=jnp.int32)
    owner_of = jnp.sum(
        jnp.where(image_class[:, None] == class_ids[None, :], class_owner[None, :], 0), axis=1
    )
    pick_ref = (owner_of[:, None] == jnp.arange(slab_count, dtype=jnp.int32)[None, :]).astype(
        jnp.bfloat16
    )
    ref_re = jnp.dot(pick_ref, both_halves[0], preferred_element_type=jnp.float32).astype(
        jnp.bfloat16
    )
    ref_im = jnp.dot(pick_ref, both_halves[1], preferred_element_type=jnp.float32).astype(
        jnp.bfloat16
    )
    pick_ctf = (image_ctf[:, None] == jnp.arange(groups_ctf, dtype=jnp.int32)[None, :]).astype(
        jnp.bfloat16
    )
    ctf_rows = jnp.dot(pick_ctf, ctf_table, preferred_element_type=jnp.float32).astype(
        jnp.bfloat16
    )
    stacked = align_frames(images, ctf_rows, ref_re, ref_im, phase, score_scale)
    member = (class_ids[:, None] == image_class[None, :]).astype(jnp.float32)
    aligned_re, aligned_im = stacked
    partial_re, partial_im = (
        jnp.dot(
            member, part, precision=lax.Precision.HIGHEST, preferred_element_type=jnp.float32
        ) * channel_scale[0]
        for part in (aligned_re, aligned_im)
    )
    half_classes = class_count // 2
    half_rows = half_classes * 2
    class_hits = (class_ids[:, None] == image_class[None, :]).astype(jnp.bfloat16)
    ctf_hits = (image_ctf[:, None] == jnp.arange(groups_ctf, dtype=jnp.int32)[None, :]).astype(
        jnp.bfloat16
    )
    counts = jnp.dot(class_hits, ctf_hits, preferred_element_type=jnp.float32)
    count_rows = class_count * groups_ctf // band_pixels
    tiled_counts = jnp.tile(counts.reshape(count_rows, band_pixels), (1, slab_count))
    rows = half_rows + count_rows
    by_half = jnp.stack(
        [
            jnp.concatenate(
                [
                    partial_re[h * half_classes : (h + 1) * half_classes],
                    partial_im[h * half_classes : (h + 1) * half_classes],
                    tiled_counts,
                ],
                axis=0,
            )
            for h in range(2)
        ]
    ).astype(jnp.bfloat16)
    y_rows = side_cells // group_count
    flat = class_count * half_cols
    stencil = (
        jnp.stack([y_base.reshape(flat), x_base.reshape(flat)]),
        jnp.stack([y_frac.reshape(flat), x_frac.reshape(flat)]),
    )
    total, halo, row_weights, col_weights = reduce_chain(
        by_half, stencil, y_rows, side_cells, slab_count // Z_CHIPS, group_count, 1
    )
    band = total[:, :half_rows].reshape(2, 2, half_classes, band_rows, half_cols)
    band = band.transpose(0, 2, 1, 3, 4).reshape(class_count, 2, band_rows, half_cols)
    total_counts = total[0, half_rows:].reshape(class_count, groups_ctf)
    halo = halo[:, :, :half_rows].reshape(2, 2, 2, half_classes, band_rows, half_cols)
    halo = halo.transpose(0, 1, 3, 2, 4, 5).reshape(2, class_count, 2, band_rows, half_cols)
    slab_index = lax.axis_index("slab")
    from_below = jnp.where(slab_index > 0, halo[0][:, :, band_rows - 1 :], 0.0)
    from_above = jnp.where(slab_index < slab_count - 1, halo[1][:, :, :1], 0.0)
    data_bands = jnp.concatenate([from_below, band, from_above], axis=2)
    slab_index = lax.axis_index("slab")
    ctf_sq = jnp.pad(
        jnp.square(ctf_table.astype(jnp.float32)), ((0, 0), (half_cols, half_cols))
    )
    window = lax.dynamic_slice_in_dim(
        ctf_sq, slab_index * band_pixels, band_pixels + 2 * half_cols, 1
    )
    weight_rows = jnp.dot(
        total_counts, window, precision=lax.Precision.HIGHEST, preferred_element_type=jnp.float32
    ) * channel_scale[2]
    class_bands = jnp.concatenate(
        [data_bands, weight_rows.reshape(class_count, 1, band_rows + 2, half_cols)], axis=1
    )
    group_index = lax.axis_index("grp")
    offset_pad = jnp.pad(z_offset, ((0, 0), (1, 1)))
    frac_pad = jnp.pad(z_frac, ((0, 0), (1, 1)))
    rows_held = band_rows + 2
    local_offset = lax.dynamic_slice_in_dim(offset_pad, slab_index * band_rows, rows_held, 1)
    local_frac = lax.dynamic_slice_in_dim(frac_pad, slab_index * band_rows, rows_held, 1)
    row_ids = jnp.arange(rows_held, dtype=jnp.int32) + (band_rows - 1)
    band_shift = (row_ids // band_rows - 1) * z_dev - 1
    target = 2 * (row_ids % band_rows)[None, :] + local_offset + 1 + band_shift[None, :]
    plane_ids = jnp.arange(z_dev, dtype=jnp.int32)
    depth_weight = jnp.where(
        plane_ids[None, None, :] == target[:, :, None], (1.0 - local_frac)[:, :, None], 0.0
    )
    depth_weight = depth_weight + jnp.where(
        plane_ids[None, None, :] == target[:, :, None] + 1, local_frac[:, :, None], 0.0
    )
    sectioned = jnp.einsum(
        "ckra,crz->kzca",
        class_bands,
        depth_weight,
        precision=lax.Precision.HIGHEST,
    ).reshape(3 * z_dev, class_count * half_cols)
    inserted = insert_planes(row_weights, sectioned, col_weights)
    return inserted.reshape(3, z_dev, y_rows, side_cells)


def insert_kernel(rows_ref, sec_ref, cols_ref, out_ref, lifted_ref):
    y_rows = rows_ref.shape[0]

    def body(i, carry):
        start = pl.multiple_of(i * y_rows, y_rows)
        lifted_ref[pl.ds(start, y_rows), :] = (
            rows_ref[...].astype(jnp.float32) * sec_ref[pl.ds(i, 1), :]
        ).astype(jnp.bfloat16)
        return carry

    lax.fori_loop(0, sec_ref.shape[0], body, 0)
    out_ref[...] = lax.dot_general(
        lifted_ref[...], cols_ref[...], (((1,), (1,)), ((), ())), preferred_element_type=jnp.float32
    )


def insert_planes(row_weights, sectioned, col_weights):
    planes = sectioned.shape[0]
    y_rows, depth = row_weights.shape
    side = col_weights.shape[0]
    return pl.pallas_call(
        insert_kernel,
        out_shape=jax.ShapeDtypeStruct((planes * y_rows, side), jnp.float32),
        in_specs=[pl.BlockSpec(memory_space=pltpu.VMEM)] * 3,
        out_specs=pl.BlockSpec(memory_space=pltpu.VMEM),
        scratch_shapes=[pltpu.VMEM((planes * y_rows, depth), jnp.bfloat16)],
        cost_estimate=pl.CostEstimate(
            flops=2 * planes * y_rows * depth * side,
            transcendentals=0,
            bytes_accessed=2 * y_rows * depth + 4 * planes * depth + 2 * depth * side
            + 4 * planes * y_rows * side,
        ),
    )(row_weights, sectioned, col_weights)


def solution(mesh):
    in_specs = (
        P(("grp", "slab"), None),
        P(("grp", "slab")),
        P(("grp", "slab")),
        P(),
        P("slab", None),
        P(),
        P(),
        P(),
        P(),
        P(),
        P(),
        P(),
    )
    out_specs = P(None, "slab", "grp", None)
    return jax.shard_map(local, mesh=mesh, in_specs=in_specs, out_specs=out_specs, check_vma=False)
```

```python
import functools
import math

import jax
import jax.numpy as jnp
from jax import lax
from jax.experimental import pallas as pl
from jax.experimental.pallas import tpu as pltpu
from jax.sharding import PartitionSpec as P

SHIFTS = 128
Z_CHIPS = 8


def exchange_kernel(count, place, picks, *refs):
    parts = len(picks)
    x_refs, out_refs = refs[:parts], refs[parts : 2 * parts]
    local_sems, send_sems, recv_sems = refs[2 * parts :]
    me, device = place()
    barrier = pltpu.get_barrier_semaphore()
    for k in range(1, count):
        pl.semaphore_signal(
            barrier,
            1,
            device_id=device(lax.rem(me + k, count)),
            device_id_type=pl.DeviceIdType.MESH,
        )
    pl.semaphore_wait(barrier, count - 1)
    owns, copies = [], []
    for part, (pick, x_ref, out_ref) in enumerate(zip(picks, x_refs, out_refs)):
        own = pltpu.make_async_copy(pick(x_ref, me), out_ref.at[me], local_sems.at[part])
        own.start()
        owns.append(own)
        for k in range(1, count):
            peer = lax.rem(me + k, count)
            copy = pltpu.make_async_remote_copy(
                src_ref=pick(x_ref, peer),
                dst_ref=out_ref.at[me],
                send_sem=send_sems.at[part, k],
                recv_sem=recv_sems.at[part, k],
                device_id=device(peer),
                device_id_type=pl.DeviceIdType.MESH,
            )
            copy.start()
            copies.append(copy)
    for own in owns:
        own.wait()
    for copy in copies:
        copy.wait_send()
        copy.wait_recv()


def slab_place():
    group = lax.axis_index("grp")
    return lax.axis_index("slab"), lambda peer: (group, peer)


def core_place():
    group, slab = lax.axis_index("grp"), lax.axis_index("slab")
    return lax.rem(group, 2), lambda peer: (group - lax.rem(group, 2) + peer, slab)


def z_place():
    group, slab = lax.axis_index("grp"), lax.axis_index("slab")
    z = lax.rem(slab, Z_CHIPS)
    return z, lambda peer: (group, slab - z + peer)


def y_place():
    group, slab = lax.axis_index("grp"), lax.axis_index("slab")
    z = lax.rem(slab, Z_CHIPS)
    return slab // Z_CHIPS, lambda peer: (group, peer * Z_CHIPS + z)


def group_place():
    slab = lax.axis_index("slab")
    return lax.axis_index("grp"), lambda peer: (peer, slab)


def whole(x_ref, peer):
    return x_ref.at[0]


def entire(x_ref, peer):
    return x_ref


def row_block(x_ref, peer):
    return x_ref.at[peer]


def lane_blocks(count):
    def pick(x_ref, peer):
        width = x_ref.shape[1] // count
        return x_ref.at[:, pl.ds(pl.multiple_of(peer * width, width), width)]

    return pick


def exchange_many(xs, count, place, picks, collective_id, block_shapes):
    parts = len(xs)
    return pl.pallas_call(
        functools.partial(exchange_kernel, count, place, tuple(picks)),
        out_shape=[
            jax.ShapeDtypeStruct((count,) + shape, x.dtype) for x, shape in zip(xs, block_shapes)
        ],
        in_specs=[pl.BlockSpec(memory_space=pltpu.VMEM)] * parts,
        out_specs=[pl.BlockSpec(memory_space=pltpu.VMEM)] * parts,
        scratch_shapes=[
            pltpu.SemaphoreType.DMA((parts,)),
            pltpu.SemaphoreType.DMA((parts, count)),
            pltpu.SemaphoreType.DMA((parts, count)),
        ],
        compiler_params=pltpu.CompilerParams(collective_id=collective_id, has_side_effects=True),
    )(*xs)


def exchange(x, count, place, pick, collective_id, block_shape):
    return exchange_many([x], count, place, [pick], collective_id, [block_shape])[0]


def signal_all(devices):
    barrier = pltpu.get_barrier_semaphore()
    for device in devices:
        pl.semaphore_signal(barrier, 1, device_id=device, device_id_type=pl.DeviceIdType.MESH)
    return lambda: pl.semaphore_wait(barrier, len(devices))


def run_phase(count, place, pick, x_ref, out_ref, local_sem, send_sems, recv_sems):
    me, device = place()
    own = pltpu.make_async_copy(pick(x_ref, me), out_ref.at[me], local_sem)
    own.start()
    copies = []
    for k in range(1, count):
        peer = lax.rem(me + k, count)
        copy = pltpu.make_async_remote_copy(
            src_ref=pick(x_ref, peer),
            dst_ref=out_ref.at[me],
            send_sem=send_sems.at[k],
            recv_sem=recv_sems.at[k],
            device_id=device(peer),
            device_id_type=pl.DeviceIdType.MESH,
        )
        copy.start()
        copies.append(copy)
    own.wait()
    for copy in copies:
        copy.wait_send()
        copy.wait_recv()


def peers(count, place):
    me, device = place()
    return [device(lax.rem(me + k, count)) for k in range(1, count)]


def stencil_kernel(base_ref, frac_ref, rows_ref, cols_ref):
    y_rows = rows_ref.shape[0]
    y_ids = lax.axis_index("grp") * y_rows + lax.broadcasted_iota(jnp.int32, rows_ref.shape, 0)
    y_base, y_frac = base_ref[0:1, :], frac_ref[0:1, :]
    rows = jnp.where(y_ids == y_base, 1.0 - y_frac, 0.0) + jnp.where(y_ids == y_base + 1, y_frac, 0.0)
    rows_ref[...] = rows.astype(rows_ref.dtype)
    x_ids = lax.broadcasted_iota(jnp.int32, cols_ref.shape, 0)
    x_base, x_frac = base_ref[1:2, :], frac_ref[1:2, :]
    cols = jnp.where(x_ids == x_base, 1.0 - x_frac, 0.0) + jnp.where(x_ids == x_base + 1, x_frac, 0.0)
    cols_ref[...] = cols.astype(cols_ref.dtype)


def neighbour_place(groups):
    slab = lax.axis_index("slab")
    count = lax.axis_size("slab")
    return [
        (peer, lax.rem(slab + step, count))
        for step in (1, count - 1)
        for peer in range(groups)
    ]


def reduce_chain_kernel(y_chips, groups, x_ref, base_ref, frac_ref,
                        total_ref, halo_ref, rows_ref, cols_ref, core_buf, y_src, y_buf, z_src, z_buf,
                        d_src, d_buf, edge_buf, local_sems, send_sems, recv_sems, halo_send, halo_recv,
                        core_local, core_send, core_recv):
    arrive = signal_all(
        peers(2, core_place)
        + peers(y_chips, y_place)
        + peers(Z_CHIPS, z_place)
        + peers(groups, group_place)
        + neighbour_place(groups)
    )
    stencil_kernel(base_ref, frac_ref, rows_ref, cols_ref)
    arrive()
    me_c, core_device = core_place()
    sibling = 1 - me_c
    me_y, y_device = y_place()
    width = x_ref.shape[2] // y_chips

    def window(w):
        return pl.ds(pl.multiple_of(w * width, width), width)

    def core_copies(w):
        own = pltpu.make_async_copy(
            x_ref.at[me_c, :, window(w)], core_buf.at[me_c, :, window(w)], core_local.at[w]
        )
        far = pltpu.make_async_remote_copy(
            src_ref=x_ref.at[sibling, :, window(w)],
            dst_ref=core_buf.at[me_c, :, window(w)],
            send_sem=core_send.at[w],
            recv_sem=core_recv.at[w],
            device_id=core_device(sibling),
            device_id_type=pl.DeviceIdType.MESH,
        )
        return own, far

    for w in range(y_chips):
        for copy in core_copies(w):
            copy.start()
    y_copies = []
    for k in range(y_chips):
        w = lax.rem(me_y + k, y_chips)
        own, far = core_copies(w)
        own.wait()
        far.wait_send()
        far.wait_recv()
        y_src[:, window(w)] = (
            core_buf[0, :, window(w)].astype(jnp.float32) + core_buf[1, :, window(w)].astype(jnp.float32)
        ).astype(y_src.dtype)
        if k == 0:
            copy = pltpu.make_async_copy(y_src.at[:, window(w)], y_buf.at[me_y], local_sems.at[1])
        else:
            copy = pltpu.make_async_remote_copy(
                src_ref=y_src.at[:, window(w)],
                dst_ref=y_buf.at[me_y],
                send_sem=send_sems.at[1, k],
                recv_sem=recv_sems.at[1, k],
                device_id=y_device(w),
                device_id_type=pl.DeviceIdType.MESH,
            )
        copy.start()
        y_copies.append(copy)
    y_copies[0].wait()
    for copy in y_copies[1:]:
        copy.wait_send()
        copy.wait_recv()
    z_src[...] = jnp.sum(y_buf[...].astype(jnp.float32), axis=0).astype(z_src.dtype)
    run_phase(
        Z_CHIPS, z_place, lane_blocks(Z_CHIPS), z_src, z_buf,
        local_sems.at[2], send_sems.at[2], recv_sems.at[2],
    )
    d_src[0] = jnp.sum(z_buf[...].astype(jnp.float32), axis=0).astype(d_src.dtype)
    group = lax.axis_index("grp")
    edge_copies = []
    for index, device in enumerate(neighbour_place(groups)):
        side, peer = divmod(index, groups)
        copy = pltpu.make_async_remote_copy(
            src_ref=d_src.at[0],
            dst_ref=edge_buf.at[side, group],
            send_sem=halo_send.at[side, peer],
            recv_sem=halo_recv.at[side, group],
            device_id=device,
            device_id_type=pl.DeviceIdType.MESH,
        )
        copy.start()
        edge_copies.append(copy)
    run_phase(groups, group_place, whole, d_src, d_buf, local_sems.at[3], send_sems.at[3], recv_sems.at[3])
    for copy in edge_copies:
        copy.wait_send()
    slab, count = lax.axis_index("slab"), lax.axis_size("slab")
    for side, step in enumerate((count - 1, 1)):
        for peer in range(groups):
            pltpu.make_async_remote_copy(
                src_ref=d_src.at[0],
                dst_ref=edge_buf.at[side, peer],
                send_sem=halo_send.at[side, peer],
                recv_sem=halo_recv.at[side, peer],
                device_id=(peer, lax.rem(slab + step, count)),
                device_id_type=pl.DeviceIdType.MESH,
            ).wait_recv()
    for half in range(2):
        total_ref[half] = jnp.sum(
            jnp.stack([d_buf[j].astype(jnp.float32) for j in range(half, groups, 2)]), axis=0
        )
        for side in range(2):
            halo_ref[side, half] = jnp.sum(
                jnp.stack([edge_buf[side, j].astype(jnp.float32) for j in range(half, groups, 2)]),
                axis=0,
            )


def reduce_chain(x, stencil, y_rows, side, y_chips, groups, collective_id):
    _, rows, width = x.shape
    band = width // (y_chips * Z_CHIPS)
    wide = 8
    depth = stencil[0].shape[1]
    return pl.pallas_call(
        functools.partial(reduce_chain_kernel, y_chips, groups),
        out_shape=[
            jax.ShapeDtypeStruct((2, rows, band), jnp.float32),
            jax.ShapeDtypeStruct((2, 2, rows, band), jnp.float32),
            jax.ShapeDtypeStruct((y_rows, depth), jnp.bfloat16),
            jax.ShapeDtypeStruct((side, depth), jnp.bfloat16),
        ],
        in_specs=[pl.BlockSpec(memory_space=pltpu.VMEM)] * 3,
        out_specs=[pl.BlockSpec(memory_space=pltpu.VMEM)] * 4,
        scratch_shapes=[
            pltpu.VMEM((2, rows, width), x.dtype),
            pltpu.VMEM((rows, width), jnp.bfloat16),
            pltpu.VMEM((y_chips, rows, width // y_chips), jnp.bfloat16),
            pltpu.VMEM((rows, width // y_chips), jnp.bfloat16),
            pltpu.VMEM((Z_CHIPS, rows, band), jnp.bfloat16),
            pltpu.VMEM((1, rows, band), jnp.bfloat16),
            pltpu.VMEM((groups, rows, band), jnp.bfloat16),
            pltpu.VMEM((2, groups, rows, band), jnp.bfloat16),
            pltpu.SemaphoreType.DMA((4,)),
            pltpu.SemaphoreType.DMA((4, wide)),
            pltpu.SemaphoreType.DMA((4, wide)),
            pltpu.SemaphoreType.DMA((2, groups)),
            pltpu.SemaphoreType.DMA((2, groups)),
            pltpu.SemaphoreType.DMA((y_chips,)),
            pltpu.SemaphoreType.DMA((y_chips,)),
            pltpu.SemaphoreType.DMA((y_chips,)),
        ],
        compiler_params=pltpu.CompilerParams(collective_id=collective_id, has_side_effects=True),
    )(x, *stencil)


def phase_kernel(row_count, half_cols, phase_ref):
    half = phase_ref.shape[1] // 2
    lanes = 128
    blocks = half // lanes
    shifts = phase_ref.shape[0]
    step = 2.0 * math.pi / row_count
    t_b = lax.broadcasted_iota(jnp.int32, (shifts, blocks), 0)
    q_b = lax.broadcasted_iota(jnp.int32, (shifts, blocks), 1)
    shift_rows_b = (t_b // 8 - SHIFTS // 16).astype(jnp.float32)
    block_rows = (q_b * (lanes // half_cols) - row_count // 2).astype(jnp.float32)
    block_angle = shift_rows_b * block_rows * step
    t_l = lax.broadcasted_iota(jnp.int32, (shifts, lanes), 0)
    l_l = lax.broadcasted_iota(jnp.int32, (shifts, lanes), 1)
    shift_rows_l = (t_l // 8 - SHIFTS // 16).astype(jnp.float32)
    shift_cols_l = (t_l % 8 - 4).astype(jnp.float32)
    lane_angle = (
        shift_rows_l * (l_l // half_cols).astype(jnp.float32)
        + shift_cols_l * (l_l % half_cols).astype(jnp.float32)
    ) * step
    cos_b, sin_b = jnp.cos(block_angle), jnp.sin(block_angle)
    c_l, s_l = jnp.cos(lane_angle), jnp.sin(lane_angle)
    for q in range(blocks):
        c_b, s_b = cos_b[:, q : q + 1], sin_b[:, q : q + 1]
        phase_ref[:, q * lanes : (q + 1) * lanes] = (c_b * c_l - s_b * s_l).astype(phase_ref.dtype)
        phase_ref[:, half + q * lanes : half + (q + 1) * lanes] = (s_b * c_l + c_b * s_l).astype(
            phase_ref.dtype
        )


def gather_chain_kernel(y_chips, row_count, half_cols, x_ref, out_ref, phase_ref, z_buf, y_buf,
                        local_sems, send_sems, recv_sems):
    arrive = signal_all(peers(Z_CHIPS, z_place) + peers(y_chips, y_place) + peers(2, core_place))
    phase_kernel(row_count, half_cols, phase_ref)
    arrive()
    run_phase(Z_CHIPS, z_place, whole, x_ref, z_buf, local_sems.at[0], send_sems.at[0], recv_sems.at[0])
    run_phase(y_chips, y_place, entire, z_buf, y_buf, local_sems.at[1], send_sems.at[1], recv_sems.at[1])
    run_phase(2, core_place, entire, y_buf, out_ref, local_sems.at[2], send_sems.at[2], recv_sems.at[2])


def gather_chain(x, row_count, half_cols, y_chips, collective_id):
    _, rows, lanes = x.shape
    shifts = SHIFTS
    table = 2 * row_count * half_cols
    return pl.pallas_call(
        functools.partial(gather_chain_kernel, y_chips, row_count, half_cols),
        out_shape=[
            jax.ShapeDtypeStruct((2, y_chips, Z_CHIPS, rows, lanes), x.dtype),
            jax.ShapeDtypeStruct((shifts, table), jnp.bfloat16),
        ],
        in_specs=[pl.BlockSpec(memory_space=pltpu.VMEM)],
        out_specs=[pl.BlockSpec(memory_space=pltpu.VMEM)] * 2,
        scratch_shapes=[
            pltpu.VMEM((Z_CHIPS, rows, lanes), x.dtype),
            pltpu.VMEM((y_chips, Z_CHIPS, rows, lanes), x.dtype),
            pltpu.SemaphoreType.DMA((3,)),
            pltpu.SemaphoreType.DMA((3, Z_CHIPS)),
            pltpu.SemaphoreType.DMA((3, Z_CHIPS)),
        ],
        compiler_params=pltpu.CompilerParams(collective_id=collective_id, has_side_effects=True),
    )(x)


def align_frames(frames, ctf_rows, ref_re, ref_im, phase, score_scale):
    pixels = ctf_rows.shape[1]
    frame_re = frames[:, :pixels].astype(jnp.float32)
    frame_im = frames[:, pixels:].astype(jnp.float32)
    ref_re = ref_re.astype(jnp.float32)
    ref_im = ref_im.astype(jnp.float32)
    weight = ctf_rows.astype(jnp.float32)
    cross_terms = jnp.concatenate(
        [
            weight * (ref_re * frame_re + ref_im * frame_im),
            weight * (ref_re * frame_im - ref_im * frame_re),
        ],
        axis=1,
    ).astype(jnp.bfloat16)
    scores = score_scale * jnp.einsum(
        "np,sp->ns", cross_terms, phase, preferred_element_type=jnp.float32
    )
    shift_probs = jax.nn.softmax(scores, axis=1).astype(jnp.bfloat16)
    shift_mix = jnp.dot(shift_probs, phase, preferred_element_type=jnp.float32)
    mix_re = shift_mix[:, :pixels]
    mix_im = shift_mix[:, pixels:]
    return (
        weight * (frame_re * mix_re + frame_im * mix_im),
        weight * (frame_im * mix_re - frame_re * mix_im),
    )


def stencil_weights(base_cell, fraction, side_cells):
    cell_ids = jnp.arange(side_cells, dtype=jnp.int32)
    dense_weight = jnp.where(
        cell_ids[None, None, :] == base_cell[:, :, None], (1.0 - fraction)[:, :, None], 0.0
    )
    dense_weight = dense_weight + jnp.where(
        cell_ids[None, None, :] == base_cell[:, :, None] + 1, fraction[:, :, None], 0.0
    )
    return dense_weight.astype(jnp.bfloat16)


def local(
    images,
    image_class,
    image_ctf,
    class_owner,
    references,
    ctf_table,
    x_base,
    y_base,
    x_frac,
    y_frac,
    z_offset,
    z_frac,
):
    slab_count = lax.axis_size("slab")
    group_count = lax.axis_size("grp")
    frame_count = images.shape[0]
    pixels = ctf_table.shape[1]
    groups_ctf = ctf_table.shape[0]
    row_count = z_offset.shape[1]
    half_cols = x_base.shape[1]
    class_count = class_owner.shape[0]
    side_cells = 2 * row_count
    band_rows = row_count // slab_count
    band_pixels = band_rows * half_cols
    z_dev = 2 * band_rows
    score_scale = 2.0 / math.sqrt(2.0 * pixels)
    channel_scale = jnp.array(
        [
            1.0 / math.sqrt(frame_count * group_count),
            1.0 / math.sqrt(frame_count * group_count),
            1.0 / (frame_count * group_count),
        ],
        jnp.float32,
    )
    lanes = 128
    core = lax.rem(lax.axis_index("grp"), 2)
    ref_halves = references.reshape(2, -1, lanes)
    my_half = lax.dynamic_slice_in_dim(ref_halves, core, 1, 0)
    y_chips = slab_count // Z_CHIPS
    gathered, phase = gather_chain(my_half, row_count, half_cols, y_chips, 0)
    both_halves = gathered.reshape(2, slab_count, pixels)
    class_ids = jnp.arange(class_count, dtype=jnp.int32)
    owner_of = jnp.sum(
        jnp.where(image_class[:, None] == class_ids[None, :], class_owner[None, :], 0), axis=1
    )
    pick_ref = (owner_of[:, None] == jnp.arange(slab_count, dtype=jnp.int32)[None, :]).astype(
        jnp.bfloat16
    )
    ref_re = jnp.dot(pick_ref, both_halves[0], preferred_element_type=jnp.float32).astype(
        jnp.bfloat16
    )
    ref_im = jnp.dot(pick_ref, both_halves[1], preferred_element_type=jnp.float32).astype(
        jnp.bfloat16
    )
    pick_ctf = (image_ctf[:, None] == jnp.arange(groups_ctf, dtype=jnp.int32)[None, :]).astype(
        jnp.bfloat16
    )
    ctf_rows = jnp.dot(pick_ctf, ctf_table, preferred_element_type=jnp.float32).astype(
        jnp.bfloat16
    )
    stacked = align_frames(images, ctf_rows, ref_re, ref_im, phase, score_scale)
    member = (class_ids[:, None] == image_class[None, :]).astype(jnp.float32)
    aligned_re, aligned_im = stacked
    partial_re, partial_im = (
        jnp.dot(
            member, part, precision=lax.Precision.HIGHEST, preferred_element_type=jnp.float32
        ) * channel_scale[0]
        for part in (aligned_re, aligned_im)
    )
    half_classes = class_count // 2
    half_rows = half_classes * 2
    class_hits = (class_ids[:, None] == image_class[None, :]).astype(jnp.bfloat16)
    ctf_hits = (image_ctf[:, None] == jnp.arange(groups_ctf, dtype=jnp.int32)[None, :]).astype(
        jnp.bfloat16
    )
    counts = jnp.dot(class_hits, ctf_hits, preferred_element_type=jnp.float32)
    count_rows = class_count * groups_ctf // band_pixels
    tiled_counts = jnp.tile(counts.reshape(count_rows, band_pixels), (1, slab_count))
    rows = half_rows + count_rows
    by_half = jnp.stack(
        [
            jnp.concatenate(
                [
                    partial_re[h * half_classes : (h + 1) * half_classes],
                    partial_im[h * half_classes : (h + 1) * half_classes],
                    tiled_counts,
                ],
                axis=0,
            )
            for h in range(2)
        ]
    ).astype(jnp.bfloat16)
    y_rows = side_cells // group_count
    flat = class_count * half_cols
    stencil = (
        jnp.stack([y_base.reshape(flat), x_base.reshape(flat)]),
        jnp.stack([y_frac.reshape(flat), x_frac.reshape(flat)]),
    )
    total, halo, row_weights, col_weights = reduce_chain(
        by_half, stencil, y_rows, side_cells, slab_count // Z_CHIPS, group_count, 1
    )
    band = total[:, :half_rows].reshape(2, 2, half_classes, band_rows, half_cols)
    band = band.transpose(0, 2, 1, 3, 4).reshape(class_count, 2, band_rows, half_cols)
    total_counts = total[0, half_rows:].reshape(class_count, groups_ctf)
    halo = halo[:, :, :half_rows].reshape(2, 2, 2, half_classes, band_rows, half_cols)
    halo = halo.transpose(0, 1, 3, 2, 4, 5).reshape(2, class_count, 2, band_rows, half_cols)
    slab_index = lax.axis_index("slab")
    from_below = jnp.where(slab_index > 0, halo[0][:, :, band_rows - 1 :], 0.0)
    from_above = jnp.where(slab_index < slab_count - 1, halo[1][:, :, :1], 0.0)
    data_bands = jnp.concatenate([from_below, band, from_above], axis=2)
    slab_index = lax.axis_index("slab")
    ctf_sq = jnp.pad(
        jnp.square(ctf_table.astype(jnp.float32)), ((0, 0), (half_cols, half_cols))
    )
    window = lax.dynamic_slice_in_dim(
        ctf_sq, slab_index * band_pixels, band_pixels + 2 * half_cols, 1
    )
    weight_rows = jnp.dot(
        total_counts, window, precision=lax.Precision.HIGHEST, preferred_element_type=jnp.float32
    ) * channel_scale[2]
    class_bands = jnp.concatenate(
        [data_bands, weight_rows.reshape(class_count, 1, band_rows + 2, half_cols)], axis=1
    )
    group_index = lax.axis_index("grp")
    offset_pad = jnp.pad(z_offset, ((0, 0), (1, 1)))
    frac_pad = jnp.pad(z_frac, ((0, 0), (1, 1)))
    rows_held = band_rows + 2
    local_offset = lax.dynamic_slice_in_dim(offset_pad, slab_index * band_rows, rows_held, 1)
    local_frac = lax.dynamic_slice_in_dim(frac_pad, slab_index * band_rows, rows_held, 1)
    row_ids = jnp.arange(rows_held, dtype=jnp.int32) + (band_rows - 1)
    band_shift = (row_ids // band_rows - 1) * z_dev - 1
    target = 2 * (row_ids % band_rows)[None, :] + local_offset + 1 + band_shift[None, :]
    plane_ids = jnp.arange(z_dev, dtype=jnp.int32)
    depth_weight = jnp.where(
        plane_ids[None, None, :] == target[:, :, None], (1.0 - local_frac)[:, :, None], 0.0
    )
    depth_weight = depth_weight + jnp.where(
        plane_ids[None, None, :] == target[:, :, None] + 1, local_frac[:, :, None], 0.0
    )
    sectioned = jnp.einsum(
        "ckra,crz->kzca",
        class_bands,
        depth_weight,
        precision=lax.Precision.HIGHEST,
    ).reshape(3 * z_dev, class_count * half_cols)
    inserted = insert_planes(row_weights, sectioned, col_weights)
    return inserted.reshape(3, z_dev, y_rows, side_cells)


def insert_kernel(rows_ref, sec_ref, cols_ref, out_ref, lifted_ref):
    y_rows = rows_ref.shape[0]

    def body(i, carry):
        start = pl.multiple_of(i * y_rows, y_rows)
        lifted_ref[pl.ds(start, y_rows), :] = (
            rows_ref[...].astype(jnp.float32) * sec_ref[pl.ds(i, 1), :]
        ).astype(jnp.bfloat16)
        return carry

    lax.fori_loop(0, sec_ref.shape[0], body, 0)
    out_ref[...] = lax.dot_general(
        lifted_ref[...], cols_ref[...], (((1,), (1,)), ((), ())), preferred_element_type=jnp.float32
    )


def insert_planes(row_weights, sectioned, col_weights):
    planes = sectioned.shape[0]
    y_rows, depth = row_weights.shape
    side = col_weights.shape[0]
    return pl.pallas_call(
        insert_kernel,
        out_shape=jax.ShapeDtypeStruct((planes * y_rows, side), jnp.float32),
        in_specs=[pl.BlockSpec(memory_space=pltpu.VMEM)] * 3,
        out_specs=pl.BlockSpec(memory_space=pltpu.VMEM),
        scratch_shapes=[pltpu.VMEM((planes * y_rows, depth), jnp.bfloat16)],
        cost_estimate=pl.CostEstimate(
            flops=2 * planes * y_rows * depth * side,
            transcendentals=0,
            bytes_accessed=2 * y_rows * depth + 4 * planes * depth + 2 * depth * side
            + 4 * planes * y_rows * side,
        ),
    )(row_weights, sectioned, col_weights)


def solution(mesh):
    in_specs = (
        P(("grp", "slab"), None),
        P(("grp", "slab")),
        P(("grp", "slab")),
        P(),
        P("slab", None),
        P(),
        P(),
        P(),
        P(),
        P(),
        P(),
        P(),
    )
    out_specs = P(None, "slab", "grp", None)
    return jax.shard_map(local, mesh=mesh, in_specs=in_specs, out_specs=out_specs, check_vma=False)
```

```python
import functools
import math

import jax
import jax.numpy as jnp
from jax import lax
from jax.experimental import pallas as pl
from jax.experimental.pallas import tpu as pltpu
from jax.sharding import PartitionSpec as P

SHIFTS = 128
Z_CHIPS = 8


def exchange_kernel(count, place, picks, *refs):
    parts = len(picks)
    x_refs, out_refs = refs[:parts], refs[parts : 2 * parts]
    local_sems, send_sems, recv_sems = refs[2 * parts :]
    me, device = place()
    barrier = pltpu.get_barrier_semaphore()
    for k in range(1, count):
        pl.semaphore_signal(
            barrier,
            1,
            device_id=device(lax.rem(me + k, count)),
            device_id_type=pl.DeviceIdType.MESH,
        )
    pl.semaphore_wait(barrier, count - 1)
    owns, copies = [], []
    for part, (pick, x_ref, out_ref) in enumerate(zip(picks, x_refs, out_refs)):
        own = pltpu.make_async_copy(pick(x_ref, me), out_ref.at[me], local_sems.at[part])
        own.start()
        owns.append(own)
        for k in range(1, count):
            peer = lax.rem(me + k, count)
            copy = pltpu.make_async_remote_copy(
                src_ref=pick(x_ref, peer),
                dst_ref=out_ref.at[me],
                send_sem=send_sems.at[part, k],
                recv_sem=recv_sems.at[part, k],
                device_id=device(peer),
                device_id_type=pl.DeviceIdType.MESH,
            )
            copy.start()
            copies.append(copy)
    for own in owns:
        own.wait()
    for copy in copies:
        copy.wait_send()
        copy.wait_recv()


def slab_place():
    group = lax.axis_index("grp")
    return lax.axis_index("slab"), lambda peer: (group, peer)


def core_place():
    group, slab = lax.axis_index("grp"), lax.axis_index("slab")
    return lax.rem(group, 2), lambda peer: (group - lax.rem(group, 2) + peer, slab)


def z_place():
    group, slab = lax.axis_index("grp"), lax.axis_index("slab")
    z = lax.rem(slab, Z_CHIPS)
    return z, lambda peer: (group, slab - z + peer)


def y_place():
    group, slab = lax.axis_index("grp"), lax.axis_index("slab")
    z = lax.rem(slab, Z_CHIPS)
    return slab // Z_CHIPS, lambda peer: (group, peer * Z_CHIPS + z)


def group_place():
    slab = lax.axis_index("slab")
    return lax.axis_index("grp"), lambda peer: (peer, slab)


def whole(x_ref, peer):
    return x_ref.at[0]


def entire(x_ref, peer):
    return x_ref


def row_block(x_ref, peer):
    return x_ref.at[peer]


def lane_blocks(count):
    def pick(x_ref, peer):
        width = x_ref.shape[1] // count
        return x_ref.at[:, pl.ds(pl.multiple_of(peer * width, width), width)]

    return pick


def exchange_many(xs, count, place, picks, collective_id, block_shapes):
    parts = len(xs)
    return pl.pallas_call(
        functools.partial(exchange_kernel, count, place, tuple(picks)),
        out_shape=[
            jax.ShapeDtypeStruct((count,) + shape, x.dtype) for x, shape in zip(xs, block_shapes)
        ],
        in_specs=[pl.BlockSpec(memory_space=pltpu.VMEM)] * parts,
        out_specs=[pl.BlockSpec(memory_space=pltpu.VMEM)] * parts,
        scratch_shapes=[
            pltpu.SemaphoreType.DMA((parts,)),
            pltpu.SemaphoreType.DMA((parts, count)),
            pltpu.SemaphoreType.DMA((parts, count)),
        ],
        compiler_params=pltpu.CompilerParams(collective_id=collective_id, has_side_effects=True),
    )(*xs)


def exchange(x, count, place, pick, collective_id, block_shape):
    return exchange_many([x], count, place, [pick], collective_id, [block_shape])[0]


def signal_all(devices):
    barrier = pltpu.get_barrier_semaphore()
    for device in devices:
        pl.semaphore_signal(barrier, 1, device_id=device, device_id_type=pl.DeviceIdType.MESH)
    return lambda: pl.semaphore_wait(barrier, len(devices))


def run_phase(count, place, pick, x_ref, out_ref, local_sem, send_sems, recv_sems):
    me, device = place()
    own = pltpu.make_async_copy(pick(x_ref, me), out_ref.at[me], local_sem)
    own.start()
    copies = []
    for k in range(1, count):
        peer = lax.rem(me + k, count)
        copy = pltpu.make_async_remote_copy(
            src_ref=pick(x_ref, peer),
            dst_ref=out_ref.at[me],
            send_sem=send_sems.at[k],
            recv_sem=recv_sems.at[k],
            device_id=device(peer),
            device_id_type=pl.DeviceIdType.MESH,
        )
        copy.start()
        copies.append(copy)
    own.wait()
    for copy in copies:
        copy.wait_send()
        copy.wait_recv()


def peers(count, place):
    me, device = place()
    return [device(lax.rem(me + k, count)) for k in range(1, count)]


def stencil_kernel(base_ref, frac_ref, rows_ref, cols_ref):
    y_rows = rows_ref.shape[0]
    y_ids = lax.axis_index("grp") * y_rows + lax.broadcasted_iota(jnp.int32, rows_ref.shape, 0)
    y_base, y_frac = base_ref[0:1, :], frac_ref[0:1, :]
    rows = jnp.where(y_ids == y_base, 1.0 - y_frac, 0.0) + jnp.where(y_ids == y_base + 1, y_frac, 0.0)
    rows_ref[...] = rows.astype(rows_ref.dtype)
    x_ids = lax.broadcasted_iota(jnp.int32, cols_ref.shape, 0)
    x_base, x_frac = base_ref[1:2, :], frac_ref[1:2, :]
    cols = jnp.where(x_ids == x_base, 1.0 - x_frac, 0.0) + jnp.where(x_ids == x_base + 1, x_frac, 0.0)
    cols_ref[...] = cols.astype(cols_ref.dtype)


def neighbour_place(groups):
    slab = lax.axis_index("slab")
    count = lax.axis_size("slab")
    return [
        (peer, lax.rem(slab + step, count))
        for step in (1, count - 1)
        for peer in range(groups)
    ]


def reduce_chain_kernel(y_chips, groups, x_ref, base_ref, frac_ref,
                        total_ref, halo_ref, rows_ref, cols_ref, core_buf, y_src, y_buf, z_src, z_buf,
                        d_src, d_buf, edge_buf, local_sems, send_sems, recv_sems, halo_send, halo_recv,
                        core_local, core_send, core_recv):
    arrive = signal_all(
        peers(2, core_place)
        + peers(y_chips, y_place)
        + peers(Z_CHIPS, z_place)
        + peers(groups, group_place)
        + neighbour_place(groups)
    )
    stencil_kernel(base_ref, frac_ref, rows_ref, cols_ref)
    arrive()
    me_c, core_device = core_place()
    sibling = 1 - me_c
    me_y, y_device = y_place()
    width = x_ref.shape[2] // y_chips

    def window(w):
        return pl.ds(pl.multiple_of(w * width, width), width)

    def core_copies(w):
        own = pltpu.make_async_copy(
            x_ref.at[me_c, :, window(w)], core_buf.at[me_c, :, window(w)], core_local.at[w]
        )
        far = pltpu.make_async_remote_copy(
            src_ref=x_ref.at[sibling, :, window(w)],
            dst_ref=core_buf.at[me_c, :, window(w)],
            send_sem=core_send.at[w],
            recv_sem=core_recv.at[w],
            device_id=core_device(sibling),
            device_id_type=pl.DeviceIdType.MESH,
        )
        return own, far

    for w in range(y_chips):
        for copy in core_copies(w):
            copy.start()
    y_copies = []
    for k in range(y_chips):
        w = lax.rem(me_y + k, y_chips)
        own, far = core_copies(w)
        own.wait()
        far.wait_send()
        far.wait_recv()
        y_src[:, window(w)] = (
            core_buf[0, :, window(w)].astype(jnp.float32) + core_buf[1, :, window(w)].astype(jnp.float32)
        ).astype(y_src.dtype)
        if k == 0:
            copy = pltpu.make_async_copy(y_src.at[:, window(w)], y_buf.at[me_y], local_sems.at[1])
        else:
            copy = pltpu.make_async_remote_copy(
                src_ref=y_src.at[:, window(w)],
                dst_ref=y_buf.at[me_y],
                send_sem=send_sems.at[1, k],
                recv_sem=recv_sems.at[1, k],
                device_id=y_device(w),
                device_id_type=pl.DeviceIdType.MESH,
            )
        copy.start()
        y_copies.append(copy)
    y_copies[0].wait()
    for copy in y_copies[1:]:
        copy.wait_send()
        copy.wait_recv()
    z_src[...] = jnp.sum(y_buf[...].astype(jnp.float32), axis=0).astype(z_src.dtype)
    run_phase(
        Z_CHIPS, z_place, lane_blocks(Z_CHIPS), z_src, z_buf,
        local_sems.at[2], send_sems.at[2], recv_sems.at[2],
    )
    d_src[0] = jnp.sum(z_buf[...].astype(jnp.float32), axis=0).astype(d_src.dtype)
    group = lax.axis_index("grp")
    edge_copies = []
    for index, device in enumerate(neighbour_place(groups)):
        side, peer = divmod(index, groups)
        copy = pltpu.make_async_remote_copy(
            src_ref=d_src.at[0],
            dst_ref=edge_buf.at[side, group],
            send_sem=halo_send.at[side, peer],
            recv_sem=halo_recv.at[side, group],
            device_id=device,
            device_id_type=pl.DeviceIdType.MESH,
        )
        copy.start()
        edge_copies.append(copy)
    run_phase(groups, group_place, whole, d_src, d_buf, local_sems.at[3], send_sems.at[3], recv_sems.at[3])
    for copy in edge_copies:
        copy.wait_send()
    slab, count = lax.axis_index("slab"), lax.axis_size("slab")
    for side, step in enumerate((count - 1, 1)):
        for peer in range(groups):
            pltpu.make_async_remote_copy(
                src_ref=d_src.at[0],
                dst_ref=edge_buf.at[side, peer],
                send_sem=halo_send.at[side, peer],
                recv_sem=halo_recv.at[side, peer],
                device_id=(peer, lax.rem(slab + step, count)),
                device_id_type=pl.DeviceIdType.MESH,
            ).wait_recv()
    for half in range(2):
        total_ref[half] = jnp.sum(
            jnp.stack([d_buf[j].astype(jnp.float32) for j in range(half, groups, 2)]), axis=0
        )
        for side in range(2):
            halo_ref[side, half] = jnp.sum(
                jnp.stack([edge_buf[side, j].astype(jnp.float32) for j in range(half, groups, 2)]),
                axis=0,
            )


def reduce_chain(x, stencil, y_rows, side, y_chips, groups, collective_id):
    _, rows, width = x.shape
    band = width // (y_chips * Z_CHIPS)
    wide = 8
    depth = stencil[0].shape[1]
    return pl.pallas_call(
        functools.partial(reduce_chain_kernel, y_chips, groups),
        out_shape=[
            jax.ShapeDtypeStruct((2, rows, band), jnp.float32),
            jax.ShapeDtypeStruct((2, 2, rows, band), jnp.float32),
            jax.ShapeDtypeStruct((y_rows, depth), jnp.bfloat16),
            jax.ShapeDtypeStruct((side, depth), jnp.bfloat16),
        ],
        in_specs=[pl.BlockSpec(memory_space=pltpu.VMEM)] * 3,
        out_specs=[pl.BlockSpec(memory_space=pltpu.VMEM)] * 4,
        scratch_shapes=[
            pltpu.VMEM((2, rows, width), x.dtype),
            pltpu.VMEM((rows, width), jnp.bfloat16),
            pltpu.VMEM((y_chips, rows, width // y_chips), jnp.bfloat16),
            pltpu.VMEM((rows, width // y_chips), jnp.bfloat16),
            pltpu.VMEM((Z_CHIPS, rows, band), jnp.bfloat16),
            pltpu.VMEM((1, rows, band), jnp.bfloat16),
            pltpu.VMEM((groups, rows, band), jnp.bfloat16),
            pltpu.VMEM((2, groups, rows, band), jnp.bfloat16),
            pltpu.SemaphoreType.DMA((4,)),
            pltpu.SemaphoreType.DMA((4, wide)),
            pltpu.SemaphoreType.DMA((4, wide)),
            pltpu.SemaphoreType.DMA((2, groups)),
            pltpu.SemaphoreType.DMA((2, groups)),
            pltpu.SemaphoreType.DMA((y_chips,)),
            pltpu.SemaphoreType.DMA((y_chips,)),
            pltpu.SemaphoreType.DMA((y_chips,)),
        ],
        compiler_params=pltpu.CompilerParams(collective_id=collective_id, has_side_effects=True),
    )(x, *stencil)


def phase_kernel(row_count, half_cols, phase_ref):
    half = phase_ref.shape[1] // 2
    lanes = 128
    blocks = half // lanes
    shifts = phase_ref.shape[0]
    step = 2.0 * math.pi / row_count
    t_b = lax.broadcasted_iota(jnp.int32, (shifts, blocks), 0)
    q_b = lax.broadcasted_iota(jnp.int32, (shifts, blocks), 1)
    shift_rows_b = (t_b // 8 - SHIFTS // 16).astype(jnp.float32)
    block_rows = (q_b * (lanes // half_cols) - row_count // 2).astype(jnp.float32)
    block_angle = shift_rows_b * block_rows * step
    t_l = lax.broadcasted_iota(jnp.int32, (shifts, lanes), 0)
    l_l = lax.broadcasted_iota(jnp.int32, (shifts, lanes), 1)
    shift_rows_l = (t_l // 8 - SHIFTS // 16).astype(jnp.float32)
    shift_cols_l = (t_l % 8 - 4).astype(jnp.float32)
    lane_angle = (
        shift_rows_l * (l_l // half_cols).astype(jnp.float32)
        + shift_cols_l * (l_l % half_cols).astype(jnp.float32)
    ) * step
    cos_b, sin_b = jnp.cos(block_angle), jnp.sin(block_angle)
    c_l, s_l = jnp.cos(lane_angle), jnp.sin(lane_angle)
    for q in range(blocks):
        c_b, s_b = cos_b[:, q : q + 1], sin_b[:, q : q + 1]
        phase_ref[:, q * lanes : (q + 1) * lanes] = (c_b * c_l - s_b * s_l).astype(phase_ref.dtype)
        phase_ref[:, half + q * lanes : half + (q + 1) * lanes] = (s_b * c_l + c_b * s_l).astype(
            phase_ref.dtype
        )


def gather_chain_kernel(y_chips, row_count, half_cols, x_ref, out_ref, phase_ref, z_buf,
                        local_sems, send_sems, recv_sems, core_send, core_recv):
    arrive = signal_all(peers(Z_CHIPS, z_place) + peers(y_chips, y_place) + peers(2, core_place))
    phase_kernel(row_count, half_cols, phase_ref)
    arrive()
    run_phase(Z_CHIPS, z_place, whole, x_ref, z_buf, local_sems.at[0], send_sems.at[0], recv_sems.at[0])
    me_c, core_device = core_place()
    me_y, y_device = y_place()
    sibling = core_device(1 - me_c)

    def forward(block, source):
        return pltpu.make_async_remote_copy(
            src_ref=source,
            dst_ref=out_ref.at[me_c, block],
            send_sem=core_send.at[block],
            recv_sem=core_recv.at[block],
            device_id=sibling,
            device_id_type=pl.DeviceIdType.MESH,
        )

    own = pltpu.make_async_copy(z_buf, out_ref.at[me_c, me_y], local_sems.at[1])
    own.start()
    sent = [forward(me_y, z_buf)]
    sent[0].start()
    y_copies = []
    for k in range(1, y_chips):
        copy = pltpu.make_async_remote_copy(
            src_ref=z_buf,
            dst_ref=out_ref.at[me_c, me_y],
            send_sem=send_sems.at[1, k],
            recv_sem=recv_sems.at[1, k],
            device_id=y_device(lax.rem(me_y + k, y_chips)),
            device_id_type=pl.DeviceIdType.MESH,
        )
        copy.start()
        y_copies.append(copy)
    for k in range(1, y_chips):
        block = lax.rem(me_y + y_chips - k, y_chips)
        pltpu.make_async_remote_copy(
            src_ref=z_buf,
            dst_ref=out_ref.at[me_c, block],
            send_sem=send_sems.at[1, k],
            recv_sem=recv_sems.at[1, k],
            device_id=y_device(block),
            device_id_type=pl.DeviceIdType.MESH,
        ).wait_recv()
        copy = forward(block, out_ref.at[me_c, block])
        copy.start()
        sent.append(copy)
    own.wait()
    for copy in y_copies:
        copy.wait_send()
    for copy in sent:
        copy.wait_send()
    for k in range(y_chips):
        block = lax.rem(me_y + k, y_chips)
        pltpu.make_async_remote_copy(
            src_ref=z_buf,
            dst_ref=out_ref.at[1 - me_c, block],
            send_sem=core_send.at[block],
            recv_sem=core_recv.at[block],
            device_id=sibling,
            device_id_type=pl.DeviceIdType.MESH,
        ).wait_recv()


def gather_chain(x, row_count, half_cols, y_chips, collective_id):
    _, rows, lanes = x.shape
    shifts = SHIFTS
    table = 2 * row_count * half_cols
    return pl.pallas_call(
        functools.partial(gather_chain_kernel, y_chips, row_count, half_cols),
        out_shape=[
            jax.ShapeDtypeStruct((2, y_chips, Z_CHIPS, rows, lanes), x.dtype),
            jax.ShapeDtypeStruct((shifts, table), jnp.bfloat16),
        ],
        in_specs=[pl.BlockSpec(memory_space=pltpu.VMEM)],
        out_specs=[pl.BlockSpec(memory_space=pltpu.VMEM)] * 2,
        scratch_shapes=[
            pltpu.VMEM((Z_CHIPS, rows, lanes), x.dtype),
            pltpu.SemaphoreType.DMA((2,)),
            pltpu.SemaphoreType.DMA((2, Z_CHIPS)),
            pltpu.SemaphoreType.DMA((2, Z_CHIPS)),
            pltpu.SemaphoreType.DMA((y_chips,)),
            pltpu.SemaphoreType.DMA((y_chips,)),
        ],
        compiler_params=pltpu.CompilerParams(collective_id=collective_id, has_side_effects=True),
    )(x)


def align_frames(frames, ctf_rows, ref_re, ref_im, phase, score_scale):
    pixels = ctf_rows.shape[1]
    frame_re = frames[:, :pixels].astype(jnp.float32)
    frame_im = frames[:, pixels:].astype(jnp.float32)
    ref_re = ref_re.astype(jnp.float32)
    ref_im = ref_im.astype(jnp.float32)
    weight = ctf_rows.astype(jnp.float32)
    cross_terms = jnp.concatenate(
        [
            weight * (ref_re * frame_re + ref_im * frame_im),
            weight * (ref_re * frame_im - ref_im * frame_re),
        ],
        axis=1,
    ).astype(jnp.bfloat16)
    scores = score_scale * jnp.einsum(
        "np,sp->ns", cross_terms, phase, preferred_element_type=jnp.float32
    )
    shift_probs = jax.nn.softmax(scores, axis=1).astype(jnp.bfloat16)
    shift_mix = jnp.dot(shift_probs, phase, preferred_element_type=jnp.float32)
    mix_re = shift_mix[:, :pixels]
    mix_im = shift_mix[:, pixels:]
    return (
        weight * (frame_re * mix_re + frame_im * mix_im),
        weight * (frame_im * mix_re - frame_re * mix_im),
    )


def stencil_weights(base_cell, fraction, side_cells):
    cell_ids = jnp.arange(side_cells, dtype=jnp.int32)
    dense_weight = jnp.where(
        cell_ids[None, None, :] == base_cell[:, :, None], (1.0 - fraction)[:, :, None], 0.0
    )
    dense_weight = dense_weight + jnp.where(
        cell_ids[None, None, :] == base_cell[:, :, None] + 1, fraction[:, :, None], 0.0
    )
    return dense_weight.astype(jnp.bfloat16)


def local(
    images,
    image_class,
    image_ctf,
    class_owner,
    references,
    ctf_table,
    x_base,
    y_base,
    x_frac,
    y_frac,
    z_offset,
    z_frac,
):
    slab_count = lax.axis_size("slab")
    group_count = lax.axis_size("grp")
    frame_count = images.shape[0]
    pixels = ctf_table.shape[1]
    groups_ctf = ctf_table.shape[0]
    row_count = z_offset.shape[1]
    half_cols = x_base.shape[1]
    class_count = class_owner.shape[0]
    side_cells = 2 * row_count
    band_rows = row_count // slab_count
    band_pixels = band_rows * half_cols
    z_dev = 2 * band_rows
    score_scale = 2.0 / math.sqrt(2.0 * pixels)
    channel_scale = jnp.array(
        [
            1.0 / math.sqrt(frame_count * group_count),
            1.0 / math.sqrt(frame_count * group_count),
            1.0 / (frame_count * group_count),
        ],
        jnp.float32,
    )
    lanes = 128
    core = lax.rem(lax.axis_index("grp"), 2)
    ref_halves = references.reshape(2, -1, lanes)
    my_half = lax.dynamic_slice_in_dim(ref_halves, core, 1, 0)
    y_chips = slab_count // Z_CHIPS
    gathered, phase = gather_chain(my_half, row_count, half_cols, y_chips, 0)
    both_halves = gathered.reshape(2, slab_count, pixels)
    class_ids = jnp.arange(class_count, dtype=jnp.int32)
    owner_of = jnp.sum(
        jnp.where(image_class[:, None] == class_ids[None, :], class_owner[None, :], 0), axis=1
    )
    pick_ref = (owner_of[:, None] == jnp.arange(slab_count, dtype=jnp.int32)[None, :]).astype(
        jnp.bfloat16
    )
    ref_re = jnp.dot(pick_ref, both_halves[0], preferred_element_type=jnp.float32).astype(
        jnp.bfloat16
    )
    ref_im = jnp.dot(pick_ref, both_halves[1], preferred_element_type=jnp.float32).astype(
        jnp.bfloat16
    )
    pick_ctf = (image_ctf[:, None] == jnp.arange(groups_ctf, dtype=jnp.int32)[None, :]).astype(
        jnp.bfloat16
    )
    ctf_rows = jnp.dot(pick_ctf, ctf_table, preferred_element_type=jnp.float32).astype(
        jnp.bfloat16
    )
    stacked = align_frames(images, ctf_rows, ref_re, ref_im, phase, score_scale)
    member = (class_ids[:, None] == image_class[None, :]).astype(jnp.float32)
    aligned_re, aligned_im = stacked
    partial_re, partial_im = (
        jnp.dot(
            member, part, precision=lax.Precision.HIGHEST, preferred_element_type=jnp.float32
        ) * channel_scale[0]
        for part in (aligned_re, aligned_im)
    )
    half_classes = class_count // 2
    half_rows = half_classes * 2
    class_hits = (class_ids[:, None] == image_class[None, :]).astype(jnp.bfloat16)
    ctf_hits = (image_ctf[:, None] == jnp.arange(groups_ctf, dtype=jnp.int32)[None, :]).astype(
        jnp.bfloat16
    )
    counts = jnp.dot(class_hits, ctf_hits, preferred_element_type=jnp.float32)
    count_rows = class_count * groups_ctf // band_pixels
    tiled_counts = jnp.tile(counts.reshape(count_rows, band_pixels), (1, slab_count))
    rows = half_rows + count_rows
    by_half = jnp.stack(
        [
            jnp.concatenate(
                [
                    partial_re[h * half_classes : (h + 1) * half_classes],
                    partial_im[h * half_classes : (h + 1) * half_classes],
                    tiled_counts,
                ],
                axis=0,
            )
            for h in range(2)
        ]
    ).astype(jnp.bfloat16)
    y_rows = side_cells // group_count
    flat = class_count * half_cols
    stencil = (
        jnp.stack([y_base.reshape(flat), x_base.reshape(flat)]),
        jnp.stack([y_frac.reshape(flat), x_frac.reshape(flat)]),
    )
    total, halo, row_weights, col_weights = reduce_chain(
        by_half, stencil, y_rows, side_cells, slab_count // Z_CHIPS, group_count, 1
    )
    band = total[:, :half_rows].reshape(2, 2, half_classes, band_rows, half_cols)
    band = band.transpose(0, 2, 1, 3, 4).reshape(class_count, 2, band_rows, half_cols)
    total_counts = total[0, half_rows:].reshape(class_count, groups_ctf)
    halo = halo[:, :, :half_rows].reshape(2, 2, 2, half_classes, band_rows, half_cols)
    halo = halo.transpose(0, 1, 3, 2, 4, 5).reshape(2, class_count, 2, band_rows, half_cols)
    slab_index = lax.axis_index("slab")
    from_below = jnp.where(slab_index > 0, halo[0][:, :, band_rows - 1 :], 0.0)
    from_above = jnp.where(slab_index < slab_count - 1, halo[1][:, :, :1], 0.0)
    data_bands = jnp.concatenate([from_below, band, from_above], axis=2)
    slab_index = lax.axis_index("slab")
    ctf_sq = jnp.pad(
        jnp.square(ctf_table.astype(jnp.float32)), ((0, 0), (half_cols, half_cols))
    )
    window = lax.dynamic_slice_in_dim(
        ctf_sq, slab_index * band_pixels, band_pixels + 2 * half_cols, 1
    )
    weight_rows = jnp.dot(
        total_counts, window, precision=lax.Precision.HIGHEST, preferred_element_type=jnp.float32
    ) * channel_scale[2]
    class_bands = jnp.concatenate(
        [data_bands, weight_rows.reshape(class_count, 1, band_rows + 2, half_cols)], axis=1
    )
    group_index = lax.axis_index("grp")
    offset_pad = jnp.pad(z_offset, ((0, 0), (1, 1)))
    frac_pad = jnp.pad(z_frac, ((0, 0), (1, 1)))
    rows_held = band_rows + 2
    local_offset = lax.dynamic_slice_in_dim(offset_pad, slab_index * band_rows, rows_held, 1)
    local_frac = lax.dynamic_slice_in_dim(frac_pad, slab_index * band_rows, rows_held, 1)
    row_ids = jnp.arange(rows_held, dtype=jnp.int32) + (band_rows - 1)
    band_shift = (row_ids // band_rows - 1) * z_dev - 1
    target = 2 * (row_ids % band_rows)[None, :] + local_offset + 1 + band_shift[None, :]
    plane_ids = jnp.arange(z_dev, dtype=jnp.int32)
    depth_weight = jnp.where(
        plane_ids[None, None, :] == target[:, :, None], (1.0 - local_frac)[:, :, None], 0.0
    )
    depth_weight = depth_weight + jnp.where(
        plane_ids[None, None, :] == target[:, :, None] + 1, local_frac[:, :, None], 0.0
    )
    sectioned = jnp.einsum(
        "ckra,crz->kzca",
        class_bands,
        depth_weight,
        precision=lax.Precision.HIGHEST,
    ).reshape(3 * z_dev, class_count * half_cols)
    inserted = insert_planes(row_weights, sectioned, col_weights)
    return inserted.reshape(3, z_dev, y_rows, side_cells)


def insert_kernel(rows_ref, sec_ref, cols_ref, out_ref, lifted_ref):
    y_rows = rows_ref.shape[0]

    def body(i, carry):
        start = pl.multiple_of(i * y_rows, y_rows)
        lifted_ref[pl.ds(start, y_rows), :] = (
            rows_ref[...].astype(jnp.float32) * sec_ref[pl.ds(i, 1), :]
        ).astype(jnp.bfloat16)
        return carry

    lax.fori_loop(0, sec_ref.shape[0], body, 0)
    out_ref[...] = lax.dot_general(
        lifted_ref[...], cols_ref[...], (((1,), (1,)), ((), ())), preferred_element_type=jnp.float32
    )


def insert_planes(row_weights, sectioned, col_weights):
    planes = sectioned.shape[0]
    y_rows, depth = row_weights.shape
    side = col_weights.shape[0]
    return pl.pallas_call(
        insert_kernel,
        out_shape=jax.ShapeDtypeStruct((planes * y_rows, side), jnp.float32),
        in_specs=[pl.BlockSpec(memory_space=pltpu.VMEM)] * 3,
        out_specs=pl.BlockSpec(memory_space=pltpu.VMEM),
        scratch_shapes=[pltpu.VMEM((planes * y_rows, depth), jnp.bfloat16)],
        cost_estimate=pl.CostEstimate(
            flops=2 * planes * y_rows * depth * side,
            transcendentals=0,
            bytes_accessed=2 * y_rows * depth + 4 * planes * depth + 2 * depth * side
            + 4 * planes * y_rows * side,
        ),
    )(row_weights, sectioned, col_weights)


def solution(mesh):
    in_specs = (
        P(("grp", "slab"), None),
        P(("grp", "slab")),
        P(("grp", "slab")),
        P(),
        P("slab", None),
        P(),
        P(),
        P(),
        P(),
        P(),
        P(),
        P(),
    )
    out_specs = P(None, "slab", "grp", None)
    return jax.shard_map(local, mesh=mesh, in_specs=in_specs, out_specs=out_specs, check_vma=False)
```

```python
import functools
import math

import jax
import jax.numpy as jnp
from jax import lax
from jax.experimental import pallas as pl
from jax.experimental.pallas import tpu as pltpu
from jax.sharding import PartitionSpec as P

SHIFTS = 128
Z_CHIPS = 8


def exchange_kernel(count, place, picks, *refs):
    parts = len(picks)
    x_refs, out_refs = refs[:parts], refs[parts : 2 * parts]
    local_sems, send_sems, recv_sems = refs[2 * parts :]
    me, device = place()
    barrier = pltpu.get_barrier_semaphore()
    for k in range(1, count):
        pl.semaphore_signal(
            barrier,
            1,
            device_id=device(lax.rem(me + k, count)),
            device_id_type=pl.DeviceIdType.MESH,
        )
    pl.semaphore_wait(barrier, count - 1)
    owns, copies = [], []
    for part, (pick, x_ref, out_ref) in enumerate(zip(picks, x_refs, out_refs)):
        own = pltpu.make_async_copy(pick(x_ref, me), out_ref.at[me], local_sems.at[part])
        own.start()
        owns.append(own)
        for k in range(1, count):
            peer = lax.rem(me + k, count)
            copy = pltpu.make_async_remote_copy(
                src_ref=pick(x_ref, peer),
                dst_ref=out_ref.at[me],
                send_sem=send_sems.at[part, k],
                recv_sem=recv_sems.at[part, k],
                device_id=device(peer),
                device_id_type=pl.DeviceIdType.MESH,
            )
            copy.start()
            copies.append(copy)
    for own in owns:
        own.wait()
    for copy in copies:
        copy.wait_send()
        copy.wait_recv()


def slab_place():
    group = lax.axis_index("grp")
    return lax.axis_index("slab"), lambda peer: (group, peer)


def core_place():
    group, slab = lax.axis_index("grp"), lax.axis_index("slab")
    return lax.rem(group, 2), lambda peer: (group - lax.rem(group, 2) + peer, slab)


def z_place():
    group, slab = lax.axis_index("grp"), lax.axis_index("slab")
    z = lax.rem(slab, Z_CHIPS)
    return z, lambda peer: (group, slab - z + peer)


def y_place():
    group, slab = lax.axis_index("grp"), lax.axis_index("slab")
    z = lax.rem(slab, Z_CHIPS)
    return slab // Z_CHIPS, lambda peer: (group, peer * Z_CHIPS + z)


def group_place():
    slab = lax.axis_index("slab")
    return lax.axis_index("grp"), lambda peer: (peer, slab)


def whole(x_ref, peer):
    return x_ref.at[0]


def entire(x_ref, peer):
    return x_ref


def row_block(x_ref, peer):
    return x_ref.at[peer]


def lane_blocks(count):
    def pick(x_ref, peer):
        width = x_ref.shape[1] // count
        return x_ref.at[:, pl.ds(pl.multiple_of(peer * width, width), width)]

    return pick


def exchange_many(xs, count, place, picks, collective_id, block_shapes):
    parts = len(xs)
    return pl.pallas_call(
        functools.partial(exchange_kernel, count, place, tuple(picks)),
        out_shape=[
            jax.ShapeDtypeStruct((count,) + shape, x.dtype) for x, shape in zip(xs, block_shapes)
        ],
        in_specs=[pl.BlockSpec(memory_space=pltpu.VMEM)] * parts,
        out_specs=[pl.BlockSpec(memory_space=pltpu.VMEM)] * parts,
        scratch_shapes=[
            pltpu.SemaphoreType.DMA((parts,)),
            pltpu.SemaphoreType.DMA((parts, count)),
            pltpu.SemaphoreType.DMA((parts, count)),
        ],
        compiler_params=pltpu.CompilerParams(collective_id=collective_id, has_side_effects=True),
    )(*xs)


def exchange(x, count, place, pick, collective_id, block_shape):
    return exchange_many([x], count, place, [pick], collective_id, [block_shape])[0]


def signal_all(devices):
    barrier = pltpu.get_barrier_semaphore()
    for device in devices:
        pl.semaphore_signal(barrier, 1, device_id=device, device_id_type=pl.DeviceIdType.MESH)
    return lambda: pl.semaphore_wait(barrier, len(devices))


def run_phase(count, place, pick, x_ref, out_ref, local_sem, send_sems, recv_sems):
    me, device = place()
    own = pltpu.make_async_copy(pick(x_ref, me), out_ref.at[me], local_sem)
    own.start()
    copies = []
    for k in range(1, count):
        peer = lax.rem(me + k, count)
        copy = pltpu.make_async_remote_copy(
            src_ref=pick(x_ref, peer),
            dst_ref=out_ref.at[me],
            send_sem=send_sems.at[k],
            recv_sem=recv_sems.at[k],
            device_id=device(peer),
            device_id_type=pl.DeviceIdType.MESH,
        )
        copy.start()
        copies.append(copy)
    own.wait()
    for copy in copies:
        copy.wait_send()
        copy.wait_recv()


def peers(count, place):
    me, device = place()
    return [device(lax.rem(me + k, count)) for k in range(1, count)]


def stencil_kernel(base_ref, frac_ref, rows_ref, cols_ref):
    y_rows = rows_ref.shape[0]
    y_ids = lax.axis_index("grp") * y_rows + lax.broadcasted_iota(jnp.int32, rows_ref.shape, 0)
    y_base, y_frac = base_ref[0:1, :], frac_ref[0:1, :]
    rows = jnp.where(y_ids == y_base, 1.0 - y_frac, 0.0) + jnp.where(y_ids == y_base + 1, y_frac, 0.0)
    rows_ref[...] = rows.astype(rows_ref.dtype)
    x_ids = lax.broadcasted_iota(jnp.int32, cols_ref.shape, 0)
    x_base, x_frac = base_ref[1:2, :], frac_ref[1:2, :]
    cols = jnp.where(x_ids == x_base, 1.0 - x_frac, 0.0) + jnp.where(x_ids == x_base + 1, x_frac, 0.0)
    cols_ref[...] = cols.astype(cols_ref.dtype)


def neighbour_place(groups):
    slab = lax.axis_index("slab")
    count = lax.axis_size("slab")
    return [
        (peer, lax.rem(slab + step, count))
        for step in (1, count - 1)
        for peer in range(groups)
    ]


def reduce_chain_kernel(y_chips, groups, x_ref, base_ref, frac_ref,
                        total_ref, halo_ref, rows_ref, cols_ref, core_buf, y_src, y_buf, z_src, z_buf,
                        d_src, d_buf, edge_buf, local_sems, send_sems, recv_sems, halo_send, halo_recv,
                        core_local, core_send, core_recv):
    arrive = signal_all(
        peers(2, core_place)
        + peers(y_chips, y_place)
        + peers(Z_CHIPS, z_place)
        + peers(groups, group_place)
        + neighbour_place(groups)
    )
    stencil_kernel(base_ref, frac_ref, rows_ref, cols_ref)
    arrive()
    me_c, core_device = core_place()
    sibling = 1 - me_c
    me_y, y_device = y_place()
    width = x_ref.shape[2] // y_chips

    def window(w):
        return pl.ds(pl.multiple_of(w * width, width), width)

    def core_copies(w):
        own = pltpu.make_async_copy(
            x_ref.at[me_c, :, window(w)], core_buf.at[me_c, :, window(w)], core_local.at[w]
        )
        far = pltpu.make_async_remote_copy(
            src_ref=x_ref.at[sibling, :, window(w)],
            dst_ref=core_buf.at[me_c, :, window(w)],
            send_sem=core_send.at[w],
            recv_sem=core_recv.at[w],
            device_id=core_device(sibling),
            device_id_type=pl.DeviceIdType.MESH,
        )
        return own, far

    for w in range(y_chips):
        for copy in core_copies(w):
            copy.start()
    y_copies = []
    for k in range(y_chips):
        w = lax.rem(me_y + k, y_chips)
        own, far = core_copies(w)
        own.wait()
        far.wait_send()
        far.wait_recv()
        y_src[:, window(w)] = (
            core_buf[0, :, window(w)].astype(jnp.float32) + core_buf[1, :, window(w)].astype(jnp.float32)
        ).astype(y_src.dtype)
        if k == 0:
            copy = pltpu.make_async_copy(y_src.at[:, window(w)], y_buf.at[me_y], local_sems.at[1])
        else:
            copy = pltpu.make_async_remote_copy(
                src_ref=y_src.at[:, window(w)],
                dst_ref=y_buf.at[me_y],
                send_sem=send_sems.at[1, k],
                recv_sem=recv_sems.at[1, k],
                device_id=y_device(w),
                device_id_type=pl.DeviceIdType.MESH,
            )
        copy.start()
        y_copies.append(copy)
    y_copies[0].wait()
    for copy in y_copies[1:]:
        copy.wait_send()
        copy.wait_recv()
    z_src[...] = jnp.sum(y_buf[...].astype(jnp.float32), axis=0).astype(z_src.dtype)
    run_phase(
        Z_CHIPS, z_place, lane_blocks(Z_CHIPS), z_src, z_buf,
        local_sems.at[2], send_sems.at[2], recv_sems.at[2],
    )
    d_src[0] = jnp.sum(z_buf[...].astype(jnp.float32), axis=0).astype(d_src.dtype)
    group = lax.axis_index("grp")
    edge_copies = []
    for index, device in enumerate(neighbour_place(groups)):
        side, peer = divmod(index, groups)
        copy = pltpu.make_async_remote_copy(
            src_ref=d_src.at[0],
            dst_ref=edge_buf.at[side, group],
            send_sem=halo_send.at[side, peer],
            recv_sem=halo_recv.at[side, group],
            device_id=device,
            device_id_type=pl.DeviceIdType.MESH,
        )
        copy.start()
        edge_copies.append(copy)
    run_phase(groups, group_place, whole, d_src, d_buf, local_sems.at[3], send_sems.at[3], recv_sems.at[3])
    for copy in edge_copies:
        copy.wait_send()
    slab, count = lax.axis_index("slab"), lax.axis_size("slab")
    for side, step in enumerate((count - 1, 1)):
        for peer in range(groups):
            pltpu.make_async_remote_copy(
                src_ref=d_src.at[0],
                dst_ref=edge_buf.at[side, peer],
                send_sem=halo_send.at[side, peer],
                recv_sem=halo_recv.at[side, peer],
                device_id=(peer, lax.rem(slab + step, count)),
                device_id_type=pl.DeviceIdType.MESH,
            ).wait_recv()
    for half in range(2):
        total_ref[half] = jnp.sum(
            jnp.stack([d_buf[j].astype(jnp.float32) for j in range(half, groups, 2)]), axis=0
        )
        for side in range(2):
            halo_ref[side, half] = jnp.sum(
                jnp.stack([edge_buf[side, j].astype(jnp.float32) for j in range(half, groups, 2)]),
                axis=0,
            )


def reduce_chain(x, stencil, y_rows, side, y_chips, groups, collective_id):
    _, rows, width = x.shape
    band = width // (y_chips * Z_CHIPS)
    wide = 8
    depth = stencil[0].shape[1]
    return pl.pallas_call(
        functools.partial(reduce_chain_kernel, y_chips, groups),
        out_shape=[
            jax.ShapeDtypeStruct((2, rows, band), jnp.float32),
            jax.ShapeDtypeStruct((2, 2, rows, band), jnp.float32),
            jax.ShapeDtypeStruct((y_rows, depth), jnp.bfloat16),
            jax.ShapeDtypeStruct((side, depth), jnp.bfloat16),
        ],
        in_specs=[pl.BlockSpec(memory_space=pltpu.VMEM)] * 3,
        out_specs=[pl.BlockSpec(memory_space=pltpu.VMEM)] * 4,
        scratch_shapes=[
            pltpu.VMEM((2, rows, width), x.dtype),
            pltpu.VMEM((rows, width), jnp.bfloat16),
            pltpu.VMEM((y_chips, rows, width // y_chips), jnp.bfloat16),
            pltpu.VMEM((rows, width // y_chips), jnp.bfloat16),
            pltpu.VMEM((Z_CHIPS, rows, band), jnp.bfloat16),
            pltpu.VMEM((1, rows, band), jnp.bfloat16),
            pltpu.VMEM((groups, rows, band), jnp.bfloat16),
            pltpu.VMEM((2, groups, rows, band), jnp.bfloat16),
            pltpu.SemaphoreType.DMA((4,)),
            pltpu.SemaphoreType.DMA((4, wide)),
            pltpu.SemaphoreType.DMA((4, wide)),
            pltpu.SemaphoreType.DMA((2, groups)),
            pltpu.SemaphoreType.DMA((2, groups)),
            pltpu.SemaphoreType.DMA((y_chips,)),
            pltpu.SemaphoreType.DMA((y_chips,)),
            pltpu.SemaphoreType.DMA((y_chips,)),
        ],
        compiler_params=pltpu.CompilerParams(collective_id=collective_id, has_side_effects=True),
    )(x, *stencil)


def phase_kernel(row_count, half_cols, phase_ref):
    half = phase_ref.shape[1] // 2
    lanes = 128
    blocks = half // lanes
    shifts = phase_ref.shape[0]
    step = 2.0 * math.pi / row_count
    t_b = lax.broadcasted_iota(jnp.int32, (shifts, blocks), 0)
    q_b = lax.broadcasted_iota(jnp.int32, (shifts, blocks), 1)
    shift_rows_b = (t_b // 8 - SHIFTS // 16).astype(jnp.float32)
    block_rows = (q_b * (lanes // half_cols) - row_count // 2).astype(jnp.float32)
    block_angle = shift_rows_b * block_rows * step
    t_l = lax.broadcasted_iota(jnp.int32, (shifts, lanes), 0)
    l_l = lax.broadcasted_iota(jnp.int32, (shifts, lanes), 1)
    shift_rows_l = (t_l // 8 - SHIFTS // 16).astype(jnp.float32)
    shift_cols_l = (t_l % 8 - 4).astype(jnp.float32)
    lane_angle = (
        shift_rows_l * (l_l // half_cols).astype(jnp.float32)
        + shift_cols_l * (l_l % half_cols).astype(jnp.float32)
    ) * step
    cos_b, sin_b = jnp.cos(block_angle), jnp.sin(block_angle)
    c_l, s_l = jnp.cos(lane_angle), jnp.sin(lane_angle)
    for q in range(blocks):
        c_b, s_b = cos_b[:, q : q + 1], sin_b[:, q : q + 1]
        phase_ref[:, q * lanes : (q + 1) * lanes] = (c_b * c_l - s_b * s_l).astype(phase_ref.dtype)
        phase_ref[:, half + q * lanes : half + (q + 1) * lanes] = (s_b * c_l + c_b * s_l).astype(
            phase_ref.dtype
        )


def gather_chain_kernel(y_chips, row_count, half_cols, x_ref, out_ref, phase_ref, z_buf, y_buf,
                        local_sems, send_sems, recv_sems):
    arrive = signal_all(peers(Z_CHIPS, z_place) + peers(y_chips, y_place) + peers(2, core_place))
    phase_kernel(row_count, half_cols, phase_ref)
    arrive()
    run_phase(Z_CHIPS, z_place, whole, x_ref, z_buf, local_sems.at[0], send_sems.at[0], recv_sems.at[0])
    run_phase(y_chips, y_place, entire, z_buf, y_buf, local_sems.at[1], send_sems.at[1], recv_sems.at[1])
    run_phase(2, core_place, entire, y_buf, out_ref, local_sems.at[2], send_sems.at[2], recv_sems.at[2])


def gather_chain(x, row_count, half_cols, y_chips, collective_id):
    _, rows, lanes = x.shape
    shifts = SHIFTS
    table = 2 * row_count * half_cols
    return pl.pallas_call(
        functools.partial(gather_chain_kernel, y_chips, row_count, half_cols),
        out_shape=[
            jax.ShapeDtypeStruct((2, y_chips, Z_CHIPS, rows, lanes), x.dtype),
            jax.ShapeDtypeStruct((shifts, table), jnp.bfloat16),
        ],
        in_specs=[pl.BlockSpec(memory_space=pltpu.VMEM)],
        out_specs=[pl.BlockSpec(memory_space=pltpu.VMEM)] * 2,
        scratch_shapes=[
            pltpu.VMEM((Z_CHIPS, rows, lanes), x.dtype),
            pltpu.VMEM((y_chips, Z_CHIPS, rows, lanes), x.dtype),
            pltpu.SemaphoreType.DMA((3,)),
            pltpu.SemaphoreType.DMA((3, Z_CHIPS)),
            pltpu.SemaphoreType.DMA((3, Z_CHIPS)),
        ],
        compiler_params=pltpu.CompilerParams(collective_id=collective_id, has_side_effects=True),
    )(x)


def align_frames(frames, ctf_rows, ref_re, ref_im, phase, score_scale):
    pixels = ctf_rows.shape[1]
    frame_re = frames[:, :pixels].astype(jnp.float32)
    frame_im = frames[:, pixels:].astype(jnp.float32)
    ref_re = ref_re.astype(jnp.float32)
    ref_im = ref_im.astype(jnp.float32)
    weight = ctf_rows.astype(jnp.float32)
    cross_terms = jnp.concatenate(
        [
            weight * (ref_re * frame_re + ref_im * frame_im),
            weight * (ref_re * frame_im - ref_im * frame_re),
        ],
        axis=1,
    ).astype(jnp.bfloat16)
    scores = score_scale * jnp.einsum(
        "np,sp->ns", cross_terms, phase, preferred_element_type=jnp.float32
    )
    shift_probs = jax.nn.softmax(scores, axis=1).astype(jnp.bfloat16)
    shift_mix = jnp.dot(shift_probs, phase, preferred_element_type=jnp.float32)
    mix_re = shift_mix[:, :pixels]
    mix_im = shift_mix[:, pixels:]
    return (
        weight * (frame_re * mix_re + frame_im * mix_im),
        weight * (frame_im * mix_re - frame_re * mix_im),
    )


def stencil_weights(base_cell, fraction, side_cells):
    cell_ids = jnp.arange(side_cells, dtype=jnp.int32)
    dense_weight = jnp.where(
        cell_ids[None, None, :] == base_cell[:, :, None], (1.0 - fraction)[:, :, None], 0.0
    )
    dense_weight = dense_weight + jnp.where(
        cell_ids[None, None, :] == base_cell[:, :, None] + 1, fraction[:, :, None], 0.0
    )
    return dense_weight.astype(jnp.bfloat16)


def local(
    images,
    image_class,
    image_ctf,
    class_owner,
    references,
    ctf_table,
    x_base,
    y_base,
    x_frac,
    y_frac,
    z_offset,
    z_frac,
):
    slab_count = lax.axis_size("slab")
    group_count = lax.axis_size("grp")
    frame_count = images.shape[0]
    pixels = ctf_table.shape[1]
    groups_ctf = ctf_table.shape[0]
    row_count = z_offset.shape[1]
    half_cols = x_base.shape[1]
    class_count = class_owner.shape[0]
    side_cells = 2 * row_count
    band_rows = row_count // slab_count
    band_pixels = band_rows * half_cols
    z_dev = 2 * band_rows
    score_scale = 2.0 / math.sqrt(2.0 * pixels)
    channel_scale = jnp.array(
        [
            1.0 / math.sqrt(frame_count * group_count),
            1.0 / math.sqrt(frame_count * group_count),
            1.0 / (frame_count * group_count),
        ],
        jnp.float32,
    )
    lanes = 128
    core = lax.rem(lax.axis_index("grp"), 2)
    ref_halves = references.reshape(2, -1, lanes)
    my_half = lax.dynamic_slice_in_dim(ref_halves, core, 1, 0)
    y_chips = slab_count // Z_CHIPS
    gathered, phase = gather_chain(my_half, row_count, half_cols, y_chips, 0)
    both_halves = gathered.reshape(2, slab_count, pixels)
    class_ids = jnp.arange(class_count, dtype=jnp.int32)
    owner_of = jnp.sum(
        jnp.where(image_class[:, None] == class_ids[None, :], class_owner[None, :], 0), axis=1
    )
    pick_ref = (owner_of[:, None] == jnp.arange(slab_count, dtype=jnp.int32)[None, :]).astype(
        jnp.bfloat16
    )
    ref_re = jnp.dot(pick_ref, both_halves[0], preferred_element_type=jnp.float32).astype(
        jnp.bfloat16
    )
    ref_im = jnp.dot(pick_ref, both_halves[1], preferred_element_type=jnp.float32).astype(
        jnp.bfloat16
    )
    pick_ctf = (image_ctf[:, None] == jnp.arange(groups_ctf, dtype=jnp.int32)[None, :]).astype(
        jnp.bfloat16
    )
    ctf_rows = jnp.dot(pick_ctf, ctf_table, preferred_element_type=jnp.float32).astype(
        jnp.bfloat16
    )
    stacked = align_frames(images, ctf_rows, ref_re, ref_im, phase, score_scale)
    member = (class_ids[:, None] == image_class[None, :]).astype(jnp.float32)
    aligned_re, aligned_im = stacked
    partial_re, partial_im = (
        jnp.dot(
            member, part, precision=lax.Precision.HIGHEST, preferred_element_type=jnp.float32
        ) * channel_scale[0]
        for part in (aligned_re, aligned_im)
    )
    half_classes = class_count // 2
    half_rows = half_classes * 2
    class_hits = (class_ids[:, None] == image_class[None, :]).astype(jnp.bfloat16)
    ctf_hits = (image_ctf[:, None] == jnp.arange(groups_ctf, dtype=jnp.int32)[None, :]).astype(
        jnp.bfloat16
    )
    counts = jnp.dot(class_hits, ctf_hits, preferred_element_type=jnp.float32)
    count_rows = class_count * groups_ctf // band_pixels
    tiled_counts = jnp.tile(counts.reshape(count_rows, band_pixels), (1, slab_count))
    rows = half_rows + count_rows
    by_half = jnp.stack(
        [
            jnp.concatenate(
                [
                    partial_re[h * half_classes : (h + 1) * half_classes],
                    partial_im[h * half_classes : (h + 1) * half_classes],
                    tiled_counts,
                ],
                axis=0,
            )
            for h in range(2)
        ]
    ).astype(jnp.bfloat16)
    y_rows = side_cells // group_count
    flat = class_count * half_cols
    stencil = (
        jnp.stack([y_base.reshape(flat), x_base.reshape(flat)]),
        jnp.stack([y_frac.reshape(flat), x_frac.reshape(flat)]),
    )
    total, halo, row_weights, col_weights = reduce_chain(
        by_half, stencil, y_rows, side_cells, slab_count // Z_CHIPS, group_count, 1
    )
    band = total[:, :half_rows].reshape(2, 2, half_classes, band_rows, half_cols)
    band = band.transpose(0, 2, 1, 3, 4).reshape(class_count, 2, band_rows, half_cols)
    total_counts = total[0, half_rows:].reshape(class_count, groups_ctf)
    halo = halo[:, :, :half_rows].reshape(2, 2, 2, half_classes, band_rows, half_cols)
    halo = halo.transpose(0, 1, 3, 2, 4, 5).reshape(2, class_count, 2, band_rows, half_cols)
    slab_index = lax.axis_index("slab")
    from_below = jnp.where(slab_index > 0, halo[0][:, :, band_rows - 1 :], 0.0)
    from_above = jnp.where(slab_index < slab_count - 1, halo[1][:, :, :1], 0.0)
    data_bands = jnp.concatenate([from_below, band, from_above], axis=2)
    slab_index = lax.axis_index("slab")
    ctf_sq = jnp.pad(
        jnp.square(ctf_table.astype(jnp.float32)), ((0, 0), (half_cols, half_cols))
    )
    window = lax.dynamic_slice_in_dim(
        ctf_sq, slab_index * band_pixels, band_pixels + 2 * half_cols, 1
    )
    weight_rows = jnp.dot(
        total_counts, window, precision=lax.Precision.HIGHEST, preferred_element_type=jnp.float32
    ) * channel_scale[2]
    class_bands = jnp.concatenate(
        [data_bands, weight_rows.reshape(class_count, 1, band_rows + 2, half_cols)], axis=1
    )
    group_index = lax.axis_index("grp")
    offset_pad = jnp.pad(z_offset, ((0, 0), (1, 1)))
    frac_pad = jnp.pad(z_frac, ((0, 0), (1, 1)))
    rows_held = band_rows + 2
    local_offset = lax.dynamic_slice_in_dim(offset_pad, slab_index * band_rows, rows_held, 1)
    local_frac = lax.dynamic_slice_in_dim(frac_pad, slab_index * band_rows, rows_held, 1)
    row_ids = jnp.arange(rows_held, dtype=jnp.int32) + (band_rows - 1)
    band_shift = (row_ids // band_rows - 1) * z_dev - 1
    target = 2 * (row_ids % band_rows)[None, :] + local_offset + 1 + band_shift[None, :]
    plane_ids = jnp.arange(z_dev, dtype=jnp.int32)
    depth_weight = jnp.where(
        plane_ids[None, None, :] == target[:, :, None], (1.0 - local_frac)[:, :, None], 0.0
    )
    depth_weight = depth_weight + jnp.where(
        plane_ids[None, None, :] == target[:, :, None] + 1, local_frac[:, :, None], 0.0
    )
    sectioned = jnp.einsum(
        "ckra,crz->kzca",
        class_bands,
        depth_weight,
        precision=lax.Precision.HIGHEST,
    ).reshape(3 * z_dev, class_count * half_cols)
    inserted = insert_planes(row_weights, sectioned, col_weights)
    return inserted.reshape(3, z_dev, y_rows, side_cells)


def insert_kernel(rows_ref, sec_ref, cols_ref, out_ref, lifted_ref):
    y_rows = rows_ref.shape[0]

    def body(i, carry):
        start = pl.multiple_of(i * y_rows, y_rows)
        lifted_ref[pl.ds(start, y_rows), :] = (
            rows_ref[...].astype(jnp.float32) * sec_ref[pl.ds(i, 1), :]
        ).astype(jnp.bfloat16)
        return carry

    lax.fori_loop(0, sec_ref.shape[0], body, 0, unroll=True)
    out_ref[...] = lax.dot_general(
        lifted_ref[...], cols_ref[...], (((1,), (1,)), ((), ())), preferred_element_type=jnp.float32
    )


def insert_planes(row_weights, sectioned, col_weights):
    planes = sectioned.shape[0]
    y_rows, depth = row_weights.shape
    side = col_weights.shape[0]
    return pl.pallas_call(
        insert_kernel,
        out_shape=jax.ShapeDtypeStruct((planes * y_rows, side), jnp.float32),
        in_specs=[pl.BlockSpec(memory_space=pltpu.VMEM)] * 3,
        out_specs=pl.BlockSpec(memory_space=pltpu.VMEM),
        scratch_shapes=[pltpu.VMEM((planes * y_rows, depth), jnp.bfloat16)],
        cost_estimate=pl.CostEstimate(
            flops=2 * planes * y_rows * depth * side,
            transcendentals=0,
            bytes_accessed=2 * y_rows * depth + 4 * planes * depth + 2 * depth * side
            + 4 * planes * y_rows * side,
        ),
    )(row_weights, sectioned, col_weights)


def solution(mesh):
    in_specs = (
        P(("grp", "slab"), None),
        P(("grp", "slab")),
        P(("grp", "slab")),
        P(),
        P("slab", None),
        P(),
        P(),
        P(),
        P(),
        P(),
        P(),
        P(),
    )
    out_specs = P(None, "slab", "grp", None)
    return jax.shard_map(local, mesh=mesh, in_specs=in_specs, out_specs=out_specs, check_vma=False)
```

```python
import functools
import math

import jax
import jax.numpy as jnp
from jax import lax
from jax.experimental import pallas as pl
from jax.experimental.pallas import tpu as pltpu
from jax.sharding import PartitionSpec as P

SHIFTS = 128
Z_CHIPS = 8


def exchange_kernel(count, place, picks, *refs):
    parts = len(picks)
    x_refs, out_refs = refs[:parts], refs[parts : 2 * parts]
    local_sems, send_sems, recv_sems = refs[2 * parts :]
    me, device = place()
    barrier = pltpu.get_barrier_semaphore()
    for k in range(1, count):
        pl.semaphore_signal(
            barrier,
            1,
            device_id=device(lax.rem(me + k, count)),
            device_id_type=pl.DeviceIdType.MESH,
        )
    pl.semaphore_wait(barrier, count - 1)
    owns, copies = [], []
    for part, (pick, x_ref, out_ref) in enumerate(zip(picks, x_refs, out_refs)):
        own = pltpu.make_async_copy(pick(x_ref, me), out_ref.at[me], local_sems.at[part])
        own.start()
        owns.append(own)
        for k in range(1, count):
            peer = lax.rem(me + k, count)
            copy = pltpu.make_async_remote_copy(
                src_ref=pick(x_ref, peer),
                dst_ref=out_ref.at[me],
                send_sem=send_sems.at[part, k],
                recv_sem=recv_sems.at[part, k],
                device_id=device(peer),
                device_id_type=pl.DeviceIdType.MESH,
            )
            copy.start()
            copies.append(copy)
    for own in owns:
        own.wait()
    for copy in copies:
        copy.wait_send()
        copy.wait_recv()


def slab_place():
    group = lax.axis_index("grp")
    return lax.axis_index("slab"), lambda peer: (group, peer)


def core_place():
    group, slab = lax.axis_index("grp"), lax.axis_index("slab")
    return lax.rem(group, 2), lambda peer: (group - lax.rem(group, 2) + peer, slab)


def z_place():
    group, slab = lax.axis_index("grp"), lax.axis_index("slab")
    z = lax.rem(slab, Z_CHIPS)
    return z, lambda peer: (group, slab - z + peer)


def y_place():
    group, slab = lax.axis_index("grp"), lax.axis_index("slab")
    z = lax.rem(slab, Z_CHIPS)
    return slab // Z_CHIPS, lambda peer: (group, peer * Z_CHIPS + z)


def group_place():
    slab = lax.axis_index("slab")
    return lax.axis_index("grp"), lambda peer: (peer, slab)


def whole(x_ref, peer):
    return x_ref.at[0]


def entire(x_ref, peer):
    return x_ref


def row_block(x_ref, peer):
    return x_ref.at[peer]


def lane_blocks(count):
    def pick(x_ref, peer):
        width = x_ref.shape[1] // count
        return x_ref.at[:, pl.ds(pl.multiple_of(peer * width, width), width)]

    return pick


def exchange_many(xs, count, place, picks, collective_id, block_shapes):
    parts = len(xs)
    return pl.pallas_call(
        functools.partial(exchange_kernel, count, place, tuple(picks)),
        out_shape=[
            jax.ShapeDtypeStruct((count,) + shape, x.dtype) for x, shape in zip(xs, block_shapes)
        ],
        in_specs=[pl.BlockSpec(memory_space=pltpu.VMEM)] * parts,
        out_specs=[pl.BlockSpec(memory_space=pltpu.VMEM)] * parts,
        scratch_shapes=[
            pltpu.SemaphoreType.DMA((parts,)),
            pltpu.SemaphoreType.DMA((parts, count)),
            pltpu.SemaphoreType.DMA((parts, count)),
        ],
        compiler_params=pltpu.CompilerParams(collective_id=collective_id, has_side_effects=True),
    )(*xs)


def exchange(x, count, place, pick, collective_id, block_shape):
    return exchange_many([x], count, place, [pick], collective_id, [block_shape])[0]


def signal_all(devices):
    barrier = pltpu.get_barrier_semaphore()
    for device in devices:
        pl.semaphore_signal(barrier, 1, device_id=device, device_id_type=pl.DeviceIdType.MESH)
    return lambda: pl.semaphore_wait(barrier, len(devices))


def run_phase(count, place, pick, x_ref, out_ref, local_sem, send_sems, recv_sems):
    me, device = place()
    own = pltpu.make_async_copy(pick(x_ref, me), out_ref.at[me], local_sem)
    own.start()
    copies = []
    for k in range(1, count):
        peer = lax.rem(me + k, count)
        copy = pltpu.make_async_remote_copy(
            src_ref=pick(x_ref, peer),
            dst_ref=out_ref.at[me],
            send_sem=send_sems.at[k],
            recv_sem=recv_sems.at[k],
            device_id=device(peer),
            device_id_type=pl.DeviceIdType.MESH,
        )
        copy.start()
        copies.append(copy)
    own.wait()
    for copy in copies:
        copy.wait_send()
        copy.wait_recv()


def peers(count, place):
    me, device = place()
    return [device(lax.rem(me + k, count)) for k in range(1, count)]


def stencil_kernel(table_ref, rows_ref, cols_ref):
    y_rows = rows_ref.shape[0]
    y_ids = (
        lax.axis_index("grp") * y_rows + lax.broadcasted_iota(jnp.int32, rows_ref.shape, 0)
    ).astype(jnp.float32)
    y_base, y_frac = table_ref[0:1, :], table_ref[1:2, :]
    rows = jnp.where(y_ids == y_base, 1.0 - y_frac, 0.0) + jnp.where(y_ids == y_base + 1, y_frac, 0.0)
    rows_ref[...] = rows.astype(rows_ref.dtype)
    x_ids = lax.broadcasted_iota(jnp.int32, cols_ref.shape, 0).astype(jnp.float32)
    x_base, x_frac = table_ref[2:3, :], table_ref[3:4, :]
    cols = jnp.where(x_ids == x_base, 1.0 - x_frac, 0.0) + jnp.where(x_ids == x_base + 1, x_frac, 0.0)
    cols_ref[...] = cols.astype(cols_ref.dtype)


def neighbour_place(groups):
    slab = lax.axis_index("slab")
    count = lax.axis_size("slab")
    return [
        (peer, lax.rem(slab + step, count))
        for step in (1, count - 1)
        for peer in range(groups)
    ]


def reduce_chain_kernel(y_chips, groups, x_ref, table_ref,
                        total_ref, halo_ref, rows_ref, cols_ref, core_buf, y_src, y_buf, z_src, z_buf,
                        d_src, d_buf, edge_buf, local_sems, send_sems, recv_sems, halo_send, halo_recv,
                        core_local, core_send, core_recv):
    arrive = signal_all(
        peers(2, core_place)
        + peers(y_chips, y_place)
        + peers(Z_CHIPS, z_place)
        + peers(groups, group_place)
        + neighbour_place(groups)
    )
    stencil_kernel(table_ref, rows_ref, cols_ref)
    arrive()
    me_c, core_device = core_place()
    sibling = 1 - me_c
    me_y, y_device = y_place()
    width = x_ref.shape[2] // y_chips

    def window(w):
        return pl.ds(pl.multiple_of(w * width, width), width)

    def core_copies(w):
        own = pltpu.make_async_copy(
            x_ref.at[me_c, :, window(w)], core_buf.at[me_c, :, window(w)], core_local.at[w]
        )
        far = pltpu.make_async_remote_copy(
            src_ref=x_ref.at[sibling, :, window(w)],
            dst_ref=core_buf.at[me_c, :, window(w)],
            send_sem=core_send.at[w],
            recv_sem=core_recv.at[w],
            device_id=core_device(sibling),
            device_id_type=pl.DeviceIdType.MESH,
        )
        return own, far

    for w in range(y_chips):
        for copy in core_copies(w):
            copy.start()
    y_copies = []
    for k in range(y_chips):
        w = lax.rem(me_y + k, y_chips)
        own, far = core_copies(w)
        own.wait()
        far.wait_send()
        far.wait_recv()
        y_src[:, window(w)] = (
            core_buf[0, :, window(w)].astype(jnp.float32) + core_buf[1, :, window(w)].astype(jnp.float32)
        ).astype(y_src.dtype)
        if k == 0:
            copy = pltpu.make_async_copy(y_src.at[:, window(w)], y_buf.at[me_y], local_sems.at[1])
        else:
            copy = pltpu.make_async_remote_copy(
                src_ref=y_src.at[:, window(w)],
                dst_ref=y_buf.at[me_y],
                send_sem=send_sems.at[1, k],
                recv_sem=recv_sems.at[1, k],
                device_id=y_device(w),
                device_id_type=pl.DeviceIdType.MESH,
            )
        copy.start()
        y_copies.append(copy)
    y_copies[0].wait()
    for copy in y_copies[1:]:
        copy.wait_send()
        copy.wait_recv()
    z_src[...] = jnp.sum(y_buf[...].astype(jnp.float32), axis=0).astype(z_src.dtype)
    run_phase(
        Z_CHIPS, z_place, lane_blocks(Z_CHIPS), z_src, z_buf,
        local_sems.at[2], send_sems.at[2], recv_sems.at[2],
    )
    d_src[0] = jnp.sum(z_buf[...].astype(jnp.float32), axis=0).astype(d_src.dtype)
    group = lax.axis_index("grp")
    edge_copies = []
    for index, device in enumerate(neighbour_place(groups)):
        side, peer = divmod(index, groups)
        copy = pltpu.make_async_remote_copy(
            src_ref=d_src.at[0],
            dst_ref=edge_buf.at[side, group],
            send_sem=halo_send.at[side, peer],
            recv_sem=halo_recv.at[side, group],
            device_id=device,
            device_id_type=pl.DeviceIdType.MESH,
        )
        copy.start()
        edge_copies.append(copy)
    run_phase(groups, group_place, whole, d_src, d_buf, local_sems.at[3], send_sems.at[3], recv_sems.at[3])
    for copy in edge_copies:
        copy.wait_send()
    slab, count = lax.axis_index("slab"), lax.axis_size("slab")
    for side, step in enumerate((count - 1, 1)):
        for peer in range(groups):
            pltpu.make_async_remote_copy(
                src_ref=d_src.at[0],
                dst_ref=edge_buf.at[side, peer],
                send_sem=halo_send.at[side, peer],
                recv_sem=halo_recv.at[side, peer],
                device_id=(peer, lax.rem(slab + step, count)),
                device_id_type=pl.DeviceIdType.MESH,
            ).wait_recv()
    for half in range(2):
        total_ref[half] = jnp.sum(
            jnp.stack([d_buf[j].astype(jnp.float32) for j in range(half, groups, 2)]), axis=0
        )
        for side in range(2):
            halo_ref[side, half] = jnp.sum(
                jnp.stack([edge_buf[side, j].astype(jnp.float32) for j in range(half, groups, 2)]),
                axis=0,
            )


def reduce_chain(x, stencil, y_rows, side, y_chips, groups, collective_id):
    _, rows, width = x.shape
    band = width // (y_chips * Z_CHIPS)
    wide = 8
    depth = stencil[0].shape[1]
    return pl.pallas_call(
        functools.partial(reduce_chain_kernel, y_chips, groups),
        out_shape=[
            jax.ShapeDtypeStruct((2, rows, band), jnp.float32),
            jax.ShapeDtypeStruct((2, 2, rows, band), jnp.float32),
            jax.ShapeDtypeStruct((y_rows, depth), jnp.bfloat16),
            jax.ShapeDtypeStruct((side, depth), jnp.bfloat16),
        ],
        in_specs=[pl.BlockSpec(memory_space=pltpu.VMEM)] * 2,
        out_specs=[pl.BlockSpec(memory_space=pltpu.VMEM)] * 4,
        scratch_shapes=[
            pltpu.VMEM((2, rows, width), x.dtype),
            pltpu.VMEM((rows, width), jnp.bfloat16),
            pltpu.VMEM((y_chips, rows, width // y_chips), jnp.bfloat16),
            pltpu.VMEM((rows, width // y_chips), jnp.bfloat16),
            pltpu.VMEM((Z_CHIPS, rows, band), jnp.bfloat16),
            pltpu.VMEM((1, rows, band), jnp.bfloat16),
            pltpu.VMEM((groups, rows, band), jnp.bfloat16),
            pltpu.VMEM((2, groups, rows, band), jnp.bfloat16),
            pltpu.SemaphoreType.DMA((4,)),
            pltpu.SemaphoreType.DMA((4, wide)),
            pltpu.SemaphoreType.DMA((4, wide)),
            pltpu.SemaphoreType.DMA((2, groups)),
            pltpu.SemaphoreType.DMA((2, groups)),
            pltpu.SemaphoreType.DMA((y_chips,)),
            pltpu.SemaphoreType.DMA((y_chips,)),
            pltpu.SemaphoreType.DMA((y_chips,)),
        ],
        compiler_params=pltpu.CompilerParams(collective_id=collective_id, has_side_effects=True),
    )(x, *stencil)


def phase_kernel(row_count, half_cols, phase_ref):
    half = phase_ref.shape[1] // 2
    lanes = 128
    blocks = half // lanes
    shifts = phase_ref.shape[0]
    step = 2.0 * math.pi / row_count
    t_b = lax.broadcasted_iota(jnp.int32, (shifts, blocks), 0)
    q_b = lax.broadcasted_iota(jnp.int32, (shifts, blocks), 1)
    shift_rows_b = (t_b // 8 - SHIFTS // 16).astype(jnp.float32)
    block_rows = (q_b * (lanes // half_cols) - row_count // 2).astype(jnp.float32)
    block_angle = shift_rows_b * block_rows * step
    t_l = lax.broadcasted_iota(jnp.int32, (shifts, lanes), 0)
    l_l = lax.broadcasted_iota(jnp.int32, (shifts, lanes), 1)
    shift_rows_l = (t_l // 8 - SHIFTS // 16).astype(jnp.float32)
    shift_cols_l = (t_l % 8 - 4).astype(jnp.float32)
    lane_angle = (
        shift_rows_l * (l_l // half_cols).astype(jnp.float32)
        + shift_cols_l * (l_l % half_cols).astype(jnp.float32)
    ) * step
    cos_b, sin_b = jnp.cos(block_angle), jnp.sin(block_angle)
    c_l, s_l = jnp.cos(lane_angle), jnp.sin(lane_angle)
    for q in range(blocks):
        c_b, s_b = cos_b[:, q : q + 1], sin_b[:, q : q + 1]
        phase_ref[:, q * lanes : (q + 1) * lanes] = (c_b * c_l - s_b * s_l).astype(phase_ref.dtype)
        phase_ref[:, half + q * lanes : half + (q + 1) * lanes] = (s_b * c_l + c_b * s_l).astype(
            phase_ref.dtype
        )


def gather_chain_kernel(y_chips, row_count, half_cols, x_ref, out_ref, phase_ref, z_buf, y_buf,
                        local_sems, send_sems, recv_sems):
    arrive = signal_all(peers(Z_CHIPS, z_place) + peers(y_chips, y_place) + peers(2, core_place))
    phase_kernel(row_count, half_cols, phase_ref)
    arrive()
    run_phase(Z_CHIPS, z_place, whole, x_ref, z_buf, local_sems.at[0], send_sems.at[0], recv_sems.at[0])
    run_phase(y_chips, y_place, entire, z_buf, y_buf, local_sems.at[1], send_sems.at[1], recv_sems.at[1])
    run_phase(2, core_place, entire, y_buf, out_ref, local_sems.at[2], send_sems.at[2], recv_sems.at[2])


def gather_chain(x, row_count, half_cols, y_chips, collective_id):
    _, rows, lanes = x.shape
    shifts = SHIFTS
    table = 2 * row_count * half_cols
    return pl.pallas_call(
        functools.partial(gather_chain_kernel, y_chips, row_count, half_cols),
        out_shape=[
            jax.ShapeDtypeStruct((2, y_chips, Z_CHIPS, rows, lanes), x.dtype),
            jax.ShapeDtypeStruct((shifts, table), jnp.bfloat16),
        ],
        in_specs=[pl.BlockSpec(memory_space=pltpu.VMEM)],
        out_specs=[pl.BlockSpec(memory_space=pltpu.VMEM)] * 2,
        scratch_shapes=[
            pltpu.VMEM((Z_CHIPS, rows, lanes), x.dtype),
            pltpu.VMEM((y_chips, Z_CHIPS, rows, lanes), x.dtype),
            pltpu.SemaphoreType.DMA((3,)),
            pltpu.SemaphoreType.DMA((3, Z_CHIPS)),
            pltpu.SemaphoreType.DMA((3, Z_CHIPS)),
        ],
        compiler_params=pltpu.CompilerParams(collective_id=collective_id, has_side_effects=True),
    )(x)


def align_frames(frames, ctf_rows, ref_re, ref_im, phase, score_scale):
    pixels = ctf_rows.shape[1]
    frame_re = frames[:, :pixels].astype(jnp.float32)
    frame_im = frames[:, pixels:].astype(jnp.float32)
    ref_re = ref_re.astype(jnp.float32)
    ref_im = ref_im.astype(jnp.float32)
    weight = ctf_rows.astype(jnp.float32)
    cross_terms = jnp.concatenate(
        [
            weight * (ref_re * frame_re + ref_im * frame_im),
            weight * (ref_re * frame_im - ref_im * frame_re),
        ],
        axis=1,
    ).astype(jnp.bfloat16)
    scores = score_scale * jnp.einsum(
        "np,sp->ns", cross_terms, phase, preferred_element_type=jnp.float32
    )
    shift_probs = jax.nn.softmax(scores, axis=1).astype(jnp.bfloat16)
    shift_mix = jnp.dot(shift_probs, phase, preferred_element_type=jnp.float32)
    mix_re = shift_mix[:, :pixels]
    mix_im = shift_mix[:, pixels:]
    return (
        weight * (frame_re * mix_re + frame_im * mix_im),
        weight * (frame_im * mix_re - frame_re * mix_im),
    )


def stencil_weights(base_cell, fraction, side_cells):
    cell_ids = jnp.arange(side_cells, dtype=jnp.int32)
    dense_weight = jnp.where(
        cell_ids[None, None, :] == base_cell[:, :, None], (1.0 - fraction)[:, :, None], 0.0
    )
    dense_weight = dense_weight + jnp.where(
        cell_ids[None, None, :] == base_cell[:, :, None] + 1, fraction[:, :, None], 0.0
    )
    return dense_weight.astype(jnp.bfloat16)


def local(
    images,
    image_class,
    image_ctf,
    class_owner,
    references,
    ctf_table,
    x_base,
    y_base,
    x_frac,
    y_frac,
    z_offset,
    z_frac,
):
    slab_count = lax.axis_size("slab")
    group_count = lax.axis_size("grp")
    frame_count = images.shape[0]
    pixels = ctf_table.shape[1]
    groups_ctf = ctf_table.shape[0]
    row_count = z_offset.shape[1]
    half_cols = x_base.shape[1]
    class_count = class_owner.shape[0]
    side_cells = 2 * row_count
    band_rows = row_count // slab_count
    band_pixels = band_rows * half_cols
    z_dev = 2 * band_rows
    score_scale = 2.0 / math.sqrt(2.0 * pixels)
    channel_scale = jnp.array(
        [
            1.0 / math.sqrt(frame_count * group_count),
            1.0 / math.sqrt(frame_count * group_count),
            1.0 / (frame_count * group_count),
        ],
        jnp.float32,
    )
    lanes = 128
    core = lax.rem(lax.axis_index("grp"), 2)
    ref_halves = references.reshape(2, -1, lanes)
    my_half = lax.dynamic_slice_in_dim(ref_halves, core, 1, 0)
    y_chips = slab_count // Z_CHIPS
    gathered, phase = gather_chain(my_half, row_count, half_cols, y_chips, 0)
    both_halves = gathered.reshape(2, slab_count, pixels)
    class_ids = jnp.arange(class_count, dtype=jnp.int32)
    owner_of = jnp.sum(
        jnp.where(image_class[:, None] == class_ids[None, :], class_owner[None, :], 0), axis=1
    )
    pick_ref = (owner_of[:, None] == jnp.arange(slab_count, dtype=jnp.int32)[None, :]).astype(
        jnp.bfloat16
    )
    ref_re = jnp.dot(pick_ref, both_halves[0], preferred_element_type=jnp.float32).astype(
        jnp.bfloat16
    )
    ref_im = jnp.dot(pick_ref, both_halves[1], preferred_element_type=jnp.float32).astype(
        jnp.bfloat16
    )
    pick_ctf = (image_ctf[:, None] == jnp.arange(groups_ctf, dtype=jnp.int32)[None, :]).astype(
        jnp.bfloat16
    )
    ctf_rows = jnp.dot(pick_ctf, ctf_table, preferred_element_type=jnp.float32).astype(
        jnp.bfloat16
    )
    stacked = align_frames(images, ctf_rows, ref_re, ref_im, phase, score_scale)
    member = (class_ids[:, None] == image_class[None, :]).astype(jnp.float32)
    aligned_re, aligned_im = stacked
    partial_re, partial_im = (
        jnp.dot(
            member, part, precision=lax.Precision.HIGHEST, preferred_element_type=jnp.float32
        ) * channel_scale[0]
        for part in (aligned_re, aligned_im)
    )
    half_classes = class_count // 2
    half_rows = half_classes * 2
    class_hits = (class_ids[:, None] == image_class[None, :]).astype(jnp.bfloat16)
    ctf_hits = (image_ctf[:, None] == jnp.arange(groups_ctf, dtype=jnp.int32)[None, :]).astype(
        jnp.bfloat16
    )
    counts = jnp.dot(class_hits, ctf_hits, preferred_element_type=jnp.float32)
    count_rows = class_count * groups_ctf // band_pixels
    tiled_counts = jnp.tile(counts.reshape(count_rows, band_pixels), (1, slab_count))
    rows = half_rows + count_rows
    by_half = jnp.stack(
        [
            jnp.concatenate(
                [
                    partial_re[h * half_classes : (h + 1) * half_classes],
                    partial_im[h * half_classes : (h + 1) * half_classes],
                    tiled_counts,
                ],
                axis=0,
            )
            for h in range(2)
        ]
    ).astype(jnp.bfloat16)
    y_rows = side_cells // group_count
    flat = class_count * half_cols
    stencil = (
        jnp.stack(
            [
                y_base.reshape(flat).astype(jnp.float32),
                y_frac.reshape(flat),
                x_base.reshape(flat).astype(jnp.float32),
                x_frac.reshape(flat),
            ]
        ),
    )
    total, halo, row_weights, col_weights = reduce_chain(
        by_half, stencil, y_rows, side_cells, slab_count // Z_CHIPS, group_count, 1
    )
    band = total[:, :half_rows].reshape(2, 2, half_classes, band_rows, half_cols)
    band = band.transpose(0, 2, 1, 3, 4).reshape(class_count, 2, band_rows, half_cols)
    total_counts = total[0, half_rows:].reshape(class_count, groups_ctf)
    halo = halo[:, :, :half_rows].reshape(2, 2, 2, half_classes, band_rows, half_cols)
    halo = halo.transpose(0, 1, 3, 2, 4, 5).reshape(2, class_count, 2, band_rows, half_cols)
    slab_index = lax.axis_index("slab")
    from_below = jnp.where(slab_index > 0, halo[0][:, :, band_rows - 1 :], 0.0)
    from_above = jnp.where(slab_index < slab_count - 1, halo[1][:, :, :1], 0.0)
    data_bands = jnp.concatenate([from_below, band, from_above], axis=2)
    slab_index = lax.axis_index("slab")
    ctf_sq = jnp.pad(
        jnp.square(ctf_table.astype(jnp.float32)), ((0, 0), (half_cols, half_cols))
    )
    window = lax.dynamic_slice_in_dim(
        ctf_sq, slab_index * band_pixels, band_pixels + 2 * half_cols, 1
    )
    weight_rows = jnp.dot(
        total_counts, window, precision=lax.Precision.HIGHEST, preferred_element_type=jnp.float32
    ) * channel_scale[2]
    class_bands = jnp.concatenate(
        [data_bands, weight_rows.reshape(class_count, 1, band_rows + 2, half_cols)], axis=1
    )
    group_index = lax.axis_index("grp")
    offset_pad = jnp.pad(z_offset, ((0, 0), (1, 1)))
    frac_pad = jnp.pad(z_frac, ((0, 0), (1, 1)))
    rows_held = band_rows + 2
    local_offset = lax.dynamic_slice_in_dim(offset_pad, slab_index * band_rows, rows_held, 1)
    local_frac = lax.dynamic_slice_in_dim(frac_pad, slab_index * band_rows, rows_held, 1)
    row_ids = jnp.arange(rows_held, dtype=jnp.int32) + (band_rows - 1)
    band_shift = (row_ids // band_rows - 1) * z_dev - 1
    target = 2 * (row_ids % band_rows)[None, :] + local_offset + 1 + band_shift[None, :]
    plane_ids = jnp.arange(z_dev, dtype=jnp.int32)
    depth_weight = jnp.where(
        plane_ids[None, None, :] == target[:, :, None], (1.0 - local_frac)[:, :, None], 0.0
    )
    depth_weight = depth_weight + jnp.where(
        plane_ids[None, None, :] == target[:, :, None] + 1, local_frac[:, :, None], 0.0
    )
    sectioned = jnp.einsum(
        "ckra,crz->kzca",
        class_bands,
        depth_weight,
        precision=lax.Precision.HIGHEST,
    ).reshape(3 * z_dev, class_count * half_cols)
    inserted = insert_planes(row_weights, sectioned, col_weights)
    return inserted.reshape(3, z_dev, y_rows, side_cells)


def insert_kernel(rows_ref, sec_ref, cols_ref, out_ref, lifted_ref):
    y_rows = rows_ref.shape[0]

    def body(i, carry):
        start = pl.multiple_of(i * y_rows, y_rows)
        lifted_ref[pl.ds(start, y_rows), :] = (
            rows_ref[...].astype(jnp.float32) * sec_ref[pl.ds(i, 1), :]
        ).astype(jnp.bfloat16)
        return carry

    lax.fori_loop(0, sec_ref.shape[0], body, 0, unroll=True)
    out_ref[...] = lax.dot_general(
        lifted_ref[...], cols_ref[...], (((1,), (1,)), ((), ())), preferred_element_type=jnp.float32
    )


def insert_planes(row_weights, sectioned, col_weights):
    planes = sectioned.shape[0]
    y_rows, depth = row_weights.shape
    side = col_weights.shape[0]
    return pl.pallas_call(
        insert_kernel,
        out_shape=jax.ShapeDtypeStruct((planes * y_rows, side), jnp.float32),
        in_specs=[pl.BlockSpec(memory_space=pltpu.VMEM)] * 3,
        out_specs=pl.BlockSpec(memory_space=pltpu.VMEM),
        scratch_shapes=[pltpu.VMEM((planes * y_rows, depth), jnp.bfloat16)],
        cost_estimate=pl.CostEstimate(
            flops=2 * planes * y_rows * depth * side,
            transcendentals=0,
            bytes_accessed=2 * y_rows * depth + 4 * planes * depth + 2 * depth * side
            + 4 * planes * y_rows * side,
        ),
    )(row_weights, sectioned, col_weights)


def solution(mesh):
    in_specs = (
        P(("grp", "slab"), None),
        P(("grp", "slab")),
        P(("grp", "slab")),
        P(),
        P("slab", None),
        P(),
        P(),
        P(),
        P(),
        P(),
        P(),
        P(),
    )
    out_specs = P(None, "slab", "grp", None)
    return jax.shard_map(local, mesh=mesh, in_specs=in_specs, out_specs=out_specs, check_vma=False)
```

```python
import functools
import math

import jax
import jax.numpy as jnp
from jax import lax
from jax.experimental import pallas as pl
from jax.experimental.pallas import tpu as pltpu
from jax.sharding import PartitionSpec as P

SHIFTS = 128
Z_CHIPS = 8


def exchange_kernel(count, place, picks, *refs):
    parts = len(picks)
    x_refs, out_refs = refs[:parts], refs[parts : 2 * parts]
    local_sems, send_sems, recv_sems = refs[2 * parts :]
    me, device = place()
    barrier = pltpu.get_barrier_semaphore()
    for k in range(1, count):
        pl.semaphore_signal(
            barrier,
            1,
            device_id=device(lax.rem(me + k, count)),
            device_id_type=pl.DeviceIdType.MESH,
        )
    pl.semaphore_wait(barrier, count - 1)
    owns, copies = [], []
    for part, (pick, x_ref, out_ref) in enumerate(zip(picks, x_refs, out_refs)):
        own = pltpu.make_async_copy(pick(x_ref, me), out_ref.at[me], local_sems.at[part])
        own.start()
        owns.append(own)
        for k in range(1, count):
            peer = lax.rem(me + k, count)
            copy = pltpu.make_async_remote_copy(
                src_ref=pick(x_ref, peer),
                dst_ref=out_ref.at[me],
                send_sem=send_sems.at[part, k],
                recv_sem=recv_sems.at[part, k],
                device_id=device(peer),
                device_id_type=pl.DeviceIdType.MESH,
            )
            copy.start()
            copies.append(copy)
    for own in owns:
        own.wait()
    for copy in copies:
        copy.wait_send()
        copy.wait_recv()


def slab_place():
    group = lax.axis_index("grp")
    return lax.axis_index("slab"), lambda peer: (group, peer)


def core_place():
    group, slab = lax.axis_index("grp"), lax.axis_index("slab")
    return lax.rem(group, 2), lambda peer: (group - lax.rem(group, 2) + peer, slab)


def z_place():
    group, slab = lax.axis_index("grp"), lax.axis_index("slab")
    z = lax.rem(slab, Z_CHIPS)
    return z, lambda peer: (group, slab - z + peer)


def y_place():
    group, slab = lax.axis_index("grp"), lax.axis_index("slab")
    z = lax.rem(slab, Z_CHIPS)
    return slab // Z_CHIPS, lambda peer: (group, peer * Z_CHIPS + z)


def group_place():
    slab = lax.axis_index("slab")
    return lax.axis_index("grp"), lambda peer: (peer, slab)


def whole(x_ref, peer):
    return x_ref.at[0]


def entire(x_ref, peer):
    return x_ref


def row_block(x_ref, peer):
    return x_ref.at[peer]


def lane_blocks(count):
    def pick(x_ref, peer):
        width = x_ref.shape[1] // count
        return x_ref.at[:, pl.ds(pl.multiple_of(peer * width, width), width)]

    return pick


def exchange_many(xs, count, place, picks, collective_id, block_shapes):
    parts = len(xs)
    return pl.pallas_call(
        functools.partial(exchange_kernel, count, place, tuple(picks)),
        out_shape=[
            jax.ShapeDtypeStruct((count,) + shape, x.dtype) for x, shape in zip(xs, block_shapes)
        ],
        in_specs=[pl.BlockSpec(memory_space=pltpu.VMEM)] * parts,
        out_specs=[pl.BlockSpec(memory_space=pltpu.VMEM)] * parts,
        scratch_shapes=[
            pltpu.SemaphoreType.DMA((parts,)),
            pltpu.SemaphoreType.DMA((parts, count)),
            pltpu.SemaphoreType.DMA((parts, count)),
        ],
        compiler_params=pltpu.CompilerParams(collective_id=collective_id, has_side_effects=True),
    )(*xs)


def exchange(x, count, place, pick, collective_id, block_shape):
    return exchange_many([x], count, place, [pick], collective_id, [block_shape])[0]


def signal_all(devices):
    barrier = pltpu.get_barrier_semaphore()
    for device in devices:
        pl.semaphore_signal(barrier, 1, device_id=device, device_id_type=pl.DeviceIdType.MESH)
    return lambda: pl.semaphore_wait(barrier, len(devices))


def run_phase(count, place, pick, x_ref, out_ref, local_sem, send_sems, recv_sems):
    me, device = place()
    own = pltpu.make_async_copy(pick(x_ref, me), out_ref.at[me], local_sem)
    own.start()
    copies = []
    for k in range(1, count):
        peer = lax.rem(me + k, count)
        copy = pltpu.make_async_remote_copy(
            src_ref=pick(x_ref, peer),
            dst_ref=out_ref.at[me],
            send_sem=send_sems.at[k],
            recv_sem=recv_sems.at[k],
            device_id=device(peer),
            device_id_type=pl.DeviceIdType.MESH,
        )
        copy.start()
        copies.append(copy)
    own.wait()
    for copy in copies:
        copy.wait_send()
        copy.wait_recv()


def peers(count, place):
    me, device = place()
    return [device(lax.rem(me + k, count)) for k in range(1, count)]


def stencil_kernel(table_ref, rows_ref, cols_ref):
    y_rows = rows_ref.shape[0]
    y_ids = (
        lax.axis_index("grp") * y_rows + lax.broadcasted_iota(jnp.int32, rows_ref.shape, 0)
    ).astype(jnp.float32)
    y_base, y_frac = table_ref[0:1, :], table_ref[1:2, :]
    rows = jnp.where(y_ids == y_base, 1.0 - y_frac, 0.0) + jnp.where(y_ids == y_base + 1, y_frac, 0.0)
    rows_ref[...] = rows.astype(rows_ref.dtype)
    x_ids = lax.broadcasted_iota(jnp.int32, cols_ref.shape, 0).astype(jnp.float32)
    x_base, x_frac = table_ref[2:3, :], table_ref[3:4, :]
    cols = jnp.where(x_ids == x_base, 1.0 - x_frac, 0.0) + jnp.where(x_ids == x_base + 1, x_frac, 0.0)
    cols_ref[...] = cols.astype(cols_ref.dtype)


def neighbour_place(groups):
    slab = lax.axis_index("slab")
    count = lax.axis_size("slab")
    return [
        (peer, lax.rem(slab + step, count))
        for step in (1, count - 1)
        for peer in range(groups)
    ]


def reduce_chain_kernel(y_chips, groups, x_ref, table_ref,
                        total_ref, halo_ref, rows_ref, cols_ref, core_buf, y_src, y_buf, z_src, z_buf,
                        d_src, d_buf, edge_buf, local_sems, send_sems, recv_sems, halo_send, halo_recv,
                        core_local, core_send, core_recv):
    arrive = signal_all(
        peers(2, core_place)
        + peers(y_chips, y_place)
        + peers(Z_CHIPS, z_place)
        + peers(groups, group_place)
        + neighbour_place(groups)
    )
    stencil_kernel(table_ref, rows_ref, cols_ref)
    arrive()
    me_c, core_device = core_place()
    sibling = 1 - me_c
    me_y, y_device = y_place()
    width = x_ref.shape[2] // y_chips

    def window(w):
        return pl.ds(pl.multiple_of(w * width, width), width)

    def core_copies(w):
        own = pltpu.make_async_copy(
            x_ref.at[me_c, :, window(w)], core_buf.at[me_c, :, window(w)], core_local.at[w]
        )
        far = pltpu.make_async_remote_copy(
            src_ref=x_ref.at[sibling, :, window(w)],
            dst_ref=core_buf.at[me_c, :, window(w)],
            send_sem=core_send.at[w],
            recv_sem=core_recv.at[w],
            device_id=core_device(sibling),
            device_id_type=pl.DeviceIdType.MESH,
        )
        return own, far

    for w in range(y_chips):
        for copy in core_copies(w):
            copy.start()
    y_copies = []
    for k in range(y_chips):
        w = lax.rem(me_y + k, y_chips)
        own, far = core_copies(w)
        own.wait()
        far.wait_send()
        far.wait_recv()
        y_src[:, window(w)] = (
            core_buf[0, :, window(w)].astype(jnp.float32) + core_buf[1, :, window(w)].astype(jnp.float32)
        ).astype(y_src.dtype)
        if k == 0:
            copy = pltpu.make_async_copy(y_src.at[:, window(w)], y_buf.at[me_y], local_sems.at[1])
        else:
            copy = pltpu.make_async_remote_copy(
                src_ref=y_src.at[:, window(w)],
                dst_ref=y_buf.at[me_y],
                send_sem=send_sems.at[1, k],
                recv_sem=recv_sems.at[1, k],
                device_id=y_device(w),
                device_id_type=pl.DeviceIdType.MESH,
            )
        copy.start()
        y_copies.append(copy)
    y_copies[0].wait()
    for copy in y_copies[1:]:
        copy.wait_send()
        copy.wait_recv()
    z_src[...] = jnp.sum(y_buf[...].astype(jnp.float32), axis=0).astype(z_src.dtype)
    run_phase(
        Z_CHIPS, z_place, lane_blocks(Z_CHIPS), z_src, z_buf,
        local_sems.at[2], send_sems.at[2], recv_sems.at[2],
    )
    d_src[0] = jnp.sum(z_buf[...].astype(jnp.float32), axis=0).astype(d_src.dtype)
    group = lax.axis_index("grp")
    edge_copies = []
    for index, device in enumerate(neighbour_place(groups)):
        side, peer = divmod(index, groups)
        copy = pltpu.make_async_remote_copy(
            src_ref=d_src.at[0, : edge_buf.shape[2]],
            dst_ref=edge_buf.at[side, group],
            send_sem=halo_send.at[side, peer],
            recv_sem=halo_recv.at[side, group],
            device_id=device,
            device_id_type=pl.DeviceIdType.MESH,
        )
        copy.start()
        edge_copies.append(copy)
    run_phase(groups, group_place, whole, d_src, d_buf, local_sems.at[3], send_sems.at[3], recv_sems.at[3])
    for copy in edge_copies:
        copy.wait_send()
    slab, count = lax.axis_index("slab"), lax.axis_size("slab")
    for side, step in enumerate((count - 1, 1)):
        for peer in range(groups):
            pltpu.make_async_remote_copy(
                src_ref=d_src.at[0, : edge_buf.shape[2]],
                dst_ref=edge_buf.at[side, peer],
                send_sem=halo_send.at[side, peer],
                recv_sem=halo_recv.at[side, peer],
                device_id=(peer, lax.rem(slab + step, count)),
                device_id_type=pl.DeviceIdType.MESH,
            ).wait_recv()
    for half in range(2):
        total_ref[half] = jnp.sum(
            jnp.stack([d_buf[j].astype(jnp.float32) for j in range(half, groups, 2)]), axis=0
        )
        for side in range(2):
            halo_ref[side, half] = jnp.sum(
                jnp.stack([edge_buf[side, j].astype(jnp.float32) for j in range(half, groups, 2)]),
                axis=0,
            )


def reduce_chain(x, stencil, y_rows, side, y_chips, groups, collective_id):
    _, rows, width = x.shape
    band = width // (y_chips * Z_CHIPS)
    wide = 8
    depth = stencil[0].shape[1]
    data_rows = rows - 8
    return pl.pallas_call(
        functools.partial(reduce_chain_kernel, y_chips, groups),
        out_shape=[
            jax.ShapeDtypeStruct((2, rows, band), jnp.float32),
            jax.ShapeDtypeStruct((2, 2, data_rows, band), jnp.float32),
            jax.ShapeDtypeStruct((y_rows, depth), jnp.bfloat16),
            jax.ShapeDtypeStruct((side, depth), jnp.bfloat16),
        ],
        in_specs=[pl.BlockSpec(memory_space=pltpu.VMEM)] * 2,
        out_specs=[pl.BlockSpec(memory_space=pltpu.VMEM)] * 4,
        scratch_shapes=[
            pltpu.VMEM((2, rows, width), x.dtype),
            pltpu.VMEM((rows, width), jnp.bfloat16),
            pltpu.VMEM((y_chips, rows, width // y_chips), jnp.bfloat16),
            pltpu.VMEM((rows, width // y_chips), jnp.bfloat16),
            pltpu.VMEM((Z_CHIPS, rows, band), jnp.bfloat16),
            pltpu.VMEM((1, rows, band), jnp.bfloat16),
            pltpu.VMEM((groups, rows, band), jnp.bfloat16),
            pltpu.VMEM((2, groups, data_rows, band), jnp.bfloat16),
            pltpu.SemaphoreType.DMA((4,)),
            pltpu.SemaphoreType.DMA((4, wide)),
            pltpu.SemaphoreType.DMA((4, wide)),
            pltpu.SemaphoreType.DMA((2, groups)),
            pltpu.SemaphoreType.DMA((2, groups)),
            pltpu.SemaphoreType.DMA((y_chips,)),
            pltpu.SemaphoreType.DMA((y_chips,)),
            pltpu.SemaphoreType.DMA((y_chips,)),
        ],
        compiler_params=pltpu.CompilerParams(collective_id=collective_id, has_side_effects=True),
    )(x, *stencil)


def phase_kernel(row_count, half_cols, phase_ref):
    half = phase_ref.shape[1] // 2
    lanes = 128
    blocks = half // lanes
    shifts = phase_ref.shape[0]
    step = 2.0 * math.pi / row_count
    t_b = lax.broadcasted_iota(jnp.int32, (shifts, blocks), 0)
    q_b = lax.broadcasted_iota(jnp.int32, (shifts, blocks), 1)
    shift_rows_b = (t_b // 8 - SHIFTS // 16).astype(jnp.float32)
    block_rows = (q_b * (lanes // half_cols) - row_count // 2).astype(jnp.float32)
    block_angle = shift_rows_b * block_rows * step
    t_l = lax.broadcasted_iota(jnp.int32, (shifts, lanes), 0)
    l_l = lax.broadcasted_iota(jnp.int32, (shifts, lanes), 1)
    shift_rows_l = (t_l // 8 - SHIFTS // 16).astype(jnp.float32)
    shift_cols_l = (t_l % 8 - 4).astype(jnp.float32)
    lane_angle = (
        shift_rows_l * (l_l // half_cols).astype(jnp.float32)
        + shift_cols_l * (l_l % half_cols).astype(jnp.float32)
    ) * step
    cos_b, sin_b = jnp.cos(block_angle), jnp.sin(block_angle)
    c_l, s_l = jnp.cos(lane_angle), jnp.sin(lane_angle)
    for q in range(blocks):
        c_b, s_b = cos_b[:, q : q + 1], sin_b[:, q : q + 1]
        phase_ref[:, q * lanes : (q + 1) * lanes] = (c_b * c_l - s_b * s_l).astype(phase_ref.dtype)
        phase_ref[:, half + q * lanes : half + (q + 1) * lanes] = (s_b * c_l + c_b * s_l).astype(
            phase_ref.dtype
        )


def gather_chain_kernel(y_chips, row_count, half_cols, x_ref, out_ref, phase_ref, z_buf, y_buf,
                        local_sems, send_sems, recv_sems):
    arrive = signal_all(peers(Z_CHIPS, z_place) + peers(y_chips, y_place) + peers(2, core_place))
    phase_kernel(row_count, half_cols, phase_ref)
    arrive()
    run_phase(Z_CHIPS, z_place, whole, x_ref, z_buf, local_sems.at[0], send_sems.at[0], recv_sems.at[0])
    run_phase(y_chips, y_place, entire, z_buf, y_buf, local_sems.at[1], send_sems.at[1], recv_sems.at[1])
    run_phase(2, core_place, entire, y_buf, out_ref, local_sems.at[2], send_sems.at[2], recv_sems.at[2])


def gather_chain(x, row_count, half_cols, y_chips, collective_id):
    _, rows, lanes = x.shape
    shifts = SHIFTS
    table = 2 * row_count * half_cols
    return pl.pallas_call(
        functools.partial(gather_chain_kernel, y_chips, row_count, half_cols),
        out_shape=[
            jax.ShapeDtypeStruct((2, y_chips, Z_CHIPS, rows, lanes), x.dtype),
            jax.ShapeDtypeStruct((shifts, table), jnp.bfloat16),
        ],
        in_specs=[pl.BlockSpec(memory_space=pltpu.VMEM)],
        out_specs=[pl.BlockSpec(memory_space=pltpu.VMEM)] * 2,
        scratch_shapes=[
            pltpu.VMEM((Z_CHIPS, rows, lanes), x.dtype),
            pltpu.VMEM((y_chips, Z_CHIPS, rows, lanes), x.dtype),
            pltpu.SemaphoreType.DMA((3,)),
            pltpu.SemaphoreType.DMA((3, Z_CHIPS)),
            pltpu.SemaphoreType.DMA((3, Z_CHIPS)),
        ],
        compiler_params=pltpu.CompilerParams(collective_id=collective_id, has_side_effects=True),
    )(x)


def align_frames(frames, ctf_rows, ref_re, ref_im, phase, score_scale):
    pixels = ctf_rows.shape[1]
    frame_re = frames[:, :pixels].astype(jnp.float32)
    frame_im = frames[:, pixels:].astype(jnp.float32)
    ref_re = ref_re.astype(jnp.float32)
    ref_im = ref_im.astype(jnp.float32)
    weight = ctf_rows.astype(jnp.float32)
    cross_terms = jnp.concatenate(
        [
            weight * (ref_re * frame_re + ref_im * frame_im),
            weight * (ref_re * frame_im - ref_im * frame_re),
        ],
        axis=1,
    ).astype(jnp.bfloat16)
    scores = score_scale * jnp.einsum(
        "np,sp->ns", cross_terms, phase, preferred_element_type=jnp.float32
    )
    shift_probs = jax.nn.softmax(scores, axis=1).astype(jnp.bfloat16)
    shift_mix = jnp.dot(shift_probs, phase, preferred_element_type=jnp.float32)
    mix_re = shift_mix[:, :pixels]
    mix_im = shift_mix[:, pixels:]
    return (
        weight * (frame_re * mix_re + frame_im * mix_im),
        weight * (frame_im * mix_re - frame_re * mix_im),
    )


def stencil_weights(base_cell, fraction, side_cells):
    cell_ids = jnp.arange(side_cells, dtype=jnp.int32)
    dense_weight = jnp.where(
        cell_ids[None, None, :] == base_cell[:, :, None], (1.0 - fraction)[:, :, None], 0.0
    )
    dense_weight = dense_weight + jnp.where(
        cell_ids[None, None, :] == base_cell[:, :, None] + 1, fraction[:, :, None], 0.0
    )
    return dense_weight.astype(jnp.bfloat16)


def local(
    images,
    image_class,
    image_ctf,
    class_owner,
    references,
    ctf_table,
    x_base,
    y_base,
    x_frac,
    y_frac,
    z_offset,
    z_frac,
):
    slab_count = lax.axis_size("slab")
    group_count = lax.axis_size("grp")
    frame_count = images.shape[0]
    pixels = ctf_table.shape[1]
    groups_ctf = ctf_table.shape[0]
    row_count = z_offset.shape[1]
    half_cols = x_base.shape[1]
    class_count = class_owner.shape[0]
    side_cells = 2 * row_count
    band_rows = row_count // slab_count
    band_pixels = band_rows * half_cols
    z_dev = 2 * band_rows
    score_scale = 2.0 / math.sqrt(2.0 * pixels)
    channel_scale = jnp.array(
        [
            1.0 / math.sqrt(frame_count * group_count),
            1.0 / math.sqrt(frame_count * group_count),
            1.0 / (frame_count * group_count),
        ],
        jnp.float32,
    )
    lanes = 128
    core = lax.rem(lax.axis_index("grp"), 2)
    ref_halves = references.reshape(2, -1, lanes)
    my_half = lax.dynamic_slice_in_dim(ref_halves, core, 1, 0)
    y_chips = slab_count // Z_CHIPS
    gathered, phase = gather_chain(my_half, row_count, half_cols, y_chips, 0)
    both_halves = gathered.reshape(2, slab_count, pixels)
    class_ids = jnp.arange(class_count, dtype=jnp.int32)
    owner_of = jnp.sum(
        jnp.where(image_class[:, None] == class_ids[None, :], class_owner[None, :], 0), axis=1
    )
    pick_ref = (owner_of[:, None] == jnp.arange(slab_count, dtype=jnp.int32)[None, :]).astype(
        jnp.bfloat16
    )
    ref_re = jnp.dot(pick_ref, both_halves[0], preferred_element_type=jnp.float32).astype(
        jnp.bfloat16
    )
    ref_im = jnp.dot(pick_ref, both_halves[1], preferred_element_type=jnp.float32).astype(
        jnp.bfloat16
    )
    pick_ctf = (image_ctf[:, None] == jnp.arange(groups_ctf, dtype=jnp.int32)[None, :]).astype(
        jnp.bfloat16
    )
    ctf_rows = jnp.dot(pick_ctf, ctf_table, preferred_element_type=jnp.float32).astype(
        jnp.bfloat16
    )
    stacked = align_frames(images, ctf_rows, ref_re, ref_im, phase, score_scale)
    member = (class_ids[:, None] == image_class[None, :]).astype(jnp.float32)
    aligned_re, aligned_im = stacked
    partial_re, partial_im = (
        jnp.dot(
            member, part, precision=lax.Precision.HIGHEST, preferred_element_type=jnp.float32
        ) * channel_scale[0]
        for part in (aligned_re, aligned_im)
    )
    half_classes = class_count // 2
    half_rows = half_classes * 2
    class_hits = (class_ids[:, None] == image_class[None, :]).astype(jnp.bfloat16)
    ctf_hits = (image_ctf[:, None] == jnp.arange(groups_ctf, dtype=jnp.int32)[None, :]).astype(
        jnp.bfloat16
    )
    counts = jnp.dot(class_hits, ctf_hits, preferred_element_type=jnp.float32)
    count_rows = class_count * groups_ctf // band_pixels
    tiled_counts = jnp.tile(counts.reshape(count_rows, band_pixels), (1, slab_count))
    rows = half_rows + count_rows
    by_half = jnp.stack(
        [
            jnp.concatenate(
                [
                    partial_re[h * half_classes : (h + 1) * half_classes],
                    partial_im[h * half_classes : (h + 1) * half_classes],
                    tiled_counts,
                ],
                axis=0,
            )
            for h in range(2)
        ]
    ).astype(jnp.bfloat16)
    y_rows = side_cells // group_count
    flat = class_count * half_cols
    stencil = (
        jnp.stack(
            [
                y_base.reshape(flat).astype(jnp.float32),
                y_frac.reshape(flat),
                x_base.reshape(flat).astype(jnp.float32),
                x_frac.reshape(flat),
            ]
        ),
    )
    total, halo, row_weights, col_weights = reduce_chain(
        by_half, stencil, y_rows, side_cells, slab_count // Z_CHIPS, group_count, 1
    )
    band = total[:, :half_rows].reshape(2, 2, half_classes, band_rows, half_cols)
    band = band.transpose(0, 2, 1, 3, 4).reshape(class_count, 2, band_rows, half_cols)
    total_counts = total[0, half_rows:].reshape(class_count, groups_ctf)
    halo = halo[:, :, :half_rows].reshape(2, 2, 2, half_classes, band_rows, half_cols)
    halo = halo.transpose(0, 1, 3, 2, 4, 5).reshape(2, class_count, 2, band_rows, half_cols)
    slab_index = lax.axis_index("slab")
    from_below = jnp.where(slab_index > 0, halo[0][:, :, band_rows - 1 :], 0.0)
    from_above = jnp.where(slab_index < slab_count - 1, halo[1][:, :, :1], 0.0)
    data_bands = jnp.concatenate([from_below, band, from_above], axis=2)
    slab_index = lax.axis_index("slab")
    ctf_sq = jnp.pad(
        jnp.square(ctf_table.astype(jnp.float32)), ((0, 0), (half_cols, half_cols))
    )
    window = lax.dynamic_slice_in_dim(
        ctf_sq, slab_index * band_pixels, band_pixels + 2 * half_cols, 1
    )
    weight_rows = jnp.dot(
        total_counts, window, precision=lax.Precision.HIGHEST, preferred_element_type=jnp.float32
    ) * channel_scale[2]
    class_bands = jnp.concatenate(
        [data_bands, weight_rows.reshape(class_count, 1, band_rows + 2, half_cols)], axis=1
    )
    group_index = lax.axis_index("grp")
    offset_pad = jnp.pad(z_offset, ((0, 0), (1, 1)))
    frac_pad = jnp.pad(z_frac, ((0, 0), (1, 1)))
    rows_held = band_rows + 2
    local_offset = lax.dynamic_slice_in_dim(offset_pad, slab_index * band_rows, rows_held, 1)
    local_frac = lax.dynamic_slice_in_dim(frac_pad, slab_index * band_rows, rows_held, 1)
    row_ids = jnp.arange(rows_held, dtype=jnp.int32) + (band_rows - 1)
    band_shift = (row_ids // band_rows - 1) * z_dev - 1
    target = 2 * (row_ids % band_rows)[None, :] + local_offset + 1 + band_shift[None, :]
    plane_ids = jnp.arange(z_dev, dtype=jnp.int32)
    depth_weight = jnp.where(
        plane_ids[None, None, :] == target[:, :, None], (1.0 - local_frac)[:, :, None], 0.0
    )
    depth_weight = depth_weight + jnp.where(
        plane_ids[None, None, :] == target[:, :, None] + 1, local_frac[:, :, None], 0.0
    )
    sectioned = jnp.einsum(
        "ckra,crz->kzca",
        class_bands,
        depth_weight,
        precision=lax.Precision.HIGHEST,
    ).reshape(3 * z_dev, class_count * half_cols)
    inserted = insert_planes(row_weights, sectioned, col_weights)
    return inserted.reshape(3, z_dev, y_rows, side_cells)


def insert_kernel(rows_ref, sec_ref, cols_ref, out_ref, lifted_ref):
    y_rows = rows_ref.shape[0]

    def body(i, carry):
        start = pl.multiple_of(i * y_rows, y_rows)
        lifted_ref[pl.ds(start, y_rows), :] = (
            rows_ref[...].astype(jnp.float32) * sec_ref[pl.ds(i, 1), :]
        ).astype(jnp.bfloat16)
        return carry

    lax.fori_loop(0, sec_ref.shape[0], body, 0, unroll=True)
    out_ref[...] = lax.dot_general(
        lifted_ref[...], cols_ref[...], (((1,), (1,)), ((), ())), preferred_element_type=jnp.float32
    )


def insert_planes(row_weights, sectioned, col_weights):
    planes = sectioned.shape[0]
    y_rows, depth = row_weights.shape
    side = col_weights.shape[0]
    return pl.pallas_call(
        insert_kernel,
        out_shape=jax.ShapeDtypeStruct((planes * y_rows, side), jnp.float32),
        in_specs=[pl.BlockSpec(memory_space=pltpu.VMEM)] * 3,
        out_specs=pl.BlockSpec(memory_space=pltpu.VMEM),
        scratch_shapes=[pltpu.VMEM((planes * y_rows, depth), jnp.bfloat16)],
        cost_estimate=pl.CostEstimate(
            flops=2 * planes * y_rows * depth * side,
            transcendentals=0,
            bytes_accessed=2 * y_rows * depth + 4 * planes * depth + 2 * depth * side
            + 4 * planes * y_rows * side,
        ),
    )(row_weights, sectioned, col_weights)


def solution(mesh):
    in_specs = (
        P(("grp", "slab"), None),
        P(("grp", "slab")),
        P(("grp", "slab")),
        P(),
        P("slab", None),
        P(),
        P(),
        P(),
        P(),
        P(),
        P(),
        P(),
    )
    out_specs = P(None, "slab", "grp", None)
    return jax.shard_map(local, mesh=mesh, in_specs=in_specs, out_specs=out_specs, check_vma=False)
```
